32 devices in a mesh: dp: 2 (over x), row: 4 (over z), col: 4 (over y, core).
Axes of the slice: x: 2, y: 2, z: 4, core: 2. Of those that a mesh axis runs over, the one named last changes fastest.
Arguments:
- layer_in: bfloat16 [16384, 1024], P(('dp', 'col'), 'row'), may hold values from -6 to 6
- first_gain: bfloat16 [1024], P('row'), may hold values from 0.099609375 to 1.8984375
- first_shift: bfloat16 [1024], P('row'), may hold values from -4 to 4
- joined_weight: bfloat16 [1024, 3072], P('row', 'col'), may hold values from -0.1875 to 0.1875
- joined_bias: bfloat16 [16, 128], P('col'), may hold values from -6 to 6
- out_weight: bfloat16 [1024, 1024], P('col', 'row'), may hold values from -0.75 to 0.75
- out_bias: bfloat16 [1024], P('row'), may hold values from -4 to 4
- second_gain: bfloat16 [1024], P('row'), may hold values from 0.099609375 to 1.8984375
- second_shift: bfloat16 [1024], P('row'), may hold values from -4 to 4
- up_weight: bfloat16 [1024, 4096], P('row', 'col'), may hold values from -0.1875 to 0.1875
- up_bias: bfloat16 [4096], P('col'), may hold values from -6 to 6
- down_weight: bfloat16 [4096, 1024], P('col', 'row'), may hold values from -0.09375 to 0.09375
- down_bias: bfloat16 [1024], P('row'), may hold values from -4 to 4
- teacher: bfloat16 [16384, 1024], P(('dp', 'col'), 'row'), may hold values from -6 to 6
- valid: int32 [16384], P(('dp', 'col')), may hold values from 0 to 1, as said below
- cotangent: bfloat16 [16384, 1024], P(('dp', 'col'), 'row'), may hold values from -6 to 6
Outputs:
- layer_out: bfloat16 [16384, 1024], P(('dp', 'col'), 'row')
- loss: float32 [], replicated
- input_grad: float32 [16384, 1024], P(('dp', 'col'), 'row')
- first_gain_grad: float32 [1024], P('row')
- first_shift_grad: float32 [1024], P('row')
- joined_weight_grad: float32 [1024, 3072], P('row', 'col')
- joined_bias_grad: float32 [16, 128], P('col')
- out_weight_grad: float32 [1024, 1024], P('col', 'row')
- out_bias_grad: float32 [1024], P('row')
- second_gain_grad: float32 [1024], P('row')
- second_shift_grad: float32 [1024], P('row')
- up_weight_grad: float32 [1024, 4096], P('row', 'col')
- up_bias_grad: float32 [4096], P('col')
- down_weight_grad: float32 [4096, 1024], P('col', 'row')
- down_bias_grad: float32 [1024], P('row')
The draws below stay inside these ranges and needn't reach their ends.
Inputs may be any that keep to these rules, and one draw needn't show every extreme that they name: The last token is valid.
All inputs are finite; a program needn't handle non-finite values.
Results may differ from the reference program's by a relative error of at most 0.013.
Values may be sent and summed in bfloat16 or wider, within the bound.
A program may use at most 192 MiB of HBM per device.

```python
import math
import jax
import jax.numpy as jnp
from jax import lax

D = 1024
HEADS = 16
HEAD_DIM = 64
FF = 4096
SEQ = 2048
BLOCK = 256
QUERY_ROWS = 512
TOKENS = 16384


def draw_valid(key, part):
    position = jnp.arange(TOKENS, dtype=jnp.int32)
    ticket = jax.random.randint(key, (TOKENS,), 0, 4 * TOKENS, dtype=jnp.int32)
    valid_draw = (ticket < TOKENS + 2 * position).astype(jnp.int32)
    return valid_draw.at[TOKENS - 1].set(1)


def shard_levels(own_key, shape, shards, low, top_value):
    level, own = 1.0, jax.random.fold_in(own_key, 6)
    for dim, shards_of in shards:
        heights = jnp.exp(jax.random.uniform(jax.random.fold_in(own, dim), (shards_of,), jnp.float32, low / len(shards), top_value / len(shards)))
        level = level * jnp.repeat(heights, shape[dim] // shards_of).reshape([-1 if axis == dim else 1 for axis in range(len(shape))])
    return level


def noise(rng, dims, scale, limit, split=(), kind=jnp.bfloat16):
    entries = scale * jax.random.normal(rng, dims, jnp.float32)
    if split:
        entries = entries * shard_levels(rng, dims, split, -0.22, 0.18)
    return jnp.clip(entries, -limit, limit).astype(kind)


def setup_inputs(seed: int = 0) -> dict:
    splits = jax.random.split(jax.random.key(seed), 17)
    layer_in = noise(splits[0], (TOKENS, D), 1.0, 6.0, ((0, 8), (1, 4)))
    first_gain = jnp.clip(1.0 + 0.18 * jax.random.normal(splits[1], (D,), jnp.float32), 0.099609375, 1.8984375).astype(jnp.bfloat16)
    first_shift = noise(splits[2], (D,), 0.3, 4.0, ((0, 4),))
    joined_weight = noise(splits[3], (D, 3 * D), D ** -0.5, 0.1875, ((0, 4), (1, 4)))
    joined_bias = noise(splits[4], (HEADS, 2 * HEAD_DIM), 0.5, 6.0, ((0, 4),))
    out_weight = noise(splits[5], (D, D), (D // 16) ** -0.5, 0.75, ((0, 4), (1, 4)))
    out_bias = noise(splits[6], (D,), 0.3, 4.0, ((0, 4),))
    second_gain = jnp.clip(1.0 + 0.18 * jax.random.normal(splits[7], (D,), jnp.float32), 0.099609375, 1.8984375).astype(jnp.bfloat16)
    second_shift = noise(splits[8], (D,), 0.3, 4.0, ((0, 4),))
    up_weight = noise(splits[9], (D, FF), D ** -0.5, 0.1875, ((0, 4), (1, 4)))
    up_bias = noise(splits[10], (FF,), 0.5, 6.0, ((0, 4),))
    down_weight = noise(splits[11], (FF, D), FF ** -0.5, 0.09375, ((0, 4), (1, 4)))
    down_bias = noise(splits[12], (D,), 0.3, 4.0, ((0, 4),))
    teacher = noise(splits[13], (TOKENS, D), 1.0, 6.0, ((0, 8), (1, 4)))
    valid = draw_valid(jax.random.fold_in(splits[16], 71), 0)
    cotangent = noise(splits[15], (TOKENS, D), 1.0, 6.0, ((0, 8), (1, 4)))
    return dict(layer_in=layer_in, first_gain=first_gain, first_shift=first_shift, joined_weight=joined_weight, joined_bias=joined_bias, out_weight=out_weight, out_bias=out_bias, second_gain=second_gain, second_shift=second_shift, up_weight=up_weight, up_bias=up_bias, down_weight=down_weight, down_bias=down_bias, teacher=teacher, valid=valid, cotangent=cotangent)


EPSILON = 1e-05

@jax.custom_vjp
def low(v):
    return lax.optimization_barrier(v.astype(jnp.bfloat16)).astype(jnp.float32)

@jax.custom_vjp
def low_back(v):
    return v

def low_keep(v):
    return (low(v), None)

def low_pass(kept, grad):
    return (grad,)

def back_keep(v):
    return (v, None)

def back_low(kept, grad):
    return (low(grad),)
low.defvjp(low_keep, low_pass)
low_back.defvjp(back_keep, back_low)

def matmul(left_side, right_side):
    return jnp.dot(left_side, right_side, precision=lax.Precision.HIGHEST, preferred_element_type=jnp.float32)

def layer_norm(inputs, norm_gain, norm_shift):
    center = lax.optimization_barrier(jnp.mean(inputs, -1, keepdims=True))
    spread = lax.optimization_barrier(jnp.mean(inputs * inputs, -1, keepdims=True)) - center * center
    return (inputs - center) * lax.rsqrt(spread + EPSILON) * norm_gain + norm_shift

def head_slopes():
    return jnp.exp2(-8.0 * (jnp.arange(HEADS).astype(jnp.float32) + 1.0) / HEADS)

def block_scores(queries, key_rows, block_index, slopes):
    plain_scores = jnp.einsum('qhd,khd->hqk', queries, key_rows, precision=lax.Precision.HIGHEST) * (1.0 / math.sqrt(HEAD_DIM))
    query_place = block_index * QUERY_ROWS + jnp.arange(QUERY_ROWS, dtype=jnp.int32)
    key_place = jnp.arange(key_rows.shape[0], dtype=jnp.int32)
    distance = jnp.abs(query_place[:, None] - key_place[None, :]).astype(jnp.float32)
    allowed = key_place[None, :] // BLOCK <= query_place[:, None] // BLOCK
    return jnp.where(allowed[None], plain_scores - slopes[:, None, None] * distance[None], -1000000000.0)

def query_block(queries, key_rows, value_rows, block_index, slopes):
    scores = low_back(block_scores(queries, key_rows, block_index, slopes))
    chances = low(jax.nn.softmax(scores, axis=-1))
    return jnp.einsum('hqk,khd->qhd', chances, value_rows, precision=lax.Precision.HIGHEST)

def attention(mixed_rows):
    sequences = mixed_rows.reshape(-1, SEQ, HEADS, 3, HEAD_DIM)
    slopes = head_slopes()
    checked = jax.checkpoint(query_block)

    def one_sequence(sequence):

        def one_block(block_index):
            queries = lax.dynamic_slice_in_dim(sequence[:, :, 0], block_index * QUERY_ROWS, QUERY_ROWS, 0)
            return checked(queries, sequence[:, :, 1], sequence[:, :, 2], block_index, slopes)
        attended = lax.map(one_block, jnp.arange(SEQ // QUERY_ROWS, dtype=jnp.int32))
        return attended.reshape(SEQ, HEADS * HEAD_DIM)
    return lax.map(one_sequence, sequences).reshape(-1, HEADS * HEAD_DIM)

def forward(inputs, params):
    first_gain, first_shift, joined_weight, joined_bias, out_weight, out_bias, second_gain, second_shift, up_weight, up_bias, down_weight, down_bias = params
    normed_one = low(layer_norm(inputs, first_gain, first_shift))
    zero_rows = jnp.zeros_like(joined_bias[:, :HEAD_DIM])
    bias_rows = jnp.stack([joined_bias[:, :HEAD_DIM], zero_rows, joined_bias[:, HEAD_DIM:]], axis=1).reshape(3 * D)
    mixed_rows = low(low_back(matmul(normed_one, joined_weight) + bias_rows))
    attended = low(low_back(attention(mixed_rows)))
    middle = inputs + low_back(matmul(attended, out_weight) + out_bias)
    normed_two = low(layer_norm(middle, second_gain, second_shift))
    before = low_back(matmul(normed_two, up_weight) + up_bias)
    active = low(jax.nn.gelu(before, approximate=True))
    return middle + low_back(matmul(active, down_weight) + down_bias)

def reference(layer_in, first_gain, first_shift, joined_weight, joined_bias, out_weight, out_bias, second_gain, second_shift, up_weight, up_bias, down_weight, down_bias, teacher, valid, cotangent):
    params = (first_gain.astype(jnp.float32), first_shift.astype(jnp.float32), joined_weight.astype(jnp.float32), joined_bias.astype(jnp.float32), out_weight.astype(jnp.float32), out_bias.astype(jnp.float32), second_gain.astype(jnp.float32), second_shift.astype(jnp.float32), up_weight.astype(jnp.float32), up_bias.astype(jnp.float32), down_weight.astype(jnp.float32), down_bias.astype(jnp.float32))
    valid_rows = valid.astype(jnp.float32)
    valid_count = jnp.sum(valid_rows)
    loss_weight = TOKENS / (2.0 * valid_count)
    group_rows = 2 * SEQ
    group_count = TOKENS // group_rows

    def by_group(whole_array):
        return whole_array.reshape((group_count, group_rows) + whole_array.shape[1:])

    def objective(group_in, group_params, group_teacher, group_valid, group_cot):
        result = forward(group_in, group_params)
        error_rows = result - group_teacher
        squares = jnp.sum(group_valid[:, None] * error_rows * error_rows)
        return (jnp.sum(group_cot * result) + loss_weight * squares, (result, squares))

    def one_group(running, pieces):
        grad_totals, error_total = running
        group_in, group_teacher, group_valid, group_cot = pieces
        value_out, pullback, extras = jax.vjp(lambda state_rows, weights: objective(state_rows, weights, group_teacher, group_valid, group_cot), group_in, params, has_aux=True)
        grad_in, grad_params = pullback(jnp.ones_like(value_out))
        grad_totals = jax.tree.map(jnp.add, grad_totals, grad_params)
        return ((grad_totals, error_total + extras[1]), (extras[0], grad_in))
    zero_grads = jax.tree.map(jnp.zeros_like, params)
    (grad_totals, error_total), (results, grad_inputs) = lax.scan(one_group, (zero_grads, jnp.zeros((), jnp.float32)), (by_group(layer_in.astype(jnp.float32)), by_group(teacher.astype(jnp.float32)), by_group(valid_rows), by_group(cotangent.astype(jnp.float32))))
    loss_value = error_total / (D * valid_count)
    return (results.reshape(TOKENS, D).astype(jnp.bfloat16), loss_value, grad_inputs.reshape(TOKENS, D), grad_totals[0], grad_totals[1], grad_totals[2], grad_totals[3], grad_totals[4], grad_totals[5], grad_totals[6], grad_totals[7], grad_totals[8], grad_totals[9], grad_totals[10], grad_totals[11])
```

```python
import functools
import math

import jax
import jax.numpy as jnp
from jax import lax
from jax.experimental import pallas as pl
from jax.experimental.pallas import tpu as pltpu
from jax.sharding import PartitionSpec as P

D = 1024
HEADS = 16
SEQ = 2048
EPSILON = 1e-05
LOG2E = 1.4426950408889634
HEAD_DIM=64
BLOCK=256
HALF=64
PAIR=128
SCALE2 = LOG2E/8.0

def nt(a,b):
    return lax.dot_general(a,b,(((1,),(1,)),((),())),preferred_element_type=jnp.float32)
def nn(a,b):
    return jnp.dot(a,b,preferred_element_type=jnp.float32)
def tn(a,b):
    return lax.dot_general(a,b,(((0,),(0,)),((),())),preferred_element_type=jnp.float32)

def low_lanes(rows):
    return lax.broadcasted_iota(jnp.int32,(rows,PAIR),1) < HALF

def swap(a):
    return jnp.concatenate([a[:,HALF:],a[:,:HALF]],axis=1)

def fwd_kernel(heads, slope_ref, mixed_ref, out_ref, lse_ref, qs, ks, vs, bias, sc, mx, ls, acc):
    pairs=heads//2
    blocks=mixed_ref.shape[0]//BLOCK
    lo=low_lanes(BLOCK)
    @pl.loop(0,blocks)
    def _(b):
        rows=pl.ds(pl.multiple_of(b*BLOCK,BLOCK),BLOCK)
        for p in range(pairs):
            t0,t1,t2=(mixed_ref[rows,(3*p+n)*PAIR:(3*p+n+1)*PAIR] for n in range(3))
            zero=jnp.zeros_like(t0)
            qs[2*p,b]=jnp.where(lo,t0,zero)
            qs[2*p+1,b]=jnp.where(lo,zero,t1)
            ks[p,b]=jnp.where(lo,swap(t0),swap(t2))
            vs[p,b,:BLOCK]=jnp.where(lo,t1,zero)
            vs[p,b,BLOCK:]=jnp.where(lo,zero,t2)
    il=lax.broadcasted_iota(jnp.int32,(BLOCK,BLOCK),0)
    jl=lax.broadcasted_iota(jnp.int32,(BLOCK,BLOCK),1)
    tent=jnp.minimum(jl,2*il-jl).astype(jnp.float32)
    for h in range(heads):
        bias[h]=tent*slope_ref[h]
    jrow=lax.broadcasted_iota(jnp.int32,(1,BLOCK),1)
    @pl.loop(0,blocks)
    def _(i):
        for h in range(heads):
            t=nt(qs[h,i],ks[h//2,i])*SCALE2+bias[h]
            sc[h,i]=t
            mx[h]=jnp.maximum(t[:,:PAIR],t[:,PAIR:])
        @pl.loop(0,i)
        def _(j):
            place=(jrow+(j-i)*BLOCK).astype(jnp.float32)
            for h in range(heads):
                t=nt(qs[h,i],ks[h//2,j])*SCALE2+place*slope_ref[h]
                sc[h,j]=t
                mx[h]=jnp.maximum(mx[h],jnp.maximum(t[:,:PAIR],t[:,PAIR:]))
        for h in range(heads):
            mx[h]=jnp.broadcast_to(jnp.max(mx[h],1,keepdims=True),(BLOCK,PAIR))
            ls[h]=jnp.zeros((BLOCK,PAIR),jnp.float32)
        for p in range(pairs):
            acc[p]=jnp.zeros((BLOCK,PAIR),jnp.float32)
        @pl.loop(0,i+1)
        def _(j):
            for p in range(pairs):
                both=[]
                for h in (2*p,2*p+1):
                    m=mx[h]
                    ea=jnp.exp2(sc[h,j,:,:PAIR]-m)
                    eb=jnp.exp2(sc[h,j,:,PAIR:]-m)
                    ls[h]+=ea+eb
                    both+=[ea.astype(jnp.bfloat16),eb.astype(jnp.bfloat16)]
                acc[p]+=nn(jnp.concatenate(both,1),vs[p,j])
        rows=pl.ds(pl.multiple_of(i*BLOCK,BLOCK),BLOCK)
        for p in range(pairs):
            tot=[jnp.broadcast_to(jnp.sum(ls[h],1,keepdims=True),(BLOCK,PAIR)) for h in (2*p,2*p+1)]
            out_ref[rows,p*PAIR:(p+1)*PAIR]=(acc[p]/jnp.where(lo,tot[0],tot[1])).astype(out_ref.dtype)
            for n,h in enumerate((2*p,2*p+1)):
                lse=mx[h]+jnp.log2(tot[n])
                lse_ref[h,pl.ds(i,1),:]=lse.T[:1]

def attention_forward(slopes2, mixed):
    tokens,width=mixed.shape
    heads=width//(3*HEAD_DIM); pairs=heads//2; blocks=tokens//BLOCK
    f32=jnp.float32; bf=jnp.bfloat16
    return pl.pallas_call(
        functools.partial(fwd_kernel,heads),
        out_shape=(jax.ShapeDtypeStruct((tokens,heads*HEAD_DIM),bf),jax.ShapeDtypeStruct((heads,blocks,BLOCK),f32)),
        in_specs=[pl.BlockSpec(memory_space=pltpu.SMEM),pl.BlockSpec(memory_space=pltpu.VMEM)],
        out_specs=(pl.BlockSpec(memory_space=pltpu.VMEM),)*2,
        scratch_shapes=[pltpu.VMEM((heads,blocks,BLOCK,PAIR),bf),pltpu.VMEM((pairs,blocks,BLOCK,PAIR),bf),
            pltpu.VMEM((pairs,blocks,2*BLOCK,PAIR),bf),pltpu.VMEM((heads,BLOCK,BLOCK),f32),
            pltpu.VMEM((heads,blocks,BLOCK,BLOCK),f32),pltpu.VMEM((heads,BLOCK,PAIR),f32),pltpu.VMEM((heads,BLOCK,PAIR),f32),
            pltpu.VMEM((pairs,BLOCK,PAIR),f32)],
        compiler_params=pltpu.CompilerParams(vmem_limit_bytes=40<<20),
        name="attention_forward",
    )(slopes2,mixed)

def bwd_kernel(heads, slope_ref, mixed_ref, dout_ref, out_ref, lse_ref, grad_ref, qs, ks, km, vp, ds_, delta, bias, dq, dk, dv):
    pairs=heads//2
    blocks=mixed_ref.shape[0]//BLOCK
    lo=low_lanes(BLOCK)
    @pl.loop(0,blocks)
    def _(b):
        rows=pl.ds(pl.multiple_of(b*BLOCK,BLOCK),BLOCK)
        for p in range(pairs):
            t0,t1,t2=(mixed_ref[rows,(3*p+n)*PAIR:(3*p+n+1)*PAIR] for n in range(3))
            zero=jnp.zeros_like(t0)
            qs[p,b,:BLOCK]=jnp.where(lo,t0,zero)
            qs[p,b,BLOCK:]=jnp.where(lo,zero,t1)
            k=jnp.where(lo,swap(t0),swap(t2))
            ks[p,b]=k
            km[p,b,:BLOCK]=jnp.where(lo,k,zero)
            km[p,b,BLOCK:]=jnp.where(lo,zero,k)
            vp[p,b]=jnp.where(lo,t1,t2)
            d=dout_ref[rows,p*PAIR:(p+1)*PAIR]
            ds_[p,b,:BLOCK]=jnp.where(lo,d,zero)
            ds_[p,b,BLOCK:]=jnp.where(lo,zero,d)
            prod=(d.astype(jnp.float32)*out_ref[rows,p*PAIR:(p+1)*PAIR].astype(jnp.float32)).T
            delta[2*p,pl.ds(b,1),:]=jnp.sum(prod[:HALF],0,keepdims=True)
            delta[2*p+1,pl.ds(b,1),:]=jnp.sum(prod[HALF:],0,keepdims=True)
    kl=lax.broadcasted_iota(jnp.int32,(BLOCK,BLOCK),0)
    ql=lax.broadcasted_iota(jnp.int32,(BLOCK,BLOCK),1)
    tent=jnp.minimum(kl,2*ql-kl).astype(jnp.float32)
    ramp=kl.astype(jnp.float32)
    for h in range(heads):
        bias[0,h]=tent*slope_ref[h]
        bias[1,h]=ramp*slope_ref[h]
    def block(i,j,first):
        for p in range(pairs):
            ps=[];gs=[]
            for n,h in enumerate((2*p,2*p+1)):
                q=qs[p,i,n*BLOCK:(n+1)*BLOCK]
                d=ds_[p,i,n*BLOCK:(n+1)*BLOCK]
                row=slope_ref[h]*((j-i)*BLOCK).astype(jnp.float32)-lse_ref[h,pl.ds(i,1),:]
                t=nt(ks[p,j],q)*SCALE2+row+bias[0 if first else 1,h]
                e=jnp.exp2(t)
                g=e*(nt(vp[p,j],d)-delta[h,pl.ds(i,1),:])
                ps.append(e.astype(jnp.bfloat16)); gs.append(g.astype(jnp.bfloat16))
            gv=nn(jnp.concatenate(ps,1),ds_[p,i])
            gk=nn(jnp.concatenate(gs,1),qs[p,i])
            gq=tn(jnp.concatenate(gs,0),km[p,j])
            if first:
                dv[p,j]=gv; dk[p,j]=gk; dq[p,i]=gq
            else:
                dv[p,j]+=gv; dk[p,j]+=gk; dq[p,i]+=gq
    @pl.loop(0,blocks)
    def _(i):
        block(i,i,True)
        @pl.loop(0,i)
        def _(j):
            block(i,j,False)
    @pl.loop(0,blocks)
    def _(b):
        rows=pl.ds(pl.multiple_of(b*BLOCK,BLOCK),BLOCK)
        for p in range(pairs):
            a=dq[p,b]*0.125; k=swap(dk[p,b]*0.125); v=dv[p,b]
            for n,t in enumerate((jnp.where(lo,a,k),jnp.where(lo,v,a),jnp.where(lo,k,v))):
                grad_ref[rows,(3*p+n)*PAIR:(3*p+n+1)*PAIR]=t.astype(grad_ref.dtype)

def attention_backward(slopes2, mixed, dout, out, lse):
    tokens,width=mixed.shape
    heads=width//(3*HEAD_DIM); pairs=heads//2; blocks=tokens//BLOCK
    f32=jnp.float32; bf=jnp.bfloat16
    V=pl.BlockSpec(memory_space=pltpu.VMEM)
    return pl.pallas_call(
        functools.partial(bwd_kernel,heads),
        out_shape=jax.ShapeDtypeStruct((tokens,width),bf),
        in_specs=[pl.BlockSpec(memory_space=pltpu.SMEM),V,V,V,V],
        out_specs=V,
        scratch_shapes=[pltpu.VMEM((pairs,blocks,2*BLOCK,PAIR),bf),pltpu.VMEM((pairs,blocks,BLOCK,PAIR),bf),
            pltpu.VMEM((pairs,blocks,2*BLOCK,PAIR),bf),pltpu.VMEM((pairs,blocks,BLOCK,PAIR),bf),
            pltpu.VMEM((pairs,blocks,2*BLOCK,PAIR),bf),pltpu.VMEM((heads,blocks,BLOCK),f32),
            pltpu.VMEM((2,heads,BLOCK,BLOCK),f32)]+[pltpu.VMEM((pairs,blocks,BLOCK,PAIR),f32)]*3,
        compiler_params=pltpu.CompilerParams(vmem_limit_bytes=40<<20),
        name="attention_backward",
    )(slopes2,mixed,dout,out,lse)


PLANE = (0, 3, 1, 2)


def plane_of(col_size):
    return PLANE if col_size == len(PLANE) else tuple(range(col_size))


def pick(stacked, index):
    return lax.dynamic_index_in_dim(stacked, index, 0, keepdims=False)


def to_tokens(local_rows):
    row_size, col_size = lax.axis_size("row"), lax.axis_size("col")
    row, col = lax.axis_index("row"), lax.axis_index("col")
    plane = plane_of(col_size)
    blocks = local_rows.reshape(col_size, local_rows.shape[0] // col_size, -1)
    came = []
    for step in range(row_size):
        moves = [
            (r * col_size + c, plane[c] * col_size + (r + step) % col_size)
            for r in range(row_size)
            for c in range(col_size)
        ]
        came.append(lax.ppermute(pick(blocks, (row + step) % col_size), ("row", "col"), moves))
    came = jnp.stack(came)
    return jnp.concatenate([pick(came, (col - f) % row_size) for f in range(row_size)], axis=1)


def to_features(local_tokens):
    row_size, col_size = lax.axis_size("row"), lax.axis_size("col")
    row, col = lax.axis_index("row"), lax.axis_index("col")
    plane = plane_of(col_size)
    width = local_tokens.shape[1] // row_size
    blocks = jnp.stack([local_tokens[:, f * width : (f + 1) * width] for f in range(row_size)])
    came = []
    for step in range(row_size):
        moves = [
            (plane[c] * col_size + (r + step) % col_size, r * col_size + c)
            for r in range(row_size)
            for c in range(col_size)
        ]
        came.append(lax.ppermute(pick(blocks, (col - step) % row_size), ("row", "col"), moves))
    came = jnp.stack(came)
    return jnp.concatenate([pick(came, (q - row) % row_size) for q in range(col_size)], axis=0)


def swap_with(value, axis, bit):
    size = lax.axis_size(axis)
    return lax.ppermute(value, axis, [(i, i ^ bit) for i in range(size)])


def small_sum(value, axes):
    for axis in axes:
        bit = 1
        while bit < lax.axis_size(axis):
            value = value + swap_with(value, axis, bit)
            bit *= 2
    return value


def gather_row(value):
    size, row = lax.axis_size("row"), lax.axis_index("row")
    came = [value]
    for step in range(1, size):
        came.append(lax.ppermute(value, "row", [(i, (i + step) % size) for i in range(size)]))
    came = jnp.stack(came)
    return jnp.stack([pick(came, (row - r) % size) for r in range(size)])


def exchange_col(value):
    size, col = lax.axis_size("col"), lax.axis_index("col")
    came = [pick(value, col)]
    for bit in range(1, size):
        came.append(swap_with(pick(value, col ^ bit), "col", bit))
    came = jnp.stack(came)
    return jnp.stack([pick(came, col ^ q) for q in range(size)])


def gather_col(value):
    size, col = lax.axis_size("col"), lax.axis_index("col")
    far = swap_with(value, "col", 2)
    near = swap_with(value, "col", 1)
    far_near = swap_with(far, "col", 1)
    came = jnp.stack([value, near, far, far_near])
    return jnp.stack([pick(came, col ^ q) for q in range(size)])


def scatter_col(value):
    col = lax.axis_index("col")
    core, chip = col % 2, col // 2
    pairs = value.reshape((2, 2) + value.shape[1:])
    mine = lax.dynamic_index_in_dim(pairs, core, 1, keepdims=False)
    other = lax.dynamic_index_in_dim(pairs, 1 - core, 1, keepdims=False)
    near = mine.astype(jnp.float32) + swap_with(other, "col", 1).astype(jnp.float32)
    keep = pick(near, chip)
    send = pick(near, 1 - chip).astype(jnp.bfloat16)
    return keep + swap_with(send, "col", 2).astype(jnp.float32)


def scatter_row(value):
    return lax.psum_scatter(value, "row", scatter_dimension=0, tiled=True)


def sum_dp(value):
    return small_sum(value, ("dp",))


def standardize(inputs):
    center = jnp.mean(inputs, 1, keepdims=True)
    spread = jnp.mean(inputs * inputs, 1, keepdims=True) - center * center
    inverse = lax.rsqrt(spread + EPSILON)
    return (inputs - center) * inverse, inverse


def norm_backward(grad_normed, standard, inverse, norm_gain):
    scaled = grad_normed * norm_gain
    first = jnp.mean(scaled, 1, keepdims=True)
    second = jnp.mean(scaled * standard, 1, keepdims=True)
    return inverse * (scaled - first - standard * second)


def gelu_local(before):
    return jax.nn.gelu(before, approximate=True)


def low(value):
    return value.astype(jnp.bfloat16)


def on_device(
    layer_in,
    first_gain,
    first_shift,
    joined_weight,
    joined_bias,
    out_weight,
    out_bias,
    second_gain,
    second_shift,
    up_weight,
    up_bias,
    down_weight,
    down_bias,
    teacher,
    valid,
    cotangent,
):
    row_size, col_size = lax.axis_size("row"), lax.axis_size("col")
    row, col = lax.axis_index("row"), lax.axis_index("col")
    f32 = jnp.float32
    head_count = joined_bias.shape[0]
    quarter = layer_in.shape[0] // col_size
    head_index = col * head_count + jnp.arange(head_count, dtype=jnp.int32)
    slopes = jnp.exp2(-8.0 * (head_index.astype(f32) + 1.0) / HEADS) * LOG2E

    tokens = to_tokens(layer_in)
    vectors = jnp.stack([first_gain, first_shift, out_bias, second_gain, second_shift, down_bias])
    vectors = gather_row(vectors).transpose(1, 0, 2).reshape(6, D).astype(f32)
    gain_one, shift_one, bias_out, gain_two, shift_two, bias_down = (vectors[i] for i in range(6))
    joined_all = gather_row(joined_weight).reshape(D, -1)
    zero_rows = jnp.zeros_like(joined_bias[:, :HEAD_DIM])
    bias_rows = jnp.stack(
        [joined_bias[:, :HEAD_DIM], zero_rows, joined_bias[:, HEAD_DIM:]], axis=1
    ).reshape(-1)

    inputs = tokens.astype(f32)
    standard_one, inverse_one = standardize(inputs)
    normed_one = low(standard_one * gain_one + shift_one)
    normed_one_all = gather_col(normed_one).reshape(-1, D)
    mixed = low(nn(normed_one_all, joined_all) + bias_rows)
    attended, log_totals = attention_forward(slopes, mixed)

    out_all = gather_row(out_weight)
    out_all = jnp.concatenate([out_all[r] for r in range(row_size)], axis=1)
    out_all = gather_col(out_all).reshape(D, D)
    up_own = gather_row(up_weight).reshape(D, -1)
    up_far = gather_row(swap_with(up_weight, "col", 2)).reshape(D, -1)
    down_own = gather_row(down_weight)
    down_far = swap_with(down_own, "col", 2)
    down_own = jnp.concatenate([down_own[r] for r in range(row_size)], axis=1)
    down_far = jnp.concatenate([down_far[r] for r in range(row_size)], axis=1)
    bias_far = swap_with(up_bias, "col", 2)

    target = to_tokens(teacher)
    cotangent_tokens = to_tokens(cotangent)
    plane = plane_of(col_size)
    valid_tokens = lax.ppermute(
        pick(valid.reshape(col_size, quarter), row),
        ("row", "col"),
        [(r * col_size + c, plane[c] * col_size + r) for r in range(row_size) for c in range(col_size)],
    ).astype(f32)[:, None]
    valid_count = small_sum(jnp.sum(valid.astype(f32)).reshape(1, 1), ("dp", "col"))[0, 0]

    attended_tokens = exchange_col(attended.reshape(col_size, quarter, -1))
    attended_tokens = jnp.concatenate([attended_tokens[q] for q in range(col_size)], axis=1)
    middle = inputs + (nn(attended_tokens, out_all) + bias_out)
    standard_two, inverse_two = standardize(middle)
    normed_two = low(standard_two * gain_two + shift_two)
    normed_chip = jnp.concatenate([normed_two, swap_with(normed_two, "col", 1)], axis=0)
    before_own = nn(normed_chip, up_own) + up_bias.astype(f32)
    before_far = nn(normed_chip, up_far) + bias_far.astype(f32)
    active_own, pull_own = jax.vjp(gelu_local, before_own)
    active_far, pull_far = jax.vjp(gelu_local, before_far)
    active_own, active_far = low(active_own), low(active_far)
    branch = nn(active_own, down_own) + nn(active_far, down_far)
    result = middle + (
        branch[:quarter] + swap_with(low(branch[quarter:]), "col", 1).astype(f32) + bias_down
    )
    layer_out = to_features(low(result))

    error_rows = result - target.astype(f32)
    error_sum = jnp.sum(valid_tokens * error_rows * error_rows)
    token_total = layer_in.shape[0] * lax.axis_size("dp") * col_size
    grad_result = cotangent_tokens.astype(f32) + valid_tokens * error_rows * (
        token_total / valid_count
    )
    grad_low = low(grad_result)
    grad_chip = jnp.concatenate([grad_low, swap_with(grad_low, "col", 1)], axis=0)
    grad_before_own = low(pull_own(nt(grad_chip, down_own))[0])
    grad_before_far = low(pull_far(nt(grad_chip, down_far))[0])
    back = nt(grad_before_own, up_own) + nt(grad_before_far, up_far)
    grad_normed_two = back[:quarter] + swap_with(low(back[quarter:]), "col", 1).astype(f32)
    grad_middle = grad_result + norm_backward(grad_normed_two, standard_two, inverse_two, gain_two)
    branch_grad = low(grad_middle)
    attended_grad = low(nt(branch_grad, out_all))
    width = attended_grad.shape[1] // col_size
    attended_grad = exchange_col(
        jnp.stack([attended_grad[:, q * width : (q + 1) * width] for q in range(col_size)])
    ).reshape(-1, width)

    down_grad_own = low(tn(grad_chip, active_own))
    down_grad_far = low(tn(grad_chip, active_far))
    up_grad_own = low(tn(normed_chip, grad_before_own))
    up_grad_far = low(tn(normed_chip, grad_before_far))
    down_grad = low(down_grad_own.astype(f32) + swap_with(down_grad_far, "col", 2).astype(f32))
    up_grad = low(up_grad_own.astype(f32) + swap_with(up_grad_far, "col", 2).astype(f32))
    down_grad = sum_dp(scatter_row(down_grad)).astype(f32).T
    up_grad = sum_dp(scatter_row(up_grad)).astype(f32)
    out_grad = low(tn(branch_grad, attended_tokens))
    out_grad = jnp.stack([out_grad[:, q * width : (q + 1) * width] for q in range(col_size)])
    out_grad = low(scatter_col(out_grad))
    out_grad = sum_dp(scatter_row(out_grad)).astype(f32).T

    mixed_grad = attention_backward(slopes, mixed, attended_grad, attended, log_totals)
    grad_normed_one = low(nt(mixed_grad, joined_all)).reshape(col_size, quarter, D)
    grad_normed_one = scatter_col(grad_normed_one)
    input_grad = grad_middle + norm_backward(grad_normed_one, standard_one, inverse_one, gain_one)
    input_grad = to_features(low(input_grad)).astype(f32)
    joined_grad = sum_dp(scatter_row(low(tn(normed_one_all, mixed_grad)))).astype(f32)

    early = jnp.stack(
        [
            jnp.sum(branch_grad, 0, dtype=f32),
            jnp.sum(grad_normed_two * standard_two, 0),
            jnp.sum(grad_normed_two, 0),
            jnp.sum(grad_low, 0, dtype=f32),
            jnp.full((D,), error_sum),
        ]
    )
    early = small_sum(early, ("dp", "row", "col"))
    loss = early[4, 0] / (D * valid_count)
    early = lax.dynamic_slice_in_dim(early, row * (D // row_size), D // row_size, 1)
    up_sums = jnp.sum(grad_before_own, 0, dtype=f32) + swap_with(
        jnp.sum(grad_before_far, 0, dtype=f32), "col", 2
    )
    up_bias_grad = small_sum(up_sums, ("dp", "row"))
    column_sums = small_sum(jnp.sum(mixed_grad, 0, dtype=f32), ("dp", "row"))
    column_sums = column_sums.reshape(head_count, 3, HEAD_DIM)
    joined_bias_grad = jnp.concatenate([column_sums[:, 0], column_sums[:, 2]], axis=1)
    late = jnp.stack([jnp.sum(grad_normed_one * standard_one, 0), jnp.sum(grad_normed_one, 0)])
    late = small_sum(late, ("dp", "row", "col"))
    late = lax.dynamic_slice_in_dim(late, row * (D // row_size), D // row_size, 1)
    return (
        layer_out,
        loss,
        input_grad,
        late[0],
        late[1],
        joined_grad,
        joined_bias_grad,
        out_grad,
        early[0],
        early[1],
        early[2],
        up_grad,
        up_bias_grad,
        down_grad,
        early[3],
    )


def solution(mesh):
    return jax.shard_map(
        on_device,
        mesh=mesh,
        in_specs=(
            P(("dp", "col"), "row"),
            P("row"),
            P("row"),
            P("row", "col"),
            P("col", None),
            P("col", "row"),
            P("row"),
            P("row"),
            P("row"),
            P("row", "col"),
            P("col"),
            P("col", "row"),
            P("row"),
            P(("dp", "col"), "row"),
            P(("dp", "col")),
            P(("dp", "col"), "row"),
        ),
        out_specs=(
            P(("dp", "col"), "row"),
            P(),
            P(("dp", "col"), "row"),
            P("row"),
            P("row"),
            P("row", "col"),
            P("col", None),
            P("col", "row"),
            P("row"),
            P("row"),
            P("row"),
            P("row", "col"),
            P("col"),
            P("col", "row"),
            P("row"),
        ),
        check_vma=False,
    )
```

```python
import functools
import math

import jax
import jax.numpy as jnp
from jax import lax
from jax.experimental import pallas as pl
from jax.experimental.pallas import tpu as pltpu
from jax.sharding import PartitionSpec as P

D = 1024
HEADS = 16
SEQ = 2048
EPSILON = 1e-05
LOG2E = 1.4426950408889634
HEAD_DIM=64
BLOCK=256
HALF=64
PAIR=128
SCALE2 = LOG2E/8.0

def nt(a,b):
    return lax.dot_general(a,b,(((1,),(1,)),((),())),preferred_element_type=jnp.float32)
def nn(a,b):
    return jnp.dot(a,b,preferred_element_type=jnp.float32)
def tn(a,b):
    return lax.dot_general(a,b,(((0,),(0,)),((),())),preferred_element_type=jnp.float32)

def low_lanes(rows):
    return lax.broadcasted_iota(jnp.int32,(rows,PAIR),1) < HALF

def swap(a):
    return jnp.concatenate([a[:,HALF:],a[:,:HALF]],axis=1)

def attention_rows(heads, order, after, slope_ref, mixed_ref, out_ref, lse_ref, qs, ks, vs, bias, sc, mx, ls, acc):
    pairs=heads//2
    blocks=mixed_ref.shape[0]//BLOCK
    lo=low_lanes(BLOCK)
    @pl.loop(0,blocks)
    def _(b):
        rows=pl.ds(pl.multiple_of(b*BLOCK,BLOCK),BLOCK)
        for p in range(pairs):
            t0,t1,t2=(mixed_ref[rows,(3*p+n)*PAIR:(3*p+n+1)*PAIR] for n in range(3))
            zero=jnp.zeros_like(t0)
            qs[2*p,b]=jnp.where(lo,t0,zero)
            qs[2*p+1,b]=jnp.where(lo,zero,t1)
            ks[p,b]=jnp.where(lo,swap(t0),swap(t2))
            vs[p,b,:BLOCK]=jnp.where(lo,t1,zero)
            vs[p,b,BLOCK:]=jnp.where(lo,zero,t2)
    il=lax.broadcasted_iota(jnp.int32,(BLOCK,BLOCK),0)
    jl=lax.broadcasted_iota(jnp.int32,(BLOCK,BLOCK),1)
    tent=jnp.minimum(jl,2*il-jl).astype(jnp.float32)
    for h in range(heads):
        bias[h]=tent*slope_ref[h]
    jrow=lax.broadcasted_iota(jnp.int32,(1,BLOCK),1)
    @pl.loop(0,blocks)
    def _(it):
        i=order(it)
        for h in range(heads):
            t=nt(qs[h,i],ks[h//2,i])*SCALE2+bias[h]
            sc[h,i]=t
            mx[h]=jnp.maximum(t[:,:PAIR],t[:,PAIR:])
        @pl.loop(0,i)
        def _(j):
            place=(jrow+(j-i)*BLOCK).astype(jnp.float32)
            for h in range(heads):
                t=nt(qs[h,i],ks[h//2,j])*SCALE2+place*slope_ref[h]
                sc[h,j]=t
                mx[h]=jnp.maximum(mx[h],jnp.maximum(t[:,:PAIR],t[:,PAIR:]))
        for h in range(heads):
            mx[h]=jnp.broadcast_to(jnp.max(mx[h],1,keepdims=True),(BLOCK,PAIR))
            ls[h]=jnp.zeros((BLOCK,PAIR),jnp.float32)
        for p in range(pairs):
            acc[p]=jnp.zeros((BLOCK,PAIR),jnp.float32)
        @pl.loop(0,i+1)
        def _(j):
            for p in range(pairs):
                both=[]
                for h in (2*p,2*p+1):
                    m=mx[h]
                    ea=jnp.exp2(sc[h,j,:,:PAIR]-m)
                    eb=jnp.exp2(sc[h,j,:,PAIR:]-m)
                    ls[h]+=ea+eb
                    both+=[ea.astype(jnp.bfloat16),eb.astype(jnp.bfloat16)]
                acc[p]+=nn(jnp.concatenate(both,1),vs[p,j])
        rows=pl.ds(pl.multiple_of(i*BLOCK,BLOCK),BLOCK)
        for p in range(pairs):
            tot=[jnp.broadcast_to(jnp.sum(ls[h],1,keepdims=True),(BLOCK,PAIR)) for h in (2*p,2*p+1)]
            out_ref[rows,p*PAIR:(p+1)*PAIR]=(acc[p]/jnp.where(lo,tot[0],tot[1])).astype(out_ref.dtype)
            for n,h in enumerate((2*p,2*p+1)):
                lse=mx[h]+jnp.log2(tot[n])
                lse_ref[h,pl.ds(i,1),:]=lse.T[:1]
        after(it,i)

def bwd_kernel(heads, slope_ref, mixed_ref, dout_ref, out_ref, lse_ref, grad_ref, qs, ks, km, vp, ds_, delta, bias, dq, dk, dv):
    pairs=heads//2
    blocks=mixed_ref.shape[0]//BLOCK
    lo=low_lanes(BLOCK)
    @pl.loop(0,blocks)
    def _(b):
        rows=pl.ds(pl.multiple_of(b*BLOCK,BLOCK),BLOCK)
        for p in range(pairs):
            t0,t1,t2=(mixed_ref[rows,(3*p+n)*PAIR:(3*p+n+1)*PAIR] for n in range(3))
            zero=jnp.zeros_like(t0)
            qs[p,b,:BLOCK]=jnp.where(lo,t0,zero)
            qs[p,b,BLOCK:]=jnp.where(lo,zero,t1)
            k=jnp.where(lo,swap(t0),swap(t2))
            ks[p,b]=k
            km[p,b,:BLOCK]=jnp.where(lo,k,zero)
            km[p,b,BLOCK:]=jnp.where(lo,zero,k)
            vp[p,b]=jnp.where(lo,t1,t2)
            d=dout_ref[rows,p*PAIR:(p+1)*PAIR]
            ds_[p,b,:BLOCK]=jnp.where(lo,d,zero)
            ds_[p,b,BLOCK:]=jnp.where(lo,zero,d)
            prod=(d.astype(jnp.float32)*out_ref[rows,p*PAIR:(p+1)*PAIR].astype(jnp.float32)).T
            delta[2*p,pl.ds(b,1),:]=jnp.sum(prod[:HALF],0,keepdims=True)
            delta[2*p+1,pl.ds(b,1),:]=jnp.sum(prod[HALF:],0,keepdims=True)
    kl=lax.broadcasted_iota(jnp.int32,(BLOCK,BLOCK),0)
    ql=lax.broadcasted_iota(jnp.int32,(BLOCK,BLOCK),1)
    tent=jnp.minimum(kl,2*ql-kl).astype(jnp.float32)
    ramp=kl.astype(jnp.float32)
    for h in range(heads):
        bias[0,h]=tent*slope_ref[h]
        bias[1,h]=ramp*slope_ref[h]
    def block(i,j,first):
        for p in range(pairs):
            ps=[];gs=[]
            for n,h in enumerate((2*p,2*p+1)):
                q=qs[p,i,n*BLOCK:(n+1)*BLOCK]
                d=ds_[p,i,n*BLOCK:(n+1)*BLOCK]
                row=slope_ref[h]*((j-i)*BLOCK).astype(jnp.float32)-lse_ref[h,pl.ds(i,1),:]
                t=nt(ks[p,j],q)*SCALE2+row+bias[0 if first else 1,h]
                e=jnp.exp2(t)
                g=e*(nt(vp[p,j],d)-delta[h,pl.ds(i,1),:])
                ps.append(e.astype(jnp.bfloat16)); gs.append(g.astype(jnp.bfloat16))
            gv=nn(jnp.concatenate(ps,1),ds_[p,i])
            gk=nn(jnp.concatenate(gs,1),qs[p,i])
            gq=tn(jnp.concatenate(gs,0),km[p,j])
            if first:
                dv[p,j]=gv; dk[p,j]=gk; dq[p,i]=gq
            else:
                dv[p,j]+=gv; dk[p,j]+=gk; dq[p,i]+=gq
    @pl.loop(0,blocks)
    def _(i):
        block(i,i,True)
        @pl.loop(0,i)
        def _(j):
            block(i,j,False)
    @pl.loop(0,blocks)
    def _(b):
        rows=pl.ds(pl.multiple_of(b*BLOCK,BLOCK),BLOCK)
        for p in range(pairs):
            a=dq[p,b]*0.125; k=swap(dk[p,b]*0.125); v=dv[p,b]
            for n,t in enumerate((jnp.where(lo,a,k),jnp.where(lo,v,a),jnp.where(lo,k,v))):
                grad_ref[rows,(3*p+n)*PAIR:(3*p+n+1)*PAIR]=t.astype(grad_ref.dtype)

def attention_backward(slopes2, mixed, dout, out, lse):
    tokens,width=mixed.shape
    heads=width//(3*HEAD_DIM); pairs=heads//2; blocks=tokens//BLOCK
    f32=jnp.float32; bf=jnp.bfloat16
    V=pl.BlockSpec(memory_space=pltpu.VMEM)
    return pl.pallas_call(
        functools.partial(bwd_kernel,heads),
        out_shape=jax.ShapeDtypeStruct((tokens,width),bf),
        in_specs=[pl.BlockSpec(memory_space=pltpu.SMEM),V,V,V,V],
        out_specs=V,
        scratch_shapes=[pltpu.VMEM((pairs,blocks,2*BLOCK,PAIR),bf),pltpu.VMEM((pairs,blocks,BLOCK,PAIR),bf),
            pltpu.VMEM((pairs,blocks,2*BLOCK,PAIR),bf),pltpu.VMEM((pairs,blocks,BLOCK,PAIR),bf),
            pltpu.VMEM((pairs,blocks,2*BLOCK,PAIR),bf),pltpu.VMEM((heads,blocks,BLOCK),f32),
            pltpu.VMEM((2,heads,BLOCK,BLOCK),f32)]+[pltpu.VMEM((pairs,blocks,BLOCK,PAIR),f32)]*3,
        compiler_params=pltpu.CompilerParams(vmem_limit_bytes=40<<20),
        name="attention_backward",
    )(slopes2,mixed,dout,out,lse)


MESH = pl.DeviceIdType.MESH


def hint(index, size):
    return pl.ds(pl.multiple_of(index * size, size), size)


def remote(src, dst, sems, number, target):
    send, recv = sems
    return pltpu.make_async_remote_copy(
        src_ref=src, dst_ref=dst, send_sem=send.at[number], recv_sem=recv.at[number],
        device_id=target, device_id_type=MESH,
    )


def partner(index, bit):
    return index + bit - 2 * bit * ((index // bit) % 2)


class Place:
    def __init__(self):
        self.dp, self.row, self.col = (lax.axis_index(a) for a in ("dp", "row", "col"))
        self.dps = lax.axis_size("dp")
        self.core, self.chip = self.col % 2, self.col // 2
        self.near, self.far = partner(self.col, 1), partner(self.col, 2)
        self.twin = partner(self.dp, 1)
        self.half = self.dp % 2
        self.plane = 3 * self.core + self.chip - 2 * self.core * self.chip
        self.source = 2 * (((self.row + 1) // 2) % 2) + self.row // 2
        self.stays = self.plane == self.row


def greet(place, transpose, counts):
    barrier = pltpu.get_barrier_semaphore()

    def signal(target):
        pl.semaphore_signal(barrier, inc=1, device_id=target, device_id_type=MESH)

    for step in (1, 2, 3):
        signal({"row": (place.row + step) % 4})
    signal({"col": place.near})
    signal({"col": place.far})
    signal({"dp": place.twin})
    amount = 6
    if counts:
        bit = 2
        while bit < place.dps:
            signal({"dp": partner(place.dp, bit)})
            amount += 1
            bit *= 2
    if transpose:
        for other in range(4):
            @pl.when(jnp.logical_not(jnp.logical_and(place.stays, place.col == other)))
            def _():
                signal({"row": place.plane, "col": other})

            @pl.when(jnp.logical_not(jnp.logical_and(place.stays, place.row == other)))
            def _():
                signal({"row": other, "col": place.source})
        amount = amount + 8 - 2 * place.stays.astype(jnp.int32)
    pl.semaphore_wait(barrier, amount)


class Transpose:
    def __init__(self, place, src, dst, sems, first):
        self.place, self.src, self.dst, self.sems, self.first = place, src, dst, sems, first
        self.rows, self.width = src.shape[0] // 4, src.shape[1]

    def out(self, other):
        p = self.place
        send, recv = self.sems
        return pltpu.make_async_remote_copy(
            src_ref=self.src.at[pl.ds(other * self.rows, self.rows)],
            dst_ref=self.dst.at[:, hint(p.row, self.width)],
            send_sem=send.at[self.first + other], recv_sem=recv.at[self.first + p.row],
            device_id={"row": p.plane, "col": other}, device_id_type=MESH,
        )

    def kept(self):
        p = self.place
        return pltpu.make_async_copy(
            self.src.at[hint(p.col, self.rows)],
            self.dst.at[:, hint(p.row, self.width)],
            self.sems[1].at[self.first + p.row],
        )

    def start(self):
        p = self.place
        for other in range(4):
            @pl.when(jnp.logical_not(jnp.logical_and(p.stays, p.col == other)))
            def _():
                self.out(other).start()

        @pl.when(p.stays)
        def _():
            self.kept().start()

    def wait_recv(self):
        p = self.place
        for other in range(4):
            mine = jnp.logical_and(p.stays, p.row == other)
            part = self.dst.at[:, pl.ds(other * self.width, self.width)]

            @pl.when(jnp.logical_not(mine))
            def _():
                pltpu.make_async_remote_copy(
                    src_ref=part, dst_ref=part, send_sem=self.sems[0].at[self.first + other],
                    recv_sem=self.sems[1].at[self.first + other],
                    device_id={"row": other, "col": p.source}, device_id_type=MESH,
                ).wait_recv()

            @pl.when(mine)
            def _():
                self.kept().wait()

    def wait_send(self):
        p = self.place
        for other in range(4):
            @pl.when(jnp.logical_not(jnp.logical_and(p.stays, p.col == other)))
            def _():
                self.out(other).wait_send()


class Weight:
    def __init__(self, place, src, dst, offset, by_rows, sems, first):
        self.place, self.src, self.dst, self.offset, self.by_rows = place, src, dst, offset, by_rows
        self.sems, self.first = sems, first
        self.rows, self.width = src.shape
        self.part = self.rows // 2

    def whole(self, side, row):
        if self.by_rows:
            return self.dst.at[side, hint(row, self.rows)]
        return self.dst.at[side, pl.ds(self.offset, self.rows), hint(row, self.width)]

    def piece(self, side, row, half):
        if self.by_rows:
            return self.dst.at[side, hint(row * 2 + half, self.part)]
        start = pl.multiple_of(self.offset + half * self.part, self.part)
        return self.dst.at[side, pl.ds(start, self.part), hint(row, self.width)]

    def own(self):
        return pltpu.make_async_copy(self.src, self.whole(0, self.place.row), self.sems[1].at[self.first])

    def across(self):
        return remote(
            self.src, self.whole(1, self.place.row), self.sems, self.first + 1, {"col": self.place.far}
        )

    def along(self, side, step):
        p = self.place
        src = self.src.at[hint(p.half, self.part)] if side == 0 else self.piece(1, p.row, p.half)
        return remote(
            src, self.piece(side, p.row, p.half), self.sems, self.first + 2 + 3 * side + step - 1,
            {"row": (p.row + step) % 4},
        )

    def came(self, side, step):
        p = self.place
        part = self.piece(side, (p.row + 4 - step) % 4, p.half)
        return remote(
            part, part, self.sems, self.first + 2 + 3 * side + step - 1, {"row": (p.row + step) % 4}
        )

    def twin(self, side, step):
        p = self.place
        part = self.piece(side, (p.row + 4 - step) % 4, p.half)
        return remote(part, part, self.sems, self.first + 8 + 3 * side + step - 1, {"dp": p.twin})

    def from_twin(self, side, step):
        p = self.place
        part = self.piece(side, (p.row + 4 - step) % 4, 1 - p.half)
        return remote(part, part, self.sems, self.first + 8 + 3 * side + step - 1, {"dp": p.twin})


WEIGHT_SEMS = 14


def first_kernel(
    heads, token_total,
    slope_ref, bias_ref, vector_ref, joined_ref, layer_ref, up_ref, down_ref, out_ref, up_bias_ref,
    teacher_ref, cot_ref, valid_ref,
    xt_ref, nall_ref, mixed_ref, att_ref, lse_ref, chip_ref, jall_ref, vall_ref, gt_ref, vt_ref, scale_ref,
    up2_ref, dn2_ref, ub2_ref,
    qs, ks, vs, bias, sc, mx, ls, acc, grad, count, sends, recvs,
):
    sems = (sends, recvs)
    p = Place()
    quarter = xt_ref.shape[0]
    greet(p, True, True)
    moved = Transpose(p, layer_ref, xt_ref, sems, 0)
    target = Transpose(p, grad, gt_ref, sems, 4)
    base = 8
    weights = []
    for n, (src, dst, offset, by_rows) in enumerate(
        ((out_ref, dn2_ref, down_ref.shape[0], False), (up_ref, up2_ref, 0, True), (down_ref, dn2_ref, 0, False))
    ):
        weights.append(Weight(p, src, dst, offset, by_rows, sems, base + n * WEIGHT_SEMS))
    base += 3 * WEIGHT_SEMS
    moved.start()
    small_base, joined_base, bias_base = base, base + 4, base + 8
    base += 10

    def small(step):
        return remote(
            vector_ref, vall_ref.at[:, hint(p.row, 256)], sems, small_base + step, {"row": (p.row + step) % 4}
        )

    def small_came(step):
        part = vall_ref.at[:, hint((p.row + 4 - step) % 4, 256)]
        return remote(part, part, sems, small_base + step, {"row": (p.row + step) % 4})

    def joined(step):
        return remote(
            joined_ref, jall_ref.at[hint(p.row, 256)], sems, joined_base + step, {"row": (p.row + step) % 4}
        )

    def joined_came(step):
        part = jall_ref.at[hint((p.row + 4 - step) % 4, 256)]
        return remote(part, part, sems, joined_base + step, {"row": (p.row + step) % 4})

    small_own = pltpu.make_async_copy(vector_ref, vall_ref.at[:, hint(p.row, 256)], recvs.at[small_base])
    joined_own = pltpu.make_async_copy(joined_ref, jall_ref.at[hint(p.row, 256)], recvs.at[joined_base])
    bias_own = pltpu.make_async_copy(up_bias_ref, ub2_ref.at[0], recvs.at[bias_base])
    bias_far = remote(up_bias_ref, ub2_ref.at[1], sems, bias_base + 1, {"col": p.far})
    small_own.start()
    joined_own.start()
    for step in (1, 2, 3):
        small(step).start()
    bias_own.start()
    bias_far.start()
    for w in weights:
        w.own().start()
        w.across().start()

    total = jnp.sum(jnp.sum(valid_ref[...], axis=0, keepdims=True), axis=1, keepdims=True) * (1.0 / 128.0)
    count[0] = jnp.broadcast_to(total, (8, 128))
    steps = [("col", 1), ("col", 2)]
    bit = 1
    while bit < p.dps:
        steps.append(("dp", bit))
        bit *= 2
    for n, (axis, bit) in enumerate(steps):
        other = partner(p.col if axis == "col" else p.dp, bit)
        tally = remote(count.at[2 * n], count.at[2 * n + 1], sems, base + n, {axis: other})
        tally.start()
        tally.wait()
        count[2 * n + 2] = count[2 * n] + count[2 * n + 1]
    base += len(steps)
    scale_ref[...] = token_total / count[2 * len(steps)]
    scale = scale_ref[:1, :1]

    @pl.loop(0, 16)
    def _(n):
        rows = hint(n, grad.shape[0] // 16)
        factor = valid_ref[rows, :] * scale
        for f in range(grad.shape[1] // 128):
            cols = slice(f * 128, (f + 1) * 128)
            grad[rows, cols] = (
                cot_ref[rows, cols].astype(jnp.float32) - factor * teacher_ref[rows, cols].astype(jnp.float32)
            ).astype(grad.dtype)

    valid_base = base
    base += 1

    def valid_out():
        return pltpu.make_async_remote_copy(
            src_ref=valid_ref.at[hint(p.row, quarter)], dst_ref=vt_ref,
            send_sem=sends.at[valid_base], recv_sem=recvs.at[valid_base],
            device_id={"row": p.plane, "col": p.row}, device_id_type=MESH,
        )

    same = jnp.logical_and(p.stays, p.col == p.row)
    valid_kept = pltpu.make_async_copy(valid_ref.at[hint(p.row, quarter)], vt_ref, recvs.at[valid_base])

    @pl.when(jnp.logical_not(same))
    def _():
        valid_out().start()

    @pl.when(same)
    def _():
        valid_kept.start()

    for step in (1, 2, 3):
        small_came(step).wait_recv()
        small(step).wait_send()
    small_own.wait()
    moved.wait_recv()
    joined_own.wait()
    for step in (1, 2, 3):
        joined(step).start()

    first = p.col * quarter
    @pl.loop(0, quarter // 128)
    def _(n):
        rows = hint(n, 128)
        x = xt_ref[rows, :].astype(jnp.float32)
        center = jnp.mean(x, 1, keepdims=True)
        spread = jnp.mean(x * x, 1, keepdims=True) - center * center
        standard = (x - center) * lax.rsqrt(spread + EPSILON)
        place = pl.ds(pl.multiple_of(first + n * 128, 128), 128)
        nall_ref[place, :] = (standard * vall_ref[0:1, :] + vall_ref[1:2, :]).astype(nall_ref.dtype)

    mine = nall_ref.at[hint(p.col, quarter)]
    to_far = remote(mine, mine, sems, base, {"col": p.far})
    to_near = remote(mine, mine, sems, base + 1, {"col": p.near})
    theirs = nall_ref.at[hint(p.far, quarter)]
    far_came = remote(theirs, theirs, sems, base, {"col": p.far})
    pass_on = remote(theirs, theirs, sems, base + 2, {"col": p.near})
    beside = nall_ref.at[hint(p.near, quarter)]
    near_came = remote(beside, beside, sems, base + 1, {"col": p.near})
    corner = partner(p.far, 1)
    across = nall_ref.at[hint(corner, quarter)]
    corner_came = remote(across, across, sems, base + 2, {"col": p.near})
    base += 3
    to_far.start()
    to_near.start()
    for w in weights:
        for step in (1, 2, 3):
            w.along(0, step).start()
        w.across().wait()
        for step in (1, 2, 3):
            w.along(1, step).start()
    target.start()

    def project(index):
        @pl.loop(0, quarter // 256)
        def _(n):
            rows = pl.ds(pl.multiple_of(index * quarter + n * 256, 256), 256)
            mixed_ref[rows, :] = (nn(nall_ref[rows, :], jall_ref[...]) + bias_ref[...]).astype(mixed_ref.dtype)

    for step in (1, 2, 3):
        joined_came(step).wait_recv()
        joined(step).wait_send()
    project(p.col)
    near_came.wait_recv()
    project(p.near)
    far_came.wait_recv()
    pass_on.start()
    project(p.far)
    corner_came.wait_recv()
    project(corner)

    own_heads = att_ref.shape[1]
    blocks = mixed_ref.shape[0] // BLOCK
    per_chip = blocks // 2

    share_base = base

    def share(n, i):
        return pltpu.make_async_remote_copy(
            src_ref=att_ref.at[hint(i, BLOCK)], dst_ref=chip_ref.at[hint(chip_place(n), BLOCK), pl.ds(own_heads, own_heads)],
            send_sem=sends.at[share_base + n], recv_sem=recvs.at[share_base + n],
            device_id={"col": p.far}, device_id_type=MESH,
        )

    def chip_place(n):
        half = per_chip // 2
        return ((n // half + p.core) % 2) * half + n % half

    def after(it, i):
        @pl.when(it < per_chip)
        def _():
            share(it, i).start()

        @pl.when(it >= per_chip)
        def _():
            chip_ref[hint(chip_place(it - per_chip), BLOCK), :own_heads] = att_ref[hint(i, BLOCK), :]

        for at, n, side in ((4, 0, 0), (4, 0, 1), (5, 1, 0), (6, 1, 1), (7, 2, 0), (7, 2, 1)):
            @pl.when(it == at)
            def _():
                for step in (1, 2, 3):
                    weights[n].came(side, step).wait_recv()
                    weights[n].twin(side, step).start()

    attention_rows(
        heads, lambda it: (it + per_chip * (1 - p.chip)) % blocks, after,
        slope_ref, mixed_ref, att_ref, lse_ref, qs, ks, vs, bias, sc, mx, ls, acc,
    )
    @pl.loop(0, per_chip)
    def _(n):
        share(n, n + per_chip * (1 - p.chip)).wait()

    moved.wait_send()
    to_far.wait_send()
    to_near.wait_send()
    pass_on.wait_send()
    bias_own.wait()
    bias_far.wait()

    @pl.when(jnp.logical_not(same))
    def _():
        valid_out().wait_send()

    kept_in = jnp.logical_and(p.stays, p.col == p.row)

    @pl.when(jnp.logical_not(kept_in))
    def _():
        valid_out().wait_recv()

    @pl.when(kept_in)
    def _():
        valid_kept.wait()

    for w in weights:
        w.own().wait()
        for side in (0, 1):
            for step in (1, 2, 3):
                w.along(side, step).wait_send()
                w.twin(side, step).wait_send()
                w.from_twin(side, step).wait_recv()
    target.wait_recv()
    target.wait_send()


def first_stage(slopes, bias_rows, vectors, joined, layer_in, up, down, out, up_bias, teacher, cot, valid, token_total):
    tokens, width = layer_in.shape
    quarter = tokens // 4
    row_size = lax.axis_size("row")
    features = width * row_size
    joined_width = joined.shape[1]
    heads = joined_width // (3 * HEAD_DIM)
    pairs, blocks = heads // 2, tokens // BLOCK
    f32, bf = jnp.float32, jnp.bfloat16
    hidden, head_rows = down.shape[0], out.shape[0]
    vmem, anyspace = pl.BlockSpec(memory_space=pltpu.VMEM), pl.BlockSpec(memory_space=pl.ANY)
    shape = jax.ShapeDtypeStruct
    bits = 2
    while (1 << (bits - 2)) < lax.axis_size("dp"):
        bits += 1
    count = 8 + 3 * WEIGHT_SEMS + 8 + 2 + bits + 1 + 3 + blocks
    return pl.pallas_call(
        functools.partial(first_kernel, heads, token_total),
        out_shape=(
            shape((quarter, features), bf), shape((tokens, features), bf), shape((tokens, joined_width), bf),
            shape((tokens, heads * HEAD_DIM), bf), shape((heads, blocks, BLOCK), f32),
            shape((tokens // 2, 2 * heads * HEAD_DIM), bf), shape((features, joined_width), bf),
            shape((8, features), f32), shape((quarter, features), bf), shape((quarter, 128), f32), shape((8, 128), f32),
            shape((2, features, up.shape[1]), bf), shape((2, hidden + head_rows, features), bf), shape((2, 8, hidden), f32),
        ),
        in_specs=[pl.BlockSpec(memory_space=pltpu.SMEM), vmem, vmem, anyspace, anyspace, anyspace, anyspace, anyspace,
                  anyspace, vmem, vmem, vmem],
        out_specs=(vmem,) * 8 + (anyspace, anyspace, vmem, anyspace, anyspace, anyspace),
        scratch_shapes=[pltpu.VMEM((heads,blocks,BLOCK,PAIR),bf),pltpu.VMEM((pairs,blocks,BLOCK,PAIR),bf),
            pltpu.VMEM((pairs,blocks,2*BLOCK,PAIR),bf),pltpu.VMEM((heads,BLOCK,BLOCK),f32),
            pltpu.VMEM((heads,blocks,BLOCK,BLOCK),f32),pltpu.VMEM((heads,BLOCK,PAIR),f32),pltpu.VMEM((heads,BLOCK,PAIR),f32),
            pltpu.VMEM((pairs,BLOCK,PAIR),f32),
            pltpu.VMEM((tokens, width), bf), pltpu.VMEM((2 * bits + 1, 8, 128), f32),
            pltpu.SemaphoreType.DMA((count,)), pltpu.SemaphoreType.DMA((count,))],
        compiler_params=pltpu.CompilerParams(vmem_limit_bytes=48 << 20, collective_id=1, has_side_effects=True),
        name="first_stage",
    )(slopes, bias_rows, vectors, joined, layer_in, up, down, out, up_bias, teacher, cot, valid)


PLANE = (0, 3, 1, 2)


def plane_of(col_size):
    return PLANE if col_size == len(PLANE) else tuple(range(col_size))


def pick(stacked, index):
    return lax.dynamic_index_in_dim(stacked, index, 0, keepdims=False)


def to_tokens(local_rows):
    row_size, col_size = lax.axis_size("row"), lax.axis_size("col")
    row, col = lax.axis_index("row"), lax.axis_index("col")
    plane = plane_of(col_size)
    blocks = local_rows.reshape(col_size, local_rows.shape[0] // col_size, -1)
    came = []
    for step in range(row_size):
        moves = [
            (r * col_size + c, plane[c] * col_size + (r + step) % col_size)
            for r in range(row_size)
            for c in range(col_size)
        ]
        came.append(lax.ppermute(pick(blocks, (row + step) % col_size), ("row", "col"), moves))
    came = jnp.stack(came)
    return jnp.concatenate([pick(came, (col - f) % row_size) for f in range(row_size)], axis=1)


def to_features(local_tokens):
    row_size, col_size = lax.axis_size("row"), lax.axis_size("col")
    row, col = lax.axis_index("row"), lax.axis_index("col")
    plane = plane_of(col_size)
    width = local_tokens.shape[1] // row_size
    blocks = jnp.stack([local_tokens[:, f * width : (f + 1) * width] for f in range(row_size)])
    came = []
    for step in range(row_size):
        moves = [
            (plane[c] * col_size + (r + step) % col_size, r * col_size + c)
            for r in range(row_size)
            for c in range(col_size)
        ]
        came.append(lax.ppermute(pick(blocks, (col - step) % row_size), ("row", "col"), moves))
    came = jnp.stack(came)
    return jnp.concatenate([pick(came, (q - row) % row_size) for q in range(col_size)], axis=0)


def swap_with(value, axis, bit):
    size = lax.axis_size(axis)
    return lax.ppermute(value, axis, [(i, i ^ bit) for i in range(size)])


def small_sum(value, axes):
    for axis in axes:
        bit = 1
        while bit < lax.axis_size(axis):
            value = value + swap_with(value, axis, bit)
            bit *= 2
    return value


def gather_row(value):
    size, row = lax.axis_size("row"), lax.axis_index("row")
    came = [value]
    for step in range(1, size):
        came.append(lax.ppermute(value, "row", [(i, (i + step) % size) for i in range(size)]))
    came = jnp.stack(came)
    return jnp.stack([pick(came, (row - r) % size) for r in range(size)])


def exchange_col(value):
    size, col = lax.axis_size("col"), lax.axis_index("col")
    came = [pick(value, col)]
    for bit in range(1, size):
        came.append(swap_with(pick(value, col ^ bit), "col", bit))
    came = jnp.stack(came)
    return jnp.stack([pick(came, col ^ q) for q in range(size)])


def gather_col(value):
    size, col = lax.axis_size("col"), lax.axis_index("col")
    far = swap_with(value, "col", 2)
    near = swap_with(value, "col", 1)
    far_near = swap_with(far, "col", 1)
    came = jnp.stack([value, near, far, far_near])
    return jnp.stack([pick(came, col ^ q) for q in range(size)])


def scatter_col(value):
    col = lax.axis_index("col")
    core, chip = col % 2, col // 2
    pairs = value.reshape((2, 2) + value.shape[1:])
    mine = lax.dynamic_index_in_dim(pairs, core, 1, keepdims=False)
    other = lax.dynamic_index_in_dim(pairs, 1 - core, 1, keepdims=False)
    near = mine.astype(jnp.float32) + swap_with(other, "col", 1).astype(jnp.float32)
    keep = pick(near, chip)
    send = pick(near, 1 - chip).astype(jnp.bfloat16)
    return keep + swap_with(send, "col", 2).astype(jnp.float32)


def scatter_row(value):
    return lax.psum_scatter(value, "row", scatter_dimension=0, tiled=True)


def sum_dp(value):
    return small_sum(value, ("dp",))


def standardize(inputs):
    center = jnp.mean(inputs, 1, keepdims=True)
    spread = jnp.mean(inputs * inputs, 1, keepdims=True) - center * center
    inverse = lax.rsqrt(spread + EPSILON)
    return (inputs - center) * inverse, inverse


def norm_backward(grad_normed, standard, inverse, norm_gain):
    scaled = grad_normed * norm_gain
    first = jnp.mean(scaled, 1, keepdims=True)
    second = jnp.mean(scaled * standard, 1, keepdims=True)
    return inverse * (scaled - first - standard * second)


def gelu_local(before):
    return jax.nn.gelu(before, approximate=True)


def low(value):
    return value.astype(jnp.bfloat16)


def partner_index(col, other):
    core = (col + other) % 2
    chip = (col // 2 + other // 2) % 2
    return 2 * chip + core


def on_device(
    layer_in,
    first_gain,
    first_shift,
    joined_weight,
    joined_bias,
    out_weight,
    out_bias,
    second_gain,
    second_shift,
    up_weight,
    up_bias,
    down_weight,
    down_bias,
    teacher,
    valid,
    cotangent,
):
    row_size, col_size = lax.axis_size("row"), lax.axis_size("col")
    row, col = lax.axis_index("row"), lax.axis_index("col")
    f32 = jnp.float32
    head_count = joined_bias.shape[0]
    quarter = layer_in.shape[0] // col_size
    head_index = col * head_count + jnp.arange(head_count, dtype=jnp.int32)
    slopes = jnp.exp2(-8.0 * (head_index.astype(f32) + 1.0) / HEADS) * LOG2E

    zero_rows = jnp.zeros_like(joined_bias[:, :HEAD_DIM])
    bias_rows = jnp.stack(
        [joined_bias[:, :HEAD_DIM], zero_rows, joined_bias[:, HEAD_DIM:]], axis=1
    ).reshape(1, -1).astype(f32)
    nothing = jnp.zeros_like(first_gain)
    vectors = jnp.stack(
        [first_gain, first_shift, out_bias, second_gain, second_shift, down_bias, nothing, nothing]
    ).astype(f32)
    token_total = layer_in.shape[0] * lax.axis_size("dp") * col_size
    (
        tokens, normed_one_all, mixed, attended, log_totals, attended_chip, joined_all,
        vectors, target, valid_tokens, scale, up_all, down_all, bias_all,
    ) = first_stage(
        slopes, bias_rows, vectors, joined_weight, layer_in, up_weight, down_weight, out_weight,
        jnp.broadcast_to(up_bias.astype(f32), (8, up_bias.shape[0])), teacher, cotangent,
        jnp.broadcast_to(valid.astype(f32)[:, None], (valid.shape[0], 128)), token_total,
    )
    gain_one, shift_one, bias_out, gain_two, shift_two, bias_down = (vectors[i] for i in range(6))
    valid_tokens, scale = valid_tokens[:, :1], scale[0, 0]
    hidden = down_weight.shape[0]
    up_own, up_far = up_all[0], up_all[1]
    down_own, down_far = down_all[0, :hidden], down_all[1, :hidden]
    out_own, out_far = down_all[0, hidden:], down_all[1, hidden:]
    head_width = attended.shape[1]

    inputs = tokens.astype(f32)
    standard_one, inverse_one = standardize(inputs)
    branch = nn(attended_chip[:, :head_width], out_own) + nn(attended_chip[:, head_width:], out_far)
    middle = inputs + (
        branch[:quarter] + swap_with(low(branch[quarter:]), "col", 1).astype(f32) + bias_out
    )
    standard_two, inverse_two = standardize(middle)
    normed_two = low(standard_two * gain_two + shift_two)
    normed_chip = jnp.concatenate([normed_two, swap_with(normed_two, "col", 1)], axis=0)
    before_own = nn(normed_chip, up_own) + bias_all[0, 0]
    before_far = nn(normed_chip, up_far) + bias_all[1, 0]
    active_own, pull_own = jax.vjp(gelu_local, before_own)
    active_far, pull_far = jax.vjp(gelu_local, before_far)
    active_own, active_far = low(active_own), low(active_far)
    branch = nn(active_own, down_own) + nn(active_far, down_far)
    result = middle + (
        branch[:quarter] + swap_with(low(branch[quarter:]), "col", 1).astype(f32) + bias_down
    )
    layer_out = to_features(low(result))
    layer_error = layer_out.astype(f32) - teacher.astype(f32)
    error_sum = jnp.sum(valid.astype(f32)[:, None] * layer_error * layer_error)
    grad_result = target.astype(f32) + valid_tokens * scale * result
    grad_low = low(grad_result)
    grad_chip = jnp.concatenate([grad_low, swap_with(grad_low, "col", 1)], axis=0)
    grad_before_own = low(pull_own(nt(grad_chip, down_own))[0])
    grad_before_far = low(pull_far(nt(grad_chip, down_far))[0])
    back = nt(grad_before_own, up_own) + nt(grad_before_far, up_far)
    grad_normed_two = back[:quarter] + swap_with(low(back[quarter:]), "col", 1).astype(f32)
    grad_middle = grad_result + norm_backward(grad_normed_two, standard_two, inverse_two, gain_two)
    branch_grad = low(grad_middle)
    branch_chip = jnp.concatenate([branch_grad, swap_with(branch_grad, "col", 1)], axis=0)
    grad_own = low(nt(branch_chip, out_own))
    grad_far = swap_with(low(nt(branch_chip, out_far)), "col", 2)
    pieces = jnp.stack([grad_own[:quarter], grad_own[quarter:], grad_far[:quarter], grad_far[quarter:]])
    attended_grad = jnp.concatenate([pick(pieces, partner_index(col, q)) for q in range(col_size)])

    down_grad_own = low(tn(grad_chip, active_own))
    down_grad_far = low(tn(grad_chip, active_far))
    up_grad_own = low(tn(normed_chip, grad_before_own))
    up_grad_far = low(tn(normed_chip, grad_before_far))
    down_grad = low(down_grad_own.astype(f32) + swap_with(down_grad_far, "col", 2).astype(f32))
    up_grad = low(up_grad_own.astype(f32) + swap_with(up_grad_far, "col", 2).astype(f32))
    down_grad = sum_dp(scatter_row(down_grad)).astype(f32).T
    up_grad = sum_dp(scatter_row(up_grad)).astype(f32)
    out_grad_own = low(tn(branch_chip, attended_chip[:, :head_width]))
    out_grad_far = low(tn(branch_chip, attended_chip[:, head_width:]))
    out_grad = low(out_grad_own.astype(f32) + swap_with(out_grad_far, "col", 2).astype(f32))
    out_grad = sum_dp(scatter_row(out_grad)).astype(f32).T

    mixed_grad = attention_backward(slopes, mixed, attended_grad, attended, log_totals)
    grad_normed_one = low(nt(mixed_grad, joined_all)).reshape(col_size, quarter, D)
    grad_normed_one = scatter_col(grad_normed_one)
    input_grad = grad_middle + norm_backward(grad_normed_one, standard_one, inverse_one, gain_one)
    input_grad = to_features(low(input_grad)).astype(f32)
    joined_grad = sum_dp(scatter_row(low(tn(normed_one_all, mixed_grad)))).astype(f32)

    early = jnp.stack(
        [
            jnp.sum(branch_grad, 0, dtype=f32),
            jnp.sum(grad_normed_two * standard_two, 0),
            jnp.sum(grad_normed_two, 0),
            jnp.sum(grad_low, 0, dtype=f32),
            jnp.full((D,), error_sum),
        ]
    )
    early = small_sum(early, ("dp", "row", "col"))
    loss = early[4, 0] * scale / (D * token_total)
    early = lax.dynamic_slice_in_dim(early, row * (D // row_size), D // row_size, 1)
    up_sums = jnp.sum(grad_before_own, 0, dtype=f32) + swap_with(
        jnp.sum(grad_before_far, 0, dtype=f32), "col", 2
    )
    up_bias_grad = small_sum(up_sums, ("dp", "row"))
    column_sums = small_sum(jnp.sum(mixed_grad, 0, dtype=f32), ("dp", "row"))
    column_sums = column_sums.reshape(head_count, 3, HEAD_DIM)
    joined_bias_grad = jnp.concatenate([column_sums[:, 0], column_sums[:, 2]], axis=1)
    late = jnp.stack([jnp.sum(grad_normed_one * standard_one, 0), jnp.sum(grad_normed_one, 0)])
    late = small_sum(late, ("dp", "row", "col"))
    late = lax.dynamic_slice_in_dim(late, row * (D // row_size), D // row_size, 1)
    return (
        layer_out,
        loss,
        input_grad,
        late[0],
        late[1],
        joined_grad,
        joined_bias_grad,
        out_grad,
        early[0],
        early[1],
        early[2],
        up_grad,
        up_bias_grad,
        down_grad,
        early[3],
    )


def solution(mesh):
    return jax.shard_map(
        on_device,
        mesh=mesh,
        in_specs=(
            P(("dp", "col"), "row"),
            P("row"),
            P("row"),
            P("row", "col"),
            P("col", None),
            P("col", "row"),
            P("row"),
            P("row"),
            P("row"),
            P("row", "col"),
            P("col"),
            P("col", "row"),
            P("row"),
            P(("dp", "col"), "row"),
            P(("dp", "col")),
            P(("dp", "col"), "row"),
        ),
        out_specs=(
            P(("dp", "col"), "row"),
            P(),
            P(("dp", "col"), "row"),
            P("row"),
            P("row"),
            P("row", "col"),
            P("col", None),
            P("col", "row"),
            P("row"),
            P("row"),
            P("row"),
            P("row", "col"),
            P("col"),
            P("col", "row"),
            P("row"),
        ),
        check_vma=False,
    )
```

```python
import functools
import math

import jax
import jax.numpy as jnp
from jax import lax
from jax.experimental import pallas as pl
from jax.experimental.pallas import tpu as pltpu
from jax.sharding import PartitionSpec as P

D = 1024
HEADS = 16
SEQ = 2048
EPSILON = 1e-05
LOG2E = 1.4426950408889634
HEAD_DIM=64
BLOCK=256
HALF=64
PAIR=128
SCALE2 = LOG2E/8.0

def nt(a,b):
    return lax.dot_general(a,b,(((1,),(1,)),((),())),preferred_element_type=jnp.float32)
def nn(a,b):
    return jnp.dot(a,b,preferred_element_type=jnp.float32)
def tn(a,b):
    return lax.dot_general(a,b,(((0,),(0,)),((),())),preferred_element_type=jnp.float32)

def low_lanes(rows):
    return lax.broadcasted_iota(jnp.int32,(rows,PAIR),1) < HALF

def swap(a):
    return jnp.concatenate([a[:,HALF:],a[:,:HALF]],axis=1)

def attention_rows(heads, order, after, slope_ref, mixed_ref, out_ref, lse_ref, qs, ks, vs, bias, sc, mx, ls, acc):
    pairs=heads//2
    blocks=mixed_ref.shape[0]//BLOCK
    lo=low_lanes(BLOCK)
    @pl.loop(0,blocks)
    def _(b):
        rows=pl.ds(pl.multiple_of(b*BLOCK,BLOCK),BLOCK)
        for p in range(pairs):
            t0,t1,t2=(mixed_ref[rows,(3*p+n)*PAIR:(3*p+n+1)*PAIR] for n in range(3))
            zero=jnp.zeros_like(t0)
            qs[2*p,b]=jnp.where(lo,t0,zero)
            qs[2*p+1,b]=jnp.where(lo,zero,t1)
            ks[p,b]=jnp.where(lo,swap(t0),swap(t2))
            vs[p,b,:BLOCK]=jnp.where(lo,t1,zero)
            vs[p,b,BLOCK:]=jnp.where(lo,zero,t2)
    il=lax.broadcasted_iota(jnp.int32,(BLOCK,BLOCK),0)
    jl=lax.broadcasted_iota(jnp.int32,(BLOCK,BLOCK),1)
    tent=jnp.minimum(jl,2*il-jl).astype(jnp.float32)
    for h in range(heads):
        bias[h]=tent*slope_ref[h]
    jrow=lax.broadcasted_iota(jnp.int32,(1,BLOCK),1)
    @pl.loop(0,blocks)
    def _(it):
        i=order(it)
        for h in range(heads):
            t=nt(qs[h,i],ks[h//2,i])*SCALE2+bias[h]
            sc[h,i]=t
            mx[h]=jnp.maximum(t[:,:PAIR],t[:,PAIR:])
        @pl.loop(0,i)
        def _(j):
            place=(jrow+(j-i)*BLOCK).astype(jnp.float32)
            for h in range(heads):
                t=nt(qs[h,i],ks[h//2,j])*SCALE2+place*slope_ref[h]
                sc[h,j]=t
                mx[h]=jnp.maximum(mx[h],jnp.maximum(t[:,:PAIR],t[:,PAIR:]))
        for h in range(heads):
            mx[h]=jnp.broadcast_to(jnp.max(mx[h],1,keepdims=True),(BLOCK,PAIR))
            ls[h]=jnp.zeros((BLOCK,PAIR),jnp.float32)
        for p in range(pairs):
            acc[p]=jnp.zeros((BLOCK,PAIR),jnp.float32)
        @pl.loop(0,i+1)
        def _(j):
            for p in range(pairs):
                both=[]
                for h in (2*p,2*p+1):
                    m=mx[h]
                    ea=jnp.exp2(sc[h,j,:,:PAIR]-m)
                    eb=jnp.exp2(sc[h,j,:,PAIR:]-m)
                    ls[h]+=ea+eb
                    both+=[ea.astype(jnp.bfloat16),eb.astype(jnp.bfloat16)]
                acc[p]+=nn(jnp.concatenate(both,1),vs[p,j])
        rows=pl.ds(pl.multiple_of(i*BLOCK,BLOCK),BLOCK)
        for p in range(pairs):
            tot=[jnp.broadcast_to(jnp.sum(ls[h],1,keepdims=True),(BLOCK,PAIR)) for h in (2*p,2*p+1)]
            out_ref[rows,p*PAIR:(p+1)*PAIR]=(acc[p]/jnp.where(lo,tot[0],tot[1])).astype(out_ref.dtype)
            for n,h in enumerate((2*p,2*p+1)):
                lse=mx[h]+jnp.log2(tot[n])
                lse_ref[h,pl.ds(i,1),:]=lse.T[:1]
        after(it,i)

def attention_rows_backward(heads, slope_ref, mixed_ref, dout_ref, out_ref, lse_ref, grad_ref, qs, ks, km, vp, ds_, delta, bias, steep, dq, dk, dv):
    pairs=heads//2
    blocks=mixed_ref.shape[0]//BLOCK
    lo=low_lanes(BLOCK)
    @pl.loop(0,blocks)
    def _(b):
        rows=pl.ds(pl.multiple_of(b*BLOCK,BLOCK),BLOCK)
        for p in range(pairs):
            t0,t1,t2=(mixed_ref[rows,(3*p+n)*PAIR:(3*p+n+1)*PAIR] for n in range(3))
            zero=jnp.zeros_like(t0)
            qs[p,b,:BLOCK]=jnp.where(lo,t0,zero)
            qs[p,b,BLOCK:]=jnp.where(lo,zero,t1)
            k=jnp.where(lo,swap(t0),swap(t2))
            ks[p,b]=k
            km[p,b,:BLOCK]=jnp.where(lo,k,zero)
            km[p,b,BLOCK:]=jnp.where(lo,zero,k)
            vp[p,b]=jnp.where(lo,t1,t2)
            d=dout_ref[rows,p*PAIR:(p+1)*PAIR]
            ds_[p,b,:BLOCK]=jnp.where(lo,d,zero)
            ds_[p,b,BLOCK:]=jnp.where(lo,zero,d)
            prod=(d.astype(jnp.float32)*out_ref[rows,p*PAIR:(p+1)*PAIR].astype(jnp.float32)).T
            delta[2*p,pl.ds(b,1),:]=jnp.sum(prod[:HALF],0,keepdims=True)
            delta[2*p+1,pl.ds(b,1),:]=jnp.sum(prod[HALF:],0,keepdims=True)
    kl=lax.broadcasted_iota(jnp.int32,(BLOCK,BLOCK),0)
    ql=lax.broadcasted_iota(jnp.int32,(BLOCK,BLOCK),1)
    tent=jnp.minimum(kl,2*ql-kl).astype(jnp.float32)
    ramp=kl.astype(jnp.float32)
    for h in range(heads):
        bias[h]=tent*slope_ref[h]
        steep[h]=ramp[:,:PAIR]*slope_ref[h]
    def block(i,j,first):
        for p in range(pairs):
            ps=[];gs=[]
            for n,h in enumerate((2*p,2*p+1)):
                q=qs[p,i,n*BLOCK:(n+1)*BLOCK]
                d=ds_[p,i,n*BLOCK:(n+1)*BLOCK]
                row=slope_ref[h]*((j-i)*BLOCK).astype(jnp.float32)-lse_ref[h,pl.ds(i,1),:]
                t=nt(ks[p,j],q)*SCALE2+row+(bias[h] if first else jnp.concatenate([steep[h],steep[h]],1))
                e=jnp.exp2(t)
                g=e*(nt(vp[p,j],d)-delta[h,pl.ds(i,1),:])
                ps.append(e.astype(jnp.bfloat16)); gs.append(g.astype(jnp.bfloat16))
            gv=nn(jnp.concatenate(ps,1),ds_[p,i])
            gk=nn(jnp.concatenate(gs,1),qs[p,i])
            gq=tn(jnp.concatenate(gs,0),km[p,j])
            if first:
                dv[p,j]=gv; dk[p,j]=gk; dq[p,i]=gq
            else:
                dv[p,j]+=gv; dk[p,j]+=gk; dq[p,i]+=gq
    @pl.loop(0,blocks)
    def _(i):
        block(i,i,True)
        @pl.loop(0,i)
        def _(j):
            block(i,j,False)
    @pl.loop(0,blocks)
    def _(b):
        rows=pl.ds(pl.multiple_of(b*BLOCK,BLOCK),BLOCK)
        for p in range(pairs):
            a=dq[p,b]*0.125; k=swap(dk[p,b]*0.125); v=dv[p,b]
            for n,t in enumerate((jnp.where(lo,a,k),jnp.where(lo,v,a),jnp.where(lo,k,v))):
                grad_ref[rows,(3*p+n)*PAIR:(3*p+n+1)*PAIR]=t.astype(grad_ref.dtype)


MESH = pl.DeviceIdType.MESH


def hint(index, size):
    return pl.ds(pl.multiple_of(index * size, size), size)


def remote(src, dst, sems, number, target):
    send, recv = sems
    return pltpu.make_async_remote_copy(
        src_ref=src, dst_ref=dst, send_sem=send.at[number], recv_sem=recv.at[number],
        device_id=target, device_id_type=MESH,
    )


def partner(index, bit):
    return index + bit - 2 * bit * ((index // bit) % 2)


class Place:
    def __init__(self):
        self.dp, self.row, self.col = (lax.axis_index(a) for a in ("dp", "row", "col"))
        self.dps = lax.axis_size("dp")
        self.core, self.chip = self.col % 2, self.col // 2
        self.near, self.far = partner(self.col, 1), partner(self.col, 2)
        self.twin = partner(self.dp, 1)
        self.half = self.dp % 2
        self.plane = 3 * self.core + self.chip - 2 * self.core * self.chip
        self.source = 2 * (((self.row + 1) // 2) % 2) + self.row // 2
        self.stays = self.plane == self.row


def greet(place, transpose, counts):
    barrier = pltpu.get_barrier_semaphore()

    def signal(target):
        pl.semaphore_signal(barrier, inc=1, device_id=target, device_id_type=MESH)

    for step in (1, 2, 3):
        signal({"row": (place.row + step) % 4})
    signal({"col": place.near})
    signal({"col": place.far})
    signal({"dp": place.twin})
    amount = 6
    if counts:
        bit = 2
        while bit < place.dps:
            signal({"dp": partner(place.dp, bit)})
            amount += 1
            bit *= 2
    if transpose:
        for other in range(4):
            @pl.when(jnp.logical_not(jnp.logical_and(place.stays, place.col == other)))
            def _():
                signal({"row": place.plane, "col": other})

            @pl.when(jnp.logical_not(jnp.logical_and(place.stays, place.row == other)))
            def _():
                signal({"row": other, "col": place.source})
        amount = amount + 8 - 2 * place.stays.astype(jnp.int32)
    pl.semaphore_wait(barrier, amount)


class Transpose:
    def __init__(self, place, src, dst, sems, first):
        self.place, self.src, self.dst, self.sems, self.first = place, src, dst, sems, first
        self.rows, self.width = src.shape[0] // 4, src.shape[1]

    def out(self, other):
        p = self.place
        send, recv = self.sems
        return pltpu.make_async_remote_copy(
            src_ref=self.src.at[pl.ds(other * self.rows, self.rows)],
            dst_ref=self.dst.at[:, hint(p.row, self.width)],
            send_sem=send.at[self.first + other], recv_sem=recv.at[self.first + p.row],
            device_id={"row": p.plane, "col": other}, device_id_type=MESH,
        )

    def kept(self):
        p = self.place
        return pltpu.make_async_copy(
            self.src.at[hint(p.col, self.rows)],
            self.dst.at[:, hint(p.row, self.width)],
            self.sems[1].at[self.first + p.row],
        )

    def start(self):
        p = self.place
        for other in range(4):
            @pl.when(jnp.logical_not(jnp.logical_and(p.stays, p.col == other)))
            def _():
                self.out(other).start()

        @pl.when(p.stays)
        def _():
            self.kept().start()

    def wait_recv(self):
        p = self.place
        for other in range(4):
            mine = jnp.logical_and(p.stays, p.row == other)
            part = self.dst.at[:, pl.ds(other * self.width, self.width)]

            @pl.when(jnp.logical_not(mine))
            def _():
                pltpu.make_async_remote_copy(
                    src_ref=part, dst_ref=part, send_sem=self.sems[0].at[self.first + other],
                    recv_sem=self.sems[1].at[self.first + other],
                    device_id={"row": other, "col": p.source}, device_id_type=MESH,
                ).wait_recv()

            @pl.when(mine)
            def _():
                self.kept().wait()

    def wait_send(self):
        p = self.place
        for other in range(4):
            @pl.when(jnp.logical_not(jnp.logical_and(p.stays, p.col == other)))
            def _():
                self.out(other).wait_send()


class Weight:
    def __init__(self, place, src, dst, offset, by_rows, sems, first):
        self.place, self.src, self.dst, self.offset, self.by_rows = place, src, dst, offset, by_rows
        self.sems, self.first = sems, first
        self.rows, self.width = src.shape
        self.part = self.rows // 2

    def whole(self, side, row):
        if self.by_rows:
            return self.dst.at[side, hint(row, self.rows)]
        return self.dst.at[side, pl.ds(self.offset, self.rows), hint(row, self.width)]

    def piece(self, side, row, half):
        if self.by_rows:
            return self.dst.at[side, hint(row * 2 + half, self.part)]
        start = pl.multiple_of(self.offset + half * self.part, self.part)
        return self.dst.at[side, pl.ds(start, self.part), hint(row, self.width)]

    def own(self):
        return pltpu.make_async_copy(self.src, self.whole(0, self.place.row), self.sems[1].at[self.first])

    def across(self):
        return remote(
            self.src, self.whole(1, self.place.row), self.sems, self.first + 1, {"col": self.place.far}
        )

    def along(self, side, step):
        p = self.place
        src = self.src.at[hint(p.half, self.part)] if side == 0 else self.piece(1, p.row, p.half)
        return remote(
            src, self.piece(side, p.row, p.half), self.sems, self.first + 2 + 3 * side + step - 1,
            {"row": (p.row + step) % 4},
        )

    def came(self, side, step):
        p = self.place
        part = self.piece(side, (p.row + 4 - step) % 4, p.half)
        return remote(
            part, part, self.sems, self.first + 2 + 3 * side + step - 1, {"row": (p.row + step) % 4}
        )

    def twin(self, side, step):
        p = self.place
        part = self.piece(side, (p.row + 4 - step) % 4, p.half)
        return remote(part, part, self.sems, self.first + 8 + 3 * side + step - 1, {"dp": p.twin})

    def from_twin(self, side, step):
        p = self.place
        part = self.piece(side, (p.row + 4 - step) % 4, 1 - p.half)
        return remote(part, part, self.sems, self.first + 8 + 3 * side + step - 1, {"dp": p.twin})


WEIGHT_SEMS = 14


def first_kernel(
    heads, token_total,
    slope_ref, bias_ref, vector_ref, joined_ref, layer_ref, up_ref, down_ref, out_ref, up_bias_ref,
    teacher_ref, cot_ref, valid_ref,
    xt_ref, nall_ref, mixed_ref, att_ref, lse_ref, chip_ref, jall_ref, vall_ref, gt_ref, vt_ref, scale_ref,
    up2_ref, dn2_ref, ub2_ref,
    qs, ks, vs, bias, sc, mx, ls, acc, grad, count, sends, recvs,
):
    sems = (sends, recvs)
    p = Place()
    quarter = xt_ref.shape[0]
    greet(p, True, True)
    moved = Transpose(p, layer_ref, xt_ref, sems, 0)
    target = Transpose(p, grad, gt_ref, sems, 4)
    base = 8
    weights = []
    for n, (src, dst, offset, by_rows) in enumerate(
        ((out_ref, dn2_ref, down_ref.shape[0], False), (up_ref, up2_ref, 0, True), (down_ref, dn2_ref, 0, False))
    ):
        weights.append(Weight(p, src, dst, offset, by_rows, sems, base + n * WEIGHT_SEMS))
    base += 3 * WEIGHT_SEMS
    moved.start()
    small_base, joined_base, bias_base = base, base + 4, base + 8
    base += 10

    def small(step):
        return remote(
            vector_ref, vall_ref.at[:, hint(p.row, 256)], sems, small_base + step, {"row": (p.row + step) % 4}
        )

    def small_came(step):
        part = vall_ref.at[:, hint((p.row + 4 - step) % 4, 256)]
        return remote(part, part, sems, small_base + step, {"row": (p.row + step) % 4})

    def joined(step):
        return remote(
            joined_ref, jall_ref.at[hint(p.row, 256)], sems, joined_base + step, {"row": (p.row + step) % 4}
        )

    def joined_came(step):
        part = jall_ref.at[hint((p.row + 4 - step) % 4, 256)]
        return remote(part, part, sems, joined_base + step, {"row": (p.row + step) % 4})

    small_own = pltpu.make_async_copy(vector_ref, vall_ref.at[:, hint(p.row, 256)], recvs.at[small_base])
    joined_own = pltpu.make_async_copy(joined_ref, jall_ref.at[hint(p.row, 256)], recvs.at[joined_base])
    bias_own = pltpu.make_async_copy(up_bias_ref, ub2_ref.at[0], recvs.at[bias_base])
    bias_far = remote(up_bias_ref, ub2_ref.at[1], sems, bias_base + 1, {"col": p.far})
    small_own.start()
    joined_own.start()
    for step in (1, 2, 3):
        small(step).start()
    bias_own.start()
    bias_far.start()
    for w in weights:
        w.own().start()
        w.across().start()

    total = jnp.sum(jnp.sum(valid_ref[...], axis=0, keepdims=True), axis=1, keepdims=True) * (1.0 / 128.0)
    count[0] = jnp.broadcast_to(total, (8, 128))
    steps = [("col", 1), ("col", 2)]
    bit = 1
    while bit < p.dps:
        steps.append(("dp", bit))
        bit *= 2
    for n, (axis, bit) in enumerate(steps):
        other = partner(p.col if axis == "col" else p.dp, bit)
        tally = remote(count.at[2 * n], count.at[2 * n + 1], sems, base + n, {axis: other})
        tally.start()
        tally.wait()
        count[2 * n + 2] = count[2 * n] + count[2 * n + 1]
    base += len(steps)
    scale_ref[...] = token_total / count[2 * len(steps)]
    scale = scale_ref[:1, :1]

    @pl.loop(0, 16)
    def _(n):
        rows = hint(n, grad.shape[0] // 16)
        factor = valid_ref[rows, :] * scale
        for f in range(grad.shape[1] // 128):
            cols = slice(f * 128, (f + 1) * 128)
            grad[rows, cols] = (
                cot_ref[rows, cols].astype(jnp.float32) - factor * teacher_ref[rows, cols].astype(jnp.float32)
            ).astype(grad.dtype)

    valid_base = base
    base += 1

    def valid_out():
        return pltpu.make_async_remote_copy(
            src_ref=valid_ref.at[hint(p.row, quarter)], dst_ref=vt_ref,
            send_sem=sends.at[valid_base], recv_sem=recvs.at[valid_base],
            device_id={"row": p.plane, "col": p.row}, device_id_type=MESH,
        )

    same = jnp.logical_and(p.stays, p.col == p.row)
    valid_kept = pltpu.make_async_copy(valid_ref.at[hint(p.row, quarter)], vt_ref, recvs.at[valid_base])

    @pl.when(jnp.logical_not(same))
    def _():
        valid_out().start()

    @pl.when(same)
    def _():
        valid_kept.start()

    for step in (1, 2, 3):
        small_came(step).wait_recv()
        small(step).wait_send()
    small_own.wait()
    moved.wait_recv()
    joined_own.wait()
    for step in (1, 2, 3):
        joined(step).start()

    first = p.col * quarter
    @pl.loop(0, quarter // 128)
    def _(n):
        rows = hint(n, 128)
        x = xt_ref[rows, :].astype(jnp.float32)
        center = jnp.mean(x, 1, keepdims=True)
        spread = jnp.mean(x * x, 1, keepdims=True) - center * center
        standard = (x - center) * lax.rsqrt(spread + EPSILON)
        place = pl.ds(pl.multiple_of(first + n * 128, 128), 128)
        nall_ref[place, :] = (standard * vall_ref[0:1, :] + vall_ref[1:2, :]).astype(nall_ref.dtype)

    mine = nall_ref.at[hint(p.col, quarter)]
    to_far = remote(mine, mine, sems, base, {"col": p.far})
    to_near = remote(mine, mine, sems, base + 1, {"col": p.near})
    theirs = nall_ref.at[hint(p.far, quarter)]
    far_came = remote(theirs, theirs, sems, base, {"col": p.far})
    pass_on = remote(theirs, theirs, sems, base + 2, {"col": p.near})
    beside = nall_ref.at[hint(p.near, quarter)]
    near_came = remote(beside, beside, sems, base + 1, {"col": p.near})
    corner = partner(p.far, 1)
    across = nall_ref.at[hint(corner, quarter)]
    corner_came = remote(across, across, sems, base + 2, {"col": p.near})
    base += 3
    to_far.start()
    to_near.start()
    for w in weights:
        for step in (1, 2, 3):
            w.along(0, step).start()
        w.across().wait()
        for step in (1, 2, 3):
            w.along(1, step).start()
    target.start()

    def project(index):
        @pl.loop(0, quarter // 256)
        def _(n):
            rows = pl.ds(pl.multiple_of(index * quarter + n * 256, 256), 256)
            mixed_ref[rows, :] = (nn(nall_ref[rows, :], jall_ref[...]) + bias_ref[...]).astype(mixed_ref.dtype)

    for step in (1, 2, 3):
        joined_came(step).wait_recv()
        joined(step).wait_send()
    project(p.col)
    near_came.wait_recv()
    project(p.near)
    far_came.wait_recv()
    pass_on.start()
    project(p.far)
    corner_came.wait_recv()
    project(corner)

    own_heads = att_ref.shape[1]
    blocks = mixed_ref.shape[0] // BLOCK
    per_chip = blocks // 2

    share_base = base

    def share(n, i):
        return pltpu.make_async_remote_copy(
            src_ref=att_ref.at[hint(i, BLOCK)], dst_ref=chip_ref.at[hint(chip_place(n), BLOCK), pl.ds(own_heads, own_heads)],
            send_sem=sends.at[share_base + n], recv_sem=recvs.at[share_base + n],
            device_id={"col": p.far}, device_id_type=MESH,
        )

    def chip_place(n):
        half = per_chip // 2
        return ((n // half + p.core) % 2) * half + n % half

    def after(it, i):
        @pl.when(it < per_chip)
        def _():
            share(it, i).start()

        @pl.when(it >= per_chip)
        def _():
            chip_ref[hint(chip_place(it - per_chip), BLOCK), :own_heads] = att_ref[hint(i, BLOCK), :]

        for at, n, side in ((4, 0, 0), (4, 0, 1), (5, 1, 0), (6, 1, 1), (7, 2, 0), (7, 2, 1)):
            @pl.when(it == at)
            def _():
                for step in (1, 2, 3):
                    weights[n].came(side, step).wait_recv()
                    weights[n].twin(side, step).start()

    attention_rows(
        heads, lambda it: (it + per_chip * (1 - p.chip)) % blocks, after,
        slope_ref, mixed_ref, att_ref, lse_ref, qs, ks, vs, bias, sc, mx, ls, acc,
    )
    @pl.loop(0, per_chip)
    def _(n):
        share(n, n + per_chip * (1 - p.chip)).wait()

    moved.wait_send()
    to_far.wait_send()
    to_near.wait_send()
    pass_on.wait_send()
    bias_own.wait()
    bias_far.wait()

    @pl.when(jnp.logical_not(same))
    def _():
        valid_out().wait_send()

    kept_in = jnp.logical_and(p.stays, p.col == p.row)

    @pl.when(jnp.logical_not(kept_in))
    def _():
        valid_out().wait_recv()

    @pl.when(kept_in)
    def _():
        valid_kept.wait()

    for w in weights:
        w.own().wait()
        for side in (0, 1):
            for step in (1, 2, 3):
                w.along(side, step).wait_send()
                w.twin(side, step).wait_send()
                w.from_twin(side, step).wait_recv()
    target.wait_recv()
    target.wait_send()


def first_stage(slopes, bias_rows, vectors, joined, layer_in, up, down, out, up_bias, teacher, cot, valid, token_total):
    tokens, width = layer_in.shape
    quarter = tokens // 4
    row_size = lax.axis_size("row")
    features = width * row_size
    joined_width = joined.shape[1]
    heads = joined_width // (3 * HEAD_DIM)
    pairs, blocks = heads // 2, tokens // BLOCK
    f32, bf = jnp.float32, jnp.bfloat16
    hidden, head_rows = down.shape[0], out.shape[0]
    vmem, anyspace = pl.BlockSpec(memory_space=pltpu.VMEM), pl.BlockSpec(memory_space=pl.ANY)
    shape = jax.ShapeDtypeStruct
    bits = 2
    while (1 << (bits - 2)) < lax.axis_size("dp"):
        bits += 1
    count = 8 + 3 * WEIGHT_SEMS + 8 + 2 + bits + 1 + 3 + blocks
    return pl.pallas_call(
        functools.partial(first_kernel, heads, token_total),
        out_shape=(
            shape((quarter, features), bf), shape((tokens, features), bf), shape((tokens, joined_width), bf),
            shape((tokens, heads * HEAD_DIM), bf), shape((heads, blocks, BLOCK), f32),
            shape((tokens // 2, 2 * heads * HEAD_DIM), bf), shape((features, joined_width), bf),
            shape((8, features), f32), shape((quarter, features), bf), shape((quarter, 128), f32), shape((8, 128), f32),
            shape((2, features, up.shape[1]), bf), shape((2, hidden + head_rows, features), bf), shape((2, 8, hidden), f32),
        ),
        in_specs=[pl.BlockSpec(memory_space=pltpu.SMEM), vmem, vmem, anyspace, anyspace, anyspace, anyspace, anyspace,
                  anyspace, vmem, vmem, vmem],
        out_specs=(vmem,) * 8 + (anyspace, anyspace, vmem, anyspace, anyspace, anyspace),
        scratch_shapes=[pltpu.VMEM((heads,blocks,BLOCK,PAIR),bf),pltpu.VMEM((pairs,blocks,BLOCK,PAIR),bf),
            pltpu.VMEM((pairs,blocks,2*BLOCK,PAIR),bf),pltpu.VMEM((heads,BLOCK,BLOCK),f32),
            pltpu.VMEM((heads,blocks,BLOCK,BLOCK),f32),pltpu.VMEM((heads,BLOCK,PAIR),f32),pltpu.VMEM((heads,BLOCK,PAIR),f32),
            pltpu.VMEM((pairs,BLOCK,PAIR),f32),
            pltpu.VMEM((tokens, width), bf), pltpu.VMEM((2 * bits + 1, 8, 128), f32),
            pltpu.SemaphoreType.DMA((count,)), pltpu.SemaphoreType.DMA((count,))],
        compiler_params=pltpu.CompilerParams(vmem_limit_bytes=48 << 20, collective_id=1, has_side_effects=True),
        name="first_stage",
    )(slopes, bias_rows, vectors, joined, layer_in, up, down, out, up_bias, teacher, cot, valid)


class Untranspose:
    def __init__(self, place, src, dst, sems, first):
        self.place, self.src, self.dst, self.sems, self.first = place, src, dst, sems, first
        self.rows, self.width = src.shape[0], src.shape[1] // 4

    def out(self, other):
        p = self.place
        return pltpu.make_async_remote_copy(
            src_ref=self.src.at[:, pl.ds(other * self.width, self.width)],
            dst_ref=self.dst.at[hint(p.col, self.rows)],
            send_sem=self.sems[0].at[self.first + other], recv_sem=self.sems[1].at[self.first + p.col],
            device_id={"row": other, "col": p.source}, device_id_type=MESH,
        )

    def kept(self):
        p = self.place
        return pltpu.make_async_copy(
            self.src.at[:, hint(p.row, self.width)],
            self.dst.at[hint(p.col, self.rows)],
            self.sems[1].at[self.first + p.col],
        )

    def start(self):
        p = self.place
        for other in range(4):
            @pl.when(jnp.logical_not(jnp.logical_and(p.stays, p.row == other)))
            def _():
                self.out(other).start()

        @pl.when(p.stays)
        def _():
            self.kept().start()

    def wait_recv(self):
        p = self.place
        for other in range(4):
            mine = jnp.logical_and(p.stays, p.col == other)
            part = self.dst.at[pl.ds(other * self.rows, self.rows)]

            @pl.when(jnp.logical_not(mine))
            def _():
                pltpu.make_async_remote_copy(
                    src_ref=part, dst_ref=part, send_sem=self.sems[0].at[self.first + other],
                    recv_sem=self.sems[1].at[self.first + other],
                    device_id={"row": p.plane, "col": other}, device_id_type=MESH,
                ).wait_recv()

            @pl.when(mine)
            def _():
                self.kept().wait()

    def wait_send(self):
        p = self.place
        for other in range(4):
            @pl.when(jnp.logical_not(jnp.logical_and(p.stays, p.row == other)))
            def _():
                self.out(other).wait_send()


def add_into(total, pieces, rows=128):
    @pl.loop(0, total.shape[0] // rows)
    def _(n):
        part = hint(n, rows)
        value = total[part, :].astype(jnp.float32)
        for piece in pieces:
            value = value + piece[part, :].astype(jnp.float32)
        total[part, :] = value.astype(total.dtype)


class Share:
    def __init__(self, place, kind, own, far, result, buffers, sems, first):
        self.p, self.kind, self.own, self.far, self.result, self.sems, self.first = (
            place, kind, own, far, result, sems, first
        )
        self.width = own.shape[1]
        self.part = self.width // 2
        self.block = own.shape[0] // 4
        self.mine, self.theirs = hint(place.half, self.part), hint(1 - place.half, self.part)
        self.buffers = buffers

    def first_copies(self):
        p, b = self.p, self.buffers
        if self.kind == "xy":
            return [
                remote(src.at[:, self.theirs], b["came"].at[n], self.sems, self.first + n, {"dp": p.twin})
                for n, src in enumerate((self.own, self.far))
            ]
        if self.kind == "yx":
            return [remote(self.far, b["came"], self.sems, self.first, {"col": p.far})]
        return [remote(self.own.at[:, self.theirs], b["half"], self.sems, self.first, {"dp": p.twin})]

    def start(self):
        for copy in self.first_copies():
            copy.start()

    def add_own(self, totals, sources):
        load = self.buffers["load"]
        parts = [
            (total.at[pl.ds(n * self.block, self.block)], source.at[pl.ds(n * self.block, self.block)])
            for total, source in zip(totals, sources)
            for n in range(4)
        ]
        copies = [
            pltpu.make_async_copy(source, load.at[n % 2], self.sems[1].at[self.first + 8 + n % 2])
            for n, (_, source) in enumerate(parts)
        ]
        copies[0].start()
        for n, (total, _) in enumerate(parts):
            if n + 1 < len(parts):
                copies[n + 1].start()
            copies[n].wait()
            add_into(total, [load.at[n % 2]])

    def second_copy(self):
        p, b = self.p, self.buffers
        if self.kind == "xy":
            return remote(b["came"].at[1], b["other"], self.sems, self.first + 2, {"col": p.far})
        return remote(b["came"].at[:, self.theirs], b["half"], self.sems, self.first + 2, {"dp": p.twin})

    def first_sum(self):
        b = self.buffers
        for copy in self.first_copies():
            copy.wait()
        if self.kind == "xy":
            self.add_own(
                [b["came"].at[n] for n in (0, 1)], [src.at[:, self.mine] for src in (self.own, self.far)]
            )
        elif self.kind == "yx":
            self.add_own([b["came"]], [self.own])
        else:
            add_into(b["half"], [self.own.at[:, self.mine]])

    def total(self):
        return self.buffers["came"].at[0] if self.kind == "xy" else self.buffers["half"]

    def second_sum(self):
        b = self.buffers
        self.second_copy().wait()
        if self.kind == "xy":
            add_into(b["came"].at[0], [b["other"]])
        else:
            add_into(b["half"], [b["came"].at[:, self.mine]])

    def row_copy(self, step):
        p = self.p
        target = (p.row + step) % 4
        return remote(
            self.total().at[hint(target, self.block)], self.buffers["rows"].at[step - 1], self.sems,
            self.first + 2 + step, {"row": target},
        )

    def start_rows(self):
        for step in (1, 2, 3):
            self.row_copy(step).start()

    def last_copy(self):
        part = self.buffers["last"]
        return remote(part.at[self.p.half], part.at[self.p.half], self.sems, self.first + 6, {"dp": self.p.twin})

    def last_came(self):
        part = self.buffers["last"]
        return remote(part.at[1 - self.p.half], part.at[1 - self.p.half], self.sems, self.first + 6, {"dp": self.p.twin})

    def row_sum(self):
        for step in (1, 2, 3):
            self.row_copy(step).wait()
        b = self.buffers
        total, last = self.total(), b["last"]

        @pl.loop(0, self.block // 64)
        def _(n):
            part = hint(n, 64)
            rows = pl.ds(pl.multiple_of(self.p.row * self.block + n * 64, 64), 64)
            value = total[rows, :].astype(jnp.float32)
            for step in range(3):
                value = value + b["rows"][step, part, :].astype(jnp.float32)
            last[self.p.half, part, :] = value.astype(last.dtype)

        self.last_copy().start()

    def finish(self):
        self.last_copy().wait_send()
        self.last_came().wait_recv()
        for half in (0, 1):
            self.result[:, half * self.part : (half + 1) * self.part] = self.buffers["last"][half].astype(
                self.result.dtype
            )


SHARE_SEMS = 10


def share_scratch(kind, features, width):
    bf, part = jnp.bfloat16, width // 2
    if kind == "xy":
        own = dict(load=(2, features // 4, part), came=(2, features, part), other=(features, part))
    elif kind == "yx":
        own = dict(load=(2, features // 4, width), came=(features, width), half=(features, part))
    else:
        own = dict(half=(features, part))
    own["rows"] = (3, features // 4, part)
    own["last"] = (2, features // 4, part)
    return {name: pltpu.VMEM(shape, bf) for name, shape in own.items()}


def last_kernel(
    heads, kinds,
    slope_ref, mixed_ref, att_ref, lse_ref, nall_ref, jall_ref, xt_ref, middle_ref, gain_ref, early_ref,
    up_sums_ref, teacher_ref, valid_ref, grads_own_ref, grads_far_ref, result_ref,
    up_own, up_far, down_own, down_far, out_own, out_far,
    layer_out_ref, input_grad_ref, up_ref, down_ref, out_ref, joined_ref, vector_ref,
    dout, grad_mixed, qs, ks, km, vp, ds_, delta, bias, steep, dq, dk, dv,
    gn, near_in, far_in, jgrad, vectors, scratch, sends, recvs,
):
    sems = (sends, recvs)
    p = Place()
    f32, bf = jnp.float32, jnp.bfloat16
    quarter, features = xt_ref.shape
    tokens = mixed_ref.shape[0]
    greet(p, True, True)
    base = 0
    back = Untranspose(p, result_ref, layer_out_ref, sems, base)
    ingrad = gn.at[0]
    grad_back = Untranspose(p, ingrad, input_grad_ref, sems, base + 4)
    base += 8

    def natural(chip, n):
        return 2 * chip + (p.core + n) % 2

    share_att = [
        remote(
            grads_far_ref.at[pl.ds(n * quarter, quarter)], dout.at[hint(natural(p.chip, n), quarter)], sems,
            base + n, {"col": p.far},
        )
        for n in (0, 1)
    ]
    for copy in share_att:
        copy.start()
    came_att = [
        remote(
            dout.at[hint(natural(1 - p.chip, n), quarter)], dout.at[hint(natural(1 - p.chip, n), quarter)], sems,
            base + n, {"col": p.far},
        )
        for n in (0, 1)
    ]
    base += 2
    up = Share(p, kinds[0], up_own, up_far, up_ref, scratch["up"], sems, base)
    down = Share(p, kinds[1], down_own, down_far, down_ref, scratch["down"], sems, base + SHARE_SEMS)
    out = Share(p, kinds[2], out_own, out_far, out_ref, scratch["out"], sems, base + 2 * SHARE_SEMS)
    joined = Share(p, "x", jgrad, None, joined_ref, scratch["joined"], sems, base + 3 * SHARE_SEMS)
    base += 4 * SHARE_SEMS
    up.start()
    out.start()
    down.start()
    back.start()
    for n in (0, 1):
        dout[hint(natural(p.chip, n), quarter), :] = grads_own_ref[n * quarter : (n + 1) * quarter, :]
    for copy in came_att:
        copy.wait_recv()
    for copy in share_att:
        copy.wait_send()

    attention_rows_backward(
        heads, slope_ref, mixed_ref, dout, att_ref, lse_ref, grad_mixed, qs, ks, km, vp, ds_, delta, bias, steep, dq, dk, dv
    )

    def product(index, slot):
        @pl.loop(0, quarter // 256)
        def _(n):
            rows = pl.ds(pl.multiple_of(index * quarter + n * 256, 256), 256)
            gn[slot, hint(n, 256), :] = nt(grad_mixed[rows, :], jall_ref[...]).astype(bf)

    corner = partner(p.far, 1)
    to_near = [
        remote(gn.at[n], near_in.at[n], sems, base + n, {"col": p.near}) for n in (0, 1)
    ]
    to_far = remote(gn.at[2], far_in, sems, base + 2, {"col": p.far})
    base += 3
    product(corner, 0)
    to_near[0].start()
    product(p.near, 1)
    to_near[1].start()
    product(p.far, 2)
    to_near[0].wait()
    add_into(gn.at[2], [near_in.at[0]])
    to_far.start()
    product(p.col, 3)
    up.first_sum()

    @pl.loop(0, features // 128)
    def _(f):
        cols = hint(f, 128)
        value = tn(nall_ref[:, cols], grad_mixed[...])
        jgrad[cols, :] = value.astype(bf)

    joined.start()
    sums = jnp.zeros((1, mixed_ref.shape[1]), f32)
    for n in range(tokens // 256):
        sums = sums + jnp.sum(grad_mixed[n * 256 : (n + 1) * 256, :].astype(f32), axis=0, keepdims=True)
    vectors[0, 0:2, :] = jnp.zeros((2, features), f32)
    vectors[0, 2:8, :] = early_ref[2:8, :]
    vectors[0, 8:16, :] = jnp.zeros((8, features), f32)
    vectors[0, pl.ds(8 + p.col, 1), :] = up_sums_ref[0:1, :]
    vectors[0, pl.ds(8 + p.far, 1), :] = up_sums_ref[1:2, :]
    vectors[0, pl.ds(12 + p.col, 1), 0 : sums.shape[1]] = sums

    to_near[1].wait()
    to_far.wait()

    @pl.loop(0, quarter // 64)
    def _(n):
        rows = hint(n, 64)
        grad = gn[3, rows, :].astype(f32) + near_in[1, rows, :].astype(f32) + far_in[rows, :].astype(f32)
        x = xt_ref[rows, :].astype(f32)
        center = jnp.mean(x, 1, keepdims=True)
        spread = jnp.mean(x * x, 1, keepdims=True) - center * center
        inverse = lax.rsqrt(spread + EPSILON)
        standard = (x - center) * inverse
        vectors[0, 0:1, :] += jnp.sum(grad * standard, axis=0, keepdims=True)
        vectors[0, 1:2, :] += jnp.sum(grad, axis=0, keepdims=True)
        scaled = grad * gain_ref[0:1, :]
        first = jnp.mean(scaled, 1, keepdims=True)
        second = jnp.mean(scaled * standard, 1, keepdims=True)
        ingrad[rows, :] = (middle_ref[rows, :] + inverse * (scaled - first - standard * second)).astype(bf)

    grad_back.start()
    up.second_copy().start()
    out.first_sum()
    out.second_copy().start()
    down.first_sum()
    down.second_copy().start()
    joined.first_sum()
    joined.start_rows()

    back.wait_recv()
    width = layer_out_ref.shape[1]
    error = jnp.zeros((1, 128), f32)
    for n in range(tokens // 128):
        rows = slice(n * 128, (n + 1) * 128)
        for f in range(width // 128):
            cols = slice(f * 128, (f + 1) * 128)
            off = layer_out_ref[rows, cols].astype(f32) - teacher_ref[rows, cols].astype(f32)
            error = error + jnp.sum(off * off * valid_ref[rows, :].astype(f32), axis=0, keepdims=True)
    vectors[0, 6:7, 0:128] = error

    steps = [("row", 1), ("row", 2), ("col", 1), ("col", 2)]
    bit = 1
    while bit < p.dps:
        steps.append(("dp", bit))
        bit *= 2
    up.second_sum()
    up.start_rows()
    for n, (axis, bit) in enumerate(steps):
        other = partner({"row": p.row, "col": p.col, "dp": p.dp}[axis], bit)
        tally = remote(vectors.at[2 * n], vectors.at[2 * n + 1], sems, base + n, {axis: other})
        tally.start()
        tally.wait()
        vectors[2 * n + 2] = vectors[2 * n] + vectors[2 * n + 1]
    vector_ref[...] = vectors[2 * len(steps)]
    out.second_sum()
    out.start_rows()
    down.second_sum()
    down.start_rows()
    joined.row_sum()
    up.row_sum()
    out.row_sum()
    down.row_sum()
    for share in (joined, up, out, down):
        share.finish()
    back.wait_send()
    grad_back.wait_recv()
    grad_back.wait_send()


def last_stage(slopes, mixed, att, lse, nall, jall, xt, middle, gain, early, up_sums, teacher, valid, grads, result,
               up_pair, down_pair, out_pair):
    tokens, joined_width = mixed.shape
    quarter, features = xt.shape
    heads = joined_width // (3 * HEAD_DIM)
    pairs, blocks = heads // 2, tokens // BLOCK
    f32, bf = jnp.float32, jnp.bfloat16
    block = features // 4
    kinds = ("xy", "yx", "yx")
    vmem, anyspace = pl.BlockSpec(memory_space=pltpu.VMEM), pl.BlockSpec(memory_space=pl.ANY)
    shape = jax.ShapeDtypeStruct
    bits = 4
    while (1 << (bits - 4)) < lax.axis_size("dp"):
        bits += 1
    count = 8 + 2 + 4 * SHARE_SEMS + 3 + bits
    widths = (up_pair[0].shape[1], down_pair[0].shape[1], out_pair[0].shape[1])
    scratch = {
        name: share_scratch(kind, features, width)
        for name, kind, width in zip(("up", "down", "out", "joined"), kinds + ("x",), widths + (joined_width,))
    }
    return pl.pallas_call(
        functools.partial(last_kernel, heads, kinds),
        out_shape=(
            shape((tokens, block), bf), shape((tokens, block), bf), shape((block, widths[0]), bf),
            shape((block, widths[1]), bf), shape((block, widths[2]), bf), shape((block, joined_width), bf),
            shape((16, features), f32),
        ),
        in_specs=[pl.BlockSpec(memory_space=pltpu.SMEM)] + [vmem] * 13 + [anyspace] + [anyspace] + [anyspace] * 6,
        out_specs=(vmem, anyspace) + (vmem,) * 5,
        scratch_shapes=[
            pltpu.VMEM((tokens, heads * HEAD_DIM), bf), pltpu.VMEM((tokens, joined_width), bf),
            pltpu.VMEM((pairs,blocks,2*BLOCK,PAIR),bf),pltpu.VMEM((pairs,blocks,BLOCK,PAIR),bf),
            pltpu.VMEM((pairs,blocks,2*BLOCK,PAIR),bf),pltpu.VMEM((pairs,blocks,BLOCK,PAIR),bf),
            pltpu.VMEM((pairs,blocks,2*BLOCK,PAIR),bf),pltpu.VMEM((heads,blocks,BLOCK),f32),
            pltpu.VMEM((heads,BLOCK,BLOCK),f32), pltpu.VMEM((heads,BLOCK,PAIR),f32),
            pltpu.VMEM((pairs,blocks,BLOCK,PAIR),f32), pltpu.VMEM((pairs,blocks,BLOCK,PAIR),f32), pltpu.VMEM((pairs,blocks,BLOCK,PAIR),f32),
            pltpu.VMEM((4, quarter, features), bf), pltpu.VMEM((2, quarter, features), bf), pltpu.VMEM((quarter, features), bf),
            pltpu.VMEM((features, joined_width), bf),
            pltpu.VMEM((2 * bits + 1, 16, features), f32), scratch,
            pltpu.SemaphoreType.DMA((count,)), pltpu.SemaphoreType.DMA((count,)),
        ],
        compiler_params=pltpu.CompilerParams(vmem_limit_bytes=62 << 20, collective_id=2, has_side_effects=True),
        name="last_stage",
    )(slopes, mixed, att, lse, nall, jall, xt, middle, gain, early, up_sums, teacher, valid, grads[0], grads[1], result,
      *up_pair, *down_pair, *out_pair)


def swap_with(value, axis, bit):
    size = lax.axis_size(axis)
    return lax.ppermute(value, axis, [(i, i ^ bit) for i in range(size)])


def small_sum(value, axes):
    for axis in axes:
        bit = 1
        while bit < lax.axis_size(axis):
            value = value + swap_with(value, axis, bit)
            bit *= 2
    return value


def standardize(inputs):
    center = jnp.mean(inputs, 1, keepdims=True)
    spread = jnp.mean(inputs * inputs, 1, keepdims=True) - center * center
    inverse = lax.rsqrt(spread + EPSILON)
    return (inputs - center) * inverse, inverse


def norm_backward(grad_normed, standard, inverse, norm_gain):
    scaled = grad_normed * norm_gain
    first = jnp.mean(scaled, 1, keepdims=True)
    second = jnp.mean(scaled * standard, 1, keepdims=True)
    return inverse * (scaled - first - standard * second)


def gelu_local(before):
    return jax.nn.gelu(before, approximate=True)


def low(value):
    return value.astype(jnp.bfloat16)


def pick(stacked, index):
    return lax.dynamic_index_in_dim(stacked, index, 0, keepdims=False)


def sum_other_pairs(value):
    bit = 2
    while bit < lax.axis_size("dp"):
        value = value + swap_with(low(value), "dp", bit).astype(jnp.float32)
        bit *= 2
    return value


def on_device(
    layer_in,
    first_gain,
    first_shift,
    joined_weight,
    joined_bias,
    out_weight,
    out_bias,
    second_gain,
    second_shift,
    up_weight,
    up_bias,
    down_weight,
    down_bias,
    teacher,
    valid,
    cotangent,
):
    row_size, col_size = lax.axis_size("row"), lax.axis_size("col")
    row, col = lax.axis_index("row"), lax.axis_index("col")
    f32 = jnp.float32
    head_count = joined_bias.shape[0]
    quarter = layer_in.shape[0] // col_size
    head_index = col * head_count + jnp.arange(head_count, dtype=jnp.int32)
    slopes = jnp.exp2(-8.0 * (head_index.astype(f32) + 1.0) / HEADS) * LOG2E

    zero_rows = jnp.zeros_like(joined_bias[:, :HEAD_DIM])
    bias_rows = jnp.stack(
        [joined_bias[:, :HEAD_DIM], zero_rows, joined_bias[:, HEAD_DIM:]], axis=1
    ).reshape(1, -1).astype(f32)
    nothing = jnp.zeros_like(first_gain)
    vectors = jnp.stack(
        [first_gain, first_shift, out_bias, second_gain, second_shift, down_bias, nothing, nothing]
    ).astype(f32)
    token_total = layer_in.shape[0] * lax.axis_size("dp") * col_size
    (
        tokens, normed_one_all, mixed, attended, log_totals, attended_chip, joined_all,
        vectors, target, valid_tokens, scale, up_all, down_all, bias_all,
    ) = first_stage(
        slopes, bias_rows, vectors, joined_weight, layer_in, up_weight, down_weight, out_weight,
        jnp.broadcast_to(up_bias.astype(f32), (8, up_bias.shape[0])), teacher, cotangent,
        jnp.broadcast_to(valid.astype(f32)[:, None], (valid.shape[0], 128)), token_total,
    )
    gain_one, shift_one, bias_out, gain_two, shift_two, bias_down = (vectors[i] for i in range(6))
    valid_tokens, scale = valid_tokens[:, :1], scale[0, 0]
    hidden = down_weight.shape[0]
    up_own, up_far = up_all[0], up_all[1]
    down_own, down_far = down_all[0, :hidden], down_all[1, :hidden]
    out_own, out_far = down_all[0, hidden:], down_all[1, hidden:]
    head_width = attended.shape[1]

    inputs = tokens.astype(f32)
    standard_one, inverse_one = standardize(inputs)
    branch = nn(attended_chip[:, :head_width], out_own) + nn(attended_chip[:, head_width:], out_far)
    middle = inputs + (
        branch[:quarter] + swap_with(low(branch[quarter:]), "col", 1).astype(f32) + bias_out
    )
    standard_two, inverse_two = standardize(middle)
    normed_two = low(standard_two * gain_two + shift_two)
    normed_chip = jnp.concatenate([normed_two, swap_with(normed_two, "col", 1)], axis=0)
    before_own = nn(normed_chip, up_own) + bias_all[0, 0]
    before_far = nn(normed_chip, up_far) + bias_all[1, 0]
    active_own, pull_own = jax.vjp(gelu_local, before_own)
    active_far, pull_far = jax.vjp(gelu_local, before_far)
    active_own, active_far = low(active_own), low(active_far)
    branch = nn(active_own, down_own) + nn(active_far, down_far)
    result = middle + (
        branch[:quarter] + swap_with(low(branch[quarter:]), "col", 1).astype(f32) + bias_down
    )
    grad_result = target.astype(f32) + valid_tokens * scale * result
    grad_low = low(grad_result)
    grad_chip = jnp.concatenate([grad_low, swap_with(grad_low, "col", 1)], axis=0)
    grad_before_own = low(pull_own(nt(grad_chip, down_own))[0])
    grad_before_far = low(pull_far(nt(grad_chip, down_far))[0])
    back = nt(grad_before_own, up_own) + nt(grad_before_far, up_far)
    grad_normed_two = back[:quarter] + swap_with(low(back[quarter:]), "col", 1).astype(f32)
    grad_middle = grad_result + norm_backward(grad_normed_two, standard_two, inverse_two, gain_two)
    branch_grad = low(grad_middle)
    branch_chip = jnp.concatenate([branch_grad, swap_with(branch_grad, "col", 1)], axis=0)
    grads = (low(nt(branch_chip, out_own)), low(nt(branch_chip, out_far)))
    down_pair = (low(tn(grad_chip, active_own)), low(tn(grad_chip, active_far)))
    up_pair = (low(tn(normed_chip, grad_before_own)), low(tn(normed_chip, grad_before_far)))
    out_pair = (
        low(tn(branch_chip, attended_chip[:, :head_width])),
        low(tn(branch_chip, attended_chip[:, head_width:])),
    )
    nothing = jnp.zeros((D,), f32)
    early = jnp.stack(
        [
            nothing,
            nothing,
            jnp.sum(branch_grad, 0, dtype=f32),
            jnp.sum(grad_normed_two * standard_two, 0),
            jnp.sum(grad_normed_two, 0),
            jnp.sum(grad_low, 0, dtype=f32),
            nothing,
            nothing,
        ]
    )
    up_sums = jnp.stack(
        [jnp.sum(grad_before_own, 0, dtype=f32), jnp.sum(grad_before_far, 0, dtype=f32)]
    )
    layer_out, input_grad, up_grad, down_grad, out_grad, joined_grad, sums = last_stage(
        slopes, mixed, attended, log_totals, normed_one_all, joined_all, tokens, grad_middle, vectors, early,
        up_sums, teacher, jnp.broadcast_to(low(valid)[:, None], (valid.shape[0], 128)), grads, low(result),
        up_pair, down_pair, out_pair,
    )
    up_grad, down_grad, out_grad, joined_grad = (
        sum_other_pairs(g.astype(f32)) for g in (up_grad, down_grad, out_grad, joined_grad)
    )
    mine = lax.dynamic_slice_in_dim(sums, row * (D // row_size), D // row_size, 1)
    loss = jnp.sum(sums[6, :128]) * scale / (D * token_total)
    up_bias_grad = pick(sums[8:12], col)
    column_sums = pick(sums[12:16], col)[: mixed.shape[1]].reshape(head_count, 3, HEAD_DIM)
    joined_bias_grad = jnp.concatenate([column_sums[:, 0], column_sums[:, 2]], axis=1)
    return (
        layer_out,
        loss,
        input_grad.astype(f32),
        mine[0],
        mine[1],
        joined_grad,
        joined_bias_grad,
        out_grad.T,
        mine[2],
        mine[3],
        mine[4],
        up_grad,
        up_bias_grad,
        down_grad.T,
        mine[5],
    )


def solution(mesh):
    return jax.shard_map(
        on_device,
        mesh=mesh,
        in_specs=(
            P(("dp", "col"), "row"),
            P("row"),
            P("row"),
            P("row", "col"),
            P("col", None),
            P("col", "row"),
            P("row"),
            P("row"),
            P("row"),
            P("row", "col"),
            P("col"),
            P("col", "row"),
            P("row"),
            P(("dp", "col"), "row"),
            P(("dp", "col")),
            P(("dp", "col"), "row"),
        ),
        out_specs=(
            P(("dp", "col"), "row"),
            P(),
            P(("dp", "col"), "row"),
            P("row"),
            P("row"),
            P("row", "col"),
            P("col", None),
            P("col", "row"),
            P("row"),
            P("row"),
            P("row"),
            P("row", "col"),
            P("col"),
            P("col", "row"),
            P("row"),
        ),
        check_vma=False,
    )
```

```python
import functools
import math

import jax
import jax.numpy as jnp
from jax import lax
from jax.experimental import pallas as pl
from jax.experimental.pallas import tpu as pltpu
from jax.sharding import PartitionSpec as P

D = 1024
HEADS = 16
SEQ = 2048
EPSILON = 1e-05
LOG2E = 1.4426950408889634
HEAD_DIM=64
BLOCK=256
HALF=64
PAIR=128
SCALE2 = LOG2E/8.0

def nt(a,b):
    return lax.dot_general(a,b,(((1,),(1,)),((),())),preferred_element_type=jnp.float32)
def nn(a,b):
    return jnp.dot(a,b,preferred_element_type=jnp.float32)
def tn(a,b):
    return lax.dot_general(a,b,(((0,),(0,)),((),())),preferred_element_type=jnp.float32)

def low_lanes(rows):
    return lax.broadcasted_iota(jnp.int32,(rows,PAIR),1) < HALF

def swap(a):
    return jnp.concatenate([a[:,HALF:],a[:,:HALF]],axis=1)

def attention_rows(heads, order, after, slope_ref, mixed_ref, out_ref, lse_ref, qs, ks, vs, bias, sc, mx, ls, acc):
    pairs=heads//2
    blocks=mixed_ref.shape[0]//BLOCK
    lo=low_lanes(BLOCK)
    @pl.loop(0,blocks)
    def _(b):
        rows=pl.ds(pl.multiple_of(b*BLOCK,BLOCK),BLOCK)
        for p in range(pairs):
            t0,t1,t2=(mixed_ref[rows,(3*p+n)*PAIR:(3*p+n+1)*PAIR] for n in range(3))
            zero=jnp.zeros_like(t0)
            qs[2*p,b]=jnp.where(lo,t0,zero)
            qs[2*p+1,b]=jnp.where(lo,zero,t1)
            ks[p,b]=jnp.where(lo,swap(t0),swap(t2))
            vs[p,b,:BLOCK]=jnp.where(lo,t1,zero)
            vs[p,b,BLOCK:]=jnp.where(lo,zero,t2)
    il=lax.broadcasted_iota(jnp.int32,(BLOCK,BLOCK),0)
    jl=lax.broadcasted_iota(jnp.int32,(BLOCK,BLOCK),1)
    tent=jnp.minimum(jl,2*il-jl).astype(jnp.float32)
    for h in range(heads):
        bias[h]=tent*slope_ref[h]
    jrow=lax.broadcasted_iota(jnp.int32,(1,BLOCK),1)
    @pl.loop(0,blocks)
    def _(it):
        i=order(it)
        for h in range(heads):
            t=nt(qs[h,i],ks[h//2,i])*SCALE2+bias[h]
            sc[h,i]=t
            mx[h]=jnp.maximum(t[:,:PAIR],t[:,PAIR:])
        @pl.loop(0,i)
        def _(j):
            place=(jrow+(j-i)*BLOCK).astype(jnp.float32)
            for h in range(heads):
                t=nt(qs[h,i],ks[h//2,j])*SCALE2+place*slope_ref[h]
                sc[h,j]=t
                mx[h]=jnp.maximum(mx[h],jnp.maximum(t[:,:PAIR],t[:,PAIR:]))
        for h in range(heads):
            mx[h]=jnp.broadcast_to(jnp.max(mx[h],1,keepdims=True),(BLOCK,PAIR))
            ls[h]=jnp.zeros((BLOCK,PAIR),jnp.float32)
        for p in range(pairs):
            acc[p]=jnp.zeros((BLOCK,PAIR),jnp.float32)
        @pl.loop(0,i+1)
        def _(j):
            for p in range(pairs):
                both=[]
                for h in (2*p,2*p+1):
                    m=mx[h]
                    ea=jnp.exp2(sc[h,j,:,:PAIR]-m)
                    eb=jnp.exp2(sc[h,j,:,PAIR:]-m)
                    ls[h]+=ea+eb
                    both+=[ea.astype(jnp.bfloat16),eb.astype(jnp.bfloat16)]
                acc[p]+=nn(jnp.concatenate(both,1),vs[p,j])
        rows=pl.ds(pl.multiple_of(i*BLOCK,BLOCK),BLOCK)
        for p in range(pairs):
            tot=[jnp.broadcast_to(jnp.sum(ls[h],1,keepdims=True),(BLOCK,PAIR)) for h in (2*p,2*p+1)]
            out_ref[rows,p*PAIR:(p+1)*PAIR]=(acc[p]/jnp.where(lo,tot[0],tot[1])).astype(out_ref.dtype)
            for n,h in enumerate((2*p,2*p+1)):
                lse=mx[h]+jnp.log2(tot[n])
                lse_ref[h,pl.ds(i,1),:]=lse.T[:1]
        after(it,i)

def attention_rows_backward(heads, slope_ref, mixed_ref, dout_ref, out_ref, lse_ref, grad_ref, qs, ks, km, vp, ds_, delta, bias, steep, dq, dk, dv):
    pairs=heads//2
    blocks=mixed_ref.shape[0]//BLOCK
    lo=low_lanes(BLOCK)
    @pl.loop(0,blocks)
    def _(b):
        rows=pl.ds(pl.multiple_of(b*BLOCK,BLOCK),BLOCK)
        for p in range(pairs):
            t0,t1,t2=(mixed_ref[rows,(3*p+n)*PAIR:(3*p+n+1)*PAIR] for n in range(3))
            zero=jnp.zeros_like(t0)
            qs[p,b,:BLOCK]=jnp.where(lo,t0,zero)
            qs[p,b,BLOCK:]=jnp.where(lo,zero,t1)
            k=jnp.where(lo,swap(t0),swap(t2))
            ks[p,b]=k
            km[p,b,:BLOCK]=jnp.where(lo,k,zero)
            km[p,b,BLOCK:]=jnp.where(lo,zero,k)
            vp[p,b]=jnp.where(lo,t1,t2)
            d=dout_ref[rows,p*PAIR:(p+1)*PAIR]
            ds_[p,b,:BLOCK]=jnp.where(lo,d,zero)
            ds_[p,b,BLOCK:]=jnp.where(lo,zero,d)
            prod=(d.astype(jnp.float32)*out_ref[rows,p*PAIR:(p+1)*PAIR].astype(jnp.float32)).T
            delta[2*p,pl.ds(b,1),:]=jnp.sum(prod[:HALF],0,keepdims=True)
            delta[2*p+1,pl.ds(b,1),:]=jnp.sum(prod[HALF:],0,keepdims=True)
    kl=lax.broadcasted_iota(jnp.int32,(BLOCK,BLOCK),0)
    ql=lax.broadcasted_iota(jnp.int32,(BLOCK,BLOCK),1)
    tent=jnp.minimum(kl,2*ql-kl).astype(jnp.float32)
    ramp=kl.astype(jnp.float32)
    for h in range(heads):
        bias[h]=tent*slope_ref[h]
        steep[h]=ramp[:,:PAIR]*slope_ref[h]
    def block(i,j,first):
        for p in range(pairs):
            ps=[];gs=[]
            for n,h in enumerate((2*p,2*p+1)):
                q=qs[p,i,n*BLOCK:(n+1)*BLOCK]
                d=ds_[p,i,n*BLOCK:(n+1)*BLOCK]
                row=slope_ref[h]*((j-i)*BLOCK).astype(jnp.float32)-lse_ref[h,pl.ds(i,1),:]
                t=nt(ks[p,j],q)*SCALE2+row+(bias[h] if first else jnp.concatenate([steep[h],steep[h]],1))
                e=jnp.exp2(t)
                g=e*(nt(vp[p,j],d)-delta[h,pl.ds(i,1),:])
                ps.append(e.astype(jnp.bfloat16)); gs.append(g.astype(jnp.bfloat16))
            gv=nn(jnp.concatenate(ps,1),ds_[p,i])
            gk=nn(jnp.concatenate(gs,1),qs[p,i])
            gq=tn(jnp.concatenate(gs,0),km[p,j])
            if first:
                dv[p,j]=gv; dk[p,j]=gk; dq[p,i]=gq
            else:
                dv[p,j]+=gv; dk[p,j]+=gk; dq[p,i]+=gq
    @pl.loop(0,blocks)
    def _(i):
        block(i,i,True)
        @pl.loop(0,i)
        def _(j):
            block(i,j,False)
    @pl.loop(0,blocks)
    def _(b):
        rows=pl.ds(pl.multiple_of(b*BLOCK,BLOCK),BLOCK)
        for p in range(pairs):
            a=dq[p,b]*0.125; k=swap(dk[p,b]*0.125); v=dv[p,b]
            for n,t in enumerate((jnp.where(lo,a,k),jnp.where(lo,v,a),jnp.where(lo,k,v))):
                grad_ref[rows,(3*p+n)*PAIR:(3*p+n+1)*PAIR]=t.astype(grad_ref.dtype)


MESH = pl.DeviceIdType.MESH


def hint(index, size):
    return pl.ds(pl.multiple_of(index * size, size), size)


def remote(src, dst, sems, number, target):
    send, recv = sems
    return pltpu.make_async_remote_copy(
        src_ref=src, dst_ref=dst, send_sem=send.at[number], recv_sem=recv.at[number],
        device_id=target, device_id_type=MESH,
    )


def partner(index, bit):
    return index + bit - 2 * bit * ((index // bit) % 2)


class Place:
    def __init__(self):
        self.dp, self.row, self.col = (lax.axis_index(a) for a in ("dp", "row", "col"))
        self.dps = lax.axis_size("dp")
        self.core, self.chip = self.col % 2, self.col // 2
        self.near, self.far = partner(self.col, 1), partner(self.col, 2)
        self.twin = partner(self.dp, 1)
        self.half = self.dp % 2
        self.plane = 3 * self.core + self.chip - 2 * self.core * self.chip
        self.source = 2 * (((self.row + 1) // 2) % 2) + self.row // 2
        self.stays = self.plane == self.row


def greet(place, transpose, counts):
    barrier = pltpu.get_barrier_semaphore()

    def signal(target):
        pl.semaphore_signal(barrier, inc=1, device_id=target, device_id_type=MESH)

    for step in (1, 2, 3):
        signal({"row": (place.row + step) % 4})
    signal({"col": place.near})
    signal({"col": place.far})
    signal({"dp": place.twin})
    amount = 6
    if counts:
        bit = 2
        while bit < place.dps:
            signal({"dp": partner(place.dp, bit)})
            amount += 1
            bit *= 2
    if transpose:
        for other in range(4):
            @pl.when(jnp.logical_not(jnp.logical_and(place.stays, place.col == other)))
            def _():
                signal({"row": place.plane, "col": other})

            @pl.when(jnp.logical_not(jnp.logical_and(place.stays, place.row == other)))
            def _():
                signal({"row": other, "col": place.source})
        amount = amount + 8 - 2 * place.stays.astype(jnp.int32)
    pl.semaphore_wait(barrier, amount)


class Transpose:
    def __init__(self, place, src, dst, sems, first):
        self.place, self.src, self.dst, self.sems, self.first = place, src, dst, sems, first
        self.rows, self.width = src.shape[0] // 4, src.shape[1]

    def out(self, other):
        p = self.place
        send, recv = self.sems
        return pltpu.make_async_remote_copy(
            src_ref=self.src.at[pl.ds(other * self.rows, self.rows)],
            dst_ref=self.dst.at[:, hint(p.row, self.width)],
            send_sem=send.at[self.first + other], recv_sem=recv.at[self.first + p.row],
            device_id={"row": p.plane, "col": other}, device_id_type=MESH,
        )

    def kept(self):
        p = self.place
        return pltpu.make_async_copy(
            self.src.at[hint(p.col, self.rows)],
            self.dst.at[:, hint(p.row, self.width)],
            self.sems[1].at[self.first + p.row],
        )

    def start(self):
        p = self.place
        for other in range(4):
            @pl.when(jnp.logical_not(jnp.logical_and(p.stays, p.col == other)))
            def _():
                self.out(other).start()

        @pl.when(p.stays)
        def _():
            self.kept().start()

    def wait_recv(self):
        p = self.place
        for other in range(4):
            mine = jnp.logical_and(p.stays, p.row == other)
            part = self.dst.at[:, pl.ds(other * self.width, self.width)]

            @pl.when(jnp.logical_not(mine))
            def _():
                pltpu.make_async_remote_copy(
                    src_ref=part, dst_ref=part, send_sem=self.sems[0].at[self.first + other],
                    recv_sem=self.sems[1].at[self.first + other],
                    device_id={"row": other, "col": p.source}, device_id_type=MESH,
                ).wait_recv()

            @pl.when(mine)
            def _():
                self.kept().wait()

    def wait_send(self):
        p = self.place
        for other in range(4):
            @pl.when(jnp.logical_not(jnp.logical_and(p.stays, p.col == other)))
            def _():
                self.out(other).wait_send()


class Weight:
    def __init__(self, place, src, dst, offset, by_rows, last, sems, first):
        self.p, self.src, self.dst, self.offset, self.by_rows, self.last = place, src, dst, offset, by_rows, last
        self.sems, self.first = sems, first
        self.rows, self.width = src.shape
        self.part = self.rows // 2

    def whole(self, side, row):
        if self.by_rows:
            return self.dst.at[side, hint(row, self.rows)]
        return self.dst.at[side, pl.ds(self.offset, self.rows), hint(row, self.width)]

    def piece(self, side, row, half):
        if self.by_rows:
            return self.dst.at[side, hint(row * 2 + half, self.part)]
        start = pl.multiple_of(self.offset + half * self.part, self.part)
        return self.dst.at[side, pl.ds(start, self.part), hint(row, self.width)]

    def other(self, step):
        return (self.p.row + 4 - step) % 4

    def move(self, src, dst, number, target):
        return remote(src, dst, self.sems, self.first + number, target)

    def pass_on(self, side, step, half, number, target):
        src = self.piece(side, self.other(step), half)
        dst = self.piece(1 if "col" in target else side, self.other(step), half)
        return self.move(src, dst, number + step - 1, target)

    def own(self):
        return pltpu.make_async_copy(self.src, self.whole(0, self.p.row), self.sems[1].at[self.first])

    def across(self):
        return self.move(self.src, self.whole(1, self.p.row), 1, {"col": self.p.far})

    def along(self, step):
        p = self.p
        return self.move(
            self.src.at[hint(p.half, self.part)], self.piece(0, p.row, p.half), 1 + step, {"row": (p.row + step) % 4}
        )

    def to_twin(self, step):
        return self.pass_on(0, step, self.p.half, 5, {"dp": self.p.twin})

    def to_far(self, step):
        return self.pass_on(0, step, self.p.half, 8, {"col": self.p.far})

    def onward(self, step):
        if self.last == "y":
            return self.pass_on(0, step, 1 - self.p.half, 11, {"col": self.p.far})
        return self.pass_on(1, step, self.p.half, 11, {"dp": self.p.twin})

    def arrival(self, side, step, half, number):
        part = self.piece(side, self.other(step), half)
        return self.move(part, part, number + step - 1, {"dp": self.p.twin})

    def start(self):
        self.own().start()
        self.across().start()

    def start_along(self):
        for step in (1, 2, 3):
            self.along(step).start()

    def spread(self):
        for step in (1, 2, 3):
            self.arrival(0, step, self.p.half, 2).wait_recv()
            self.to_twin(step).start()
            self.to_far(step).start()

    def spread_last(self):
        p = self.p
        for step in (1, 2, 3):
            if self.last == "y":
                self.arrival(0, step, 1 - p.half, 5).wait_recv()
            else:
                self.arrival(1, step, p.half, 8).wait_recv()
            self.onward(step).start()

    def ready(self):
        p = self.p
        self.own().wait()
        self.across().wait_recv()
        for step in (1, 2, 3):
            if self.last == "y":
                self.arrival(1, step, p.half, 8).wait_recv()
            else:
                self.arrival(0, step, 1 - p.half, 5).wait_recv()
            self.arrival(1, step, 1 - p.half, 11).wait_recv()

    def sent(self):
        self.across().wait_send()
        for step in (1, 2, 3):
            for copy in (self.along(step), self.to_twin(step), self.to_far(step), self.onward(step)):
                copy.wait_send()


WEIGHT_SEMS = 14


class Halves:
    def __init__(self, place, src, dst, sems, first):
        self.p, self.src, self.dst, self.sems, self.first = place, src, dst, sems, first
        self.rows = src.shape[0]
        self.part = self.rows // 2

    def own(self):
        return pltpu.make_async_copy(self.src, self.dst.at[hint(self.p.row, self.rows)], self.sems[1].at[self.first])

    def along(self, step):
        p = self.p
        return remote(
            self.src.at[hint(p.half, self.part)], self.dst.at[hint(2 * p.row + p.half, self.part)], self.sems,
            self.first + step, {"row": (p.row + step) % 4},
        )

    def part_of(self, step, half):
        return self.dst.at[hint(2 * ((self.p.row + 4 - step) % 4) + half, self.part)]

    def to_twin(self, step, half):
        part = self.part_of(step, half)
        return remote(part, part, self.sems, self.first + 3 + step, {"dp": self.p.twin})

    def start(self):
        self.own().start()
        for step in (1, 2, 3):
            self.along(step).start()

    def ready(self):
        p = self.p
        for step in (1, 2, 3):
            part = self.part_of(step, p.half)
            remote(part, part, self.sems, self.first + step, {"dp": p.twin}).wait_recv()
            self.to_twin(step, p.half).start()
        for step in (1, 2, 3):
            self.to_twin(step, 1 - p.half).wait_recv()
        self.own().wait()

    def sent(self):
        for step in (1, 2, 3):
            self.along(step).wait_send()
            self.to_twin(step, self.p.half).wait_send()


HALVES_SEMS = 7


GELU_ROOT = math.sqrt(2.0 / math.pi)
GELU_CUBE = 0.044715


def gelu_pair(x):
    square = x * x
    t = jnp.tanh(GELU_ROOT * x * (1.0 + GELU_CUBE * square))
    half = 0.5 * (1.0 + t)
    slope = half + 0.5 * x * (1.0 - t * t) * (GELU_ROOT * (1.0 + 3.0 * GELU_CUBE * square))
    return x * half, slope


def moments(x):
    center = jnp.mean(x, 1, keepdims=True)
    spread = jnp.mean(x * x, 1, keepdims=True) - center * center
    inverse = lax.rsqrt(spread + EPSILON)
    return (x - center) * inverse, inverse


class Chip:
    def __init__(self, place, sems, first):
        self.p, self.sems, self.first = place, sems, first

    def copy(self, number, src, dst):
        return remote(src, dst, self.sems, self.first + number, {"col": self.p.near})


def first_kernel(
    heads, token_total,
    slope_ref, bias_ref, vector_ref, joined_ref, layer_ref, up_ref, down_ref, out_ref, up_bias_ref,
    teacher_ref, cot_ref, valid_ref,
    xt_ref, nall_ref, mixed_ref, att_ref, lse_ref, jall_ref, vall_ref, scale_ref,
    layer_out_ref, gmid_ref, gown_ref, gfar_ref, early_ref, up_sums_ref,
    upg_own, upg_far, dng_own, dng_far, outg_own, outg_far,
    chip_ref, gt_ref, vt_ref, up2_ref, dn2_ref, ub2_ref, normed, gchip, bchip, give, take, middle, gres, low_ref, stage,
    grad, count, sends, recvs,
):
    sems = (sends, recvs)
    f32, bf = jnp.float32, jnp.bfloat16
    p = Place()
    quarter, features = xt_ref.shape
    hidden = down_ref.shape[0]
    greet(p, True, True)
    moved = Transpose(p, layer_ref, xt_ref, sems, 0)
    target = Transpose(p, grad, gt_ref, sems, 4)
    back = Untranspose(p, low_ref, layer_out_ref, sems, 8)
    base = 12
    w_out = Weight(p, out_ref, dn2_ref, hidden, False, "y", sems, base)
    w_up = Weight(p, up_ref, up2_ref, 0, True, "y", sems, base + WEIGHT_SEMS)
    w_downs = [
        Weight(
            p, down_ref.at[pl.ds(n * (hidden // 2), hidden // 2)], dn2_ref, n * (hidden // 2), False, "x", sems,
            base + (2 + n) * WEIGHT_SEMS,
        )
        for n in (0, 1)
    ]
    weights = [w_out, w_up] + w_downs
    base += 4 * WEIGHT_SEMS
    w_joined = Halves(p, joined_ref, jall_ref, sems, base)
    base += HALVES_SEMS
    moved.start()
    small_base, bias_base = base, base + 4
    base += 6

    def small(step):
        return remote(
            vector_ref, vall_ref.at[:, hint(p.row, 256)], sems, small_base + step, {"row": (p.row + step) % 4}
        )

    def small_came(step):
        part = vall_ref.at[:, hint((p.row + 4 - step) % 4, 256)]
        return remote(part, part, sems, small_base + step, {"row": (p.row + step) % 4})

    small_own = pltpu.make_async_copy(vector_ref, vall_ref.at[:, hint(p.row, 256)], recvs.at[small_base])
    bias_own = pltpu.make_async_copy(up_bias_ref, ub2_ref.at[0], recvs.at[bias_base])
    bias_far = remote(up_bias_ref, ub2_ref.at[1], sems, bias_base + 1, {"col": p.far})
    small_own.start()
    for step in (1, 2, 3):
        small(step).start()
    bias_own.start()
    bias_far.start()
    for w in weights:
        w.start()

    tokens = valid_ref.shape[0]
    counted = jnp.zeros((8, 128), f32)
    for n in range(tokens // 256):
        counted = counted + jnp.sum(
            valid_ref[n * 256 : (n + 1) * 256, :].astype(f32), axis=0, keepdims=True
        )
    count[0] = counted
    steps = [("col", 1), ("col", 2)]
    bit = 1
    while bit < p.dps:
        steps.append(("dp", bit))
        bit *= 2
    for n, (axis, bit) in enumerate(steps):
        other = partner(p.col if axis == "col" else p.dp, bit)
        tally = remote(count.at[2 * n], count.at[2 * n + 1], sems, base + n, {axis: other})
        tally.start()
        tally.wait()
        count[2 * n + 2] = count[2 * n] + count[2 * n + 1]
    base += len(steps)
    scale_ref[...] = token_total / count[2 * len(steps)]
    scale = scale_ref[:1, :1]

    @pl.loop(0, 32)
    def _(n):
        rows = hint(n, grad.shape[0] // 32)
        factor = valid_ref[rows, :].astype(f32) * scale
        for f in range(grad.shape[1] // 128):
            cols = slice(f * 128, (f + 1) * 128)
            grad[rows, cols] = (
                cot_ref[rows, cols].astype(f32) - factor * teacher_ref[rows, cols].astype(f32)
            ).astype(bf)

    valid_base = base
    base += 1

    def valid_out():
        return pltpu.make_async_remote_copy(
            src_ref=valid_ref.at[hint(p.row, quarter)], dst_ref=vt_ref,
            send_sem=sends.at[valid_base], recv_sem=recvs.at[valid_base],
            device_id={"row": p.plane, "col": p.row}, device_id_type=MESH,
        )

    same = jnp.logical_and(p.stays, p.col == p.row)
    valid_kept = pltpu.make_async_copy(valid_ref.at[hint(p.row, quarter)], vt_ref, recvs.at[valid_base])

    for step in (1, 2, 3):
        small_came(step).wait_recv()
        small(step).wait_send()
    small_own.wait()
    moved.wait_recv()
    w_joined.start()

    first = p.col * quarter

    def norm_one(n):
        rows = hint(n, 128)
        standard, _ = moments(xt_ref[rows, :].astype(f32))
        place = pl.ds(pl.multiple_of(first + n * 128, 128), 128)
        nall_ref[place, :] = (standard * vall_ref[0:1, :] + vall_ref[1:2, :]).astype(bf)

    pl.loop(0, quarter // 128)(norm_one)
    mine = nall_ref.at[hint(p.col, quarter)]
    to_far = remote(mine, mine, sems, base, {"col": p.far})
    to_near = remote(mine, mine, sems, base + 1, {"col": p.near})
    theirs = nall_ref.at[hint(p.far, quarter)]
    far_came = remote(theirs, theirs, sems, base, {"col": p.far})
    pass_on = remote(theirs, theirs, sems, base + 2, {"col": p.near})
    beside = nall_ref.at[hint(p.near, quarter)]
    near_came = remote(beside, beside, sems, base + 1, {"col": p.near})
    corner = partner(p.far, 1)
    across = nall_ref.at[hint(corner, quarter)]
    corner_came = remote(across, across, sems, base + 2, {"col": p.near})
    base += 3
    to_far.start()
    to_near.start()

    @pl.when(jnp.logical_not(same))
    def _():
        valid_out().start()

    @pl.when(same)
    def _():
        valid_kept.start()

    def project(index):
        @pl.loop(0, quarter // 256)
        def _(n):
            rows = pl.ds(pl.multiple_of(index * quarter + n * 256, 256), 256)
            mixed_ref[rows, :] = (nn(nall_ref[rows, :], jall_ref[...]) + bias_ref[...]).astype(bf)

    w_joined.ready()
    w_out.start_along()
    w_up.start_along()
    project(p.col)
    near_came.wait_recv()
    project(p.near)
    far_came.wait_recv()
    pass_on.start()
    project(p.far)
    corner_came.wait_recv()
    project(corner)
    w_out.spread()

    own_heads = att_ref.shape[1]
    blocks = tokens // BLOCK
    per_chip = blocks // 2
    share_base = base
    base += per_chip

    def chip_place(n):
        half = per_chip // 2
        return ((n // half + p.core) % 2) * half + n % half

    def share(n, i):
        return pltpu.make_async_remote_copy(
            src_ref=att_ref.at[hint(i, BLOCK)], dst_ref=chip_ref.at[hint(chip_place(n), BLOCK), pl.ds(own_heads, own_heads)],
            send_sem=sends.at[share_base + n], recv_sem=recvs.at[share_base + n],
            device_id={"col": p.far}, device_id_type=MESH,
        )

    def after(it, i):
        @pl.when(it < per_chip)
        def _():
            share(it, i).start()

        @pl.when(it >= per_chip)
        def _():
            chip_ref[hint(chip_place(it - per_chip), BLOCK), :own_heads] = att_ref[hint(i, BLOCK), :]

        @pl.when(it == p.chip)
        def _():
            w_out.spread_last()

        @pl.when(it == 2 + 3 * p.chip)
        def _():
            w_up.spread()
            w_downs[0].start_along()
            w_downs[1].start_along()

    def attend(*scratch):
        attention_rows(
            heads, lambda it: (it + per_chip * (1 - p.chip)) % blocks, after,
            slope_ref, mixed_ref, att_ref, lse_ref, *scratch,
        )

    pairs = heads // 2
    pl.run_scoped(
        attend,
        pltpu.VMEM((heads, blocks, BLOCK, PAIR), bf), pltpu.VMEM((pairs, blocks, BLOCK, PAIR), bf),
        pltpu.VMEM((pairs, blocks, 2 * BLOCK, PAIR), bf), pltpu.VMEM((heads, BLOCK, BLOCK), f32),
        pltpu.VMEM((heads, blocks, BLOCK, BLOCK), f32), pltpu.VMEM((heads, BLOCK, PAIR), f32),
        pltpu.VMEM((heads, BLOCK, PAIR), f32), pltpu.VMEM((pairs, BLOCK, PAIR), f32),
    )

    @pl.loop(0, per_chip)
    def _(n):
        share(n, n + per_chip * (1 - p.chip)).wait()

    w_out.ready()
    w_up.spread_last()
    target.start()
    core = Chip(p, sems, base)
    base += 12
    ROWS = 256
    halves = quarter // ROWS

    def swap_rows(number, buffer, n):
        return core.copy(
            number + n, buffer.at[pl.ds(n * ROWS, ROWS)], buffer.at[pl.ds(quarter + n * ROWS, ROWS)]
        )

    def swap_came(number, buffer, n):
        part = buffer.at[pl.ds(quarter + n * ROWS, ROWS)]
        return core.copy(number + n, part, part)

    def give_rows(number, n):
        return core.copy(number + n, give.at[pl.ds(n * ROWS, ROWS)], take.at[pl.ds(n * ROWS, ROWS)])

    def take_rows(number, n):
        part = take.at[pl.ds(n * ROWS, ROWS)]
        return core.copy(number + n, part, part)

    def partial(number, keep, product, again):
        if again:
            for n in range(halves):
                give_rows(number - 4, n).wait_send()
        for n in range(halves):
            give[n * ROWS : (n + 1) * ROWS, :] = product(pl.ds(quarter + n * ROWS, ROWS)).astype(bf)
            give_rows(number, n).start()
        for n in range(halves):
            keep[n * ROWS : (n + 1) * ROWS, :] = product(pl.ds(n * ROWS, ROWS))

    partial(
        0, middle,
        lambda rows: nn(chip_ref[rows, :own_heads], dn2_ref[0, hidden:, :])
        + nn(chip_ref[rows, own_heads:], dn2_ref[1, hidden:, :]),
        False,
    )
    for n in range(halves):
        take_rows(0, n).wait_recv()

        @pl.loop(0, ROWS // 64)
        def _(m):
            rows = pl.ds(pl.multiple_of(n * ROWS + m * 64, 64), 64)
            value = xt_ref[rows, :].astype(f32) + (
                middle[rows, :] + take[rows, :].astype(f32) + vall_ref[2:3, :]
            )
            middle[rows, :] = value
            standard, _ = moments(value)
            normed[rows, :] = (standard * vall_ref[3:4, :] + vall_ref[4:5, :]).astype(bf)

        swap_rows(2, normed, n).start()
    for w in w_downs:
        w.spread()
    w_up.ready()
    bias_own.wait()
    bias_far.wait()

    def middle_part(act, der, keep):
        wide = 256

        def up_rows(n):
            rows = pl.ds(pl.multiple_of(n * ROWS, ROWS), ROWS)

            @pl.loop(0, 2 * hidden // wide, unroll=2)
            def _(m):
                side, cols = m // (hidden // wide), hint(m % (hidden // wide), wide)
                before = nn(normed[rows, :], up2_ref[side, :, cols]) + ub2_ref[side, 0:1, cols]
                value, slope = gelu_pair(before)
                act[side, rows, cols] = value.astype(bf)
                der[side, rows, cols] = slope.astype(bf)

        pl.loop(0, halves)(up_rows)
        for n in range(halves):
            swap_came(2, normed, n).wait_recv()
        for w in w_downs:
            w.spread_last()
        pl.loop(halves, 2 * halves)(up_rows)
        for w in w_downs:
            w.ready()
        partial(
            4, gres,
            lambda rows: nn(act[0, rows, :], dn2_ref[0, :hidden, :]) + nn(act[1, rows, :], dn2_ref[1, :hidden, :]),
            True,
        )
        target.wait_recv()

        @pl.when(jnp.logical_not(same))
        def _():
            valid_out().wait_send()
            valid_out().wait_recv()

        @pl.when(same)
        def _():
            valid_kept.wait()

        early_ref[...] = jnp.zeros_like(early_ref)
        for n in range(halves):
            take_rows(4, n).wait_recv()

            @pl.loop(0, ROWS // 64)
            def _(m):
                rows = pl.ds(pl.multiple_of(n * ROWS + m * 64, 64), 64)
                result = middle[rows, :] + (gres[rows, :] + take[rows, :].astype(f32) + vall_ref[5:6, :])
                low_ref[rows, :] = result.astype(bf)
                factor = vt_ref[rows, :].astype(f32)[:, :1] * scale
                value = gt_ref[rows, :].astype(f32) + factor * result
                gres[rows, :] = value
                rounded = value.astype(bf)
                gchip[rows, :] = rounded
                early_ref[5:6, :] += jnp.sum(rounded.astype(f32), axis=0, keepdims=True)

            swap_rows(6, gchip, n).start()
        back.start()
        up_sums_ref[...] = jnp.zeros_like(up_sums_ref)

        def before_rows(n):
            rows = pl.ds(pl.multiple_of(n * ROWS, ROWS), ROWS)

            @pl.loop(0, 2 * hidden // wide, unroll=2)
            def _(m):
                side, cols = m // (hidden // wide), hint(m % (hidden // wide), wide)
                value = nt(gchip[rows, :], dn2_ref[side, cols, :]) * der[side, rows, cols].astype(f32)
                rounded = value.astype(bf)
                der[side, rows, cols] = rounded
                up_sums_ref[side, 0:1, cols] += jnp.sum(rounded.astype(f32), axis=0, keepdims=True)

        pl.loop(0, halves)(before_rows)
        for n in range(halves):
            swap_came(6, gchip, n).wait_recv()
        pl.loop(halves, 2 * halves)(before_rows)
        partial(
            8, keep, lambda rows: nt(der[0, rows, :], up2_ref[0]) + nt(der[1, rows, :], up2_ref[1]), True
        )

        outs = [(dng_own, gchip, act, 0), (dng_far, gchip, act, 1), (upg_own, normed, der, 0), (upg_far, normed, der, 1)]

        def weight_grad(slot, source, values, sinks):
            @pl.loop(0, features // 256)
            def _(f):
                cols = hint(f, 256)
                turned = source[:, cols].T
                for side, sink in enumerate(sinks):
                    copy = pltpu.make_async_copy(stage.at[side], sink.at[cols], recvs.at[slot + side])

                    @pl.when(f > 0)
                    def _():
                        copy.wait()

                    stage[side] = nn(turned, values[side]).astype(bf)
                    copy.start()

            for side, sink in enumerate(sinks):
                pltpu.make_async_copy(stage.at[side], sink.at[pl.ds(0, 256)], recvs.at[slot + side]).wait()

        weight_grad(stage_base, gchip, act, (dng_own, dng_far))
        for n in range(halves):
            take_rows(8, n).wait_recv()

            @pl.loop(0, ROWS // 64)
            def _(m):
                rows = pl.ds(pl.multiple_of(n * ROWS + m * 64, 64), 64)
                value = keep[rows, :] + take[rows, :].astype(f32)
                standard, inverse = moments(middle[rows, :])
                early_ref[3:4, :] += jnp.sum(value * standard, axis=0, keepdims=True)
                early_ref[4:5, :] += jnp.sum(value, axis=0, keepdims=True)
                scaled = value * vall_ref[3:4, :]
                one = jnp.mean(scaled, 1, keepdims=True)
                two = jnp.mean(scaled * standard, 1, keepdims=True)
                value = gres[rows, :] + inverse * (scaled - one - standard * two)
                gmid_ref[rows, :] = value
                rounded = value.astype(bf)
                bchip[rows, :] = rounded
                early_ref[2:3, :] += jnp.sum(rounded.astype(f32), axis=0, keepdims=True)

            swap_rows(10, bchip, n).start()
        weight_grad(stage_base, normed, der, (upg_own, upg_far))

    stage_base = base
    base += 2
    pl.run_scoped(
        middle_part,
        pltpu.VMEM((2, 2 * quarter, hidden), bf), pltpu.VMEM((2, 2 * quarter, hidden), bf), pltpu.VMEM((quarter, features), f32),
    )
    for n in range(halves):
        swap_came(10, bchip, n).wait_recv()
    for n in range(2 * halves):
        rows = pl.ds(n * ROWS, ROWS)
        gown_ref[rows, :] = nt(bchip[rows, :], dn2_ref[0, hidden:, :]).astype(bf)
        gfar_ref[rows, :] = nt(bchip[rows, :], dn2_ref[1, hidden:, :]).astype(bf)

    @pl.loop(0, features // 256)
    def _(f):
        cols = hint(f, 256)
        turned = bchip[:, cols].T
        outg_own[cols, :] = nn(turned, chip_ref[:, :own_heads]).astype(bf)
        outg_far[cols, :] = nn(turned, chip_ref[:, own_heads:]).astype(bf)

    back.wait_recv()
    error = jnp.zeros((1, 128), f32)
    for n in range(tokens // 128):
        rows = slice(n * 128, (n + 1) * 128)
        for f in range(layer_out_ref.shape[1] // 128):
            cols = slice(f * 128, (f + 1) * 128)
            off = layer_out_ref[rows, cols].astype(f32) - teacher_ref[rows, cols].astype(f32)
            error = error + jnp.sum(off * off * valid_ref[rows, :].astype(f32), axis=0, keepdims=True)
    early_ref[6:7, 0:128] = error

    moved.wait_send()
    to_far.wait_send()
    to_near.wait_send()
    pass_on.wait_send()
    w_joined.sent()
    for w in weights:
        w.sent()
    target.wait_send()
    back.wait_send()
    for n in range(halves):
        for number, buffer in ((2, normed), (6, gchip), (10, bchip)):
            swap_rows(number, buffer, n).wait_send()
        give_rows(8, n).wait_send()


def first_stage(slopes, bias_rows, vectors, joined, layer_in, up, down, out, up_bias, teacher, cot, valid, token_total):
    tokens, width = layer_in.shape
    quarter = tokens // 4
    features = width * lax.axis_size("row")
    joined_width = joined.shape[1]
    heads = joined_width // (3 * HEAD_DIM)
    blocks = tokens // BLOCK
    f32, bf = jnp.float32, jnp.bfloat16
    hidden, head_rows = down.shape[0], out.shape[0]
    vmem, anyspace = pl.BlockSpec(memory_space=pltpu.VMEM), pl.BlockSpec(memory_space=pl.ANY)
    shape = jax.ShapeDtypeStruct
    bits = 2
    while (1 << (bits - 2)) < lax.axis_size("dp"):
        bits += 1
    count = 12 + 4 * WEIGHT_SEMS + HALVES_SEMS + 6 + bits + 1 + 3 + blocks // 2 + 12 + 2
    return pl.pallas_call(
        functools.partial(first_kernel, heads, token_total),
        out_shape=(
            shape((quarter, features), bf), shape((tokens, features), bf), shape((tokens, joined_width), bf),
            shape((tokens, heads * HEAD_DIM), bf), shape((heads, blocks, BLOCK), f32),
            shape((features, joined_width), bf), shape((8, features), f32), shape((8, 128), f32),
            shape((tokens, width), bf), shape((quarter, features), f32), shape((2 * quarter, head_rows), bf),
            shape((2 * quarter, head_rows), bf), shape((8, features), f32), shape((2, 1, hidden), f32),
        ) + (shape((features, hidden), bf),) * 4 + (shape((features, head_rows), bf),) * 2,
        in_specs=[pl.BlockSpec(memory_space=pltpu.SMEM), vmem, vmem] + [anyspace] * 6 + [vmem] * 3,
        out_specs=(vmem,) * 14 + (anyspace,) * 4 + (vmem,) * 2,
        scratch_shapes=[
            pltpu.VMEM((2 * quarter, 2 * head_rows), bf), pltpu.VMEM((quarter, features), bf), pltpu.VMEM((quarter, 128), bf),
            pltpu.VMEM((2, features, hidden), bf), pltpu.VMEM((2, hidden + head_rows, features), bf),
            pltpu.VMEM((2, 8, hidden), f32), pltpu.VMEM((2 * quarter, features), bf), pltpu.VMEM((2 * quarter, features), bf),
            pltpu.VMEM((2 * quarter, features), bf), pltpu.VMEM((quarter, features), bf), pltpu.VMEM((quarter, features), bf),
            pltpu.VMEM((quarter, features), f32), pltpu.VMEM((quarter, features), f32), pltpu.VMEM((quarter, features), bf),
            pltpu.VMEM((2, 256, hidden), bf), pltpu.VMEM((tokens, width), bf), pltpu.VMEM((2 * bits + 1, 8, 128), f32),
            pltpu.SemaphoreType.DMA((count,)), pltpu.SemaphoreType.DMA((count,)),
        ],
        compiler_params=pltpu.CompilerParams(vmem_limit_bytes=62 << 20, collective_id=1, has_side_effects=True),
        name="first_stage",
    )(slopes, bias_rows, vectors, joined, layer_in, up, down, out, up_bias, teacher, cot, valid)


class Untranspose:
    def __init__(self, place, src, dst, sems, first):
        self.place, self.src, self.dst, self.sems, self.first = place, src, dst, sems, first
        self.rows, self.width = src.shape[0], src.shape[1] // 4

    def out(self, other):
        p = self.place
        return pltpu.make_async_remote_copy(
            src_ref=self.src.at[:, pl.ds(other * self.width, self.width)],
            dst_ref=self.dst.at[hint(p.col, self.rows)],
            send_sem=self.sems[0].at[self.first + other], recv_sem=self.sems[1].at[self.first + p.col],
            device_id={"row": other, "col": p.source}, device_id_type=MESH,
        )

    def kept(self):
        p = self.place
        return pltpu.make_async_copy(
            self.src.at[:, hint(p.row, self.width)],
            self.dst.at[hint(p.col, self.rows)],
            self.sems[1].at[self.first + p.col],
        )

    def start(self):
        p = self.place
        for other in range(4):
            @pl.when(jnp.logical_not(jnp.logical_and(p.stays, p.row == other)))
            def _():
                self.out(other).start()

        @pl.when(p.stays)
        def _():
            self.kept().start()

    def wait_recv(self):
        p = self.place
        for other in range(4):
            mine = jnp.logical_and(p.stays, p.col == other)
            part = self.dst.at[pl.ds(other * self.rows, self.rows)]

            @pl.when(jnp.logical_not(mine))
            def _():
                pltpu.make_async_remote_copy(
                    src_ref=part, dst_ref=part, send_sem=self.sems[0].at[self.first + other],
                    recv_sem=self.sems[1].at[self.first + other],
                    device_id={"row": p.plane, "col": other}, device_id_type=MESH,
                ).wait_recv()

            @pl.when(mine)
            def _():
                self.kept().wait()

    def wait_send(self):
        p = self.place
        for other in range(4):
            @pl.when(jnp.logical_not(jnp.logical_and(p.stays, p.row == other)))
            def _():
                self.out(other).wait_send()


def add_into(total, pieces, rows=128):
    @pl.loop(0, total.shape[0] // rows)
    def _(n):
        part = hint(n, rows)
        value = total[part, :].astype(jnp.float32)
        for piece in pieces:
            value = value + piece[part, :].astype(jnp.float32)
        total[part, :] = value.astype(total.dtype)


class Share:
    def __init__(self, place, kind, own, far, result, buffers, sems, first):
        self.p, self.kind, self.own, self.far, self.result, self.sems, self.first = (
            place, kind, own, far, result, sems, first
        )
        self.width = own.shape[1]
        self.part = self.width // 2
        self.block = own.shape[0] // 4
        self.mine, self.theirs = hint(place.half, self.part), hint(1 - place.half, self.part)
        self.buffers = buffers

    def first_copies(self):
        p, b = self.p, self.buffers
        if self.kind == "xy":
            return [
                remote(src.at[:, self.theirs], b["came"].at[n], self.sems, self.first + n, {"dp": p.twin})
                for n, src in enumerate((self.own, self.far))
            ]
        if self.kind == "yx":
            return [remote(self.far, b["came"], self.sems, self.first, {"col": p.far})]
        return [remote(self.own.at[:, self.theirs], b["half"], self.sems, self.first, {"dp": p.twin})]

    def start(self):
        for copy in self.first_copies():
            copy.start()

    def add_own(self, totals, sources):
        load = self.buffers["load"]
        parts = [
            (total.at[pl.ds(n * self.block, self.block)], source.at[pl.ds(n * self.block, self.block)])
            for total, source in zip(totals, sources)
            for n in range(4)
        ]
        copies = [
            pltpu.make_async_copy(source, load.at[n % 2], self.sems[1].at[self.first + 8 + n % 2])
            for n, (_, source) in enumerate(parts)
        ]
        copies[0].start()
        for n, (total, _) in enumerate(parts):
            if n + 1 < len(parts):
                copies[n + 1].start()
            copies[n].wait()
            add_into(total, [load.at[n % 2]])

    def second_copy(self):
        p, b = self.p, self.buffers
        if self.kind == "xy":
            return remote(b["came"].at[1], b["other"], self.sems, self.first + 2, {"col": p.far})
        return remote(b["came"].at[:, self.theirs], b["half"], self.sems, self.first + 2, {"dp": p.twin})

    def first_sum(self):
        b = self.buffers
        for copy in self.first_copies():
            copy.wait()
        if self.kind == "xy":
            self.add_own(
                [b["came"].at[n] for n in (0, 1)], [src.at[:, self.mine] for src in (self.own, self.far)]
            )
        elif self.kind == "yx":
            self.add_own([b["came"]], [self.own])
        else:
            add_into(b["half"], [self.own.at[:, self.mine]])

    def total(self):
        return self.buffers["came"].at[0] if self.kind == "xy" else self.buffers["half"]

    def second_sum(self):
        b = self.buffers
        self.second_copy().wait()
        if self.kind == "xy":
            add_into(b["came"].at[0], [b["other"]])
        else:
            add_into(b["half"], [b["came"].at[:, self.mine]])

    def row_copy(self, step):
        p = self.p
        target = (p.row + step) % 4
        return remote(
            self.total().at[hint(target, self.block)], self.buffers["rows"].at[step - 1], self.sems,
            self.first + 2 + step, {"row": target},
        )

    def start_rows(self):
        for step in (1, 2, 3):
            self.row_copy(step).start()

    def last_copy(self):
        part = self.buffers["last"]
        return remote(part.at[self.p.half], part.at[self.p.half], self.sems, self.first + 6, {"dp": self.p.twin})

    def last_came(self):
        part = self.buffers["last"]
        return remote(part.at[1 - self.p.half], part.at[1 - self.p.half], self.sems, self.first + 6, {"dp": self.p.twin})

    def row_sum(self):
        for step in (1, 2, 3):
            self.row_copy(step).wait()
        b = self.buffers
        total, last = self.total(), b["last"]

        @pl.loop(0, self.block // 64)
        def _(n):
            part = hint(n, 64)
            rows = pl.ds(pl.multiple_of(self.p.row * self.block + n * 64, 64), 64)
            value = total[rows, :].astype(jnp.float32)
            for step in range(3):
                value = value + b["rows"][step, part, :].astype(jnp.float32)
            last[self.p.half, part, :] = value.astype(last.dtype)

        self.last_copy().start()

    def finish(self):
        self.last_copy().wait_send()
        self.last_came().wait_recv()
        for half in (0, 1):
            self.result[:, half * self.part : (half + 1) * self.part] = self.buffers["last"][half].astype(
                self.result.dtype
            )


SHARE_SEMS = 10


def share_scratch(kind, features, width):
    bf, part = jnp.bfloat16, width // 2
    if kind == "xy":
        own = dict(load=(2, features // 4, part), came=(2, features, part), other=(features, part))
    elif kind == "yx":
        own = dict(load=(2, features // 4, width), came=(features, width), half=(features, part))
    else:
        own = dict(half=(features, part))
    own["rows"] = (3, features // 4, part)
    own["last"] = (2, features // 4, part)
    return {name: pltpu.VMEM(shape, bf) for name, shape in own.items()}


def last_kernel(
    heads, kinds,
    slope_ref, mixed_ref, att_ref, lse_ref, nall_ref, jall_ref, xt_ref, middle_ref, gain_ref, early_ref,
    up_sums_ref, grads_own_ref, grads_far_ref,
    up_own, up_far, down_own, down_far, out_own, out_far,
    input_grad_ref, up_ref, down_ref, out_ref, joined_ref, vector_ref,
    dout, grad_mixed, qs, ks, km, vp, ds_, delta, bias, steep, dq, dk, dv,
    gn, near_in, far_in, jgrad, vectors, scratch, sends, recvs,
):
    sems = (sends, recvs)
    p = Place()
    f32, bf = jnp.float32, jnp.bfloat16
    quarter, features = xt_ref.shape
    tokens = mixed_ref.shape[0]
    greet(p, True, True)
    base = 0
    ingrad = gn.at[0]
    grad_back = Untranspose(p, ingrad, input_grad_ref, sems, base)
    base += 4

    def natural(chip, n):
        return 2 * chip + (p.core + n) % 2

    share_att = [
        remote(
            grads_far_ref.at[pl.ds(n * quarter, quarter)], dout.at[hint(natural(p.chip, n), quarter)], sems,
            base + n, {"col": p.far},
        )
        for n in (0, 1)
    ]
    for copy in share_att:
        copy.start()
    came_att = [
        remote(
            dout.at[hint(natural(1 - p.chip, n), quarter)], dout.at[hint(natural(1 - p.chip, n), quarter)], sems,
            base + n, {"col": p.far},
        )
        for n in (0, 1)
    ]
    base += 2
    up = Share(p, kinds[0], up_own, up_far, up_ref, scratch["up"], sems, base)
    down = Share(p, kinds[1], down_own, down_far, down_ref, scratch["down"], sems, base + SHARE_SEMS)
    out = Share(p, kinds[2], out_own, out_far, out_ref, scratch["out"], sems, base + 2 * SHARE_SEMS)
    joined = Share(p, "x", jgrad, None, joined_ref, scratch["joined"], sems, base + 3 * SHARE_SEMS)
    base += 4 * SHARE_SEMS
    up.start()
    out.start()
    down.start()
    for n in (0, 1):
        dout[hint(natural(p.chip, n), quarter), :] = grads_own_ref[n * quarter : (n + 1) * quarter, :]
    for copy in came_att:
        copy.wait_recv()
    for copy in share_att:
        copy.wait_send()

    attention_rows_backward(
        heads, slope_ref, mixed_ref, dout, att_ref, lse_ref, grad_mixed, qs, ks, km, vp, ds_, delta, bias, steep, dq, dk, dv
    )

    def product(index, slot):
        @pl.loop(0, quarter // 256)
        def _(n):
            rows = pl.ds(pl.multiple_of(index * quarter + n * 256, 256), 256)
            gn[slot, hint(n, 256), :] = nt(grad_mixed[rows, :], jall_ref[...]).astype(bf)

    corner = partner(p.far, 1)
    to_near = [
        remote(gn.at[n], near_in.at[n], sems, base + n, {"col": p.near}) for n in (0, 1)
    ]
    to_far = remote(gn.at[2], far_in, sems, base + 2, {"col": p.far})
    base += 3
    product(corner, 0)
    to_near[0].start()
    product(p.near, 1)
    to_near[1].start()
    product(p.far, 2)
    to_near[0].wait()
    add_into(gn.at[2], [near_in.at[0]])
    to_far.start()
    product(p.col, 3)
    up.first_sum()

    @pl.loop(0, features // 128)
    def _(f):
        cols = hint(f, 128)
        value = tn(nall_ref[:, cols], grad_mixed[...])
        jgrad[cols, :] = value.astype(bf)

    joined.start()
    sums = jnp.zeros((1, mixed_ref.shape[1]), f32)
    for n in range(tokens // 256):
        sums = sums + jnp.sum(grad_mixed[n * 256 : (n + 1) * 256, :].astype(f32), axis=0, keepdims=True)
    vectors[0, 0:2, :] = jnp.zeros((2, features), f32)
    vectors[0, 2:8, :] = early_ref[2:8, :]
    vectors[0, 8:16, :] = jnp.zeros((8, features), f32)
    vectors[0, pl.ds(8 + p.col, 1), :] = up_sums_ref[0]
    vectors[0, pl.ds(8 + p.far, 1), :] = up_sums_ref[1]
    vectors[0, pl.ds(12 + p.col, 1), 0 : sums.shape[1]] = sums

    to_near[1].wait()
    to_far.wait()

    @pl.loop(0, quarter // 64)
    def _(n):
        rows = hint(n, 64)
        grad = gn[3, rows, :].astype(f32) + near_in[1, rows, :].astype(f32) + far_in[rows, :].astype(f32)
        x = xt_ref[rows, :].astype(f32)
        center = jnp.mean(x, 1, keepdims=True)
        spread = jnp.mean(x * x, 1, keepdims=True) - center * center
        inverse = lax.rsqrt(spread + EPSILON)
        standard = (x - center) * inverse
        vectors[0, 0:1, :] += jnp.sum(grad * standard, axis=0, keepdims=True)
        vectors[0, 1:2, :] += jnp.sum(grad, axis=0, keepdims=True)
        scaled = grad * gain_ref[0:1, :]
        first = jnp.mean(scaled, 1, keepdims=True)
        second = jnp.mean(scaled * standard, 1, keepdims=True)
        ingrad[rows, :] = (middle_ref[rows, :] + inverse * (scaled - first - standard * second)).astype(bf)

    grad_back.start()
    up.second_copy().start()
    out.first_sum()
    out.second_copy().start()
    down.first_sum()
    down.second_copy().start()
    joined.first_sum()
    joined.start_rows()

    steps = [("row", 1), ("row", 2), ("col", 1), ("col", 2)]
    bit = 1
    while bit < p.dps:
        steps.append(("dp", bit))
        bit *= 2
    up.second_sum()
    up.start_rows()
    for n, (axis, bit) in enumerate(steps):
        other = partner({"row": p.row, "col": p.col, "dp": p.dp}[axis], bit)
        tally = remote(vectors.at[2 * n], vectors.at[2 * n + 1], sems, base + n, {axis: other})
        tally.start()
        tally.wait()
        vectors[2 * n + 2] = vectors[2 * n] + vectors[2 * n + 1]
    vector_ref[...] = vectors[2 * len(steps)]
    out.second_sum()
    out.start_rows()
    down.second_sum()
    down.start_rows()
    joined.row_sum()
    up.row_sum()
    out.row_sum()
    down.row_sum()
    for share in (joined, up, out, down):
        share.finish()
    grad_back.wait_recv()
    grad_back.wait_send()


def last_stage(slopes, mixed, att, lse, nall, jall, xt, middle, gain, early, up_sums, grads,
               up_pair, down_pair, out_pair):
    tokens, joined_width = mixed.shape
    quarter, features = xt.shape
    heads = joined_width // (3 * HEAD_DIM)
    pairs, blocks = heads // 2, tokens // BLOCK
    f32, bf = jnp.float32, jnp.bfloat16
    block = features // 4
    kinds = ("xy", "yx", "yx")
    vmem, anyspace = pl.BlockSpec(memory_space=pltpu.VMEM), pl.BlockSpec(memory_space=pl.ANY)
    shape = jax.ShapeDtypeStruct
    bits = 4
    while (1 << (bits - 4)) < lax.axis_size("dp"):
        bits += 1
    count = 4 + 2 + 4 * SHARE_SEMS + 3 + bits
    widths = (up_pair[0].shape[1], down_pair[0].shape[1], out_pair[0].shape[1])
    scratch = {
        name: share_scratch(kind, features, width)
        for name, kind, width in zip(("up", "down", "out", "joined"), kinds + ("x",), widths + (joined_width,))
    }
    return pl.pallas_call(
        functools.partial(last_kernel, heads, kinds),
        out_shape=(
            shape((tokens, block), bf), shape((block, widths[0]), bf),
            shape((block, widths[1]), bf), shape((block, widths[2]), bf), shape((block, joined_width), bf),
            shape((16, features), f32),
        ),
        in_specs=[pl.BlockSpec(memory_space=pltpu.SMEM)] + [vmem] * 11 + [anyspace] * 7,
        out_specs=(anyspace,) + (vmem,) * 5,
        scratch_shapes=[
            pltpu.VMEM((tokens, heads * HEAD_DIM), bf), pltpu.VMEM((tokens, joined_width), bf),
            pltpu.VMEM((pairs,blocks,2*BLOCK,PAIR),bf),pltpu.VMEM((pairs,blocks,BLOCK,PAIR),bf),
            pltpu.VMEM((pairs,blocks,2*BLOCK,PAIR),bf),pltpu.VMEM((pairs,blocks,BLOCK,PAIR),bf),
            pltpu.VMEM((pairs,blocks,2*BLOCK,PAIR),bf),pltpu.VMEM((heads,blocks,BLOCK),f32),
            pltpu.VMEM((heads,BLOCK,BLOCK),f32), pltpu.VMEM((heads,BLOCK,PAIR),f32),
            pltpu.VMEM((pairs,blocks,BLOCK,PAIR),f32), pltpu.VMEM((pairs,blocks,BLOCK,PAIR),f32), pltpu.VMEM((pairs,blocks,BLOCK,PAIR),f32),
            pltpu.VMEM((4, quarter, features), bf), pltpu.VMEM((2, quarter, features), bf), pltpu.VMEM((quarter, features), bf),
            pltpu.VMEM((features, joined_width), bf),
            pltpu.VMEM((2 * bits + 1, 16, features), f32), scratch,
            pltpu.SemaphoreType.DMA((count,)), pltpu.SemaphoreType.DMA((count,)),
        ],
        compiler_params=pltpu.CompilerParams(vmem_limit_bytes=62 << 20, collective_id=2, has_side_effects=True),
        name="last_stage",
    )(slopes, mixed, att, lse, nall, jall, xt, middle, gain, early, up_sums, grads[0], grads[1],
      *up_pair, *down_pair, *out_pair)


def swap_with(value, axis, bit):
    size = lax.axis_size(axis)
    return lax.ppermute(value, axis, [(i, i ^ bit) for i in range(size)])


def low(value):
    return value.astype(jnp.bfloat16)


def pick(stacked, index):
    return lax.dynamic_index_in_dim(stacked, index, 0, keepdims=False)


def sum_other_pairs(value):
    bit = 2
    while bit < lax.axis_size("dp"):
        value = value + swap_with(low(value), "dp", bit).astype(jnp.float32)
        bit *= 2
    return value


def on_device(
    layer_in,
    first_gain,
    first_shift,
    joined_weight,
    joined_bias,
    out_weight,
    out_bias,
    second_gain,
    second_shift,
    up_weight,
    up_bias,
    down_weight,
    down_bias,
    teacher,
    valid,
    cotangent,
):
    row_size, col_size = lax.axis_size("row"), lax.axis_size("col")
    row, col = lax.axis_index("row"), lax.axis_index("col")
    f32 = jnp.float32
    head_count = joined_bias.shape[0]
    quarter = layer_in.shape[0] // col_size
    head_index = col * head_count + jnp.arange(head_count, dtype=jnp.int32)
    slopes = jnp.exp2(-8.0 * (head_index.astype(f32) + 1.0) / HEADS) * LOG2E

    zero_rows = jnp.zeros_like(joined_bias[:, :HEAD_DIM])
    bias_rows = jnp.stack(
        [joined_bias[:, :HEAD_DIM], zero_rows, joined_bias[:, HEAD_DIM:]], axis=1
    ).reshape(1, -1).astype(f32)
    nothing = jnp.zeros_like(first_gain)
    vectors = jnp.stack(
        [first_gain, first_shift, out_bias, second_gain, second_shift, down_bias, nothing, nothing]
    ).astype(f32)
    token_total = layer_in.shape[0] * lax.axis_size("dp") * col_size
    (
        tokens, normed_one_all, mixed, attended, log_totals, joined_all, vectors, scale, layer_out, grad_middle,
        grads_own, grads_far, early, up_sums, up_own, up_far, down_own, down_far, out_own, out_far,
    ) = first_stage(
        slopes, bias_rows, vectors, joined_weight, layer_in, up_weight, down_weight, out_weight,
        jnp.broadcast_to(up_bias.astype(f32), (8, up_bias.shape[0])), teacher, cotangent,
        jnp.broadcast_to(low(valid)[:, None], (valid.shape[0], 128)), token_total,
    )
    input_grad, up_grad, down_grad, out_grad, joined_grad, sums = last_stage(
        slopes, mixed, attended, log_totals, normed_one_all, joined_all, tokens, grad_middle, vectors, early,
        up_sums, (grads_own, grads_far), (up_own, up_far), (down_own, down_far), (out_own, out_far),
    )
    up_grad, down_grad, out_grad, joined_grad = (
        sum_other_pairs(g.astype(f32)) for g in (up_grad, down_grad, out_grad, joined_grad)
    )
    mine = lax.dynamic_slice_in_dim(sums, row * (D // row_size), D // row_size, 1)
    loss = jnp.sum(sums[6, :128]) * scale[0, 0] / (D * token_total)
    up_bias_grad = pick(sums[8:12], col)
    column_sums = pick(sums[12:16], col)[: mixed.shape[1]].reshape(head_count, 3, HEAD_DIM)
    joined_bias_grad = jnp.concatenate([column_sums[:, 0], column_sums[:, 2]], axis=1)
    return (
        layer_out,
        loss,
        input_grad.astype(f32),
        mine[0],
        mine[1],
        joined_grad,
        joined_bias_grad,
        out_grad.T,
        mine[2],
        mine[3],
        mine[4],
        up_grad,
        up_bias_grad,
        down_grad.T,
        mine[5],
    )


def solution(mesh):
    return jax.shard_map(
        on_device,
        mesh=mesh,
        in_specs=(
            P(("dp", "col"), "row"),
            P("row"),
            P("row"),
            P("row", "col"),
            P("col", None),
            P("col", "row"),
            P("row"),
            P("row"),
            P("row"),
            P("row", "col"),
            P("col"),
            P("col", "row"),
            P("row"),
            P(("dp", "col"), "row"),
            P(("dp", "col")),
            P(("dp", "col"), "row"),
        ),
        out_specs=(
            P(("dp", "col"), "row"),
            P(),
            P(("dp", "col"), "row"),
            P("row"),
            P("row"),
            P("row", "col"),
            P("col", None),
            P("col", "row"),
            P("row"),
            P("row"),
            P("row"),
            P("row", "col"),
            P("col"),
            P("col", "row"),
            P("row"),
        ),
        check_vma=False,
    )
```

```python
import functools
import math

import jax
import jax.numpy as jnp
from jax import lax
from jax.experimental import pallas as pl
from jax.experimental.pallas import tpu as pltpu
from jax.sharding import PartitionSpec as P

D = 1024
HEADS = 16
SEQ = 2048
EPSILON = 1e-05
LOG2E = 1.4426950408889634
HEAD_DIM=64
BLOCK=256
HALF=64
PAIR=128
SCALE2 = LOG2E/8.0

def nt(a,b):
    return lax.dot_general(a,b,(((1,),(1,)),((),())),preferred_element_type=jnp.float32)
def nn(a,b):
    return jnp.dot(a,b,preferred_element_type=jnp.float32)
def tn(a,b):
    return lax.dot_general(a,b,(((0,),(0,)),((),())),preferred_element_type=jnp.float32)

def low_lanes(rows):
    return lax.broadcasted_iota(jnp.int32,(rows,PAIR),1) < HALF

def swap(a):
    return jnp.concatenate([a[:,HALF:],a[:,:HALF]],axis=1)

def attention_rows(heads, order, after, slope_ref, mixed_ref, out_ref, lse_ref, qs, ks, vs, bias, sc, mx, ls, acc):
    pairs=heads//2
    blocks=mixed_ref.shape[0]//BLOCK
    lo=low_lanes(BLOCK)
    @pl.loop(0,blocks)
    def _(b):
        rows=pl.ds(pl.multiple_of(b*BLOCK,BLOCK),BLOCK)
        for p in range(pairs):
            t0,t1,t2=(mixed_ref[rows,(3*p+n)*PAIR:(3*p+n+1)*PAIR] for n in range(3))
            zero=jnp.zeros_like(t0)
            qs[2*p,b]=jnp.where(lo,t0,zero)
            qs[2*p+1,b]=jnp.where(lo,zero,t1)
            ks[p,b]=jnp.where(lo,swap(t0),swap(t2))
            vs[p,b,:BLOCK]=jnp.where(lo,t1,zero)
            vs[p,b,BLOCK:]=jnp.where(lo,zero,t2)
    il=lax.broadcasted_iota(jnp.int32,(BLOCK,BLOCK),0)
    jl=lax.broadcasted_iota(jnp.int32,(BLOCK,BLOCK),1)
    tent=jnp.minimum(jl,2*il-jl).astype(jnp.float32)
    for h in range(heads):
        bias[h]=tent*slope_ref[h]
    jrow=lax.broadcasted_iota(jnp.int32,(1,BLOCK),1)
    @pl.loop(0,blocks)
    def _(it):
        i=order(it)
        for h in range(heads):
            t=nt(qs[h,i],ks[h//2,i])*SCALE2+bias[h]
            sc[h,i]=t
            mx[h]=jnp.maximum(t[:,:PAIR],t[:,PAIR:])
        @pl.loop(0,i)
        def _(j):
            place=(jrow+(j-i)*BLOCK).astype(jnp.float32)
            for h in range(heads):
                t=nt(qs[h,i],ks[h//2,j])*SCALE2+place*slope_ref[h]
                sc[h,j]=t
                mx[h]=jnp.maximum(mx[h],jnp.maximum(t[:,:PAIR],t[:,PAIR:]))
        for h in range(heads):
            mx[h]=jnp.broadcast_to(jnp.max(mx[h],1,keepdims=True),(BLOCK,PAIR))
            ls[h]=jnp.zeros((BLOCK,PAIR),jnp.float32)
        for p in range(pairs):
            acc[p]=jnp.zeros((BLOCK,PAIR),jnp.float32)
        @pl.loop(0,i+1)
        def _(j):
            for p in range(pairs):
                both=[]
                for h in (2*p,2*p+1):
                    m=mx[h]
                    ea=jnp.exp2(sc[h,j,:,:PAIR]-m)
                    eb=jnp.exp2(sc[h,j,:,PAIR:]-m)
                    ls[h]+=ea+eb
                    both+=[ea.astype(jnp.bfloat16),eb.astype(jnp.bfloat16)]
                acc[p]+=nn(jnp.concatenate(both,1),vs[p,j])
        rows=pl.ds(pl.multiple_of(i*BLOCK,BLOCK),BLOCK)
        for p in range(pairs):
            tot=[jnp.broadcast_to(jnp.sum(ls[h],1,keepdims=True),(BLOCK,PAIR)) for h in (2*p,2*p+1)]
            out_ref[rows,p*PAIR:(p+1)*PAIR]=(acc[p]/jnp.where(lo,tot[0],tot[1])).astype(out_ref.dtype)
            for n,h in enumerate((2*p,2*p+1)):
                lse=mx[h]+jnp.log2(tot[n])
                lse_ref[h,pl.ds(i,1),:]=lse.T[:1]
        after(it,i)

def attention_rows_backward(heads, after, slope_ref, mixed_ref, dout_ref, out_ref, lse_ref, grad_ref, qs, ks, km, vp, ds_, delta, bias, steep, dq, dk, dv):
    pairs=heads//2
    blocks=mixed_ref.shape[0]//BLOCK
    lo=low_lanes(BLOCK)
    @pl.loop(0,blocks)
    def _(b):
        rows=pl.ds(pl.multiple_of(b*BLOCK,BLOCK),BLOCK)
        for p in range(pairs):
            t0,t1,t2=(mixed_ref[rows,(3*p+n)*PAIR:(3*p+n+1)*PAIR] for n in range(3))
            zero=jnp.zeros_like(t0)
            qs[p,b,:BLOCK]=jnp.where(lo,t0,zero)
            qs[p,b,BLOCK:]=jnp.where(lo,zero,t1)
            k=jnp.where(lo,swap(t0),swap(t2))
            ks[p,b]=k
            km[p,b,:BLOCK]=jnp.where(lo,k,zero)
            km[p,b,BLOCK:]=jnp.where(lo,zero,k)
            vp[p,b]=jnp.where(lo,t1,t2)
            d=dout_ref[rows,p*PAIR:(p+1)*PAIR]
            ds_[p,b,:BLOCK]=jnp.where(lo,d,zero)
            ds_[p,b,BLOCK:]=jnp.where(lo,zero,d)
            prod=(d.astype(jnp.float32)*out_ref[rows,p*PAIR:(p+1)*PAIR].astype(jnp.float32)).T
            delta[2*p,pl.ds(b,1),:]=jnp.sum(prod[:HALF],0,keepdims=True)
            delta[2*p+1,pl.ds(b,1),:]=jnp.sum(prod[HALF:],0,keepdims=True)
    kl=lax.broadcasted_iota(jnp.int32,(BLOCK,BLOCK),0)
    ql=lax.broadcasted_iota(jnp.int32,(BLOCK,BLOCK),1)
    tent=jnp.minimum(kl,2*ql-kl).astype(jnp.float32)
    ramp=kl.astype(jnp.float32)
    for h in range(heads):
        bias[h]=tent*slope_ref[h]
        steep[h]=ramp[:,:PAIR]*slope_ref[h]
    def block(i,j,first):
        for p in range(pairs):
            ps=[];gs=[]
            for n,h in enumerate((2*p,2*p+1)):
                q=qs[p,i,n*BLOCK:(n+1)*BLOCK]
                d=ds_[p,i,n*BLOCK:(n+1)*BLOCK]
                row=slope_ref[h]*((j-i)*BLOCK).astype(jnp.float32)-lse_ref[h,pl.ds(i,1),:]
                t=nt(ks[p,j],q)*SCALE2+row+(bias[h] if first else jnp.concatenate([steep[h],steep[h]],1))
                e=jnp.exp2(t)
                g=e*(nt(vp[p,j],d)-delta[h,pl.ds(i,1),:])
                ps.append(e.astype(jnp.bfloat16)); gs.append(g.astype(jnp.bfloat16))
            gv=nn(jnp.concatenate(ps,1),ds_[p,i])
            gk=nn(jnp.concatenate(gs,1),qs[p,i])
            gq=tn(jnp.concatenate(gs,0),km[p,j])
            if first:
                dv[p,j]=gv; dk[p,j]=gk; dq[p,i]=gq
            else:
                dv[p,j]+=gv; dk[p,j]+=gk; dq[p,i]+=gq
    @pl.loop(0,blocks)
    def _(i):
        block(i,i,True)
        @pl.loop(0,i)
        def _(j):
            block(i,j,False)
        after(i)
    @pl.loop(0,blocks)
    def _(b):
        rows=pl.ds(pl.multiple_of(b*BLOCK,BLOCK),BLOCK)
        for p in range(pairs):
            a=dq[p,b]*0.125; k=swap(dk[p,b]*0.125); v=dv[p,b]
            for n,t in enumerate((jnp.where(lo,a,k),jnp.where(lo,v,a),jnp.where(lo,k,v))):
                grad_ref[rows,(3*p+n)*PAIR:(3*p+n+1)*PAIR]=t.astype(grad_ref.dtype)


MESH = pl.DeviceIdType.MESH


def hint(index, size):
    return pl.ds(pl.multiple_of(index * size, size), size)


def remote(src, dst, sems, number, target):
    send, recv = sems
    return pltpu.make_async_remote_copy(
        src_ref=src, dst_ref=dst, send_sem=send.at[number], recv_sem=recv.at[number],
        device_id=target, device_id_type=MESH,
    )


def partner(index, bit):
    return index + bit - 2 * bit * ((index // bit) % 2)


class Place:
    def __init__(self):
        self.dp, self.row, self.col = (lax.axis_index(a) for a in ("dp", "row", "col"))
        self.dps = lax.axis_size("dp")
        self.core, self.chip = self.col % 2, self.col // 2
        self.near, self.far = partner(self.col, 1), partner(self.col, 2)
        self.twin = partner(self.dp, 1)
        self.half = self.dp % 2
        self.plane = 3 * self.core + self.chip - 2 * self.core * self.chip
        self.source = 2 * (((self.row + 1) // 2) % 2) + self.row // 2
        self.corner = partner(self.far, 1)
        self.stays = self.plane == self.row
        self.far_plane = 3 * self.core + (1 - self.chip) - 2 * self.core * (1 - self.chip)
        self.sender = 2 * self.chip + self.source % 2
        self.home = jnp.logical_or(self.stays, self.far_plane == self.row)


def greet(place):
    barrier = pltpu.get_barrier_semaphore()

    def signal(target):
        pl.semaphore_signal(barrier, inc=1, device_id=target, device_id_type=MESH)

    for step in (1, 2, 3):
        signal({"row": (place.row + step) % 4})
    for col in (place.near, place.far, place.corner):
        signal({"col": col})
    amount = 6
    bit = 1
    while bit < place.dps:
        signal({"dp": partner(place.dp, bit)})
        amount += 1
        bit *= 2

    for plane, stays in ((place.plane, place.stays), (place.far_plane, place.far_plane == place.row)):
        signal({"row": plane, "col": place.near})

        @pl.when(jnp.logical_not(stays))
        def _():
            signal({"row": plane, "col": place.col})

    for other in range(4):
        @pl.when(jnp.logical_not(jnp.logical_and(place.home, place.row == other)))
        def _():
            signal({"row": other, "col": place.sender})

        @pl.when(jnp.logical_not(jnp.logical_and(place.stays, place.col == other)))
        def _():
            signal({"row": place.plane, "col": other})

        @pl.when(jnp.logical_not(jnp.logical_and(place.stays, place.row == other)))
        def _():
            signal({"row": other, "col": place.source})

    amount = amount + 16 - 2 * place.home.astype(jnp.int32) - 2 * place.stays.astype(jnp.int32)
    pl.semaphore_wait(barrier, amount)


class Transpose:
    def __init__(self, place, src, dst, relay, sems, first):
        self.p, self.src, self.dst, self.relay, self.sems, self.first = place, src, dst, relay, sems, first
        self.rows, self.width = src.shape[0] // 4, src.shape[1]

    def part(self):
        return self.dst.at[:, hint(self.p.row, self.width)]

    def cross(self, n):
        src = self.src.at[hint(2 * (1 - self.p.chip) + n, self.rows)]
        return remote(src, self.relay.at[n], self.sems, self.first + 4 + n, {"col": self.p.far})

    def out(self, relayed, n):
        p = self.p
        col = p.col if n == 0 else p.near
        src = self.relay.at[col % 2] if relayed else self.src.at[hint(col, self.rows)]
        return pltpu.make_async_remote_copy(
            src_ref=src, dst_ref=self.part(),
            send_sem=self.sems[0].at[self.first + 2 * relayed + n], recv_sem=self.sems[1].at[self.first + p.row],
            device_id={"row": p.far_plane if relayed else p.plane, "col": col}, device_id_type=MESH,
        )

    def kept(self, relayed):
        p = self.p
        src = self.relay.at[p.core] if relayed else self.src.at[hint(p.col, self.rows)]
        return pltpu.make_async_copy(src, self.part(), self.sems[1].at[self.first + p.row])

    def leaves(self, relayed):
        return (self.p.far_plane if relayed else self.p.plane) != self.p.row

    def send(self, relayed):
        self.out(relayed, 1).start()

        @pl.when(self.leaves(relayed))
        def _():
            self.out(relayed, 0).start()

        @pl.when(jnp.logical_not(self.leaves(relayed)))
        def _():
            self.kept(relayed).start()

    def start_cross(self):
        for n in (0, 1):
            self.cross(n).start()

    def forward(self):
        for n in (0, 1):
            self.cross(n).wait_recv()
        self.send(1)

    def wait_recv(self):
        p = self.p
        for other in range(4):
            mine = jnp.logical_and(p.home, p.row == other)
            part = self.dst.at[:, pl.ds(other * self.width, self.width)]

            @pl.when(jnp.logical_not(mine))
            def _():
                pltpu.make_async_remote_copy(
                    src_ref=part, dst_ref=part, send_sem=self.sems[0].at[self.first + other],
                    recv_sem=self.sems[1].at[self.first + other],
                    device_id={"row": other, "col": p.sender}, device_id_type=MESH,
                ).wait_recv()

            @pl.when(mine)
            def _():
                self.kept(0).wait()

    def wait_send(self):
        for n in (0, 1):
            self.cross(n).wait_send()
        for relayed in (0, 1):
            self.out(relayed, 1).wait_send()

            @pl.when(self.leaves(relayed))
            def _():
                self.out(relayed, 0).wait_send()


TRANSPOSE_SEMS = 6


class Weight:
    def __init__(self, place, src, dst, offset, by_rows, last, sems, first):
        self.p, self.src, self.dst, self.offset, self.by_rows, self.last = place, src, dst, offset, by_rows, last
        self.sems, self.first = sems, first
        self.rows, self.width = src.shape
        self.part = self.rows // 2

    def whole(self, side, row):
        if self.by_rows:
            return self.dst.at[side, hint(row, self.rows)]
        return self.dst.at[side, pl.ds(self.offset, self.rows), hint(row, self.width)]

    def piece(self, side, row, half):
        if self.by_rows:
            return self.dst.at[side, hint(row * 2 + half, self.part)]
        start = pl.multiple_of(self.offset + half * self.part, self.part)
        return self.dst.at[side, pl.ds(start, self.part), hint(row, self.width)]

    def other(self, step):
        return (self.p.row + 4 - step) % 4

    def move(self, src, dst, number, target):
        return remote(src, dst, self.sems, self.first + number, target)

    def pass_on(self, side, step, half, number, target):
        src = self.piece(side, self.other(step), half)
        dst = self.piece(1 if "col" in target else side, self.other(step), half)
        return self.move(src, dst, number + step - 1, target)

    def own(self):
        return pltpu.make_async_copy(self.src, self.whole(0, self.p.row), self.sems[1].at[self.first])

    def across(self):
        return self.move(self.src, self.whole(1, self.p.row), 1, {"col": self.p.far})

    def along(self, step):
        p = self.p
        return self.move(
            self.src.at[hint(p.half, self.part)], self.piece(0, p.row, p.half), 1 + step, {"row": (p.row + step) % 4}
        )

    def to_twin(self, step):
        return self.pass_on(0, step, self.p.half, 5, {"dp": self.p.twin})

    def to_far(self, step):
        return self.pass_on(0, step, self.p.half, 8, {"col": self.p.far})

    def onward(self, step):
        if self.last == "y":
            return self.pass_on(0, step, 1 - self.p.half, 11, {"col": self.p.far})
        return self.pass_on(1, step, self.p.half, 11, {"dp": self.p.twin})

    def arrival(self, side, step, half, number):
        part = self.piece(side, self.other(step), half)
        return self.move(part, part, number + step - 1, {"dp": self.p.twin})

    def start_along(self):
        for step in (1, 2, 3):
            self.along(step).start()

    def spread(self, steps=(1, 2, 3)):
        for step in steps:
            self.arrival(0, step, self.p.half, 2).wait_recv()
            self.to_twin(step).start()
            self.to_far(step).start()

    def spread_last(self, steps=(1, 2, 3)):
        p = self.p
        for step in steps:
            if self.last == "y":
                self.arrival(0, step, 1 - p.half, 5).wait_recv()
            else:
                self.arrival(1, step, p.half, 8).wait_recv()
            self.onward(step).start()

    def ready(self, side):
        p = self.p
        if side == 0:
            self.own().wait()
        else:
            self.across().wait_recv()
        for step in (1, 2, 3):
            if side == 0 and self.last == "x":
                self.arrival(0, step, 1 - p.half, 5).wait_recv()
            if side == 1 and self.last == "y":
                self.arrival(1, step, p.half, 8).wait_recv()
            if side == 1:
                self.arrival(1, step, 1 - p.half, 11).wait_recv()

    def sent(self):
        self.across().wait_send()
        for step in (1, 2, 3):
            for copy in (self.along(step), self.to_twin(step), self.to_far(step), self.onward(step)):
                copy.wait_send()


WEIGHT_SEMS = 14


class Halves:
    def __init__(self, place, src, dst, sems, first):
        self.p, self.src, self.dst, self.sems, self.first = place, src, dst, sems, first
        self.rows = src.shape[0]
        self.part = self.rows // 2

    def own(self):
        return pltpu.make_async_copy(self.src, self.dst.at[hint(self.p.row, self.rows)], self.sems[1].at[self.first])

    def along(self, step):
        p = self.p
        return remote(
            self.src.at[hint(p.half, self.part)], self.dst.at[hint(2 * p.row + p.half, self.part)], self.sems,
            self.first + step, {"row": (p.row + step) % 4},
        )

    def part_of(self, step, half):
        return self.dst.at[hint(2 * ((self.p.row + 4 - step) % 4) + half, self.part)]

    def to_twin(self, step, half):
        part = self.part_of(step, half)
        return remote(part, part, self.sems, self.first + 3 + step, {"dp": self.p.twin})

    def start(self):
        self.own().start()
        for step in (1, 2, 3):
            self.along(step).start()

    def spread(self):
        p = self.p
        for step in (1, 2, 3):
            part = self.part_of(step, p.half)
            remote(part, part, self.sems, self.first + step, {"dp": p.twin}).wait_recv()
            self.to_twin(step, p.half).start()

    def ready(self):
        p = self.p
        for step in (1, 2, 3):
            self.to_twin(step, 1 - p.half).wait_recv()
        self.own().wait()

    def sent(self):
        for step in (1, 2, 3):
            self.along(step).wait_send()
            self.to_twin(step, self.p.half).wait_send()


HALVES_SEMS = 7


GELU_ROOT = math.sqrt(2.0 / math.pi)
GELU_CUBE = 0.044715


def gelu_pair(x):
    square = x * x
    t = jnp.tanh(GELU_ROOT * x * (1.0 + GELU_CUBE * square))
    half = 0.5 * (1.0 + t)
    slope = half + 0.5 * x * (1.0 - t * t) * (GELU_ROOT * (1.0 + 3.0 * GELU_CUBE * square))
    return x * half, slope


def moments(x):
    center = jnp.mean(x, 1, keepdims=True)
    spread = jnp.mean(x * x, 1, keepdims=True) - center * center
    inverse = lax.rsqrt(spread + EPSILON)
    return (x - center) * inverse, inverse


class Chip:
    def __init__(self, place, sems, first):
        self.p, self.sems, self.first = place, sems, first

    def copy(self, number, src, dst):
        return remote(src, dst, self.sems, self.first + number, {"col": self.p.near})


class Untranspose:
    def __init__(self, place, src, dst, sems, first):
        self.place, self.src, self.dst, self.sems, self.first = place, src, dst, sems, first
        self.rows, self.width = src.shape[0], src.shape[1] // 4

    def out(self, other):
        p = self.place
        return pltpu.make_async_remote_copy(
            src_ref=self.src.at[:, pl.ds(other * self.width, self.width)],
            dst_ref=self.dst.at[hint(p.col, self.rows)],
            send_sem=self.sems[0].at[self.first + other], recv_sem=self.sems[1].at[self.first + p.col],
            device_id={"row": other, "col": p.source}, device_id_type=MESH,
        )

    def kept(self):
        p = self.place
        return pltpu.make_async_copy(
            self.src.at[:, hint(p.row, self.width)],
            self.dst.at[hint(p.col, self.rows)],
            self.sems[1].at[self.first + p.col],
        )

    def start(self):
        p = self.place
        for other in range(4):
            @pl.when(jnp.logical_not(jnp.logical_and(p.stays, p.row == other)))
            def _():
                self.out(other).start()

        @pl.when(p.stays)
        def _():
            self.kept().start()

    def wait_recv(self):
        p = self.place
        for other in range(4):
            mine = jnp.logical_and(p.stays, p.col == other)
            part = self.dst.at[pl.ds(other * self.rows, self.rows)]

            @pl.when(jnp.logical_not(mine))
            def _():
                pltpu.make_async_remote_copy(
                    src_ref=part, dst_ref=part, send_sem=self.sems[0].at[self.first + other],
                    recv_sem=self.sems[1].at[self.first + other],
                    device_id={"row": p.plane, "col": other}, device_id_type=MESH,
                ).wait_recv()

            @pl.when(mine)
            def _():
                self.kept().wait()

    def wait_send(self):
        p = self.place
        for other in range(4):
            @pl.when(jnp.logical_not(jnp.logical_and(p.stays, p.row == other)))
            def _():
                self.out(other).wait_send()


def add_rows(total, pieces, rows=64):
    @pl.loop(0, total.shape[0] // rows)
    def _(n):
        part = hint(n, rows)
        value = pieces[0][part, :].astype(jnp.float32)
        for piece in pieces[1:]:
            value = value + piece[part, :].astype(jnp.float32)
        total[part, :] = value.astype(total.dtype)


class Share:
    def __init__(self, place, kind, own, far, result, came, other, rows, totals, slots, sems, first):
        self.p, self.kind, self.own, self.far, self.result = place, kind, own, far, result
        self.came, self.other_ref, self.rows, self.totals, self.slots = came, other, rows, totals, slots
        self.sems, self.first = sems, first
        self.width = own.shape[1]
        self.part = self.width // 2
        self.block = own.shape[0] // 4
        self.mine, self.theirs = hint(place.half, self.part), hint(1 - place.half, self.part)

    def first_copies(self):
        p = self.p
        if self.kind == "xy":
            return [
                remote(src.at[:, self.theirs], self.came.at[n], self.sems, self.first + n, {"dp": p.twin})
                for n, src in enumerate((self.own, self.far))
            ]
        if self.kind == "yx":
            return [remote(self.far, self.came, self.sems, self.first, {"col": p.far})]
        return [remote(self.own.at[:, self.theirs], self.came, self.sems, self.first, {"dp": p.twin})]

    def start(self):
        for copy in self.first_copies():
            copy.start()

    def gather_sum(self, jobs):
        blocks = []
        for total, sources in jobs:
            for n in range(4):
                part = pl.ds(n * self.block, self.block)
                blocks.append((total.at[part], [src.at[part] for src in sources]))
        copies = []
        for n, (_, sources) in enumerate(blocks):
            copies.append([
                pltpu.make_async_copy(
                    src, self.slots[2 * (n % 2) + m].at[:, : src.shape[1]],
                    self.sems[1].at[self.first + 8 + 2 * (n % 2) + m],
                )
                for m, src in enumerate(sources)
            ])
        for copy in copies[0]:
            copy.start()
        for n, (total, sources) in enumerate(blocks):
            if n + 1 < len(blocks):
                for copy in copies[n + 1]:
                    copy.start()
            for copy in copies[n]:
                copy.wait()
            add_rows(total, [self.slots[2 * (n % 2) + m].at[:, : total.shape[1]] for m in range(len(sources))])

    def second_copy(self):
        p = self.p
        if self.kind == "xy":
            return remote(self.totals[1], self.other_ref, self.sems, self.first + 2, {"col": p.far})
        return remote(self.totals[0].at[:, self.theirs], self.other_ref, self.sems, self.first + 2, {"dp": p.twin})

    def first_sum(self):
        for copy in self.first_copies():
            copy.wait()
        if self.kind == "xy":
            self.gather_sum([
                (self.totals[1], [self.came.at[1], self.far.at[:, self.mine]]),
                (self.totals[0], [self.came.at[0], self.own.at[:, self.mine]]),
            ])
        elif self.kind == "yx":
            self.gather_sum([(self.totals[0], [self.came, self.own])])
        else:
            self.gather_sum([(self.totals[0], [self.came, self.own.at[:, self.mine]])])

    def total(self):
        return self.totals[1] if self.kind == "yx" else self.totals[0]

    def second_sum(self):
        self.second_copy().wait()
        if self.kind == "xy":
            self.gather_sum([(self.totals[0], [self.other_ref, self.totals[0]])])
        else:
            self.gather_sum([(self.totals[1], [self.other_ref, self.totals[0].at[:, self.mine]])])

    def row_copy(self, step):
        row = self.p.row
        target = partner(row, 1) if step < 2 else partner(row, 2)
        block = partner(target, 2) if step == 1 else target
        return remote(
            self.total().at[hint(block, self.block)], self.rows.at[step], self.sems, self.first + 3 + step, {"row": target}
        )

    def start_rows(self):
        for step in (1, 0):
            self.row_copy(step).start()

    def row_add(self, block, step, target):
        load = pltpu.make_async_copy(
            self.rows.at[step], self.slots[step].at[:, : self.part], self.sems[1].at[self.first + 8 + step]
        )
        load.start()
        load.wait()
        add_rows(target, [self.total().at[hint(block, self.block)], self.slots[step].at[:, : self.part]])

    def row_half(self):
        other = partner(self.p.row, 2)
        self.row_copy(1).wait()
        self.row_add(other, 1, self.total().at[hint(other, self.block)])
        self.row_copy(2).start()
        self.row_copy(0).wait()
        self.row_add(self.p.row, 0, self.total().at[hint(self.p.row, self.block)])

    def last_copy(self, half):
        part = self.result.at[:, hint(half, self.part)]
        return remote(part, part, self.sems, self.first + 6, {"dp": self.p.twin})

    def row_sum(self):
        self.row_copy(2).wait()
        self.row_add(self.p.row, 2, self.result.at[:, self.mine])
        self.last_copy(self.p.half).start()

    def finish(self):
        self.last_copy(self.p.half).wait_send()
        self.last_copy(1 - self.p.half).wait_recv()


SHARE_SEMS = 12


class Tally:
    def __init__(self, place, slots, axes, sems, first):
        self.slots = slots
        p = place
        peers = dict(
            row=[{"row": (p.row + step) % 4} for step in (1, 2, 3)],
            col=[{"col": p.near}, {"col": p.far}, {"col": p.corner}],
        )
        bit = 1
        while bit < p.dps:
            peers["dp%d" % bit] = [{"dp": partner(p.dp, bit)}]
            bit *= 2
        names = []
        for axis in axes:
            names += [name for name in peers if name.startswith(axis)]
        self.stages, at = [], 0
        for name in names:
            copies = [
                remote(slots.at[at], slots.at[at + 1 + n], sems, first + n, target)
                for n, target in enumerate(peers[name])
            ]
            self.stages.append((at, copies))
            at += len(copies) + 1
            first += len(copies)
        self.names, self.last, self.next_sem = names, at, first

    def send(self, n):
        for copy in self.stages[n][1]:
            copy.start()

    def add(self, n):
        at, copies = self.stages[n]
        value = self.slots[at]
        for m, copy in enumerate(copies):
            copy.wait()
            value = value + self.slots[at + 1 + m]
        self.slots[at + len(copies) + 1] = value

    def after(self, n):
        at, copies = self.stages[n]
        return at + len(copies) + 1


def tally_slots(bits, axes):
    return sum({"row": 4, "col": 4, "dp": 2 * bits}[axis] for axis in axes) + 1


def layer_kernel(
    heads, token_total,
    slope_ref, bias_ref, vector_ref, joined_ref, layer_ref, up_ref, down_ref, out_ref, up_bias_ref,
    teacher_ref, cot_ref, valid_ref,
    layer_out_ref, input_grad_ref, upg_ref, dng_ref, outg_ref, joinedg_ref, vector_sum_ref, scale_ref,
    upg_own, upg_far, dng_own, dng_far, came_up, came_down, came_out, came_joined, other_up, other_down, other_out,
    rows_up, rows_down, rows_out, rows_joined,
    xt_ref, nall_ref, mixed_ref, att_ref, lse_ref, jall_ref, vall_ref, early_ref, up_sums_ref,
    chip_ref, gt_ref, vt_ref, up2_ref, dn2_ref, ub2_ref, normed, gchip, bchip, give, take, middle, gres, low_ref, stage,
    grad, gfar, dout, relay, vectors, late, count, sends, recvs,
):
    sems = (sends, recvs)
    f32, bf = jnp.float32, jnp.bfloat16
    p = Place()
    quarter, features = xt_ref.shape
    hidden = down_ref.shape[0]
    moved = Transpose(p, layer_ref, xt_ref, relay.at[0], sems, 0)
    target = Transpose(p, grad, gt_ref, relay.at[1], sems, TRANSPOSE_SEMS)
    base = 2 * TRANSPOSE_SEMS
    back = Untranspose(p, low_ref, layer_out_ref, sems, base)
    base += 4
    w_out = Weight(p, out_ref, dn2_ref, hidden, False, "y", sems, base)
    w_up = Weight(p, up_ref, up2_ref, 0, True, "y", sems, base + WEIGHT_SEMS)
    w_downs = [
        Weight(
            p, down_ref.at[pl.ds(n * (hidden // 2), hidden // 2)], dn2_ref, n * (hidden // 2), False, "x", sems,
            base + (2 + n) * WEIGHT_SEMS,
        )
        for n in (0, 1)
    ]
    weights = [w_out, w_up] + w_downs
    base += 4 * WEIGHT_SEMS
    w_joined = Halves(p, joined_ref, jall_ref, sems, base)
    base += HALVES_SEMS
    small_base, bias_base = base, base + 4
    base += 6

    def small(step):
        return remote(
            vector_ref, vall_ref.at[:, hint(p.row, 256)], sems, small_base + step, {"row": (p.row + step) % 4}
        )

    def small_came(step):
        part = vall_ref.at[:, hint((p.row + 4 - step) % 4, 256)]
        return remote(part, part, sems, small_base + step, {"row": (p.row + step) % 4})

    small_own = pltpu.make_async_copy(vector_ref, vall_ref.at[:, hint(p.row, 256)], recvs.at[small_base])
    bias_own = pltpu.make_async_copy(up_bias_ref, ub2_ref.at[0], recvs.at[bias_base])
    bias_far = remote(up_bias_ref, ub2_ref.at[1], sems, bias_base + 1, {"col": p.far})
    counted = Tally(p, count, ("col", "dp"), sems, base)
    base = counted.next_sem
    tokens = valid_ref.shape[0]
    number = jnp.zeros((8, 128), f32)
    for n in range(tokens // 256):
        number = number + jnp.sum(valid_ref[n * 256 : (n + 1) * 256, :].astype(f32), axis=0, keepdims=True)
    count[0] = number
    greet(p)
    counted.send(0)
    for step in (1, 2, 3):
        small(step).start()
    moved.start_cross()
    moved.send(0)
    bias_far.start()
    w_out.across().start()
    w_up.across().start()
    small_own.start()
    bias_own.start()
    for w in weights:
        w.own().start()
    for n in range(len(counted.stages)):
        counted.add(n)
        if n + 1 < len(counted.stages):
            counted.send(n + 1)
    moved.forward()

    scale_ref[...] = token_total / count[counted.last]
    scale = scale_ref[:1, :1]

    @pl.loop(0, 32)
    def _(n):
        rows = hint(n, grad.shape[0] // 32)
        factor = valid_ref[rows, :].astype(f32) * scale
        for f in range(grad.shape[1] // 128):
            cols = slice(f * 128, (f + 1) * 128)
            grad[rows, cols] = (
                cot_ref[rows, cols].astype(f32) - factor * teacher_ref[rows, cols].astype(f32)
            ).astype(bf)

    valid_base = base
    base += 1

    def valid_out():
        return pltpu.make_async_remote_copy(
            src_ref=valid_ref.at[hint(p.row, quarter)], dst_ref=vt_ref,
            send_sem=sends.at[valid_base], recv_sem=recvs.at[valid_base],
            device_id={"row": p.plane, "col": p.row}, device_id_type=MESH,
        )

    same = jnp.logical_and(p.stays, p.col == p.row)
    valid_kept = pltpu.make_async_copy(valid_ref.at[hint(p.row, quarter)], vt_ref, recvs.at[valid_base])

    for step in (1, 2, 3):
        small_came(step).wait_recv()
        small(step).wait_send()
    small_own.wait()
    moved.wait_recv()
    w_joined.start()

    first = p.col * quarter

    def norm_one(n):
        rows = hint(n, 128)
        standard, _ = moments(xt_ref[rows, :].astype(f32))
        place = pl.ds(pl.multiple_of(first + n * 128, 128), 128)
        nall_ref[place, :] = (standard * vall_ref[0:1, :] + vall_ref[1:2, :]).astype(bf)

    pl.loop(0, quarter // 128)(norm_one)
    mine = nall_ref.at[hint(p.col, quarter)]
    to_far = remote(mine, mine, sems, base, {"col": p.far})
    to_near = remote(mine, mine, sems, base + 1, {"col": p.near})
    theirs = nall_ref.at[hint(p.far, quarter)]
    far_came = remote(theirs, theirs, sems, base, {"col": p.far})
    pass_on = remote(theirs, theirs, sems, base + 2, {"col": p.near})
    beside = nall_ref.at[hint(p.near, quarter)]
    near_came = remote(beside, beside, sems, base + 1, {"col": p.near})
    across = nall_ref.at[hint(p.corner, quarter)]
    corner_came = remote(across, across, sems, base + 2, {"col": p.near})
    base += 3
    to_far.start()
    to_near.start()
    for w in w_downs:
        w.across().start()

    @pl.when(jnp.logical_not(same))
    def _():
        valid_out().start()

    @pl.when(same)
    def _():
        valid_kept.start()

    def project(index):
        @pl.loop(0, quarter // 256)
        def _(n):
            rows = pl.ds(pl.multiple_of(index * quarter + n * 256, 256), 256)
            mixed_ref[rows, :] = (nn(nall_ref[rows, :], jall_ref[...]) + bias_ref[...]).astype(bf)

    w_joined.spread()
    for w in weights:
        w.start_along()
    w_joined.ready()
    project(p.col)
    near_came.wait_recv()
    project(p.near)
    far_came.wait_recv()
    pass_on.start()
    project(p.far)
    corner_came.wait_recv()
    project(p.corner)
    w_out.spread()

    own_heads = att_ref.shape[1]
    blocks = tokens // BLOCK
    per_chip = blocks // 2
    share_base = base
    base += per_chip

    def chip_place(n):
        half = per_chip // 2
        return ((n // half + p.core) % 2) * half + n % half

    def share(n, i):
        return pltpu.make_async_remote_copy(
            src_ref=att_ref.at[hint(i, BLOCK)], dst_ref=chip_ref.at[hint(chip_place(n), BLOCK), pl.ds(own_heads, own_heads)],
            send_sem=sends.at[share_base + n], recv_sem=recvs.at[share_base + n],
            device_id={"col": p.far}, device_id_type=MESH,
        )

    def after(it, i):
        @pl.when(it < per_chip)
        def _():
            share(it, i).start()

        @pl.when(it >= per_chip)
        def _():
            chip_ref[hint(chip_place(it - per_chip), BLOCK), :own_heads] = att_ref[hint(i, BLOCK), :]

        for units, action in plan:
            @pl.when(it == at_units(units))
            def _():
                action()

    order = (
        [per_chip + n + 1 for n in range(per_chip)] + [n + 1 for n in range(per_chip)],
        [n + 1 for n in range(blocks)],
    )

    def at_units(units):
        found = []
        for counts in order:
            total, it = 0, 0
            for it, n in enumerate(counts):
                total += n
                if total >= units:
                    break
            found.append(it)
        return found[0] * (1 - p.chip) + found[1] * p.chip

    plan = [
        (3, lambda: w_out.spread_last()),
        (6, lambda: w_up.spread((1,))),
        (11, lambda: w_up.spread((2,))),
        (18, lambda: w_up.spread((3,))),
        (27, lambda: w_up.spread_last((1, 2))),
        (32, lambda: w_downs[0].spread((1, 2))),
    ]

    def attend(*scratch):
        attention_rows(
            heads, lambda it: (it + per_chip * (1 - p.chip)) % blocks, after,
            slope_ref, mixed_ref, att_ref, lse_ref, *scratch,
        )

    pairs = heads // 2
    pl.run_scoped(
        attend,
        pltpu.VMEM((heads, blocks, BLOCK, PAIR), bf), pltpu.VMEM((pairs, blocks, BLOCK, PAIR), bf),
        pltpu.VMEM((pairs, blocks, 2 * BLOCK, PAIR), bf), pltpu.VMEM((heads, BLOCK, BLOCK), f32),
        pltpu.VMEM((heads, blocks, BLOCK, BLOCK), f32), pltpu.VMEM((heads, BLOCK, PAIR), f32),
        pltpu.VMEM((heads, BLOCK, PAIR), f32), pltpu.VMEM((pairs, BLOCK, PAIR), f32),
    )

    @pl.loop(0, per_chip)
    def _(n):
        share(n, n + per_chip * (1 - p.chip)).wait()

    w_up.spread_last((3,))
    w_downs[0].spread((3,))
    target.start_cross()
    w_out.ready(0)
    w_out.ready(1)
    core = Chip(p, sems, base)
    base += 12
    ROWS = 256
    halves = quarter // ROWS

    def swap_rows(number, buffer, n):
        return core.copy(
            number + n, buffer.at[pl.ds(n * ROWS, ROWS)], buffer.at[pl.ds(quarter + n * ROWS, ROWS)]
        )

    def swap_came(number, buffer, n):
        part = buffer.at[pl.ds(quarter + n * ROWS, ROWS)]
        return core.copy(number + n, part, part)

    def give_rows(number, n):
        return core.copy(number + n, give.at[pl.ds(n * ROWS, ROWS)], take.at[pl.ds(n * ROWS, ROWS)])

    def take_rows(number, n):
        part = take.at[pl.ds(n * ROWS, ROWS)]
        return core.copy(number + n, part, part)

    def partial(number, keep, product, again):
        if again:
            for n in range(halves):
                give_rows(number - 4, n).wait_send()
        for n in range(halves):
            give[n * ROWS : (n + 1) * ROWS, :] = product(pl.ds(quarter + n * ROWS, ROWS)).astype(bf)
            give_rows(number, n).start()
        for n in range(halves):
            keep[n * ROWS : (n + 1) * ROWS, :] = product(pl.ds(n * ROWS, ROWS))

    partial(
        0, middle,
        lambda rows: nn(chip_ref[rows, :own_heads], dn2_ref[0, hidden:, :])
        + nn(chip_ref[rows, own_heads:], dn2_ref[1, hidden:, :]),
        False,
    )
    w_downs[1].spread()
    target.send(0)
    for n in range(halves):
        take_rows(0, n).wait_recv()

        @pl.loop(0, ROWS // 64)
        def _(m):
            rows = pl.ds(pl.multiple_of(n * ROWS + m * 64, 64), 64)
            value = xt_ref[rows, :].astype(f32) + (
                middle[rows, :] + take[rows, :].astype(f32) + vall_ref[2:3, :]
            )
            middle[rows, :] = value
            standard, _ = moments(value)
            normed[rows, :] = (standard * vall_ref[3:4, :] + vall_ref[4:5, :]).astype(bf)

        swap_rows(2, normed, n).start()
    w_up.ready(0)
    bias_own.wait()
    bias_far.wait()

    slots = [give.at[pl.ds(256 * (n // 2), 256), pl.ds(hidden // 2 * (n % 2), hidden // 2)] for n in range(4)]
    outg_own, outg_far = (dn2_ref.at[0, :features, pl.ds(own_heads * n, own_heads)] for n in (0, 1))
    jgrad = dn2_ref.at[1, :features, : mixed_ref.shape[1]]
    s_down = Share(
        p, "xy", dng_own, dng_far, dng_ref, came_down, other_down, rows_down,
        [up2_ref.at[1, :, pl.ds(hidden // 2 * n, hidden // 2)] for n in (0, 1)], slots, sems, base,
    )
    s_up = Share(
        p, "xy", upg_own, upg_far, upg_ref, came_up, other_up, rows_up,
        [up2_ref.at[0, :, pl.ds(hidden // 2 * n, hidden // 2)] for n in (0, 1)], slots, sems, base + SHARE_SEMS,
    )
    s_out = Share(
        p, "yx", outg_own, outg_far, outg_ref, came_out, other_out, rows_out,
        [dn2_ref.at[1, :features, pl.ds(768, 256)], dn2_ref.at[0, :features, pl.ds(896, 128)]], slots, sems,
        base + 2 * SHARE_SEMS,
    )
    s_joined = Share(
        p, "x", jgrad, None, joinedg_ref, came_joined, None, rows_joined,
        [dn2_ref.at[0, :features, pl.ds(512, 384)]], slots, sems, base + 3 * SHARE_SEMS,
    )
    base += 4 * SHARE_SEMS

    def natural(chip, n):
        return hint(2 * chip + (p.core + n) % 2, quarter)

    att_base = base
    base += 2

    def share_grad(n):
        return remote(
            gfar.at[pl.ds(n * quarter, quarter)], dout.at[natural(p.chip, n)], sems, att_base + n, {"col": p.far}
        )

    def share_grad_came(n):
        part = dout.at[natural(1 - p.chip, n)]
        return remote(part, part, sems, att_base + n, {"col": p.far})

    stage_base = base
    base += 2

    def middle_part(act, der, keep):
        wide = 256

        def up_rows(side):
            def body(n):
                rows = pl.ds(pl.multiple_of(n * ROWS, ROWS), ROWS)

                @pl.loop(0, hidden // wide, unroll=2)
                def _(m):
                    cols = hint(m, wide)
                    before = nn(normed[rows, :], up2_ref[side, :, cols]) + ub2_ref[side, 0:1, cols]
                    value, slope = gelu_pair(before)
                    act[side, rows, cols] = value.astype(bf)
                    der[side, rows, cols] = slope.astype(bf)

            return body

        pl.loop(0, halves)(up_rows(0))
        for n in range(halves):
            swap_came(2, normed, n).wait_recv()
        w_downs[0].spread_last()
        target.forward()
        pl.loop(halves, 2 * halves)(up_rows(0))
        w_up.ready(1)
        pl.loop(0, 2 * halves)(up_rows(1))
        w_downs[1].spread_last()
        for w in w_downs:
            w.ready(0)
            w.ready(1)
        partial(
            4, gres,
            lambda rows: nn(act[0, rows, :], dn2_ref[0, :hidden, :]) + nn(act[1, rows, :], dn2_ref[1, :hidden, :]),
            True,
        )
        target.wait_recv()

        @pl.when(jnp.logical_not(same))
        def _():
            valid_out().wait_send()
            valid_out().wait_recv()

        @pl.when(same)
        def _():
            valid_kept.wait()

        early_ref[...] = jnp.zeros_like(early_ref)
        for n in range(halves):
            take_rows(4, n).wait_recv()

            @pl.loop(0, ROWS // 64)
            def _(m):
                rows = pl.ds(pl.multiple_of(n * ROWS + m * 64, 64), 64)
                result = middle[rows, :] + (gres[rows, :] + take[rows, :].astype(f32) + vall_ref[5:6, :])
                low_ref[rows, :] = result.astype(bf)
                factor = vt_ref[rows, :].astype(f32)[:, :1] * scale
                value = gt_ref[rows, :].astype(f32) + factor * result
                gres[rows, :] = value
                rounded = value.astype(bf)
                gchip[rows, :] = rounded
                early_ref[5:6, :] += jnp.sum(rounded.astype(f32), axis=0, keepdims=True)

            swap_rows(6, gchip, n).start()
        back.start()
        up_sums_ref[...] = jnp.zeros_like(up_sums_ref)

        def before_rows(n):
            rows = pl.ds(pl.multiple_of(n * ROWS, ROWS), ROWS)

            @pl.loop(0, 2 * hidden // wide, unroll=2)
            def _(m):
                side, cols = m // (hidden // wide), hint(m % (hidden // wide), wide)
                value = nt(gchip[rows, :], dn2_ref[side, cols, :]) * der[side, rows, cols].astype(f32)
                rounded = value.astype(bf)
                der[side, rows, cols] = rounded
                up_sums_ref[side, 0:1, cols] += jnp.sum(rounded.astype(f32), axis=0, keepdims=True)

        def weight_grad(slot, source, values, sinks):
            @pl.loop(0, features // 256)
            def _(f):
                cols = hint(f, 256)
                turned = source[:, cols].T
                for side, sink in enumerate(sinks):
                    copy = pltpu.make_async_copy(stage.at[side], sink.at[cols], recvs.at[slot + side])

                    @pl.when(f > 0)
                    def _():
                        copy.wait()

                    stage[side] = nn(turned, values[side]).astype(bf)
                    copy.start()

            for side, sink in enumerate(sinks):
                pltpu.make_async_copy(stage.at[side], sink.at[pl.ds(0, 256)], recvs.at[slot + side]).wait()

        pl.loop(0, halves)(before_rows)
        for n in range(halves):
            swap_came(6, gchip, n).wait_recv()
        weight_grad(stage_base, gchip, act, (dng_own, dng_far))
        s_down.start()
        pl.loop(halves, 2 * halves)(before_rows)
        partial(
            8, keep, lambda rows: nt(der[0, rows, :], up2_ref[0]) + nt(der[1, rows, :], up2_ref[1]), True
        )

        for n in range(halves):
            for number, buffer in ((2, normed), (6, gchip)):
                swap_rows(number, buffer, n).wait_send()
        for n in range(halves):
            take_rows(8, n).wait_recv()

            @pl.loop(0, ROWS // 64)
            def _(m):
                rows = pl.ds(pl.multiple_of(n * ROWS + m * 64, 64), 64)
                value = keep[rows, :] + take[rows, :].astype(f32)
                standard, inverse = moments(middle[rows, :])
                early_ref[3:4, :] += jnp.sum(value * standard, axis=0, keepdims=True)
                early_ref[4:5, :] += jnp.sum(value, axis=0, keepdims=True)
                scaled = value * vall_ref[3:4, :]
                one = jnp.mean(scaled, 1, keepdims=True)
                two = jnp.mean(scaled * standard, 1, keepdims=True)
                value = gres[rows, :] + inverse * (scaled - one - standard * two)
                gres[rows, :] = value
                rounded = value.astype(bf)
                bchip[rows, :] = rounded
                early_ref[2:3, :] += jnp.sum(rounded.astype(f32), axis=0, keepdims=True)

            swap_rows(10, bchip, n).start()
        for n in range(2 * halves):
            if n >= halves:
                swap_came(10, bchip, n - halves).wait_recv()
            rows = pl.ds(n * ROWS, ROWS)
            place = pl.ds(
                pl.multiple_of((2 * p.chip + (p.core + n // halves) % 2) * quarter + n % halves * ROWS, ROWS), ROWS
            )
            dout[place, :] = nt(bchip[rows, :], dn2_ref[0, hidden:, :]).astype(bf)
            gfar[rows, :] = nt(bchip[rows, :], dn2_ref[1, hidden:, :]).astype(bf)
            if n % halves == halves - 1:
                share_grad(n // halves).start()
        weight_grad(stage_base, normed, der, (upg_own, upg_far))
        s_up.start()

    pl.run_scoped(
        middle_part,
        pltpu.VMEM((2, 2 * quarter, hidden), bf), pltpu.VMEM((2, 2 * quarter, hidden), bf), pltpu.VMEM((quarter, features), f32),
    )

    for w in weights:
        w.sent()

    @pl.loop(0, features // 256)
    def _(f):
        cols = hint(f, 256)
        turned = bchip[:, cols].T
        outg_own[cols, :] = nn(turned, chip_ref[:, :own_heads]).astype(bf)
        outg_far[cols, :] = nn(turned, chip_ref[:, own_heads:]).astype(bf)

    for n in range(halves):
        give_rows(8, n).wait_send()
        swap_rows(10, bchip, n).wait_send()
    back.wait_recv()
    target.wait_send()
    fetch = pltpu.make_async_copy(layer_out_ref, grad, recvs.at[stage_base])
    fetch.start()
    fetch.wait()
    error = jnp.zeros((1, 128), f32)
    for n in range(tokens // 128):
        rows = slice(n * 128, (n + 1) * 128)
        for f in range(grad.shape[1] // 128):
            cols = slice(f * 128, (f + 1) * 128)
            off = grad[rows, cols].astype(f32) - teacher_ref[rows, cols].astype(f32)
            error = error + jnp.sum(off * off * valid_ref[rows, :].astype(f32), axis=0, keepdims=True)
    early_ref[6:7, 0:128] = error
    vectors[0, 0:8, :] = early_ref[...]
    vectors[0, 8:16, :] = jnp.zeros((8, features), f32)
    vectors[0, pl.ds(8 + p.col, 1), :] = up_sums_ref[0]
    vectors[0, pl.ds(8 + p.far, 1), :] = up_sums_ref[1]
    summed = Tally(p, vectors, ("row", "col", "dp"), sems, base)
    base = summed.next_sem
    lately = Tally(p, late, ("row", "dp", "col"), sems, base)
    base = lately.next_sem
    for n in (0, 1):
        share_grad_came(n).wait_recv()
        share_grad(n).wait_send()
    s_out.start()


    def turn(i):
        for at, stage_number in ((0, 0), (2, 1), (3, 2)):
            @pl.when(i == at)
            def _():
                if stage_number > 0:
                    summed.add(stage_number - 1)
                summed.send(stage_number)

        @pl.when(i == 4)
        def _():
            s_down.first_sum()
            s_down.second_copy().start()

    def attend_back(*scratch):
        attention_rows_backward(heads, turn, slope_ref, mixed_ref, dout, att_ref, lse_ref, mixed_ref, *scratch)

    pl.run_scoped(
        attend_back,
        pltpu.VMEM((pairs, blocks, 2 * BLOCK, PAIR), bf), pltpu.VMEM((pairs, blocks, BLOCK, PAIR), bf),
        pltpu.VMEM((pairs, blocks, 2 * BLOCK, PAIR), bf), pltpu.VMEM((pairs, blocks, BLOCK, PAIR), bf),
        pltpu.VMEM((pairs, blocks, 2 * BLOCK, PAIR), bf), pltpu.VMEM((heads, blocks, BLOCK), f32),
        pltpu.VMEM((heads, BLOCK, BLOCK), f32), pltpu.VMEM((heads, BLOCK, PAIR), f32),
        pltpu.VMEM((pairs, blocks, BLOCK, PAIR), f32), pltpu.VMEM((pairs, blocks, BLOCK, PAIR), f32),
        pltpu.VMEM((pairs, blocks, BLOCK, PAIR), f32),
    )

    sums_at = [bchip.at[pl.ds(0, quarter)], bchip.at[pl.ds(quarter, quarter)],
               normed.at[pl.ds(0, quarter)], normed.at[pl.ds(quarter, quarter)]]
    near_in = [gchip.at[pl.ds(0, quarter)], gchip.at[pl.ds(quarter, quarter)]]

    def product(index, slot):
        @pl.loop(0, quarter // 256)
        def _(n):
            rows = pl.ds(pl.multiple_of(index * quarter + n * 256, 256), 256)
            sums_at[slot][hint(n, 256), :] = nt(mixed_ref[rows, :], jall_ref[...]).astype(bf)

    grad_near = [remote(sums_at[n], near_in[n], sems, base + n, {"col": p.near}) for n in (0, 1)]
    grad_far = remote(sums_at[2], take, sems, base + 2, {"col": p.far})
    base += 3
    product(p.corner, 0)
    grad_near[0].start()
    product(p.near, 1)
    grad_near[1].start()
    product(p.far, 2)
    grad_near[0].wait()
    add_rows(sums_at[2], [sums_at[2], near_in[0]])
    grad_far.start()
    product(p.col, 3)
    s_down.second_sum()
    s_down.start_rows()

    @pl.loop(0, features // 128)
    def _(f):
        cols = hint(f, 128)
        jgrad[cols, :] = tn(nall_ref[:, cols], mixed_ref[...]).astype(bf)

    s_joined.start()
    s_out.first_sum()
    s_out.second_copy().start()
    sums = jnp.zeros((1, mixed_ref.shape[1]), f32)
    for n in range(tokens // 256):
        sums = sums + jnp.sum(mixed_ref[n * 256 : (n + 1) * 256, :].astype(f32), axis=0, keepdims=True)
    late[0] = jnp.zeros((8, features), f32)
    late[0, 2:3, 0 : sums.shape[1]] = sums
    s_down.row_half()
    s_up.first_sum()
    s_up.second_copy().start()
    grad_near[1].wait()
    grad_far.wait()
    gin = bchip.at[pl.ds(0, quarter)]
    grad_back = Untranspose(p, gin, input_grad_ref, sems, base)
    base += 4

    @pl.loop(0, quarter // 64)
    def _(n):
        rows = hint(n, 64)
        value = sums_at[3][rows, :].astype(f32) + near_in[1][rows, :].astype(f32) + take[rows, :].astype(f32)
        standard, inverse = moments(xt_ref[rows, :].astype(f32))
        late[0, 0:1, :] += jnp.sum(value * standard, axis=0, keepdims=True)
        late[0, 1:2, :] += jnp.sum(value, axis=0, keepdims=True)
        scaled = value * vall_ref[0:1, :]
        one = jnp.mean(scaled, 1, keepdims=True)
        two = jnp.mean(scaled * standard, 1, keepdims=True)
        gin[rows, :] = (gres[rows, :] + inverse * (scaled - one - standard * two)).astype(bf)

    lately.send(0)
    grad_back.start()
    s_joined.first_sum()
    s_joined.start_rows()
    s_out.second_sum()
    s_out.start_rows()
    s_down.row_sum()
    for n in range(2, len(summed.stages)):
        summed.add(n)
        if n + 1 < len(summed.stages):
            summed.send(n + 1)
    lately.add(0)
    lately.send(1)
    s_up.second_sum()
    s_up.start_rows()
    s_joined.row_half()
    s_out.row_half()
    for n in range(1, len(lately.stages)):
        lately.add(n)
        if n + 1 < len(lately.stages):
            lately.send(n + 1)
    s_up.row_half()
    vector_sum_ref[...] = vectors[summed.last]
    vector_sum_ref[0:2, :] = late[lately.last, 0:2, :]
    joined_at = lately.after(len(lately.stages) - 2)
    vector_sum_ref[7:8, :] = late[joined_at, 2:3, :]
    for share in (s_joined, s_out, s_up):
        share.row_sum()
    for share in (s_down, s_joined, s_out, s_up):
        share.finish()
    grad_back.wait_recv()
    grad_back.wait_send()
    moved.wait_send()
    to_far.wait_send()
    to_near.wait_send()
    pass_on.wait_send()
    w_joined.sent()
    back.wait_send()


def layer_stage(slopes, bias_rows, vectors, joined, layer_in, up, down, out, up_bias, teacher, cot, valid, token_total):
    tokens, width = layer_in.shape
    quarter = tokens // 4
    features = width * lax.axis_size("row")
    joined_width = joined.shape[1]
    heads = joined_width // (3 * HEAD_DIM)
    blocks = tokens // BLOCK
    f32, bf = jnp.float32, jnp.bfloat16
    hidden, head_rows = down.shape[0], out.shape[0]
    vmem, anyspace = pl.BlockSpec(memory_space=pltpu.VMEM), pl.BlockSpec(memory_space=pl.ANY)
    shape = jax.ShapeDtypeStruct
    bits = 0
    while (1 << bits) < lax.axis_size("dp"):
        bits += 1
    count = (
        2 * TRANSPOSE_SEMS + 4 + 4 * WEIGHT_SEMS + HALVES_SEMS + 6 + (3 + bits) + 1 + 3 + blocks // 2 + 12
        + 4 * SHARE_SEMS + 2 + 2 + 2 * (6 + bits) + 3 + 4
    )
    outs = pl.pallas_call(
        functools.partial(layer_kernel, heads, token_total),
        out_shape=(
            shape((tokens, width), bf), shape((tokens, width), bf), shape((width, hidden), bf), shape((width, hidden), bf),
            shape((width, head_rows), bf), shape((width, joined_width), bf), shape((16, features), f32), shape((8, 128), f32),
        ) + (shape((features, hidden), bf),) * 4 + (
            shape((2, features, hidden // 2), bf), shape((2, features, hidden // 2), bf), shape((features, head_rows), bf),
            shape((features, joined_width // 2), bf), shape((features, hidden // 2), bf), shape((features, hidden // 2), bf),
            shape((features, head_rows // 2), bf), shape((3, width, hidden // 2), bf), shape((3, width, hidden // 2), bf),
            shape((3, width, head_rows // 2), bf), shape((3, width, joined_width // 2), bf),
        ),
        in_specs=[pl.BlockSpec(memory_space=pltpu.SMEM), vmem, vmem] + [anyspace] * 6 + [vmem] * 3,
        out_specs=(anyspace,) * 2 + (vmem,) * 6 + (anyspace,) * 15,
        scratch_shapes=[
            pltpu.VMEM((quarter, features), bf), pltpu.VMEM((tokens, features), bf), pltpu.VMEM((tokens, joined_width), bf),
            pltpu.VMEM((tokens, heads * HEAD_DIM), bf), pltpu.VMEM((heads, blocks, BLOCK), f32),
            pltpu.VMEM((features, joined_width), bf), pltpu.VMEM((8, features), f32), pltpu.VMEM((8, features), f32),
            pltpu.VMEM((2, 1, hidden), f32),
            pltpu.VMEM((2 * quarter, 2 * head_rows), bf), pltpu.VMEM((quarter, features), bf), pltpu.VMEM((quarter, 128), bf),
            pltpu.VMEM((2, features, hidden), bf), pltpu.VMEM((2, hidden + head_rows, features), bf),
            pltpu.VMEM((2, 8, hidden), f32), pltpu.VMEM((2 * quarter, features), bf), pltpu.VMEM((2 * quarter, features), bf),
            pltpu.VMEM((2 * quarter, features), bf), pltpu.VMEM((quarter, features), bf), pltpu.VMEM((quarter, features), bf),
            pltpu.VMEM((quarter, features), f32), pltpu.VMEM((quarter, features), f32), pltpu.VMEM((quarter, features), bf),
            pltpu.VMEM((2, 256, hidden), bf), pltpu.VMEM((tokens, width), bf), pltpu.VMEM((2 * quarter, head_rows), bf),
            pltpu.VMEM((tokens, head_rows), bf), pltpu.VMEM((2, 2, quarter, width), bf),
            pltpu.VMEM((tally_slots(bits, ("row", "col", "dp")), 16, features), f32),
            pltpu.VMEM((tally_slots(bits, ("row", "col", "dp")), 8, features), f32),
            pltpu.VMEM((tally_slots(bits, ("col", "dp")), 8, 128), f32),
            pltpu.SemaphoreType.DMA((count,)), pltpu.SemaphoreType.DMA((count,)),
        ],
        compiler_params=pltpu.CompilerParams(vmem_limit_bytes=63 << 20, collective_id=1, has_side_effects=True),
        name="layer_stage",
    )(slopes, bias_rows, vectors, joined, layer_in, up, down, out, up_bias, teacher, cot, valid)
    return outs[:8]


def swap_with(value, axis, bit):
    size = lax.axis_size(axis)
    return lax.ppermute(value, axis, [(i, i ^ bit) for i in range(size)])


def low(value):
    return value.astype(jnp.bfloat16)


def pick(stacked, index):
    return lax.dynamic_index_in_dim(stacked, index, 0, keepdims=False)


def sum_other_pairs(value):
    bit = 2
    while bit < lax.axis_size("dp"):
        value = value + swap_with(low(value), "dp", bit).astype(jnp.float32)
        bit *= 2
    return value


def on_device(
    layer_in,
    first_gain,
    first_shift,
    joined_weight,
    joined_bias,
    out_weight,
    out_bias,
    second_gain,
    second_shift,
    up_weight,
    up_bias,
    down_weight,
    down_bias,
    teacher,
    valid,
    cotangent,
):
    row_size, col_size = lax.axis_size("row"), lax.axis_size("col")
    row, col = lax.axis_index("row"), lax.axis_index("col")
    f32 = jnp.float32
    head_count = joined_bias.shape[0]
    quarter = layer_in.shape[0] // col_size
    head_index = col * head_count + jnp.arange(head_count, dtype=jnp.int32)
    slopes = jnp.exp2(-8.0 * (head_index.astype(f32) + 1.0) / HEADS) * LOG2E

    zero_rows = jnp.zeros_like(joined_bias[:, :HEAD_DIM])
    bias_rows = jnp.stack(
        [joined_bias[:, :HEAD_DIM], zero_rows, joined_bias[:, HEAD_DIM:]], axis=1
    ).reshape(1, -1).astype(f32)
    nothing = jnp.zeros_like(first_gain)
    vectors = jnp.stack(
        [first_gain, first_shift, out_bias, second_gain, second_shift, down_bias, nothing, nothing]
    ).astype(f32)
    token_total = layer_in.shape[0] * lax.axis_size("dp") * col_size
    layer_out, input_grad, up_grad, down_grad, out_grad, joined_grad, sums, scale = layer_stage(
        slopes, bias_rows, vectors, joined_weight, layer_in, up_weight, down_weight, out_weight,
        jnp.broadcast_to(up_bias.astype(f32), (8, up_bias.shape[0])), teacher, cotangent,
        jnp.broadcast_to(low(valid)[:, None], (valid.shape[0], 128)), token_total,
    )
    up_grad, down_grad, out_grad, joined_grad = (
        sum_other_pairs(g.astype(f32)) for g in (up_grad, down_grad, out_grad, joined_grad)
    )
    mine = lax.dynamic_slice_in_dim(sums, row * (D // row_size), D // row_size, 1)
    loss = jnp.sum(sums[6, :128]) * scale[0, 0] / (D * token_total)
    up_bias_grad = pick(sums[8:12], col)
    column_sums = sums[7, : joined_weight.shape[1]].reshape(head_count, 3, HEAD_DIM)
    joined_bias_grad = jnp.concatenate([column_sums[:, 0], column_sums[:, 2]], axis=1)
    return (
        layer_out,
        loss,
        input_grad.astype(f32),
        mine[0],
        mine[1],
        joined_grad,
        joined_bias_grad,
        out_grad.T,
        mine[2],
        mine[3],
        mine[4],
        up_grad,
        up_bias_grad,
        down_grad.T,
        mine[5],
    )


def solution(mesh):
    return jax.shard_map(
        on_device,
        mesh=mesh,
        in_specs=(
            P(("dp", "col"), "row"),
            P("row"),
            P("row"),
            P("row", "col"),
            P("col", None),
            P("col", "row"),
            P("row"),
            P("row"),
            P("row"),
            P("row", "col"),
            P("col"),
            P("col", "row"),
            P("row"),
            P(("dp", "col"), "row"),
            P(("dp", "col")),
            P(("dp", "col"), "row"),
        ),
        out_specs=(
            P(("dp", "col"), "row"),
            P(),
            P(("dp", "col"), "row"),
            P("row"),
            P("row"),
            P("row", "col"),
            P("col", None),
            P("col", "row"),
            P("row"),
            P("row"),
            P("row"),
            P("row", "col"),
            P("col"),
            P("col", "row"),
            P("row"),
        ),
        check_vma=False,
    )
```

```python
import functools
import math

import jax
import jax.numpy as jnp
from jax import lax
from jax.experimental import pallas as pl
from jax.experimental.pallas import tpu as pltpu
from jax.sharding import PartitionSpec as P

D = 1024
HEADS = 16
SEQ = 2048
EPSILON = 1e-05
LOG2E = 1.4426950408889634
HEAD_DIM=64
BLOCK=256
HALF=64
PAIR=128
SCALE2 = LOG2E/8.0

def nt(a,b):
    return lax.dot_general(a,b,(((1,),(1,)),((),())),preferred_element_type=jnp.float32)
def nn(a,b):
    return jnp.dot(a,b,preferred_element_type=jnp.float32)
def tn(a,b):
    return lax.dot_general(a,b,(((0,),(0,)),((),())),preferred_element_type=jnp.float32)

def low_lanes(rows):
    return lax.broadcasted_iota(jnp.int32,(rows,PAIR),1) < HALF

def swap(a):
    return jnp.concatenate([a[:,HALF:],a[:,:HALF]],axis=1)

def attention_rows(heads, order, after, slopes, mixed_ref, out_ref, lse_ref, qs, ks, vs, bias, sc, mx, ls, acc):
    pairs=heads//2
    blocks=mixed_ref.shape[0]//BLOCK
    lo=low_lanes(BLOCK)
    @pl.loop(0,blocks)
    def _(b):
        rows=pl.ds(pl.multiple_of(b*BLOCK,BLOCK),BLOCK)
        for p in range(pairs):
            t0,t1,t2=(mixed_ref[rows,(3*p+n)*PAIR:(3*p+n+1)*PAIR] for n in range(3))
            zero=jnp.zeros_like(t0)
            qs[2*p,b]=jnp.where(lo,t0,zero)
            qs[2*p+1,b]=jnp.where(lo,zero,t1)
            ks[p,b]=jnp.where(lo,swap(t0),swap(t2))
            vs[p,b,:BLOCK]=jnp.where(lo,t1,zero)
            vs[p,b,BLOCK:]=jnp.where(lo,zero,t2)
    il=lax.broadcasted_iota(jnp.int32,(BLOCK,BLOCK),0)
    jl=lax.broadcasted_iota(jnp.int32,(BLOCK,BLOCK),1)
    tent=jnp.minimum(jl,2*il-jl).astype(jnp.float32)
    for h in range(heads):
        bias[h]=tent*slopes[h]
    jrow=lax.broadcasted_iota(jnp.int32,(1,BLOCK),1)
    @pl.loop(0,blocks)
    def _(it):
        i=order(it)
        for h in range(heads):
            t=nt(qs[h,i],ks[h//2,i])*SCALE2+bias[h]
            sc[h,i]=t
            mx[h]=jnp.maximum(t[:,:PAIR],t[:,PAIR:])
        @pl.loop(0,i)
        def _(j):
            place=(jrow+(j-i)*BLOCK).astype(jnp.float32)
            for h in range(heads):
                t=nt(qs[h,i],ks[h//2,j])*SCALE2+place*slopes[h]
                sc[h,j]=t
                mx[h]=jnp.maximum(mx[h],jnp.maximum(t[:,:PAIR],t[:,PAIR:]))
        for h in range(heads):
            mx[h]=jnp.broadcast_to(jnp.max(mx[h],1,keepdims=True),(BLOCK,PAIR))
            ls[h]=jnp.zeros((BLOCK,PAIR),jnp.float32)
        for p in range(pairs):
            acc[p]=jnp.zeros((BLOCK,PAIR),jnp.float32)
        @pl.loop(0,i+1)
        def _(j):
            for p in range(pairs):
                both=[]
                for h in (2*p,2*p+1):
                    m=mx[h]
                    ea=jnp.exp2(sc[h,j,:,:PAIR]-m)
                    eb=jnp.exp2(sc[h,j,:,PAIR:]-m)
                    ls[h]+=ea+eb
                    both+=[ea.astype(jnp.bfloat16),eb.astype(jnp.bfloat16)]
                acc[p]+=nn(jnp.concatenate(both,1),vs[p,j])
        rows=pl.ds(pl.multiple_of(i*BLOCK,BLOCK),BLOCK)
        for p in range(pairs):
            tot=[jnp.broadcast_to(jnp.sum(ls[h],1,keepdims=True),(BLOCK,PAIR)) for h in (2*p,2*p+1)]
            out_ref[rows,p*PAIR:(p+1)*PAIR]=(acc[p]/jnp.where(lo,tot[0],tot[1])).astype(out_ref.dtype)
            for n,h in enumerate((2*p,2*p+1)):
                lse=mx[h]+jnp.log2(tot[n])
                lse_ref[h,pl.ds(i,1),:]=lse.T[:1]
        after(it,i)

def attention_rows_backward(heads, after, slopes, mixed_ref, dout_ref, out_ref, lse_ref, grad_ref, qs, ks, km, vp, ds_, delta, bias, steep, dq, dk, dv):
    pairs=heads//2
    blocks=mixed_ref.shape[0]//BLOCK
    lo=low_lanes(BLOCK)
    @pl.loop(0,blocks)
    def _(b):
        rows=pl.ds(pl.multiple_of(b*BLOCK,BLOCK),BLOCK)
        for p in range(pairs):
            t0,t1,t2=(mixed_ref[rows,(3*p+n)*PAIR:(3*p+n+1)*PAIR] for n in range(3))
            zero=jnp.zeros_like(t0)
            qs[p,b,:BLOCK]=jnp.where(lo,t0,zero)
            qs[p,b,BLOCK:]=jnp.where(lo,zero,t1)
            k=jnp.where(lo,swap(t0),swap(t2))
            ks[p,b]=k
            km[p,b,:BLOCK]=jnp.where(lo,k,zero)
            km[p,b,BLOCK:]=jnp.where(lo,zero,k)
            vp[p,b]=jnp.where(lo,t1,t2)
            d=dout_ref[rows,p*PAIR:(p+1)*PAIR]
            ds_[p,b,:BLOCK]=jnp.where(lo,d,zero)
            ds_[p,b,BLOCK:]=jnp.where(lo,zero,d)
            prod=(d.astype(jnp.float32)*out_ref[rows,p*PAIR:(p+1)*PAIR].astype(jnp.float32)).T
            delta[2*p,pl.ds(b,1),:]=jnp.sum(prod[:HALF],0,keepdims=True)
            delta[2*p+1,pl.ds(b,1),:]=jnp.sum(prod[HALF:],0,keepdims=True)
    kl=lax.broadcasted_iota(jnp.int32,(BLOCK,BLOCK),0)
    ql=lax.broadcasted_iota(jnp.int32,(BLOCK,BLOCK),1)
    tent=jnp.minimum(kl,2*ql-kl).astype(jnp.float32)
    ramp=kl.astype(jnp.float32)
    for h in range(heads):
        bias[h]=tent*slopes[h]
        steep[h]=ramp[:,:PAIR]*slopes[h]
    def block(i,j,first):
        for p in range(pairs):
            ps=[];gs=[]
            for n,h in enumerate((2*p,2*p+1)):
                q=qs[p,i,n*BLOCK:(n+1)*BLOCK]
                d=ds_[p,i,n*BLOCK:(n+1)*BLOCK]
                row=slopes[h]*((j-i)*BLOCK).astype(jnp.float32)-lse_ref[h,pl.ds(i,1),:]
                t=nt(ks[p,j],q)*SCALE2+row+(bias[h] if first else jnp.concatenate([steep[h],steep[h]],1))
                e=jnp.exp2(t)
                g=e*(nt(vp[p,j],d)-delta[h,pl.ds(i,1),:])
                ps.append(e.astype(jnp.bfloat16)); gs.append(g.astype(jnp.bfloat16))
            gv=nn(jnp.concatenate(ps,1),ds_[p,i])
            gk=nn(jnp.concatenate(gs,1),qs[p,i])
            gq=tn(jnp.concatenate(gs,0),km[p,j])
            if first:
                dv[p,j]=gv; dk[p,j]=gk; dq[p,i]=gq
            else:
                dv[p,j]+=gv; dk[p,j]+=gk; dq[p,i]+=gq
    @pl.loop(0,blocks)
    def _(i):
        block(i,i,True)
        @pl.loop(0,i)
        def _(j):
            block(i,j,False)
        after(i)
    @pl.loop(0,blocks)
    def _(b):
        rows=pl.ds(pl.multiple_of(b*BLOCK,BLOCK),BLOCK)
        for p in range(pairs):
            a=dq[p,b]*0.125; k=swap(dk[p,b]*0.125); v=dv[p,b]
            for n,t in enumerate((jnp.where(lo,a,k),jnp.where(lo,v,a),jnp.where(lo,k,v))):
                grad_ref[rows,(3*p+n)*PAIR:(3*p+n+1)*PAIR]=t.astype(grad_ref.dtype)


MESH = pl.DeviceIdType.MESH


def hint(index, size):
    return pl.ds(pl.multiple_of(index * size, size), size)


def remote(src, dst, sems, number, target):
    send, recv = sems
    return pltpu.make_async_remote_copy(
        src_ref=src, dst_ref=dst, send_sem=send.at[number], recv_sem=recv.at[number],
        device_id=target, device_id_type=MESH,
    )


def partner(index, bit):
    return index + bit - 2 * bit * ((index // bit) % 2)


class Place:
    def __init__(self):
        self.dp, self.row, self.col = (lax.axis_index(a) for a in ("dp", "row", "col"))
        self.dps = lax.axis_size("dp")
        self.core, self.chip = self.col % 2, self.col // 2
        self.near, self.far = partner(self.col, 1), partner(self.col, 2)
        self.twin = partner(self.dp, 1)
        self.half = self.dp % 2
        self.plane = 3 * self.core + self.chip - 2 * self.core * self.chip
        self.source = 2 * (((self.row + 1) // 2) % 2) + self.row // 2
        self.corner = partner(self.far, 1)
        self.stays = self.plane == self.row
        self.far_plane = 3 * self.core + (1 - self.chip) - 2 * self.core * (1 - self.chip)
        self.sender = 2 * self.chip + self.source % 2
        self.home = jnp.logical_or(self.stays, self.far_plane == self.row)


def greet(place):
    barrier = pltpu.get_barrier_semaphore()

    def signal(target):
        pl.semaphore_signal(barrier, inc=1, device_id=target, device_id_type=MESH)

    for step in (1, 2, 3):
        signal({"row": (place.row + step) % 4})
    for col in (place.near, place.far, place.corner):
        signal({"col": col})
    amount = 6
    bit = 1
    while bit < place.dps:
        signal({"dp": partner(place.dp, bit)})
        amount += 1
        bit *= 2

    for plane, stays in ((place.plane, place.stays), (place.far_plane, place.far_plane == place.row)):
        signal({"row": plane, "col": place.near})

        @pl.when(jnp.logical_not(stays))
        def _():
            signal({"row": plane, "col": place.col})

    for other in range(4):
        @pl.when(jnp.logical_not(jnp.logical_and(place.home, place.row == other)))
        def _():
            signal({"row": other, "col": place.sender})

        @pl.when(jnp.logical_not(jnp.logical_and(place.stays, place.col == other)))
        def _():
            signal({"row": place.plane, "col": other})

        @pl.when(jnp.logical_not(jnp.logical_and(place.stays, place.row == other)))
        def _():
            signal({"row": other, "col": place.source})

    amount = amount + 16 - 2 * place.home.astype(jnp.int32) - 2 * place.stays.astype(jnp.int32)
    pl.semaphore_wait(barrier, amount)


class Transpose:
    def __init__(self, place, src, dst, relay, sems, first, part=0, parts=1):
        self.p, self.src, self.dst, self.relay, self.sems, self.first = place, src, dst, relay, sems, first
        self.quarter, self.width = src.shape[0] // 4, src.shape[1]
        self.rows = self.quarter // parts
        self.offset = part * self.rows

    def tokens(self, quarter):
        return self.src.at[pl.ds(pl.multiple_of(quarter * self.quarter + self.offset, self.rows), self.rows)]

    def part(self):
        return self.dst.at[pl.ds(self.offset, self.rows), hint(self.p.row, self.width)]

    def cross(self, n):
        src = self.tokens(2 * (1 - self.p.chip) + n)
        return remote(src, self.relay.at[n], self.sems, self.first + 4 + n, {"col": self.p.far})

    def out(self, relayed, n):
        p = self.p
        col = p.col if n == 0 else p.near
        src = self.relay.at[col % 2] if relayed else self.tokens(col)
        return pltpu.make_async_remote_copy(
            src_ref=src, dst_ref=self.part(),
            send_sem=self.sems[0].at[self.first + 2 * relayed + n], recv_sem=self.sems[1].at[self.first + p.row],
            device_id={"row": p.far_plane if relayed else p.plane, "col": col}, device_id_type=MESH,
        )

    def kept(self, relayed):
        p = self.p
        src = self.relay.at[p.core] if relayed else self.tokens(p.col)
        return pltpu.make_async_copy(src, self.part(), self.sems[1].at[self.first + p.row])

    def leaves(self, relayed):
        return (self.p.far_plane if relayed else self.p.plane) != self.p.row

    def send(self, relayed):
        self.out(relayed, 1).start()

        @pl.when(self.leaves(relayed))
        def _():
            self.out(relayed, 0).start()

        @pl.when(jnp.logical_not(self.leaves(relayed)))
        def _():
            self.kept(relayed).start()

    def start_cross(self):
        for n in (0, 1):
            self.cross(n).start()

    def forward(self):
        for n in (0, 1):
            self.cross(n).wait_recv()
        self.send(1)

    def wait_recv(self):
        p = self.p
        for other in range(4):
            mine = jnp.logical_and(p.home, p.row == other)
            part = self.dst.at[pl.ds(self.offset, self.rows), pl.ds(other * self.width, self.width)]

            @pl.when(jnp.logical_not(mine))
            def _():
                pltpu.make_async_remote_copy(
                    src_ref=part, dst_ref=part, send_sem=self.sems[0].at[self.first + other],
                    recv_sem=self.sems[1].at[self.first + other],
                    device_id={"row": other, "col": p.sender}, device_id_type=MESH,
                ).wait_recv()

            @pl.when(mine)
            def _():
                self.kept(0).wait()

    def wait_send(self):
        for n in (0, 1):
            self.cross(n).wait_send()
        for relayed in (0, 1):
            self.out(relayed, 1).wait_send()

            @pl.when(self.leaves(relayed))
            def _():
                self.out(relayed, 0).wait_send()


TRANSPOSE_SEMS = 6


class Slopes:
    def __init__(self, heads):
        self.heads = heads
        col = lax.axis_index("col")
        self.column = jnp.float32(1.0)
        for c in range(1, lax.axis_size("col")):
            self.column = jnp.where(col == c, jnp.float32(2.0 ** (-8.0 * heads * c / HEADS)), self.column)

    def __getitem__(self, head):
        return self.column * (2.0 ** (-8.0 * (head + 1) / HEADS) * LOG2E)


class Weight:
    def __init__(self, place, src, dst, offset, by_rows, last, sems, first):
        self.p, self.src, self.dst, self.offset, self.by_rows, self.last = place, src, dst, offset, by_rows, last
        self.sems, self.first = sems, first
        self.rows, self.width = src.shape
        self.part = self.rows // 2

    def whole(self, side, row):
        if self.by_rows:
            return self.dst.at[side, hint(row, self.rows)]
        return self.dst.at[side, pl.ds(self.offset, self.rows), hint(row, self.width)]

    def piece(self, side, row, half):
        if self.by_rows:
            return self.dst.at[side, hint(row * 2 + half, self.part)]
        start = pl.multiple_of(self.offset + half * self.part, self.part)
        return self.dst.at[side, pl.ds(start, self.part), hint(row, self.width)]

    def other(self, step):
        return (self.p.row + 4 - step) % 4

    def move(self, src, dst, number, target):
        return remote(src, dst, self.sems, self.first + number, target)

    def pass_on(self, side, step, half, number, target):
        src = self.piece(side, self.other(step), half)
        dst = self.piece(1 if "col" in target else side, self.other(step), half)
        return self.move(src, dst, number + step - 1, target)

    def own(self):
        return pltpu.make_async_copy(self.src, self.whole(0, self.p.row), self.sems[1].at[self.first])

    def across(self):
        return self.move(self.src, self.whole(1, self.p.row), 1, {"col": self.p.far})

    def along(self, step):
        p = self.p
        return self.move(
            self.src.at[hint(p.half, self.part)], self.piece(0, p.row, p.half), 1 + step, {"row": (p.row + step) % 4}
        )

    def to_twin(self, step):
        return self.pass_on(0, step, self.p.half, 5, {"dp": self.p.twin})

    def to_far(self, step):
        return self.pass_on(0, step, self.p.half, 8, {"col": self.p.far})

    def onward(self, step):
        if self.last == "y":
            return self.pass_on(0, step, 1 - self.p.half, 11, {"col": self.p.far})
        return self.pass_on(1, step, self.p.half, 11, {"dp": self.p.twin})

    def arrival(self, side, step, half, number):
        part = self.piece(side, self.other(step), half)
        return self.move(part, part, number + step - 1, {"dp": self.p.twin})

    def start_along(self):
        for step in (1, 2, 3):
            self.along(step).start()

    def spread(self, steps=(1, 2, 3)):
        for step in steps:
            self.arrival(0, step, self.p.half, 2).wait_recv()
            self.to_twin(step).start()
            self.to_far(step).start()

    def spread_last(self, steps=(1, 2, 3)):
        p = self.p
        for step in steps:
            if self.last == "y":
                self.arrival(0, step, 1 - p.half, 5).wait_recv()
            else:
                self.arrival(1, step, p.half, 8).wait_recv()
            self.onward(step).start()

    def ready(self, side):
        p = self.p
        if side == 0:
            self.own().wait()
        else:
            self.across().wait_recv()
        for step in (1, 2, 3):
            if side == 0 and self.last == "x":
                self.arrival(0, step, 1 - p.half, 5).wait_recv()
            if side == 1 and self.last == "y":
                self.arrival(1, step, p.half, 8).wait_recv()
            if side == 1:
                self.arrival(1, step, 1 - p.half, 11).wait_recv()

    def sent(self):
        self.across().wait_send()
        for step in (1, 2, 3):
            for copy in (self.along(step), self.to_twin(step), self.to_far(step), self.onward(step)):
                copy.wait_send()


WEIGHT_SEMS = 14


class Halves:
    def __init__(self, place, src, dst, sems, first):
        self.p, self.src, self.dst, self.sems, self.first = place, src, dst, sems, first
        self.rows = src.shape[0]
        self.part = self.rows // 2

    def own(self):
        return pltpu.make_async_copy(self.src, self.dst.at[hint(self.p.row, self.rows)], self.sems[1].at[self.first])

    def along(self, step):
        p = self.p
        return remote(
            self.src.at[hint(p.half, self.part)], self.dst.at[hint(2 * p.row + p.half, self.part)], self.sems,
            self.first + step, {"row": (p.row + step) % 4},
        )

    def part_of(self, step, half):
        return self.dst.at[hint(2 * ((self.p.row + 4 - step) % 4) + half, self.part)]

    def to_twin(self, step, half):
        part = self.part_of(step, half)
        return remote(part, part, self.sems, self.first + 3 + step, {"dp": self.p.twin})

    def start(self):
        self.own().start()
        for step in (1, 2, 3):
            self.along(step).start()

    def spread(self):
        p = self.p
        for step in (1, 2, 3):
            part = self.part_of(step, p.half)
            remote(part, part, self.sems, self.first + step, {"dp": p.twin}).wait_recv()
            self.to_twin(step, p.half).start()

    def ready(self):
        p = self.p
        for step in (1, 2, 3):
            self.to_twin(step, 1 - p.half).wait_recv()
        self.own().wait()

    def sent(self):
        for step in (1, 2, 3):
            self.along(step).wait_send()
            self.to_twin(step, self.p.half).wait_send()


HALVES_SEMS = 7


GELU_ROOT = math.sqrt(2.0 / math.pi)
GELU_CUBE = 0.044715


def gelu_pair(x):
    square = x * x
    t = jnp.tanh(GELU_ROOT * x * (1.0 + GELU_CUBE * square))
    half = 0.5 * (1.0 + t)
    slope = half + 0.5 * x * (1.0 - t * t) * (GELU_ROOT * (1.0 + 3.0 * GELU_CUBE * square))
    return x * half, slope


def moments(x):
    center = jnp.mean(x, 1, keepdims=True)
    spread = jnp.mean(x * x, 1, keepdims=True) - center * center
    inverse = lax.rsqrt(spread + EPSILON)
    return (x - center) * inverse, inverse


class Chip:
    def __init__(self, place, sems, first):
        self.p, self.sems, self.first = place, sems, first

    def copy(self, number, src, dst):
        return remote(src, dst, self.sems, self.first + number, {"col": self.p.near})


class Untranspose:
    def __init__(self, place, src, dst, sems, first):
        self.place, self.src, self.dst, self.sems, self.first = place, src, dst, sems, first
        self.rows, self.width = src.shape[0], src.shape[1] // 4

    def out(self, other):
        p = self.place
        return pltpu.make_async_remote_copy(
            src_ref=self.src.at[:, pl.ds(other * self.width, self.width)],
            dst_ref=self.dst.at[hint(p.col, self.rows)],
            send_sem=self.sems[0].at[self.first + other], recv_sem=self.sems[1].at[self.first + p.col],
            device_id={"row": other, "col": p.source}, device_id_type=MESH,
        )

    def kept(self):
        p = self.place
        return pltpu.make_async_copy(
            self.src.at[:, hint(p.row, self.width)],
            self.dst.at[hint(p.col, self.rows)],
            self.sems[1].at[self.first + p.col],
        )

    def start(self):
        p = self.place
        for other in range(4):
            @pl.when(jnp.logical_not(jnp.logical_and(p.stays, p.row == other)))
            def _():
                self.out(other).start()

        @pl.when(p.stays)
        def _():
            self.kept().start()

    def wait_recv(self):
        p = self.place
        for other in range(4):
            mine = jnp.logical_and(p.stays, p.col == other)
            part = self.dst.at[pl.ds(other * self.rows, self.rows)]

            @pl.when(jnp.logical_not(mine))
            def _():
                pltpu.make_async_remote_copy(
                    src_ref=part, dst_ref=part, send_sem=self.sems[0].at[self.first + other],
                    recv_sem=self.sems[1].at[self.first + other],
                    device_id={"row": p.plane, "col": other}, device_id_type=MESH,
                ).wait_recv()

            @pl.when(mine)
            def _():
                self.kept().wait()

    def wait_send(self):
        p = self.place
        for other in range(4):
            @pl.when(jnp.logical_not(jnp.logical_and(p.stays, p.row == other)))
            def _():
                self.out(other).wait_send()


def add_rows(total, pieces, rows=64):
    @pl.loop(0, total.shape[0] // rows)
    def _(n):
        part = hint(n, rows)
        value = pieces[0][part, :].astype(jnp.float32)
        for piece in pieces[1:]:
            value = value + piece[part, :].astype(jnp.float32)
        total[part, :] = value.astype(total.dtype)


class Share:
    def __init__(self, place, kind, own, far, result, came, other, rows, totals, slots, sems, first):
        self.p, self.kind, self.own, self.far, self.result = place, kind, own, far, result
        self.came, self.other_ref, self.rows, self.totals, self.slots = came, other, rows, totals, slots
        self.sems, self.first = sems, first
        self.width = own.shape[1]
        self.part = self.width // 2
        self.block = own.shape[0] // 4
        self.mine, self.theirs = hint(place.half, self.part), hint(1 - place.half, self.part)

    def first_copies(self):
        p = self.p
        if self.kind == "xy":
            return [
                remote(src.at[:, self.theirs], self.came[n], self.sems, self.first + n, {"dp": p.twin})
                for n, src in enumerate((self.own, self.far))
            ]
        if self.kind == "yx":
            return [remote(self.far, self.came, self.sems, self.first, {"col": p.far})]
        return [remote(self.own.at[:, self.theirs], self.came, self.sems, self.first, {"dp": p.twin})]

    def start(self):
        for copy in self.first_copies():
            copy.start()

    def gather_sum(self, jobs):
        blocks = []
        for total, sources in jobs:
            for n in range(4):
                part = pl.ds(n * self.block, self.block)
                blocks.append((total.at[part], [src.at[part] for src in sources]))
        copies = []
        for n, (_, sources) in enumerate(blocks):
            copies.append([
                pltpu.make_async_copy(
                    src, self.slots[2 * (n % 2) + m].at[:, : src.shape[1]],
                    self.sems[1].at[self.first + 8 + 2 * (n % 2) + m],
                )
                for m, src in enumerate(sources)
            ])
        for copy in copies[0]:
            copy.start()
        for n, (total, sources) in enumerate(blocks):
            if n + 1 < len(blocks):
                for copy in copies[n + 1]:
                    copy.start()
            for copy in copies[n]:
                copy.wait()
            add_rows(total, [self.slots[2 * (n % 2) + m].at[:, : total.shape[1]] for m in range(len(sources))])

    def second_copy(self):
        p = self.p
        if self.kind == "xy":
            return remote(self.totals[1], self.other_ref, self.sems, self.first + 2, {"col": p.far})
        return remote(self.totals[0].at[:, self.theirs], self.other_ref, self.sems, self.first + 2, {"dp": p.twin})

    def first_sum(self):
        for copy in self.first_copies():
            copy.wait()
        if self.kind == "xy":
            self.gather_sum([
                (self.totals[1], [self.came[1], self.far.at[:, self.mine]]),
                (self.totals[0], [self.came[0], self.own.at[:, self.mine]]),
            ])
        elif self.kind == "yx":
            self.gather_sum([(self.totals[0], [self.came, self.own])])
        else:
            self.gather_sum([(self.totals[0], [self.came, self.own.at[:, self.mine]])])

    def total(self):
        return self.totals[1] if self.kind == "yx" else self.totals[0]

    def second_sum(self):
        self.second_copy().wait()
        if self.kind == "xy":
            self.gather_sum([(self.totals[0], [self.other_ref, self.totals[0]])])
        else:
            self.gather_sum([(self.totals[1], [self.other_ref, self.totals[0].at[:, self.mine]])])

    def row_copy(self, step):
        row = self.p.row
        target = partner(row, 1) if step < 2 else partner(row, 2)
        block = partner(target, 2) if step == 1 else target
        return remote(
            self.total().at[hint(block, self.block)], self.rows.at[step], self.sems, self.first + 3 + step, {"row": target}
        )

    def start_rows(self):
        for step in (1, 0):
            self.row_copy(step).start()

    def row_add(self, block, step, target):
        load = pltpu.make_async_copy(
            self.rows.at[step], self.slots[step].at[:, : self.part], self.sems[1].at[self.first + 8 + step]
        )
        load.start()
        load.wait()
        add_rows(target, [self.total().at[hint(block, self.block)], self.slots[step].at[:, : self.part]])

    def row_half(self):
        other = partner(self.p.row, 2)
        self.row_copy(1).wait()
        self.row_add(other, 1, self.total().at[hint(other, self.block)])
        self.row_copy(2).start()
        self.row_copy(0).wait()
        self.row_add(self.p.row, 0, self.total().at[hint(self.p.row, self.block)])

    def last_copy(self, half):
        part = self.result.at[:, hint(half, self.part)]
        return remote(part, part, self.sems, self.first + 6, {"dp": self.p.twin})

    def row_sum(self):
        self.row_copy(2).wait()
        self.row_add(self.p.row, 2, self.result.at[:, self.mine])
        self.last_copy(self.p.half).start()

    def finish(self):
        self.last_copy(self.p.half).wait_send()
        self.last_copy(1 - self.p.half).wait_recv()


SHARE_SEMS = 12


class Tally:
    def __init__(self, place, slots, axes, sems, first):
        self.slots = slots
        p = place
        peers = dict(
            row=[{"row": (p.row + step) % 4} for step in (1, 2, 3)],
            col=[{"col": p.near}, {"col": p.far}, {"col": p.corner}],
        )
        bit = 1
        while bit < p.dps:
            peers["dp%d" % bit] = [{"dp": partner(p.dp, bit)}]
            bit *= 2
        names = []
        for axis in axes:
            names += [name for name in peers if name.startswith(axis)]
        self.stages, at = [], 0
        for name in names:
            copies = [
                remote(slots.at[at], slots.at[at + 1 + n], sems, first + n, target)
                for n, target in enumerate(peers[name])
            ]
            self.stages.append((at, copies))
            at += len(copies) + 1
            first += len(copies)
        self.names, self.last, self.next_sem = names, at, first

    def send(self, n):
        for copy in self.stages[n][1]:
            copy.start()

    def add(self, n):
        at, copies = self.stages[n]
        value = self.slots[at]
        for m, copy in enumerate(copies):
            copy.wait()
            value = value + self.slots[at + 1 + m]
        self.slots[at + len(copies) + 1] = value

    def after(self, n):
        at, copies = self.stages[n]
        return at + len(copies) + 1


def tally_slots(bits, axes):
    return sum({"row": 4, "col": 4, "dp": 2 * bits}[axis] for axis in axes) + 1


def layer_kernel(
    heads, token_total,
    small_ref, joined_ref, layer_ref, up_ref, down_ref, out_ref, teacher_ref, cot_ref,
    layer_out_ref, input_grad_ref, upg_ref, dng_ref, outg_ref, joinedg_ref, vector_sum_ref,
    upg_own, upg_far, dng_own, dng_far, came_up, came_down, came_out, came_joined, other_up, other_down, other_out,
    rows_up, rows_down, rows_out, rows_joined,
    xt_ref, nall_ref, mixed_ref, att_ref, lse_ref, jall_ref, vall_ref, early_ref, up_sums_ref,
    chip_ref, gt_ref, vt_ref, up2_ref, dn2_ref, ub2_ref, normed, gchip, bchip, give, take, middle, gres, low_ref, stage,
    grad, gfar, dout, relay, vectors, late, count, valid_ref, bias_ref, sync, sends, recvs,
):
    sems = (sends, recvs)
    f32, bf = jnp.float32, jnp.bfloat16
    p = Place()
    quarter, features = xt_ref.shape
    hidden = down_ref.shape[0]
    moved = [
        Transpose(p, layer_ref, xt_ref, relay.at[0, :, pl.ds(256 * n, 256)], sems, n * TRANSPOSE_SEMS, n, 2) for n in (0, 1)
    ]
    target = Transpose(p, grad, gt_ref, relay.at[1], sems, 2 * TRANSPOSE_SEMS)
    base = 3 * TRANSPOSE_SEMS
    back = Untranspose(p, low_ref, layer_out_ref, sems, base)
    base += 4
    w_out = Weight(p, out_ref, dn2_ref, hidden, False, "y", sems, base)
    w_up = Weight(p, up_ref, up2_ref, 0, True, "x", sems, base + WEIGHT_SEMS)
    w_downs = [
        Weight(
            p, down_ref.at[pl.ds(n * (hidden // 2), hidden // 2)], dn2_ref, n * (hidden // 2), False, "xy"[n], sems,
            base + (2 + n) * WEIGHT_SEMS,
        )
        for n in (0, 1)
    ]
    weights = [w_out, w_up] + w_downs
    base += 4 * WEIGHT_SEMS
    w_joined = Halves(p, joined_ref, jall_ref, sems, base)
    base += HALVES_SEMS
    small_base, bias_base = base, base + 4
    base += 6

    def small(step):
        part = vall_ref.at[:, hint(p.row, 256)]
        return remote(part, part, sems, small_base + step, {"row": (p.row + step) % 4})

    def small_came(step):
        part = vall_ref.at[:, hint((p.row + 4 - step) % 4, 256)]
        return remote(part, part, sems, small_base + step, {"row": (p.row + step) % 4})

    bias_far = remote(ub2_ref.at[0], ub2_ref.at[1], sems, bias_base + 1, {"col": p.far})
    counted = Tally(p, count, ("col", "dp"), sems, base)
    base = counted.next_sem
    tokens = nall_ref.shape[0]
    greet(p)
    for half in moved:
        half.start_cross()
    moved[0].send(0)
    width = layer_ref.shape[1]
    lanes = width // 128
    for n in range(6):
        for m in range(lanes):
            place = pl.ds(pl.multiple_of(p.row * width + m * 128, 128), 128)
            vall_ref[n : n + 1, place] = small_ref[lanes * n + m : lanes * n + m + 1, :]
    vall_ref[6:8, hint(p.row, width)] = jnp.zeros((2, width), f32)
    at = 6 * lanes
    for n in range(hidden // 128):
        ub2_ref[0, :, n * 128 : (n + 1) * 128] = jnp.broadcast_to(small_ref[at + n : at + n + 1, :], (8, 128))
    at += hidden // 128
    lo = low_lanes(1)
    for n in range(heads // 2):
        even, odd = (small_ref[at + 2 * n + m : at + 2 * n + m + 1, :] for m in (0, 1))
        for m, part in enumerate(
            (jnp.where(lo, even, 0.0), jnp.where(lo, swap(even), swap(odd)), jnp.where(lo, 0.0, odd))
        ):
            bias_ref[0:1, (3 * n + m) * 128 : (3 * n + m + 1) * 128] = part
    at += heads
    number = jnp.zeros((1, 128), f32)
    for n in range(tokens // 128):
        row = small_ref[at + n : at + n + 1, :]
        number = number + row
        valid_ref[n * 128 : (n + 1) * 128, :] = jnp.broadcast_to(row, (128, 128)).T.astype(bf)
    count[0] = jnp.broadcast_to(jnp.sum(number, axis=1, keepdims=True), (8, 128))
    counted.send(0)
    for step in (1, 2, 3):
        small(step).start()
    bias_far.start()
    w_out.across().start()
    w_up.across().start()
    for w in weights:
        w.own().start()
    moved[0].forward()
    moved[1].send(0)
    moved[1].forward()
    for n in range(len(counted.stages)):
        counted.add(n)
        if n + 1 < len(counted.stages):
            counted.send(n + 1)

    scale = token_total / count[counted.last, :1, :1]

    @pl.loop(0, 32)
    def _(n):
        rows = hint(n, grad.shape[0] // 32)
        factor = valid_ref[rows, :].astype(f32) * scale
        for f in range(grad.shape[1] // 128):
            cols = slice(f * 128, (f + 1) * 128)
            grad[rows, cols] = (
                cot_ref[rows, cols].astype(f32) - factor * teacher_ref[rows, cols].astype(f32)
            ).astype(bf)

    valid_base = base
    base += 1

    def valid_out():
        return pltpu.make_async_remote_copy(
            src_ref=valid_ref.at[hint(p.row, quarter)], dst_ref=vt_ref,
            send_sem=sends.at[valid_base], recv_sem=recvs.at[valid_base],
            device_id={"row": p.plane, "col": p.row}, device_id_type=MESH,
        )

    same = jnp.logical_and(p.stays, p.col == p.row)
    valid_kept = pltpu.make_async_copy(valid_ref.at[hint(p.row, quarter)], vt_ref, recvs.at[valid_base])

    for step in (1, 2, 3):
        small_came(step).wait_recv()
        small(step).wait_send()
    first = p.col * quarter

    def norm_one(n):
        rows = hint(n, 128)
        standard, _ = moments(xt_ref[rows, :].astype(f32))
        place = pl.ds(pl.multiple_of(first + n * 128, 128), 128)
        nall_ref[place, :] = (standard * vall_ref[0:1, :] + vall_ref[1:2, :]).astype(bf)

    def half_of(col, n):
        return nall_ref.at[pl.ds(pl.multiple_of(col * quarter + n * 256, 256), 256)]

    def spread_copy(col, n, number, to):
        return remote(half_of(col, n), half_of(col, n), sems, gather_base + 2 * number + n, {"col": to})

    gather_base = base
    base += 6
    to_far = [spread_copy(p.col, n, 0, p.far) for n in (0, 1)]
    to_near = [spread_copy(p.col, n, 1, p.near) for n in (0, 1)]
    far_came = [spread_copy(p.far, n, 0, p.far) for n in (0, 1)]
    near_came = [spread_copy(p.near, n, 1, p.near) for n in (0, 1)]
    pass_on = [spread_copy(p.far, n, 2, p.near) for n in (0, 1)]
    corner_came = [spread_copy(p.corner, n, 2, p.near) for n in (0, 1)]
    for n in (0, 1):
        moved[n].wait_recv()
        pl.loop(2 * n, 2 * n + 2)(norm_one)
        to_far[n].start()
        to_near[n].start()
    for step in (1, 2, 3):
        pl.semaphore_signal(sync, inc=1, device_id={"row": (p.row + step) % 4}, device_id_type=MESH)
    pl.semaphore_wait(sync, 3)
    w_joined.start()
    target.start_cross()
    for w in w_downs:
        w.across().start()

    @pl.when(jnp.logical_not(same))
    def _():
        valid_out().start()

    @pl.when(same)
    def _():
        valid_kept.start()

    def project(index, n):
        rows = pl.ds(pl.multiple_of(index * quarter + n * 256, 256), 256)
        mixed_ref[rows, :] = (nn(nall_ref[rows, :], jall_ref[...]) + bias_ref[0:1, :]).astype(bf)

    far_came[0].wait_recv()
    pass_on[0].start()
    w_joined.spread()
    for w in weights:
        w.start_along()
    far_came[1].wait_recv()
    pass_on[1].start()
    w_joined.ready()
    for came in near_came + corner_came:
        came.wait_recv()

    @pl.loop(0, tokens // 256)
    def _(n):
        project(n // 2, n % 2)

    w_out.spread()

    own_heads = att_ref.shape[1]
    blocks = tokens // BLOCK
    per_chip = blocks // 2
    share_base = base
    base += per_chip

    def chip_place(n):
        half = per_chip // 2
        return ((n // half + p.core) % 2) * half + n % half

    def share(n, i):
        return pltpu.make_async_remote_copy(
            src_ref=att_ref.at[hint(i, BLOCK)], dst_ref=chip_ref.at[hint(chip_place(n), BLOCK), pl.ds(own_heads, own_heads)],
            send_sem=sends.at[share_base + n], recv_sem=recvs.at[share_base + n],
            device_id={"col": p.far}, device_id_type=MESH,
        )

    def after(it, i):
        @pl.when(it < per_chip)
        def _():
            share(it, i).start()

        @pl.when(it >= per_chip)
        def _():
            chip_ref[hint(chip_place(it - per_chip), BLOCK), :own_heads] = att_ref[hint(i, BLOCK), :]

        for units, action in plan:
            @pl.when(it == at_units(units))
            def _():
                action()

    order = (
        [per_chip + n + 1 for n in range(per_chip)] + [n + 1 for n in range(per_chip)],
        [n + 1 for n in range(blocks)],
    )

    def at_units(units):
        found = []
        for counts in order:
            total, it = 0, 0
            for it, n in enumerate(counts):
                total += n
                if total >= units:
                    break
            found.append(it)
        return found[0] * (1 - p.chip) + found[1] * p.chip

    plan = [
        (3, lambda: w_out.spread_last()),
        (6, lambda: w_up.spread((1,))),
        (11, lambda: w_up.spread((2,))),
        (18, lambda: w_up.spread((3,))),
        (27, lambda: w_up.spread_last((1, 2))),
        (29, lambda: (target.send(0), target.forward())),
        (32, lambda: w_downs[0].spread((1, 2))),
    ]

    def attend(*scratch):
        attention_rows(
            heads, lambda it: (it + per_chip * (1 - p.chip)) % blocks, after,
            Slopes(heads), mixed_ref, att_ref, lse_ref, *scratch,
        )

    pairs = heads // 2
    pl.run_scoped(
        attend,
        pltpu.VMEM((heads, blocks, BLOCK, PAIR), bf), pltpu.VMEM((pairs, blocks, BLOCK, PAIR), bf),
        pltpu.VMEM((pairs, blocks, 2 * BLOCK, PAIR), bf), pltpu.VMEM((heads, BLOCK, BLOCK), f32),
        pltpu.VMEM((heads, blocks, BLOCK, BLOCK), f32), pltpu.VMEM((heads, BLOCK, PAIR), f32),
        pltpu.VMEM((heads, BLOCK, PAIR), f32), pltpu.VMEM((pairs, BLOCK, PAIR), f32),
    )

    @pl.loop(0, per_chip)
    def _(n):
        share(n, n + per_chip * (1 - p.chip)).wait_recv()

    w_up.spread_last((3,))
    w_downs[0].spread((3,))
    w_out.ready(0)
    w_out.ready(1)
    core = Chip(p, sems, base)
    base += 12
    ROWS = 256
    halves = quarter // ROWS

    def swap_rows(number, buffer, n):
        return core.copy(
            number + n, buffer.at[pl.ds(n * ROWS, ROWS)], buffer.at[pl.ds(quarter + n * ROWS, ROWS)]
        )

    def swap_came(number, buffer, n):
        part = buffer.at[pl.ds(quarter + n * ROWS, ROWS)]
        return core.copy(number + n, part, part)

    def give_rows(number, n):
        return core.copy(number + n, give.at[pl.ds(n * ROWS, ROWS)], take.at[pl.ds(n * ROWS, ROWS)])

    def take_rows(number, n):
        part = take.at[pl.ds(n * ROWS, ROWS)]
        return core.copy(number + n, part, part)

    def partial(number, keep, product, again):
        if again:
            for n in range(halves):
                give_rows(number - 4, n).wait_send()
        for n in range(halves):
            give[n * ROWS : (n + 1) * ROWS, :] = product(pl.ds(quarter + n * ROWS, ROWS)).astype(bf)
            give_rows(number, n).start()
        for n in range(halves):
            keep[n * ROWS : (n + 1) * ROWS, :] = product(pl.ds(n * ROWS, ROWS))

    partial(
        0, middle,
        lambda rows: nn(chip_ref[rows, :own_heads], dn2_ref[0, hidden:, :])
        + nn(chip_ref[rows, own_heads:], dn2_ref[1, hidden:, :]),
        False,
    )
    w_downs[1].spread()
    for n in range(halves):
        take_rows(0, n).wait_recv()

        @pl.loop(0, ROWS // 64)
        def _(m):
            rows = pl.ds(pl.multiple_of(n * ROWS + m * 64, 64), 64)
            value = xt_ref[rows, :].astype(f32) + (
                middle[rows, :] + take[rows, :].astype(f32) + vall_ref[2:3, :]
            )
            middle[rows, :] = value
            standard, _ = moments(value)
            normed[rows, :] = (standard * vall_ref[3:4, :] + vall_ref[4:5, :]).astype(bf)

        swap_rows(2, normed, n).start()
    w_up.ready(0)
    bias_far.wait()

    slots = [give.at[pl.ds(256 * (n // 2), 256), pl.ds(hidden // 2 * (n % 2), hidden // 2)] for n in range(4)]
    outg_own, outg_far = (dn2_ref.at[0, :features, pl.ds(own_heads * n, own_heads)] for n in (0, 1))
    jgrad = dn2_ref.at[1, :features, : mixed_ref.shape[1]]
    s_down = Share(
        p, "xy", dng_own, dng_far, dng_ref, [came_down.at[n] for n in (0, 1)], other_down, rows_down,
        [up2_ref.at[1, :, pl.ds(hidden // 2 * n, hidden // 2)] for n in (0, 1)], slots, sems, base,
    )
    low_part, high_part = pl.ds(0, hidden // 2), pl.ds(hidden // 2, hidden // 2)
    quarters = [up2_ref.at[0, :, pl.ds(hidden // 4 * n, hidden // 4)] for n in range(3)]
    s_up = Share(
        p, "yx", upg_own.at[:, low_part], upg_far.at[:, low_part], upg_ref.at[:, low_part], came_up.at[0], other_up.at[0],
        rows_up.at[0], [chip_ref, quarters[0]], slots, sems, base + SHARE_SEMS,
    )
    s_up_high = Share(
        p, "xy", upg_own.at[:, high_part], upg_far.at[:, high_part], upg_ref.at[:, high_part],
        [came_up.at[1, :, pl.ds(hidden // 4 * n, hidden // 4)] for n in (0, 1)], other_up.at[1], rows_up.at[1],
        [quarters[1], quarters[2]], slots, sems, base + 4 * SHARE_SEMS,
    )
    s_out = Share(
        p, "yx", outg_own, outg_far, outg_ref, came_out, other_out, rows_out,
        [dn2_ref.at[1, :features, pl.ds(768, 256)], dn2_ref.at[0, :features, pl.ds(896, 128)]], slots, sems,
        base + 2 * SHARE_SEMS,
    )
    s_joined = Share(
        p, "x", jgrad, None, joinedg_ref, came_joined, None, rows_joined,
        [dn2_ref.at[0, :features, pl.ds(512, 384)]], slots, sems, base + 3 * SHARE_SEMS,
    )
    base += 5 * SHARE_SEMS

    def natural(chip, n):
        return hint(2 * chip + (p.core + n) % 2, quarter)

    att_base = base
    base += 2

    def share_grad(n):
        return remote(
            gfar.at[pl.ds(n * quarter, quarter)], dout.at[natural(p.chip, n)], sems, att_base + n, {"col": p.far}
        )

    def share_grad_came(n):
        part = dout.at[natural(1 - p.chip, n)]
        return remote(part, part, sems, att_base + n, {"col": p.far})

    stage_base = base
    base += 2

    def middle_part(act, der, keep):
        wide = 256

        def up_rows(side):
            def body(n):
                rows = pl.ds(pl.multiple_of(n * ROWS, ROWS), ROWS)

                @pl.loop(0, hidden // wide, unroll=2)
                def _(m):
                    cols = hint(m, wide)
                    before = nn(normed[rows, :], up2_ref[side, :, cols]) + ub2_ref[side, 0:1, cols]
                    value, slope = gelu_pair(before)
                    act[side, rows, cols] = value.astype(bf)
                    der[side, rows, cols] = slope.astype(bf)

            return body

        pl.loop(0, halves)(up_rows(0))
        for n in range(halves):
            swap_came(2, normed, n).wait_recv()
        pl.loop(halves, 2 * halves)(up_rows(0))
        w_up.ready(1)
        pl.loop(0, halves)(up_rows(1))
        w_downs[0].spread_last()
        pl.loop(halves, 2 * halves)(up_rows(1))
        w_downs[1].spread_last()
        for w in w_downs:
            w.ready(0)
            w.ready(1)
        partial(
            4, gres,
            lambda rows: nn(act[0, rows, :], dn2_ref[0, :hidden, :]) + nn(act[1, rows, :], dn2_ref[1, :hidden, :]),
            True,
        )
        target.wait_recv()

        @pl.when(jnp.logical_not(same))
        def _():
            valid_out().wait_send()
            valid_out().wait_recv()

        @pl.when(same)
        def _():
            valid_kept.wait()

        early_ref[...] = jnp.zeros_like(early_ref)
        for n in range(halves):
            take_rows(4, n).wait_recv()

            @pl.loop(0, ROWS // 64)
            def _(m):
                rows = pl.ds(pl.multiple_of(n * ROWS + m * 64, 64), 64)
                result = middle[rows, :] + (gres[rows, :] + take[rows, :].astype(f32) + vall_ref[5:6, :])
                low_ref[rows, :] = result.astype(bf)
                factor = vt_ref[rows, :].astype(f32)[:, :1] * scale
                value = gt_ref[rows, :].astype(f32) + factor * result
                gres[rows, :] = value
                rounded = value.astype(bf)
                gchip[rows, :] = rounded
                early_ref[5:6, :] += jnp.sum(rounded.astype(f32), axis=0, keepdims=True)

            swap_rows(6, gchip, n).start()
        back.start()
        up_sums_ref[...] = jnp.zeros_like(up_sums_ref)

        def before_rows(n):
            rows = pl.ds(pl.multiple_of(n * ROWS, ROWS), ROWS)

            @pl.loop(0, 2 * hidden // wide, unroll=2)
            def _(m):
                side, cols = m // (hidden // wide), hint(m % (hidden // wide), wide)
                value = nt(gchip[rows, :], dn2_ref[side, cols, :]) * der[side, rows, cols].astype(f32)
                rounded = value.astype(bf)
                der[side, rows, cols] = rounded
                up_sums_ref[side, 0:1, cols] += jnp.sum(rounded.astype(f32), axis=0, keepdims=True)

        def weight_grad(slot, source, values, sinks):
            @pl.loop(0, features // 256)
            def _(f):
                cols = hint(f, 256)
                turned = source[:, cols].T
                for side, sink in enumerate(sinks):
                    copy = pltpu.make_async_copy(stage.at[side], sink.at[cols], recvs.at[slot + side])

                    @pl.when(f > 0)
                    def _():
                        copy.wait()

                    stage[side] = nn(turned, values[side]).astype(bf)
                    copy.start()

            for side, sink in enumerate(sinks):
                pltpu.make_async_copy(stage.at[side], sink.at[pl.ds(0, 256)], recvs.at[slot + side]).wait()

        pl.loop(0, halves)(before_rows)
        for n in range(halves):
            swap_came(6, gchip, n).wait_recv()
        weight_grad(stage_base, gchip, act, (dng_own, dng_far))
        s_down.start()
        pl.loop(halves, 2 * halves)(before_rows)
        partial(
            8, keep, lambda rows: nt(der[0, rows, :], up2_ref[0]) + nt(der[1, rows, :], up2_ref[1]), True
        )

        for n in range(halves):
            for number, buffer in ((2, normed), (6, gchip)):
                swap_rows(number, buffer, n).wait_send()
        for n in range(halves):
            take_rows(8, n).wait_recv()

            @pl.loop(0, ROWS // 64)
            def _(m):
                rows = pl.ds(pl.multiple_of(n * ROWS + m * 64, 64), 64)
                value = keep[rows, :] + take[rows, :].astype(f32)
                standard, inverse = moments(middle[rows, :])
                early_ref[3:4, :] += jnp.sum(value * standard, axis=0, keepdims=True)
                early_ref[4:5, :] += jnp.sum(value, axis=0, keepdims=True)
                scaled = value * vall_ref[3:4, :]
                one = jnp.mean(scaled, 1, keepdims=True)
                two = jnp.mean(scaled * standard, 1, keepdims=True)
                value = gres[rows, :] + inverse * (scaled - one - standard * two)
                gres[rows, :] = value
                rounded = value.astype(bf)
                bchip[rows, :] = rounded
                early_ref[2:3, :] += jnp.sum(rounded.astype(f32), axis=0, keepdims=True)

            swap_rows(10, bchip, n).start()
        for n in range(2 * halves):
            if n >= halves:
                swap_came(10, bchip, n - halves).wait_recv()
            rows = pl.ds(n * ROWS, ROWS)
            place = pl.ds(
                pl.multiple_of((2 * p.chip + (p.core + n // halves) % 2) * quarter + n % halves * ROWS, ROWS), ROWS
            )
            dout[place, :] = nt(bchip[rows, :], dn2_ref[0, hidden:, :]).astype(bf)
            gfar[rows, :] = nt(bchip[rows, :], dn2_ref[1, hidden:, :]).astype(bf)
            if n % halves == halves - 1:
                share_grad(n // halves).start()
        weight_grad(stage_base, normed, der, (upg_own, upg_far))
        s_up.start()
        s_up_high.start()

    pl.run_scoped(
        middle_part,
        pltpu.VMEM((2, 2 * quarter, hidden), bf), pltpu.VMEM((2, 2 * quarter, hidden), bf), pltpu.VMEM((quarter, features), f32),
    )

    for w in weights:
        w.sent()

    @pl.loop(0, features // 256)
    def _(f):
        cols = hint(f, 256)
        turned = bchip[:, cols].T
        outg_own[cols, :] = nn(turned, chip_ref[:, :own_heads]).astype(bf)
        outg_far[cols, :] = nn(turned, chip_ref[:, own_heads:]).astype(bf)

    for n in range(halves):
        give_rows(8, n).wait_send()
        swap_rows(10, bchip, n).wait_send()
    back.wait_recv()
    target.wait_send()
    fetch = pltpu.make_async_copy(layer_out_ref, grad, recvs.at[stage_base])
    fetch.start()
    fetch.wait()
    error = jnp.zeros((1, 128), f32)
    for n in range(tokens // 128):
        rows = slice(n * 128, (n + 1) * 128)
        for f in range(grad.shape[1] // 128):
            cols = slice(f * 128, (f + 1) * 128)
            off = grad[rows, cols].astype(f32) - teacher_ref[rows, cols].astype(f32)
            error = error + jnp.sum(off * off * valid_ref[rows, :].astype(f32), axis=0, keepdims=True)
    early_ref[6:7, 0:128] = error
    vectors[0, 0:8, :] = early_ref[...]
    vectors[0, 8:16, :] = jnp.zeros((8, features), f32)
    vectors[0, pl.ds(8 + p.col, 1), :] = up_sums_ref[0]
    vectors[0, pl.ds(8 + p.far, 1), :] = up_sums_ref[1]
    summed = Tally(p, vectors, ("row", "col", "dp"), sems, base)
    base = summed.next_sem
    lately = Tally(p, late, ("row", "dp", "col"), sems, base)
    base = lately.next_sem
    summed.send(0)
    for n in (0, 1):
        share_grad_came(n).wait_recv()
        share_grad(n).wait_send()
    s_out.start()


    def turn(i):
        @pl.when(i == 1)
        def _():
            summed.add(0)
            summed.send(1)

        @pl.when(i == 4)
        def _():
            s_down.first_sum()
            s_down.second_copy().start()

        @pl.when(i == 6)
        def _():
            s_up.first_sum()
            s_up.second_copy().start()

    def attend_back(*scratch):
        attention_rows_backward(heads, turn, Slopes(heads), mixed_ref, dout, att_ref, lse_ref, mixed_ref, *scratch)

    pl.run_scoped(
        attend_back,
        pltpu.VMEM((pairs, blocks, 2 * BLOCK, PAIR), bf), pltpu.VMEM((pairs, blocks, BLOCK, PAIR), bf),
        pltpu.VMEM((pairs, blocks, 2 * BLOCK, PAIR), bf), pltpu.VMEM((pairs, blocks, BLOCK, PAIR), bf),
        pltpu.VMEM((pairs, blocks, 2 * BLOCK, PAIR), bf), pltpu.VMEM((heads, blocks, BLOCK), f32),
        pltpu.VMEM((heads, BLOCK, BLOCK), f32), pltpu.VMEM((heads, BLOCK, PAIR), f32),
        pltpu.VMEM((pairs, blocks, BLOCK, PAIR), f32), pltpu.VMEM((pairs, blocks, BLOCK, PAIR), f32),
        pltpu.VMEM((pairs, blocks, BLOCK, PAIR), f32),
    )

    @pl.loop(0, features // 128)
    def _(f):
        cols = hint(f, 128)
        jgrad[cols, :] = tn(nall_ref[:, cols], mixed_ref[...]).astype(bf)

    s_joined.start()

    sums_at = [bchip.at[pl.ds(0, quarter)], bchip.at[pl.ds(quarter, quarter)],
               normed.at[pl.ds(0, quarter)], normed.at[pl.ds(quarter, quarter)]]
    near_in = [gchip.at[pl.ds(0, quarter)], gchip.at[pl.ds(quarter, quarter)]]

    def product(index, slot):
        @pl.loop(0, quarter // 256)
        def _(n):
            rows = pl.ds(pl.multiple_of(index * quarter + n * 256, 256), 256)
            sums_at[slot][hint(n, 256), :] = nt(mixed_ref[rows, :], jall_ref[...]).astype(bf)

    grad_near = [remote(sums_at[n], near_in[n], sems, base + n, {"col": p.near}) for n in (0, 1)]
    grad_far = remote(sums_at[2], take, sems, base + 2, {"col": p.far})
    base += 3
    product(p.corner, 0)
    grad_near[0].start()
    product(p.near, 1)
    grad_near[1].start()
    product(p.far, 2)
    grad_near[0].wait()
    add_rows(sums_at[2], [sums_at[2], near_in[0]])
    grad_far.start()
    product(p.col, 3)
    s_down.second_sum()
    s_down.start_rows()

    s_up.second_sum()
    s_up.start_rows()
    s_out.first_sum()
    s_out.second_copy().start()
    sums = jnp.zeros((1, mixed_ref.shape[1]), f32)
    for n in range(tokens // 256):
        sums = sums + jnp.sum(mixed_ref[n * 256 : (n + 1) * 256, :].astype(f32), axis=0, keepdims=True)
    late[0] = jnp.zeros((8, features), f32)
    late[0, 2:3, 0 : sums.shape[1]] = sums
    s_up_high.first_sum()
    s_up_high.second_copy().start()
    s_down.row_half()
    s_up.row_half()
    s_joined.first_sum()
    s_joined.start_rows()
    grad_near[1].wait()
    grad_far.wait()
    gin = bchip.at[pl.ds(0, quarter)]
    grad_back = Untranspose(p, gin, input_grad_ref, sems, base)
    base += 4

    @pl.loop(0, quarter // 64)
    def _(n):
        rows = hint(n, 64)
        value = sums_at[3][rows, :].astype(f32) + near_in[1][rows, :].astype(f32) + take[rows, :].astype(f32)
        standard, inverse = moments(xt_ref[rows, :].astype(f32))
        late[0, 0:1, :] += jnp.sum(value * standard, axis=0, keepdims=True)
        late[0, 1:2, :] += jnp.sum(value, axis=0, keepdims=True)
        scaled = value * vall_ref[0:1, :]
        one = jnp.mean(scaled, 1, keepdims=True)
        two = jnp.mean(scaled * standard, 1, keepdims=True)
        gin[rows, :] = (gres[rows, :] + inverse * (scaled - one - standard * two)).astype(bf)

    lately.send(0)
    grad_back.start()
    s_out.second_sum()
    s_out.start_rows()
    s_down.row_sum()
    s_up.row_sum()
    s_joined.row_half()
    s_up_high.second_sum()
    s_up_high.start_rows()
    for n in range(1, len(summed.stages)):
        summed.add(n)
        if n + 1 < len(summed.stages):
            summed.send(n + 1)
    lately.add(0)
    lately.send(1)
    s_joined.row_sum()
    for n in range(1, len(lately.stages)):
        lately.add(n)
        if n + 1 < len(lately.stages):
            lately.send(n + 1)
    s_out.row_half()
    s_up_high.row_half()
    joined_at = lately.after(len(lately.stages) - 2)
    at = 0
    for n in range(6):
        place = hint(p.row, width)
        value = late[lately.last, n : n + 1, place] if n < 2 else vectors[summed.last, n : n + 1, place]
        for m in range(lanes):
            vector_sum_ref[at : at + 1, :] = value[:, m * 128 : (m + 1) * 128]
            at += 1
    value = vectors[summed.last, pl.ds(8 + p.col, 1), :]
    for m in range(hidden // 128):
        vector_sum_ref[at : at + 1, :] = value[:, m * 128 : (m + 1) * 128]
        at += 1
    for n in range(heads // 2):
        first, second, third = (
            late[joined_at, 2:3, (3 * n + m) * 128 : (3 * n + m + 1) * 128] for m in range(3)
        )
        vector_sum_ref[at : at + 1, :] = jnp.where(lo, first, swap(second))
        vector_sum_ref[at + 1 : at + 2, :] = jnp.where(lo, swap(second), third)
        at += 2
    value = jnp.sum(vectors[summed.last, 6:7, 0:128], axis=1, keepdims=True) * (scale * (1.0 / (features * token_total)))
    vector_sum_ref[at:, :] = jnp.broadcast_to(value, (vector_sum_ref.shape[0] - at, 128))
    s_out.row_sum()
    s_up_high.row_sum()
    for part in (s_down, s_up, s_joined, s_out, s_up_high):
        part.finish()
    grad_back.wait_recv()
    grad_back.wait_send()
    for n in (0, 1):
        moved[n].wait_send()
        for copies in (to_far, to_near, pass_on):
            copies[n].wait_send()
    w_joined.sent()
    back.wait_send()

    @pl.loop(0, per_chip)
    def _(n):
        share(n, n + per_chip * (1 - p.chip)).wait_send()


def layer_stage(small, joined, layer_in, up, down, out, teacher, cot, token_total):
    tokens, width = layer_in.shape
    quarter = tokens // 4
    features = width * lax.axis_size("row")
    joined_width = joined.shape[1]
    heads = joined_width // (3 * HEAD_DIM)
    blocks = tokens // BLOCK
    f32, bf = jnp.float32, jnp.bfloat16
    hidden, head_rows = down.shape[0], out.shape[0]
    vmem, anyspace = pl.BlockSpec(memory_space=pltpu.VMEM), pl.BlockSpec(memory_space=pl.ANY)
    shape = jax.ShapeDtypeStruct
    bits = 0
    while (1 << bits) < lax.axis_size("dp"):
        bits += 1
    count = (
        3 * TRANSPOSE_SEMS + 4 + 4 * WEIGHT_SEMS + HALVES_SEMS + 6 + (3 + bits) + 1 + 6 + blocks // 2 + 12
        + 5 * SHARE_SEMS + 2 + 2 + 2 * (6 + bits) + 3 + 4
    )
    small_rows = 8 * ((6 * width // 128 + hidden // 128 + heads) // 8 + 1)
    outs = pl.pallas_call(
        functools.partial(layer_kernel, heads, token_total),
        out_shape=(
            shape((tokens, width), bf), shape((tokens, width), bf), shape((width, hidden), bf), shape((width, hidden), bf),
            shape((width, head_rows), bf), shape((width, joined_width), bf), shape((small_rows, 128), f32),
        ) + (shape((features, hidden), bf),) * 4 + (
            shape((2, features, hidden // 2), bf), shape((2, features, hidden // 2), bf), shape((features, head_rows), bf),
            shape((features, joined_width // 2), bf), shape((2, features, hidden // 4), bf), shape((features, hidden // 2), bf),
            shape((features, head_rows // 2), bf), shape((2, 3, width, hidden // 4), bf), shape((3, width, hidden // 2), bf),
            shape((3, width, head_rows // 2), bf), shape((3, width, joined_width // 2), bf),
        ),
        in_specs=[vmem] + [anyspace] * 5 + [vmem] * 2,
        out_specs=(anyspace,) * 2 + (vmem,) * 5 + (anyspace,) * 15,
        scratch_shapes=[
            pltpu.VMEM((quarter, features), bf), pltpu.VMEM((tokens, features), bf), pltpu.VMEM((tokens, joined_width), bf),
            pltpu.VMEM((tokens, heads * HEAD_DIM), bf), pltpu.VMEM((heads, blocks, BLOCK), f32),
            pltpu.VMEM((features, joined_width), bf), pltpu.VMEM((8, features), f32), pltpu.VMEM((8, features), f32),
            pltpu.VMEM((2, 1, hidden), f32),
            pltpu.VMEM((2 * quarter, 2 * head_rows), bf), pltpu.VMEM((quarter, features), bf), pltpu.VMEM((quarter, 128), bf),
            pltpu.VMEM((2, features, hidden), bf), pltpu.VMEM((2, hidden + head_rows, features), bf),
            pltpu.VMEM((2, 8, hidden), f32), pltpu.VMEM((2 * quarter, features), bf), pltpu.VMEM((2 * quarter, features), bf),
            pltpu.VMEM((2 * quarter, features), bf), pltpu.VMEM((quarter, features), bf), pltpu.VMEM((quarter, features), bf),
            pltpu.VMEM((quarter, features), f32), pltpu.VMEM((quarter, features), f32), pltpu.VMEM((quarter, features), bf),
            pltpu.VMEM((2, 256, hidden), bf), pltpu.VMEM((tokens, width), bf), pltpu.VMEM((2 * quarter, head_rows), bf),
            pltpu.VMEM((tokens, head_rows), bf), pltpu.VMEM((2, 2, quarter, width), bf),
            pltpu.VMEM((tally_slots(bits, ("row", "col", "dp")), 16, features), f32),
            pltpu.VMEM((tally_slots(bits, ("row", "col", "dp")), 8, features), f32),
            pltpu.VMEM((tally_slots(bits, ("col", "dp")), 8, 128), f32),
            pltpu.VMEM((tokens, 128), bf), pltpu.VMEM((8, joined_width), f32),
            pltpu.SemaphoreType.REGULAR, pltpu.SemaphoreType.DMA((count,)), pltpu.SemaphoreType.DMA((count,)),
        ],
        compiler_params=pltpu.CompilerParams(vmem_limit_bytes=63 << 20, collective_id=1, has_side_effects=True),
        name="layer_stage",
    )(small, joined, layer_in, up, down, out, teacher, cot)
    return outs[:7]


def swap_with(value, axis, bit):
    size = lax.axis_size(axis)
    return lax.ppermute(value, axis, [(i, i ^ bit) for i in range(size)])


def low(value):
    return value.astype(jnp.bfloat16)


def sum_other_pairs(value):
    bit = 2
    while bit < lax.axis_size("dp"):
        value = value + swap_with(low(value), "dp", bit).astype(jnp.float32)
        bit *= 2
    return value


def on_device(
    layer_in,
    first_gain,
    first_shift,
    joined_weight,
    joined_bias,
    out_weight,
    out_bias,
    second_gain,
    second_shift,
    up_weight,
    up_bias,
    down_weight,
    down_bias,
    teacher,
    valid,
    cotangent,
):
    f32 = jnp.float32
    token_total = layer_in.shape[0] * lax.axis_size("dp") * lax.axis_size("col")
    arrays = (
        first_gain, first_shift, out_bias, second_gain, second_shift, down_bias, up_bias, joined_bias.reshape(-1), valid,
    )
    small = jnp.concatenate([a.astype(f32) for a in arrays]).reshape(-1, 128)
    layer_out, input_grad, up_grad, down_grad, out_grad, joined_grad, sums = layer_stage(
        small, joined_weight, layer_in, up_weight, down_weight, out_weight, teacher, cotangent, token_total
    )
    up_grad, down_grad, out_grad, joined_grad = (
        sum_other_pairs(g.astype(f32)) for g in (up_grad, down_grad, out_grad, joined_grad)
    )
    sums = sums.reshape(-1)
    pieces, at = [], 0
    for size in [layer_in.shape[1]] * 6 + [up_bias.shape[0], joined_bias.size, 1]:
        pieces.append(sums[at : at + size])
        at += size
    return (
        layer_out,
        pieces[8][0],
        input_grad.astype(f32),
        pieces[0],
        pieces[1],
        joined_grad,
        pieces[7].reshape(joined_bias.shape),
        out_grad.T,
        pieces[2],
        pieces[3],
        pieces[4],
        up_grad,
        pieces[6],
        down_grad.T,
        pieces[5],
    )


def solution(mesh):
    return jax.shard_map(
        on_device,
        mesh=mesh,
        in_specs=(
            P(("dp", "col"), "row"),
            P("row"),
            P("row"),
            P("row", "col"),
            P("col", None),
            P("col", "row"),
            P("row"),
            P("row"),
            P("row"),
            P("row", "col"),
            P("col"),
            P("col", "row"),
            P("row"),
            P(("dp", "col"), "row"),
            P(("dp", "col")),
            P(("dp", "col"), "row"),
        ),
        out_specs=(
            P(("dp", "col"), "row"),
            P(),
            P(("dp", "col"), "row"),
            P("row"),
            P("row"),
            P("row", "col"),
            P("col", None),
            P("col", "row"),
            P("row"),
            P("row"),
            P("row"),
            P("row", "col"),
            P("col"),
            P("col", "row"),
            P("row"),
        ),
        check_vma=False,
    )
```

```python
import functools
import math

import jax
import jax.numpy as jnp
from jax import lax
from jax.experimental import pallas as pl
from jax.experimental.pallas import tpu as pltpu
from jax.sharding import PartitionSpec as P

D = 1024
HEADS = 16
SEQ = 2048
EPSILON = 1e-05
LOG2E = 1.4426950408889634
HEAD_DIM=64
BLOCK=256
HALF=64
PAIR=128
SCALE2 = LOG2E/8.0

def nt(a,b):
    return lax.dot_general(a,b,(((1,),(1,)),((),())),preferred_element_type=jnp.float32)
def nn(a,b):
    return jnp.dot(a,b,preferred_element_type=jnp.float32)
def tn(a,b):
    return lax.dot_general(a,b,(((0,),(0,)),((),())),preferred_element_type=jnp.float32)

def low_lanes(rows):
    return lax.broadcasted_iota(jnp.int32,(rows,PAIR),1) < HALF

def swap(a):
    return jnp.concatenate([a[:,HALF:],a[:,:HALF]],axis=1)

def attention_rows(heads, order, after, slopes, mixed_ref, out_ref, lse_ref, qs, ks, vs, bias, sc, mx, ls, acc):
    pairs=heads//2
    blocks=mixed_ref.shape[0]//BLOCK
    lo=low_lanes(BLOCK)
    @pl.loop(0,blocks)
    def _(b):
        rows=pl.ds(pl.multiple_of(b*BLOCK,BLOCK),BLOCK)
        for p in range(pairs):
            t0,t1,t2=(mixed_ref[rows,(3*p+n)*PAIR:(3*p+n+1)*PAIR] for n in range(3))
            zero=jnp.zeros_like(t0)
            qs[2*p,b]=jnp.where(lo,t0,zero)
            qs[2*p+1,b]=jnp.where(lo,zero,t1)
            ks[p,b]=jnp.where(lo,swap(t0),swap(t2))
            vs[p,b,:BLOCK]=jnp.where(lo,t1,zero)
            vs[p,b,BLOCK:]=jnp.where(lo,zero,t2)
    il=lax.broadcasted_iota(jnp.int32,(BLOCK,BLOCK),0)
    jl=lax.broadcasted_iota(jnp.int32,(BLOCK,BLOCK),1)
    tent=jnp.minimum(jl,2*il-jl).astype(jnp.float32)
    for h in range(heads):
        bias[h]=tent*slopes[h]
    jrow=lax.broadcasted_iota(jnp.int32,(1,BLOCK),1)
    @pl.loop(0,blocks)
    def _(it):
        i=order(it)
        for h in range(heads):
            t=nt(qs[h,i],ks[h//2,i])*SCALE2+bias[h]
            sc[h,i]=t
            mx[h]=jnp.maximum(t[:,:PAIR],t[:,PAIR:])
        @pl.loop(0,i)
        def _(j):
            place=(jrow+(j-i)*BLOCK).astype(jnp.float32)
            for h in range(heads):
                t=nt(qs[h,i],ks[h//2,j])*SCALE2+place*slopes[h]
                sc[h,j]=t
                mx[h]=jnp.maximum(mx[h],jnp.maximum(t[:,:PAIR],t[:,PAIR:]))
        for h in range(heads):
            mx[h]=jnp.broadcast_to(jnp.max(mx[h],1,keepdims=True),(BLOCK,PAIR))
            ls[h]=jnp.zeros((BLOCK,PAIR),jnp.float32)
        for p in range(pairs):
            acc[p]=jnp.zeros((BLOCK,PAIR),jnp.float32)
        @pl.loop(0,i+1)
        def _(j):
            for p in range(pairs):
                both=[]
                for h in (2*p,2*p+1):
                    m=mx[h]
                    ea=jnp.exp2(sc[h,j,:,:PAIR]-m)
                    eb=jnp.exp2(sc[h,j,:,PAIR:]-m)
                    ls[h]+=ea+eb
                    both+=[ea.astype(jnp.bfloat16),eb.astype(jnp.bfloat16)]
                acc[p]+=nn(jnp.concatenate(both,1),vs[p,j])
        rows=pl.ds(pl.multiple_of(i*BLOCK,BLOCK),BLOCK)
        for p in range(pairs):
            tot=[jnp.broadcast_to(jnp.sum(ls[h],1,keepdims=True),(BLOCK,PAIR)) for h in (2*p,2*p+1)]
            out_ref[rows,p*PAIR:(p+1)*PAIR]=(acc[p]/jnp.where(lo,tot[0],tot[1])).astype(out_ref.dtype)
            for n,h in enumerate((2*p,2*p+1)):
                lse=mx[h]+jnp.log2(tot[n])
                lse_ref[h,pl.ds(i,1),:]=lse.T[:1]
        after(it,i)

def attention_rows_backward(heads, after, slopes, mixed_ref, dout_ref, out_ref, lse_ref, grad_ref, qs, ks, km, vp, ds_, delta, bias, steep, dq, dk, dv):
    pairs=heads//2
    blocks=mixed_ref.shape[0]//BLOCK
    lo=low_lanes(BLOCK)
    @pl.loop(0,blocks)
    def _(b):
        rows=pl.ds(pl.multiple_of(b*BLOCK,BLOCK),BLOCK)
        for p in range(pairs):
            t0,t1,t2=(mixed_ref[rows,(3*p+n)*PAIR:(3*p+n+1)*PAIR] for n in range(3))
            zero=jnp.zeros_like(t0)
            qs[p,b,:BLOCK]=jnp.where(lo,t0,zero)
            qs[p,b,BLOCK:]=jnp.where(lo,zero,t1)
            k=jnp.where(lo,swap(t0),swap(t2))
            ks[p,b]=k
            km[p,b,:BLOCK]=jnp.where(lo,k,zero)
            km[p,b,BLOCK:]=jnp.where(lo,zero,k)
            vp[p,b]=jnp.where(lo,t1,t2)
            d=dout_ref[rows,p*PAIR:(p+1)*PAIR]
            ds_[p,b,:BLOCK]=jnp.where(lo,d,zero)
            ds_[p,b,BLOCK:]=jnp.where(lo,zero,d)
            prod=(d.astype(jnp.float32)*out_ref[rows,p*PAIR:(p+1)*PAIR].astype(jnp.float32)).T
            delta[2*p,pl.ds(b,1),:]=jnp.sum(prod[:HALF],0,keepdims=True)
            delta[2*p+1,pl.ds(b,1),:]=jnp.sum(prod[HALF:],0,keepdims=True)
    kl=lax.broadcasted_iota(jnp.int32,(BLOCK,BLOCK),0)
    ql=lax.broadcasted_iota(jnp.int32,(BLOCK,BLOCK),1)
    tent=jnp.minimum(kl,2*ql-kl).astype(jnp.float32)
    ramp=kl.astype(jnp.float32)
    for h in range(heads):
        bias[h]=tent*slopes[h]
        steep[h]=ramp[:,:PAIR]*slopes[h]
    def block(i,j,first):
        for p in range(pairs):
            ps=[];gs=[]
            for n,h in enumerate((2*p,2*p+1)):
                q=qs[p,i,n*BLOCK:(n+1)*BLOCK]
                d=ds_[p,i,n*BLOCK:(n+1)*BLOCK]
                row=slopes[h]*((j-i)*BLOCK).astype(jnp.float32)-lse_ref[h,pl.ds(i,1),:]
                t=nt(ks[p,j],q)*SCALE2+row+(bias[h] if first else jnp.concatenate([steep[h],steep[h]],1))
                e=jnp.exp2(t)
                g=e*(nt(vp[p,j],d)-delta[h,pl.ds(i,1),:])
                ps.append(e.astype(jnp.bfloat16)); gs.append(g.astype(jnp.bfloat16))
            gv=nn(jnp.concatenate(ps,1),ds_[p,i])
            gk=nn(jnp.concatenate(gs,1),qs[p,i])
            gq=tn(jnp.concatenate(gs,0),km[p,j])
            if first:
                dv[p,j]=gv; dk[p,j]=gk; dq[p,i]=gq
            else:
                dv[p,j]+=gv; dk[p,j]+=gk; dq[p,i]+=gq
    @pl.loop(0,blocks)
    def _(i):
        block(i,i,True)
        @pl.loop(0,i)
        def _(j):
            block(i,j,False)
        after(i)
    @pl.loop(0,blocks)
    def _(b):
        rows=pl.ds(pl.multiple_of(b*BLOCK,BLOCK),BLOCK)
        for p in range(pairs):
            a=dq[p,b]*0.125; k=swap(dk[p,b]*0.125); v=dv[p,b]
            for n,t in enumerate((jnp.where(lo,a,k),jnp.where(lo,v,a),jnp.where(lo,k,v))):
                grad_ref[rows,(3*p+n)*PAIR:(3*p+n+1)*PAIR]=t.astype(grad_ref.dtype)


MESH = pl.DeviceIdType.MESH


def hint(index, size):
    return pl.ds(pl.multiple_of(index * size, size), size)


def remote(src, dst, sems, number, target):
    send, recv = sems
    return pltpu.make_async_remote_copy(
        src_ref=src, dst_ref=dst, send_sem=send.at[number], recv_sem=recv.at[number],
        device_id=target, device_id_type=MESH,
    )


def partner(index, bit):
    return index + bit - 2 * bit * ((index // bit) % 2)


class Place:
    def __init__(self):
        self.dp, self.row, self.col = (lax.axis_index(a) for a in ("dp", "row", "col"))
        self.dps = lax.axis_size("dp")
        self.core, self.chip = self.col % 2, self.col // 2
        self.near, self.far = partner(self.col, 1), partner(self.col, 2)
        self.twin = partner(self.dp, 1)
        self.half = self.dp % 2
        self.plane = 3 * self.core + self.chip - 2 * self.core * self.chip
        self.source = 2 * (((self.row + 1) // 2) % 2) + self.row // 2
        self.corner = partner(self.far, 1)
        self.stays = self.plane == self.row
        self.far_plane = 3 * self.core + (1 - self.chip) - 2 * self.core * (1 - self.chip)
        self.sender = 2 * self.chip + self.source % 2
        self.home = jnp.logical_or(self.stays, self.far_plane == self.row)


def greet(place):
    barrier = pltpu.get_barrier_semaphore()

    def signal(target):
        pl.semaphore_signal(barrier, inc=1, device_id=target, device_id_type=MESH)

    for step in (1, 2, 3):
        signal({"row": (place.row + step) % 4})
    for col in (place.near, place.far, place.corner):
        signal({"col": col})
    amount = 6
    bit = 1
    while bit < place.dps:
        signal({"dp": partner(place.dp, bit)})
        amount += 1
        bit *= 2

    for plane, stays in ((place.plane, place.stays), (place.far_plane, place.far_plane == place.row)):
        signal({"row": plane, "col": place.near})

        @pl.when(jnp.logical_not(stays))
        def _():
            signal({"row": plane, "col": place.col})

    for other in range(4):
        @pl.when(jnp.logical_not(jnp.logical_and(place.home, place.row == other)))
        def _():
            signal({"row": other, "col": place.sender})

        @pl.when(jnp.logical_not(jnp.logical_and(place.stays, place.col == other)))
        def _():
            signal({"row": place.plane, "col": other})

        @pl.when(jnp.logical_not(jnp.logical_and(place.stays, place.row == other)))
        def _():
            signal({"row": other, "col": place.source})

    amount = amount + 16 - 2 * place.home.astype(jnp.int32) - 2 * place.stays.astype(jnp.int32)
    pl.semaphore_wait(barrier, amount)


class Transpose:
    def __init__(self, place, src, dst, relay, sems, first, part=0, parts=1):
        self.p, self.src, self.dst, self.relay, self.sems, self.first = place, src, dst, relay, sems, first
        self.quarter, self.width = src.shape[0] // 4, src.shape[1]
        self.rows = self.quarter // parts
        self.offset = part * self.rows

    def tokens(self, quarter):
        return self.src.at[pl.ds(pl.multiple_of(quarter * self.quarter + self.offset, self.rows), self.rows)]

    def part(self):
        return self.dst.at[pl.ds(self.offset, self.rows), hint(self.p.row, self.width)]

    def cross(self, n):
        src = self.tokens(2 * (1 - self.p.chip) + n)
        return remote(src, self.relay.at[n], self.sems, self.first + 4 + n, {"col": self.p.far})

    def out(self, relayed, n):
        p = self.p
        col = p.col if n == 0 else p.near
        src = self.relay.at[col % 2] if relayed else self.tokens(col)
        return pltpu.make_async_remote_copy(
            src_ref=src, dst_ref=self.part(),
            send_sem=self.sems[0].at[self.first + 2 * relayed + n], recv_sem=self.sems[1].at[self.first + p.row],
            device_id={"row": p.far_plane if relayed else p.plane, "col": col}, device_id_type=MESH,
        )

    def kept(self, relayed):
        p = self.p
        src = self.relay.at[p.core] if relayed else self.tokens(p.col)
        return pltpu.make_async_copy(src, self.part(), self.sems[1].at[self.first + p.row])

    def leaves(self, relayed):
        return (self.p.far_plane if relayed else self.p.plane) != self.p.row

    def send(self, relayed):
        self.out(relayed, 1).start()

        @pl.when(self.leaves(relayed))
        def _():
            self.out(relayed, 0).start()

        @pl.when(jnp.logical_not(self.leaves(relayed)))
        def _():
            self.kept(relayed).start()

    def start_cross(self):
        for n in (0, 1):
            self.cross(n).start()

    def forward(self):
        for n in (0, 1):
            self.cross(n).wait_recv()
        self.send(1)

    def wait_recv(self):
        p = self.p
        for other in range(4):
            mine = jnp.logical_and(p.home, p.row == other)
            part = self.dst.at[pl.ds(self.offset, self.rows), pl.ds(other * self.width, self.width)]

            @pl.when(jnp.logical_not(mine))
            def _():
                pltpu.make_async_remote_copy(
                    src_ref=part, dst_ref=part, send_sem=self.sems[0].at[self.first + other],
                    recv_sem=self.sems[1].at[self.first + other],
                    device_id={"row": other, "col": p.sender}, device_id_type=MESH,
                ).wait_recv()

            @pl.when(mine)
            def _():
                self.kept(0).wait()

    def wait_send(self):
        for n in (0, 1):
            self.cross(n).wait_send()
        for relayed in (0, 1):
            self.out(relayed, 1).wait_send()

            @pl.when(self.leaves(relayed))
            def _():
                self.out(relayed, 0).wait_send()


TRANSPOSE_SEMS = 6


class Slopes:
    def __init__(self, heads):
        self.heads = heads
        col = lax.axis_index("col")
        self.column = jnp.float32(1.0)
        for c in range(1, lax.axis_size("col")):
            self.column = jnp.where(col == c, jnp.float32(2.0 ** (-8.0 * heads * c / HEADS)), self.column)

    def __getitem__(self, head):
        return self.column * (2.0 ** (-8.0 * (head + 1) / HEADS) * LOG2E)


class Weight:
    def __init__(self, place, src, dst, offset, by_rows, last, sems, first):
        self.p, self.src, self.dst, self.offset, self.by_rows, self.last = place, src, dst, offset, by_rows, last
        self.sems, self.first = sems, first
        self.rows, self.width = src.shape
        self.part = self.rows // 2

    def whole(self, side, row):
        if self.by_rows:
            return self.dst.at[side, hint(row, self.rows)]
        return self.dst.at[side, pl.ds(self.offset, self.rows), hint(row, self.width)]

    def piece(self, side, row, half):
        if self.by_rows:
            return self.dst.at[side, hint(row * 2 + half, self.part)]
        start = pl.multiple_of(self.offset + half * self.part, self.part)
        return self.dst.at[side, pl.ds(start, self.part), hint(row, self.width)]

    def other(self, step):
        return (self.p.row + 4 - step) % 4

    def move(self, src, dst, number, target):
        return remote(src, dst, self.sems, self.first + number, target)

    def pass_on(self, side, step, half, number, target):
        src = self.piece(side, self.other(step), half)
        dst = self.piece(1 if "col" in target else side, self.other(step), half)
        return self.move(src, dst, number + step - 1, target)

    def own(self):
        return pltpu.make_async_copy(self.src, self.whole(0, self.p.row), self.sems[1].at[self.first])

    def across(self):
        return self.move(self.src, self.whole(1, self.p.row), 1, {"col": self.p.far})

    def along(self, step):
        p = self.p
        return self.move(
            self.src.at[hint(p.half, self.part)], self.piece(0, p.row, p.half), 1 + step, {"row": (p.row + step) % 4}
        )

    def to_twin(self, step):
        return self.pass_on(0, step, self.p.half, 5, {"dp": self.p.twin})

    def to_far(self, step):
        return self.pass_on(0, step, self.p.half, 8, {"col": self.p.far})

    def onward(self, step):
        if self.last == "y":
            return self.pass_on(0, step, 1 - self.p.half, 11, {"col": self.p.far})
        return self.pass_on(1, step, self.p.half, 11, {"dp": self.p.twin})

    def arrival(self, side, step, half, number):
        part = self.piece(side, self.other(step), half)
        return self.move(part, part, number + step - 1, {"dp": self.p.twin})

    def start_along(self):
        for step in (1, 2, 3):
            self.along(step).start()

    def spread(self, steps=(1, 2, 3)):
        for step in steps:
            self.arrival(0, step, self.p.half, 2).wait_recv()
            self.to_twin(step).start()
            self.to_far(step).start()

    def spread_last(self, steps=(1, 2, 3)):
        p = self.p
        for step in steps:
            if self.last == "y":
                self.arrival(0, step, 1 - p.half, 5).wait_recv()
            else:
                self.arrival(1, step, p.half, 8).wait_recv()
            self.onward(step).start()

    def ready(self, side):
        p = self.p
        if side == 0:
            self.own().wait()
        else:
            self.across().wait_recv()
        for step in (1, 2, 3):
            if side == 0 and self.last == "x":
                self.arrival(0, step, 1 - p.half, 5).wait_recv()
            if side == 1 and self.last == "y":
                self.arrival(1, step, p.half, 8).wait_recv()
            if side == 1:
                self.arrival(1, step, 1 - p.half, 11).wait_recv()

    def sent(self):
        self.across().wait_send()
        for step in (1, 2, 3):
            for copy in (self.along(step), self.to_twin(step), self.to_far(step), self.onward(step)):
                copy.wait_send()


WEIGHT_SEMS = 14


class Halves:
    def __init__(self, place, src, dst, sems, first):
        self.p, self.src, self.dst, self.sems, self.first = place, src, dst, sems, first
        self.rows = src.shape[0]
        self.part = self.rows // 2

    def own(self):
        return pltpu.make_async_copy(self.src, self.dst.at[hint(self.p.row, self.rows)], self.sems[1].at[self.first])

    def along(self, step):
        p = self.p
        return remote(
            self.src.at[hint(p.half, self.part)], self.dst.at[hint(2 * p.row + p.half, self.part)], self.sems,
            self.first + step, {"row": (p.row + step) % 4},
        )

    def part_of(self, step, half):
        return self.dst.at[hint(2 * ((self.p.row + 4 - step) % 4) + half, self.part)]

    def to_twin(self, step, half):
        part = self.part_of(step, half)
        return remote(part, part, self.sems, self.first + 3 + step, {"dp": self.p.twin})

    def start(self):
        self.own().start()
        for step in (1, 2, 3):
            self.along(step).start()

    def spread(self):
        p = self.p
        for step in (1, 2, 3):
            part = self.part_of(step, p.half)
            remote(part, part, self.sems, self.first + step, {"dp": p.twin}).wait_recv()
            self.to_twin(step, p.half).start()

    def ready(self):
        p = self.p
        for step in (1, 2, 3):
            self.to_twin(step, 1 - p.half).wait_recv()
        self.own().wait()

    def sent(self):
        for step in (1, 2, 3):
            self.along(step).wait_send()
            self.to_twin(step, self.p.half).wait_send()


HALVES_SEMS = 7


GELU_ROOT = math.sqrt(2.0 / math.pi)
GELU_CUBE = 0.044715


def gelu_pair(x):
    square = x * x
    t = jnp.tanh(GELU_ROOT * x * (1.0 + GELU_CUBE * square))
    half = 0.5 * (1.0 + t)
    slope = half + 0.5 * x * (1.0 - t * t) * (GELU_ROOT * (1.0 + 3.0 * GELU_CUBE * square))
    return x * half, slope


def moments(x):
    center = jnp.mean(x, 1, keepdims=True)
    spread = jnp.mean(x * x, 1, keepdims=True) - center * center
    inverse = lax.rsqrt(spread + EPSILON)
    return (x - center) * inverse, inverse


class Chip:
    def __init__(self, place, sems, first):
        self.p, self.sems, self.first = place, sems, first

    def copy(self, number, src, dst):
        return remote(src, dst, self.sems, self.first + number, {"col": self.p.near})


class Untranspose:
    def __init__(self, place, src, dst, sems, first):
        self.place, self.src, self.dst, self.sems, self.first = place, src, dst, sems, first
        self.rows, self.width = src.shape[0], src.shape[1] // 4

    def out(self, other):
        p = self.place
        return pltpu.make_async_remote_copy(
            src_ref=self.src.at[:, pl.ds(other * self.width, self.width)],
            dst_ref=self.dst.at[hint(p.col, self.rows)],
            send_sem=self.sems[0].at[self.first + other], recv_sem=self.sems[1].at[self.first + p.col],
            device_id={"row": other, "col": p.source}, device_id_type=MESH,
        )

    def kept(self):
        p = self.place
        return pltpu.make_async_copy(
            self.src.at[:, hint(p.row, self.width)],
            self.dst.at[hint(p.col, self.rows)],
            self.sems[1].at[self.first + p.col],
        )

    def start(self):
        p = self.place
        for other in range(4):
            @pl.when(jnp.logical_not(jnp.logical_and(p.stays, p.row == other)))
            def _():
                self.out(other).start()

        @pl.when(p.stays)
        def _():
            self.kept().start()

    def wait_recv(self):
        p = self.place
        for other in range(4):
            mine = jnp.logical_and(p.stays, p.col == other)
            part = self.dst.at[pl.ds(other * self.rows, self.rows)]

            @pl.when(jnp.logical_not(mine))
            def _():
                pltpu.make_async_remote_copy(
                    src_ref=part, dst_ref=part, send_sem=self.sems[0].at[self.first + other],
                    recv_sem=self.sems[1].at[self.first + other],
                    device_id={"row": p.plane, "col": other}, device_id_type=MESH,
                ).wait_recv()

            @pl.when(mine)
            def _():
                self.kept().wait()

    def wait_send(self):
        p = self.place
        for other in range(4):
            @pl.when(jnp.logical_not(jnp.logical_and(p.stays, p.row == other)))
            def _():
                self.out(other).wait_send()


def add_rows(total, pieces, rows=64):
    @pl.loop(0, total.shape[0] // rows)
    def _(n):
        part = hint(n, rows)
        value = pieces[0][part, :].astype(jnp.float32)
        for piece in pieces[1:]:
            value = value + piece[part, :].astype(jnp.float32)
        total[part, :] = value.astype(total.dtype)


class Share:
    def __init__(self, place, kind, own, far, result, came, other, rows, totals, slots, sems, first):
        self.p, self.kind, self.own, self.far, self.result = place, kind, own, far, result
        self.came, self.other_ref, self.rows, self.totals, self.slots = came, other, rows, totals, slots
        self.sems, self.first = sems, first
        self.width = own.shape[1]
        self.part = self.width // 2
        self.block = own.shape[0] // 4
        self.mine, self.theirs = hint(place.half, self.part), hint(1 - place.half, self.part)

    def first_copies(self):
        p = self.p
        if self.kind == "xy":
            return [
                remote(src.at[:, self.theirs], self.came[n], self.sems, self.first + n, {"dp": p.twin})
                for n, src in enumerate((self.own, self.far))
            ]
        if self.kind == "yx":
            return [remote(self.far, self.came, self.sems, self.first, {"col": p.far})]
        return [remote(self.own.at[:, self.theirs], self.came, self.sems, self.first, {"dp": p.twin})]

    def start(self):
        for copy in self.first_copies():
            copy.start()

    def gather_sum(self, jobs):
        blocks = []
        for total, sources in jobs:
            for n in range(4):
                part = pl.ds(n * self.block, self.block)
                blocks.append((total.at[part], [src.at[part] for src in sources]))
        self.block_sums(blocks)

    def block_sums(self, blocks):
        copies = []
        for n, (_, sources) in enumerate(blocks):
            copies.append([
                pltpu.make_async_copy(
                    src, self.slots[2 * (n % 2) + m].at[:, : src.shape[1]],
                    self.sems[1].at[self.first + 8 + 2 * (n % 2) + m],
                )
                for m, src in enumerate(sources)
            ])
        for copy in copies[0]:
            copy.start()
        for n, (total, sources) in enumerate(blocks):
            if n + 1 < len(blocks):
                for copy in copies[n + 1]:
                    copy.start()
            for copy in copies[n]:
                copy.wait()
            add_rows(total, [self.slots[2 * (n % 2) + m].at[:, : total.shape[1]] for m in range(len(sources))])

    def second_copy(self):
        p = self.p
        if self.kind == "xy":
            return remote(self.totals[1], self.other_ref, self.sems, self.first + 2, {"col": p.far})
        return remote(self.totals[0].at[:, self.theirs], self.other_ref, self.sems, self.first + 2, {"dp": p.twin})

    def first_sum(self):
        for copy in self.first_copies():
            copy.wait()
        if self.kind == "xy":
            self.gather_sum([
                (self.totals[1], [self.came[1], self.far.at[:, self.mine]]),
                (self.totals[0], [self.came[0], self.own.at[:, self.mine]]),
            ])
        elif self.kind == "yx":
            self.gather_sum([(self.totals[0], [self.came, self.own])])
        else:
            self.gather_sum([(self.totals[0], [self.came, self.own.at[:, self.mine]])])

    def total(self):
        return self.totals[1] if self.kind == "yx" else self.totals[0]

    def second_sum(self):
        self.second_copy().wait()
        if self.kind == "xy":
            self.gather_sum([(self.totals[0], [self.other_ref, self.totals[0]])])
        else:
            self.gather_sum([(self.totals[1], [self.other_ref, self.totals[0].at[:, self.mine]])])

    def row_copy(self, step):
        row = self.p.row
        target = partner(row, 1) if step < 2 else partner(row, 2)
        block = partner(target, 2) if step == 1 else target
        return remote(
            self.total().at[hint(block, self.block)], self.rows.at[step], self.sems, self.first + 3 + step, {"row": target}
        )

    def start_rows(self):
        for step in (1, 0):
            self.row_copy(step).start()

    def row_add(self, block, step, target):
        load = pltpu.make_async_copy(
            self.rows.at[step], self.slots[step].at[:, : self.part], self.sems[1].at[self.first + 8 + step]
        )
        load.start()
        load.wait()
        add_rows(target, [self.total().at[hint(block, self.block)], self.slots[step].at[:, : self.part]])

    def row_half(self):
        other = partner(self.p.row, 2)
        self.row_copy(1).wait()
        self.row_add(other, 1, self.total().at[hint(other, self.block)])
        self.row_copy(2).start()
        self.row_copy(0).wait()
        self.row_add(self.p.row, 0, self.total().at[hint(self.p.row, self.block)])

    def last_copy(self, half):
        part = self.result.at[:, hint(half, self.part)]
        return remote(part, part, self.sems, self.first + 6, {"dp": self.p.twin})

    def row_sum(self):
        self.row_copy(2).wait()
        self.row_add(self.p.row, 2, self.result.at[:, self.mine])
        self.last_copy(self.p.half).start()

    def finish(self):
        self.last_copy(self.p.half).wait_send()
        self.last_copy(1 - self.p.half).wait_recv()


SHARE_SEMS = 12


class RowsFirst(Share):
    def __init__(self, place, own, far, result, from_next, from_other, from_far, from_twin, total, slots, sems, first):
        super().__init__(place, "zyx", own, far, result, None, None, None, None, slots, sems, first)
        self.from_next, self.from_other, self.from_far, self.from_twin = from_next, from_other, from_far, from_twin
        self.parts = [[total.at[pl.ds((2 * side + n) * self.block, self.block)] for n in (0, 1)] for side in (0, 1)]

    def next_copies(self):
        target = partner(self.p.row, 1)
        rows = (target, partner(target, 2))
        return [
            remote(
                source.at[hint(rows[n], self.block)], self.from_next.at[2 * side + n], self.sems,
                self.first + 2 * side + n, {"row": target},
            )
            for side, source in enumerate((self.own, self.far))
            for n in (0, 1)
        ]

    def start(self):
        for copy in self.next_copies():
            copy.start()

    def other_copies(self):
        return [
            remote(
                self.parts[side][1], self.from_other.at[side], self.sems, self.first + 4 + side,
                {"row": partner(self.p.row, 2)},
            )
            for side in (0, 1)
        ]

    def row_half(self):
        for copy in self.next_copies():
            copy.wait()
        rows = (self.p.row, partner(self.p.row, 2))
        for n in (1, 0):
            self.block_sums([
                (self.parts[side][n], [source.at[hint(rows[n], self.block)], self.from_next.at[2 * side + n]])
                for side, source in enumerate((self.own, self.far))
            ])
            if n == 1:
                for copy in self.other_copies():
                    copy.start()

    def far_copy(self):
        return remote(self.parts[1][0], self.from_far, self.sems, self.first + 6, {"col": self.p.far})

    def row_sum(self):
        for copy in self.other_copies():
            copy.wait()
        self.block_sums([(self.parts[side][0], [self.parts[side][0], self.from_other.at[side]]) for side in (1, 0)])
        self.far_copy().start()

    def twin_copy(self):
        return remote(self.parts[0][0].at[:, self.theirs], self.from_twin, self.sems, self.first + 7, {"dp": self.p.twin})

    def far_sum(self):
        self.far_copy().wait()
        self.block_sums([(self.parts[0][0], [self.parts[0][0], self.from_far])])
        self.twin_copy().start()

    def last_copy(self, half):
        part = self.result.at[:, hint(half, self.part)]
        return remote(part, part, self.sems, self.first + 12, {"dp": self.p.twin})

    def twin_sum(self):
        self.twin_copy().wait()
        self.block_sums([(self.result.at[:, self.mine], [self.parts[0][0].at[:, self.mine], self.from_twin])])
        self.last_copy(self.p.half).start()


ROWS_FIRST_SEMS = 13


class Tally:
    def __init__(self, place, slots, axes, sems, first):
        self.slots = slots
        p = place
        peers = dict(
            row=[{"row": (p.row + step) % 4} for step in (1, 2, 3)],
            col=[{"col": p.near}, {"col": p.far}, {"col": p.corner}],
        )
        bit = 1
        while bit < p.dps:
            peers["dp%d" % bit] = [{"dp": partner(p.dp, bit)}]
            bit *= 2
        names = []
        for axis in axes:
            names += [name for name in peers if name.startswith(axis)]
        self.stages, at = [], 0
        for name in names:
            copies = [
                remote(slots.at[at], slots.at[at + 1 + n], sems, first + n, target)
                for n, target in enumerate(peers[name])
            ]
            self.stages.append((at, copies))
            at += len(copies) + 1
            first += len(copies)
        self.names, self.last, self.next_sem = names, at, first

    def send(self, n):
        for copy in self.stages[n][1]:
            copy.start()

    def add(self, n):
        at, copies = self.stages[n]
        value = self.slots[at]
        for m, copy in enumerate(copies):
            copy.wait()
            value = value + self.slots[at + 1 + m]
        self.slots[at + len(copies) + 1] = value

    def after(self, n):
        at, copies = self.stages[n]
        return at + len(copies) + 1


def tally_slots(bits, axes):
    return sum({"row": 4, "col": 4, "dp": 2 * bits}[axis] for axis in axes) + 1


def layer_kernel(
    heads, token_total,
    small_ref, joined_ref, layer_ref, up_ref, down_ref, out_ref, teacher_ref, cot_ref,
    layer_out_ref, input_grad_ref, upg_ref, dng_ref, outg_ref, joinedg_ref, vector_sum_ref,
    upg_own, upg_far, dng_own, dng_far, came_up, came_down, came_out, came_joined, other_up, other_down, other_out,
    rows_up, rows_down, rows_out, rows_joined, from_next, from_other, from_far, from_twin,
    xt_ref, nall_ref, mixed_ref, att_ref, lse_ref, jall_ref, vall_ref, early_ref, up_sums_ref,
    chip_ref, gt_ref, vt_ref, up2_ref, dn2_ref, ub2_ref, normed, gchip, bchip, give, take, middle, gres, low_ref, stage,
    grad, gfar, dout, relay, vectors, late, count, valid_ref, bias_ref, sync, sends, recvs,
):
    sems = (sends, recvs)
    f32, bf = jnp.float32, jnp.bfloat16
    p = Place()
    quarter, features = xt_ref.shape
    hidden = down_ref.shape[0]
    moved = [
        Transpose(p, layer_ref, xt_ref, relay.at[0, :, pl.ds(256 * n, 256)], sems, n * TRANSPOSE_SEMS, n, 2) for n in (0, 1)
    ]
    target = Transpose(p, grad, gt_ref, relay.at[1], sems, 2 * TRANSPOSE_SEMS)
    base = 3 * TRANSPOSE_SEMS
    back = Untranspose(p, low_ref, layer_out_ref, sems, base)
    base += 4
    w_out = Weight(p, out_ref, dn2_ref, hidden, False, "y", sems, base)
    w_up = Weight(p, up_ref, up2_ref, 0, True, "x", sems, base + WEIGHT_SEMS)
    w_downs = [
        Weight(
            p, down_ref.at[pl.ds(n * (hidden // 2), hidden // 2)], dn2_ref, n * (hidden // 2), False, "xy"[n], sems,
            base + (2 + n) * WEIGHT_SEMS,
        )
        for n in (0, 1)
    ]
    weights = [w_out, w_up] + w_downs
    base += 4 * WEIGHT_SEMS
    w_joined = Halves(p, joined_ref, jall_ref, sems, base)
    base += HALVES_SEMS
    small_base, bias_base = base, base + 4
    base += 6

    def small(step):
        part = vall_ref.at[:, hint(p.row, 256)]
        return remote(part, part, sems, small_base + step, {"row": (p.row + step) % 4})

    def small_came(step):
        part = vall_ref.at[:, hint((p.row + 4 - step) % 4, 256)]
        return remote(part, part, sems, small_base + step, {"row": (p.row + step) % 4})

    bias_far = remote(ub2_ref.at[0], ub2_ref.at[1], sems, bias_base + 1, {"col": p.far})
    counted = Tally(p, count, ("col", "dp"), sems, base)
    base = counted.next_sem
    tokens = nall_ref.shape[0]
    greet(p)
    for half in moved:
        half.start_cross()
    moved[0].send(0)
    width = layer_ref.shape[1]
    lanes = width // 128
    for n in range(6):
        for m in range(lanes):
            place = pl.ds(pl.multiple_of(p.row * width + m * 128, 128), 128)
            vall_ref[n : n + 1, place] = small_ref[lanes * n + m : lanes * n + m + 1, :]
    vall_ref[6:8, hint(p.row, width)] = jnp.zeros((2, width), f32)
    at = 6 * lanes
    for n in range(hidden // 128):
        ub2_ref[0, :, n * 128 : (n + 1) * 128] = jnp.broadcast_to(small_ref[at + n : at + n + 1, :], (8, 128))
    at += hidden // 128
    lo = low_lanes(1)
    for n in range(heads // 2):
        even, odd = (small_ref[at + 2 * n + m : at + 2 * n + m + 1, :] for m in (0, 1))
        for m, part in enumerate(
            (jnp.where(lo, even, 0.0), jnp.where(lo, swap(even), swap(odd)), jnp.where(lo, 0.0, odd))
        ):
            bias_ref[0:1, (3 * n + m) * 128 : (3 * n + m + 1) * 128] = part
    at += heads
    number = jnp.zeros((1, 128), f32)
    for n in range(tokens // 128):
        row = small_ref[at + n : at + n + 1, :]
        number = number + row
        valid_ref[n * 128 : (n + 1) * 128, :] = jnp.broadcast_to(row, (128, 128)).T.astype(bf)
    count[0] = jnp.broadcast_to(jnp.sum(number, axis=1, keepdims=True), (8, 128))
    counted.send(0)
    for step in (1, 2, 3):
        small(step).start()
    bias_far.start()
    w_out.across().start()
    w_up.across().start()
    for w in weights:
        w.own().start()
    moved[0].forward()
    moved[1].send(0)
    moved[1].forward()
    for n in range(len(counted.stages)):
        counted.add(n)
        if n + 1 < len(counted.stages):
            counted.send(n + 1)

    scale = token_total / count[counted.last, :1, :1]

    @pl.loop(0, 32)
    def _(n):
        rows = hint(n, grad.shape[0] // 32)
        factor = valid_ref[rows, :].astype(f32) * scale
        for f in range(grad.shape[1] // 128):
            cols = slice(f * 128, (f + 1) * 128)
            grad[rows, cols] = (
                cot_ref[rows, cols].astype(f32) - factor * teacher_ref[rows, cols].astype(f32)
            ).astype(bf)

    valid_base = base
    base += 1

    def valid_out():
        return pltpu.make_async_remote_copy(
            src_ref=valid_ref.at[hint(p.row, quarter)], dst_ref=vt_ref,
            send_sem=sends.at[valid_base], recv_sem=recvs.at[valid_base],
            device_id={"row": p.plane, "col": p.row}, device_id_type=MESH,
        )

    same = jnp.logical_and(p.stays, p.col == p.row)
    valid_kept = pltpu.make_async_copy(valid_ref.at[hint(p.row, quarter)], vt_ref, recvs.at[valid_base])

    for step in (1, 2, 3):
        small_came(step).wait_recv()
        small(step).wait_send()
    first = p.col * quarter

    def norm_one(n):
        rows = hint(n, 128)
        standard, _ = moments(xt_ref[rows, :].astype(f32))
        place = pl.ds(pl.multiple_of(first + n * 128, 128), 128)
        nall_ref[place, :] = (standard * vall_ref[0:1, :] + vall_ref[1:2, :]).astype(bf)

    def half_of(col, n):
        return nall_ref.at[pl.ds(pl.multiple_of(col * quarter + n * 256, 256), 256)]

    def spread_copy(col, n, number, to):
        return remote(half_of(col, n), half_of(col, n), sems, gather_base + 2 * number + n, {"col": to})

    gather_base = base
    base += 6
    to_far = [spread_copy(p.col, n, 0, p.far) for n in (0, 1)]
    to_near = [spread_copy(p.col, n, 1, p.near) for n in (0, 1)]
    far_came = [spread_copy(p.far, n, 0, p.far) for n in (0, 1)]
    near_came = [spread_copy(p.near, n, 1, p.near) for n in (0, 1)]
    pass_on = [spread_copy(p.far, n, 2, p.near) for n in (0, 1)]
    corner_came = [spread_copy(p.corner, n, 2, p.near) for n in (0, 1)]
    for n in (0, 1):
        moved[n].wait_recv()
        pl.loop(2 * n, 2 * n + 2)(norm_one)
        to_far[n].start()
        to_near[n].start()
    for step in (1, 2, 3):
        pl.semaphore_signal(sync, inc=1, device_id={"row": (p.row + step) % 4}, device_id_type=MESH)
    pl.semaphore_wait(sync, 3)
    w_joined.start()
    target.start_cross()
    for w in w_downs:
        w.across().start()

    @pl.when(jnp.logical_not(same))
    def _():
        valid_out().start()

    @pl.when(same)
    def _():
        valid_kept.start()

    def project(index, n):
        rows = pl.ds(pl.multiple_of(index * quarter + n * 256, 256), 256)
        mixed_ref[rows, :] = (nn(nall_ref[rows, :], jall_ref[...]) + bias_ref[0:1, :]).astype(bf)

    far_came[0].wait_recv()
    pass_on[0].start()
    w_joined.spread()
    for w in weights:
        w.start_along()
    far_came[1].wait_recv()
    pass_on[1].start()
    w_joined.ready()
    for came in near_came + corner_came:
        came.wait_recv()

    @pl.loop(0, tokens // 256)
    def _(n):
        project(n // 2, n % 2)

    w_out.spread()

    own_heads = att_ref.shape[1]
    blocks = tokens // BLOCK
    per_chip = blocks // 2
    share_base = base
    base += per_chip

    def chip_place(n):
        half = per_chip // 2
        return ((n // half + p.core) % 2) * half + n % half

    def share(n, i):
        return pltpu.make_async_remote_copy(
            src_ref=att_ref.at[hint(i, BLOCK)], dst_ref=chip_ref.at[hint(chip_place(n), BLOCK), pl.ds(own_heads, own_heads)],
            send_sem=sends.at[share_base + n], recv_sem=recvs.at[share_base + n],
            device_id={"col": p.far}, device_id_type=MESH,
        )

    def after(it, i):
        @pl.when(it < per_chip)
        def _():
            share(it, i).start()

        @pl.when(it >= per_chip)
        def _():
            chip_ref[hint(chip_place(it - per_chip), BLOCK), :own_heads] = att_ref[hint(i, BLOCK), :]

        for units, action in plan:
            @pl.when(it == at_units(units))
            def _():
                action()

    order = (
        [per_chip + n + 1 for n in range(per_chip)] + [n + 1 for n in range(per_chip)],
        [n + 1 for n in range(blocks)],
    )

    def at_units(units):
        found = []
        for counts in order:
            total, it = 0, 0
            for it, n in enumerate(counts):
                total += n
                if total >= units:
                    break
            found.append(it)
        return found[0] * (1 - p.chip) + found[1] * p.chip

    plan = [
        (3, lambda: w_out.spread_last()),
        (6, lambda: w_up.spread((1,))),
        (11, lambda: w_up.spread((2,))),
        (18, lambda: w_up.spread((3,))),
        (27, lambda: w_up.spread_last((1, 2))),
        (29, lambda: (target.send(0), target.forward())),
        (32, lambda: w_downs[0].spread((1, 2))),
    ]

    def attend(*scratch):
        attention_rows(
            heads, lambda it: (it + per_chip * (1 - p.chip)) % blocks, after,
            Slopes(heads), mixed_ref, att_ref, lse_ref, *scratch,
        )

    pairs = heads // 2
    pl.run_scoped(
        attend,
        pltpu.VMEM((heads, blocks, BLOCK, PAIR), bf), pltpu.VMEM((pairs, blocks, BLOCK, PAIR), bf),
        pltpu.VMEM((pairs, blocks, 2 * BLOCK, PAIR), bf), pltpu.VMEM((heads, BLOCK, BLOCK), f32),
        pltpu.VMEM((heads, blocks, BLOCK, BLOCK), f32), pltpu.VMEM((heads, BLOCK, PAIR), f32),
        pltpu.VMEM((heads, BLOCK, PAIR), f32), pltpu.VMEM((pairs, BLOCK, PAIR), f32),
    )

    @pl.loop(0, per_chip)
    def _(n):
        share(n, n + per_chip * (1 - p.chip)).wait_recv()

    w_up.spread_last((3,))
    w_downs[0].spread((3,))
    w_out.ready(0)
    w_out.ready(1)
    core = Chip(p, sems, base)
    base += 12
    ROWS = 256
    halves = quarter // ROWS

    def swap_rows(number, buffer, n):
        return core.copy(
            number + n, buffer.at[pl.ds(n * ROWS, ROWS)], buffer.at[pl.ds(quarter + n * ROWS, ROWS)]
        )

    def swap_came(number, buffer, n):
        part = buffer.at[pl.ds(quarter + n * ROWS, ROWS)]
        return core.copy(number + n, part, part)

    def give_rows(number, n):
        return core.copy(number + n, give.at[pl.ds(n * ROWS, ROWS)], take.at[pl.ds(n * ROWS, ROWS)])

    def take_rows(number, n):
        part = take.at[pl.ds(n * ROWS, ROWS)]
        return core.copy(number + n, part, part)

    def partial(number, keep, product, again):
        if again:
            for n in range(halves):
                give_rows(number - 4, n).wait_send()
        for n in range(halves):
            give[n * ROWS : (n + 1) * ROWS, :] = product(pl.ds(quarter + n * ROWS, ROWS)).astype(bf)
            give_rows(number, n).start()
        for n in range(halves):
            keep[n * ROWS : (n + 1) * ROWS, :] = product(pl.ds(n * ROWS, ROWS))

    partial(
        0, middle,
        lambda rows: nn(chip_ref[rows, :own_heads], dn2_ref[0, hidden:, :])
        + nn(chip_ref[rows, own_heads:], dn2_ref[1, hidden:, :]),
        False,
    )
    w_downs[1].spread()
    for n in range(halves):
        take_rows(0, n).wait_recv()

        @pl.loop(0, ROWS // 64)
        def _(m):
            rows = pl.ds(pl.multiple_of(n * ROWS + m * 64, 64), 64)
            value = xt_ref[rows, :].astype(f32) + (
                middle[rows, :] + take[rows, :].astype(f32) + vall_ref[2:3, :]
            )
            middle[rows, :] = value
            standard, _ = moments(value)
            normed[rows, :] = (standard * vall_ref[3:4, :] + vall_ref[4:5, :]).astype(bf)

        swap_rows(2, normed, n).start()
    w_up.ready(0)
    bias_far.wait()

    slots = [give.at[pl.ds(256 * (n // 2), 256), pl.ds(hidden // 2 * (n % 2), hidden // 2)] for n in range(4)]
    outg_own, outg_far = (dn2_ref.at[0, :features, pl.ds(own_heads * n, own_heads)] for n in (0, 1))
    jgrad = dn2_ref.at[1, :features, : mixed_ref.shape[1]]
    low_part, high_part = pl.ds(0, hidden // 2), pl.ds(hidden // 2, hidden // 2)

    def both(ref, n):
        return [ref.at[n, :, pl.ds(hidden // 4 * m, hidden // 4)] for m in (0, 1)]

    s_down = Share(
        p, "xy", dng_own.at[:, low_part], dng_far.at[:, low_part], dng_ref.at[:, low_part], both(came_down, 0), other_down,
        rows_down, both(up2_ref, 1), slots, sems, base,
    )
    s_up = Share(
        p, "xy", upg_own.at[:, low_part], upg_far.at[:, low_part], upg_ref.at[:, low_part], both(came_up, 0), other_up,
        rows_up, both(up2_ref, 0), slots, sems, base + SHARE_SEMS,
    )
    z_down = RowsFirst(
        p, dng_own.at[:, high_part], dng_far.at[:, high_part], dng_ref.at[:, high_part], from_next.at[0], from_other.at[0],
        from_far.at[0], from_twin.at[0], up2_ref.at[1, :, high_part], slots, sems, base + 4 * SHARE_SEMS,
    )
    z_up = RowsFirst(
        p, upg_own.at[:, high_part], upg_far.at[:, high_part], upg_ref.at[:, high_part], from_next.at[1], from_other.at[1],
        from_far.at[1], from_twin.at[1], chip_ref, slots, sems, base + 4 * SHARE_SEMS + ROWS_FIRST_SEMS,
    )
    s_out = Share(
        p, "yx", outg_own, outg_far, outg_ref, came_out, other_out, rows_out,
        [dn2_ref.at[1, :features, pl.ds(768, 256)], dn2_ref.at[0, :features, pl.ds(896, 128)]], slots, sems,
        base + 2 * SHARE_SEMS,
    )
    s_joined = Share(
        p, "x", jgrad, None, joinedg_ref, came_joined, None, rows_joined,
        [dn2_ref.at[0, :features, pl.ds(512, 384)]], slots, sems, base + 3 * SHARE_SEMS,
    )
    base += 4 * SHARE_SEMS + 2 * ROWS_FIRST_SEMS

    def natural(chip, n):
        return hint(2 * chip + (p.core + n) % 2, quarter)

    att_base = base
    base += 2

    def share_grad(n):
        return remote(
            gfar.at[pl.ds(n * quarter, quarter)], dout.at[natural(p.chip, n)], sems, att_base + n, {"col": p.far}
        )

    def share_grad_came(n):
        part = dout.at[natural(1 - p.chip, n)]
        return remote(part, part, sems, att_base + n, {"col": p.far})

    stage_base = base
    base += 2

    def middle_part(act, der, keep):
        wide = 256

        def up_rows(side):
            def body(n):
                rows = pl.ds(pl.multiple_of(n * ROWS, ROWS), ROWS)

                @pl.loop(0, hidden // wide, unroll=2)
                def _(m):
                    cols = hint(m, wide)
                    before = nn(normed[rows, :], up2_ref[side, :, cols]) + ub2_ref[side, 0:1, cols]
                    value, slope = gelu_pair(before)
                    act[side, rows, cols] = value.astype(bf)
                    der[side, rows, cols] = slope.astype(bf)

            return body

        pl.loop(0, halves)(up_rows(0))
        for n in range(halves):
            swap_came(2, normed, n).wait_recv()
        pl.loop(halves, 2 * halves)(up_rows(0))
        w_up.ready(1)
        pl.loop(0, halves)(up_rows(1))
        w_downs[0].spread_last()
        pl.loop(halves, 2 * halves)(up_rows(1))
        w_downs[1].spread_last()
        for w in w_downs:
            w.ready(0)
            w.ready(1)
        partial(
            4, gres,
            lambda rows: nn(act[0, rows, :], dn2_ref[0, :hidden, :]) + nn(act[1, rows, :], dn2_ref[1, :hidden, :]),
            True,
        )
        target.wait_recv()

        @pl.when(jnp.logical_not(same))
        def _():
            valid_out().wait_send()
            valid_out().wait_recv()

        @pl.when(same)
        def _():
            valid_kept.wait()

        early_ref[...] = jnp.zeros_like(early_ref)
        for n in range(halves):
            take_rows(4, n).wait_recv()

            @pl.loop(0, ROWS // 64)
            def _(m):
                rows = pl.ds(pl.multiple_of(n * ROWS + m * 64, 64), 64)
                result = middle[rows, :] + (gres[rows, :] + take[rows, :].astype(f32) + vall_ref[5:6, :])
                low_ref[rows, :] = result.astype(bf)
                factor = vt_ref[rows, :].astype(f32)[:, :1] * scale
                value = gt_ref[rows, :].astype(f32) + factor * result
                gres[rows, :] = value
                rounded = value.astype(bf)
                gchip[rows, :] = rounded
                early_ref[5:6, :] += jnp.sum(rounded.astype(f32), axis=0, keepdims=True)

            swap_rows(6, gchip, n).start()
        back.start()
        up_sums_ref[...] = jnp.zeros_like(up_sums_ref)

        def before_rows(n):
            rows = pl.ds(pl.multiple_of(n * ROWS, ROWS), ROWS)

            @pl.loop(0, 2 * hidden // wide, unroll=2)
            def _(m):
                side, cols = m // (hidden // wide), hint(m % (hidden // wide), wide)
                value = nt(gchip[rows, :], dn2_ref[side, cols, :]) * der[side, rows, cols].astype(f32)
                rounded = value.astype(bf)
                der[side, rows, cols] = rounded
                up_sums_ref[side, 0:1, cols] += jnp.sum(rounded.astype(f32), axis=0, keepdims=True)

        def weight_grad(slot, source, values, sinks):
            @pl.loop(0, features // 256)
            def _(f):
                cols = hint(f, 256)
                turned = source[:, cols].T
                for side, sink in enumerate(sinks):
                    copy = pltpu.make_async_copy(stage.at[side], sink.at[cols], recvs.at[slot + side])

                    @pl.when(f > 0)
                    def _():
                        copy.wait()

                    stage[side] = nn(turned, values[side]).astype(bf)
                    copy.start()

            for side, sink in enumerate(sinks):
                pltpu.make_async_copy(stage.at[side], sink.at[pl.ds(0, 256)], recvs.at[slot + side]).wait()

        pl.loop(0, halves)(before_rows)
        for n in range(halves):
            swap_came(6, gchip, n).wait_recv()
        weight_grad(stage_base, gchip, act, (dng_own, dng_far))
        s_down.start()
        z_down.start()
        pl.loop(halves, 2 * halves)(before_rows)
        partial(
            8, keep, lambda rows: nt(der[0, rows, :], up2_ref[0]) + nt(der[1, rows, :], up2_ref[1]), True
        )

        for n in range(halves):
            for number, buffer in ((2, normed), (6, gchip)):
                swap_rows(number, buffer, n).wait_send()
        for n in range(halves):
            take_rows(8, n).wait_recv()

            @pl.loop(0, ROWS // 64)
            def _(m):
                rows = pl.ds(pl.multiple_of(n * ROWS + m * 64, 64), 64)
                value = keep[rows, :] + take[rows, :].astype(f32)
                standard, inverse = moments(middle[rows, :])
                early_ref[3:4, :] += jnp.sum(value * standard, axis=0, keepdims=True)
                early_ref[4:5, :] += jnp.sum(value, axis=0, keepdims=True)
                scaled = value * vall_ref[3:4, :]
                one = jnp.mean(scaled, 1, keepdims=True)
                two = jnp.mean(scaled * standard, 1, keepdims=True)
                value = gres[rows, :] + inverse * (scaled - one - standard * two)
                gres[rows, :] = value
                rounded = value.astype(bf)
                bchip[rows, :] = rounded
                early_ref[2:3, :] += jnp.sum(rounded.astype(f32), axis=0, keepdims=True)

            swap_rows(10, bchip, n).start()
        for n in range(2 * halves):
            if n >= halves:
                swap_came(10, bchip, n - halves).wait_recv()
            rows = pl.ds(n * ROWS, ROWS)
            place = pl.ds(
                pl.multiple_of((2 * p.chip + (p.core + n // halves) % 2) * quarter + n % halves * ROWS, ROWS), ROWS
            )
            dout[place, :] = nt(bchip[rows, :], dn2_ref[0, hidden:, :]).astype(bf)
            gfar[rows, :] = nt(bchip[rows, :], dn2_ref[1, hidden:, :]).astype(bf)
            if n % halves == halves - 1:
                share_grad(n // halves).start()
        weight_grad(stage_base, normed, der, (upg_own, upg_far))
        s_up.start()
        z_up.start()

    pl.run_scoped(
        middle_part,
        pltpu.VMEM((2, 2 * quarter, hidden), bf), pltpu.VMEM((2, 2 * quarter, hidden), bf), pltpu.VMEM((quarter, features), f32),
    )

    for w in weights:
        w.sent()

    @pl.loop(0, features // 256)
    def _(f):
        cols = hint(f, 256)
        turned = bchip[:, cols].T
        outg_own[cols, :] = nn(turned, chip_ref[:, :own_heads]).astype(bf)
        outg_far[cols, :] = nn(turned, chip_ref[:, own_heads:]).astype(bf)

    for n in range(halves):
        give_rows(8, n).wait_send()
        swap_rows(10, bchip, n).wait_send()
    back.wait_recv()
    target.wait_send()
    fetch = pltpu.make_async_copy(layer_out_ref, grad, recvs.at[stage_base])
    fetch.start()
    fetch.wait()
    error = jnp.zeros((1, 128), f32)
    for n in range(tokens // 128):
        rows = slice(n * 128, (n + 1) * 128)
        for f in range(grad.shape[1] // 128):
            cols = slice(f * 128, (f + 1) * 128)
            off = grad[rows, cols].astype(f32) - teacher_ref[rows, cols].astype(f32)
            error = error + jnp.sum(off * off * valid_ref[rows, :].astype(f32), axis=0, keepdims=True)
    early_ref[6:7, 0:128] = error
    vectors[0, 0:8, :] = early_ref[...]
    vectors[0, 8:16, :] = jnp.zeros((8, features), f32)
    vectors[0, pl.ds(8 + p.col, 1), :] = up_sums_ref[0]
    vectors[0, pl.ds(8 + p.far, 1), :] = up_sums_ref[1]
    summed = Tally(p, vectors, ("row", "col", "dp"), sems, base)
    base = summed.next_sem
    lately = Tally(p, late, ("row", "dp", "col"), sems, base)
    base = lately.next_sem
    summed.send(0)
    for n in (0, 1):
        share_grad_came(n).wait_recv()
        share_grad(n).wait_send()
    s_out.start()


    def turn(i):
        for at, action in back_plan:
            @pl.when(i == at)
            def _():
                action()

    back_plan = [
        (2, lambda: (s_down.first_sum(), s_down.second_copy().start())),
        (3, lambda: (s_out.first_sum(), s_out.second_copy().start())),
        (4, lambda: z_down.row_half()),
        (5, lambda: (s_down.second_sum(), s_down.start_rows(), s_out.second_sum(), s_out.start_rows())),
        (6, lambda: (s_up.first_sum(), s_up.second_copy().start())),
        (7, lambda: (z_up.row_half(), z_down.row_sum(), summed.add(0), summed.send(1))),
    ]

    def attend_back(*scratch):
        attention_rows_backward(heads, turn, Slopes(heads), mixed_ref, dout, att_ref, lse_ref, mixed_ref, *scratch)

    pl.run_scoped(
        attend_back,
        pltpu.VMEM((pairs, blocks, 2 * BLOCK, PAIR), bf), pltpu.VMEM((pairs, blocks, BLOCK, PAIR), bf),
        pltpu.VMEM((pairs, blocks, 2 * BLOCK, PAIR), bf), pltpu.VMEM((pairs, blocks, BLOCK, PAIR), bf),
        pltpu.VMEM((pairs, blocks, 2 * BLOCK, PAIR), bf), pltpu.VMEM((heads, blocks, BLOCK), f32),
        pltpu.VMEM((heads, BLOCK, BLOCK), f32), pltpu.VMEM((heads, BLOCK, PAIR), f32),
        pltpu.VMEM((pairs, blocks, BLOCK, PAIR), f32), pltpu.VMEM((pairs, blocks, BLOCK, PAIR), f32),
        pltpu.VMEM((pairs, blocks, BLOCK, PAIR), f32),
    )

    @pl.loop(0, features // 128)
    def _(f):
        cols = hint(f, 128)
        jgrad[cols, :] = tn(nall_ref[:, cols], mixed_ref[...]).astype(bf)

    s_joined.start()

    sums_at = [bchip.at[pl.ds(0, quarter)], bchip.at[pl.ds(quarter, quarter)],
               normed.at[pl.ds(0, quarter)], normed.at[pl.ds(quarter, quarter)]]
    near_in = [gchip.at[pl.ds(0, quarter)], gchip.at[pl.ds(quarter, quarter)]]

    def product(index, slot):
        @pl.loop(0, quarter // 256)
        def _(n):
            rows = pl.ds(pl.multiple_of(index * quarter + n * 256, 256), 256)
            sums_at[slot][hint(n, 256), :] = nt(mixed_ref[rows, :], jall_ref[...]).astype(bf)

    grad_near = [remote(sums_at[n], near_in[n], sems, base + n, {"col": p.near}) for n in (0, 1)]
    grad_far = remote(sums_at[2], take, sems, base + 2, {"col": p.far})
    base += 3
    product(p.corner, 0)
    grad_near[0].start()
    product(p.near, 1)
    grad_near[1].start()
    product(p.far, 2)
    grad_near[0].wait()
    add_rows(sums_at[2], [sums_at[2], near_in[0]])
    grad_far.start()
    product(p.col, 3)
    s_up.second_sum()
    s_up.start_rows()
    z_down.far_sum()
    s_down.row_half()
    s_out.row_half()
    z_up.row_sum()
    sums = jnp.zeros((1, mixed_ref.shape[1]), f32)
    for n in range(tokens // 256):
        sums = sums + jnp.sum(mixed_ref[n * 256 : (n + 1) * 256, :].astype(f32), axis=0, keepdims=True)
    late[0] = jnp.zeros((8, features), f32)
    late[0, 2:3, 0 : sums.shape[1]] = sums
    s_joined.first_sum()
    s_joined.start_rows()
    s_up.row_half()
    z_down.twin_sum()
    grad_near[1].wait()
    grad_far.wait()
    gin = bchip.at[pl.ds(0, quarter)]
    grad_back = Untranspose(p, gin, input_grad_ref, sems, base)
    base += 4

    @pl.loop(0, quarter // 64)
    def _(n):
        rows = hint(n, 64)
        value = sums_at[3][rows, :].astype(f32) + near_in[1][rows, :].astype(f32) + take[rows, :].astype(f32)
        standard, inverse = moments(xt_ref[rows, :].astype(f32))
        late[0, 0:1, :] += jnp.sum(value * standard, axis=0, keepdims=True)
        late[0, 1:2, :] += jnp.sum(value, axis=0, keepdims=True)
        scaled = value * vall_ref[0:1, :]
        one = jnp.mean(scaled, 1, keepdims=True)
        two = jnp.mean(scaled * standard, 1, keepdims=True)
        gin[rows, :] = (gres[rows, :] + inverse * (scaled - one - standard * two)).astype(bf)

    lately.send(0)
    s_joined.row_half()
    grad_back.start()
    z_up.far_sum()
    s_down.row_sum()
    z_up.twin_sum()
    s_up.row_sum()
    s_out.row_sum()
    for n in range(1, len(summed.stages)):
        summed.add(n)
        if n + 1 < len(summed.stages):
            summed.send(n + 1)
    lately.add(0)
    lately.send(1)
    s_joined.row_sum()
    for n in range(1, len(lately.stages)):
        lately.add(n)
        if n + 1 < len(lately.stages):
            lately.send(n + 1)
    joined_at = lately.after(len(lately.stages) - 2)
    at = 0
    for n in range(6):
        place = hint(p.row, width)
        value = late[lately.last, n : n + 1, place] if n < 2 else vectors[summed.last, n : n + 1, place]
        for m in range(lanes):
            vector_sum_ref[at : at + 1, :] = value[:, m * 128 : (m + 1) * 128]
            at += 1
    value = vectors[summed.last, pl.ds(8 + p.col, 1), :]
    for m in range(hidden // 128):
        vector_sum_ref[at : at + 1, :] = value[:, m * 128 : (m + 1) * 128]
        at += 1
    for n in range(heads // 2):
        first, second, third = (
            late[joined_at, 2:3, (3 * n + m) * 128 : (3 * n + m + 1) * 128] for m in range(3)
        )
        vector_sum_ref[at : at + 1, :] = jnp.where(lo, first, swap(second))
        vector_sum_ref[at + 1 : at + 2, :] = jnp.where(lo, swap(second), third)
        at += 2
    value = jnp.sum(vectors[summed.last, 6:7, 0:128], axis=1, keepdims=True) * (scale * (1.0 / (features * token_total)))
    vector_sum_ref[at:, :] = jnp.broadcast_to(value, (vector_sum_ref.shape[0] - at, 128))
    for part in (s_down, s_up, z_down, z_up, s_joined, s_out):
        part.finish()
    grad_back.wait_recv()
    grad_back.wait_send()
    for n in (0, 1):
        moved[n].wait_send()
        for copies in (to_far, to_near, pass_on):
            copies[n].wait_send()
    w_joined.sent()
    back.wait_send()

    @pl.loop(0, per_chip)
    def _(n):
        share(n, n + per_chip * (1 - p.chip)).wait_send()


def layer_stage(small, joined, layer_in, up, down, out, teacher, cot, token_total):
    tokens, width = layer_in.shape
    quarter = tokens // 4
    features = width * lax.axis_size("row")
    joined_width = joined.shape[1]
    heads = joined_width // (3 * HEAD_DIM)
    blocks = tokens // BLOCK
    f32, bf = jnp.float32, jnp.bfloat16
    hidden, head_rows = down.shape[0], out.shape[0]
    vmem, anyspace = pl.BlockSpec(memory_space=pltpu.VMEM), pl.BlockSpec(memory_space=pl.ANY)
    shape = jax.ShapeDtypeStruct
    bits = 0
    while (1 << bits) < lax.axis_size("dp"):
        bits += 1
    count = (
        3 * TRANSPOSE_SEMS + 4 + 4 * WEIGHT_SEMS + HALVES_SEMS + 6 + (3 + bits) + 1 + 6 + blocks // 2 + 12
        + 4 * SHARE_SEMS + 2 * ROWS_FIRST_SEMS + 2 + 2 + 2 * (6 + bits) + 3 + 4
    )
    small_rows = 8 * ((6 * width // 128 + hidden // 128 + heads) // 8 + 1)
    outs = pl.pallas_call(
        functools.partial(layer_kernel, heads, token_total),
        out_shape=(
            shape((tokens, width), bf), shape((tokens, width), bf), shape((width, hidden), bf), shape((width, hidden), bf),
            shape((width, head_rows), bf), shape((width, joined_width), bf), shape((small_rows, 128), f32),
        ) + (shape((features, hidden), bf),) * 4 + (
            shape((1, features, hidden // 2), bf), shape((1, features, hidden // 2), bf), shape((features, head_rows), bf),
            shape((features, joined_width // 2), bf), shape((features, hidden // 4), bf), shape((features, hidden // 4), bf),
            shape((features, head_rows // 2), bf), shape((3, width, hidden // 4), bf), shape((3, width, hidden // 4), bf),
            shape((3, width, head_rows // 2), bf), shape((3, width, joined_width // 2), bf),
            shape((2, 4, width, hidden // 2), bf), shape((2, 2, width, hidden // 2), bf), shape((2, width, hidden // 2), bf),
            shape((2, width, hidden // 4), bf),
        ),
        in_specs=[vmem] + [anyspace] * 5 + [vmem] * 2,
        out_specs=(anyspace,) * 2 + (vmem,) * 5 + (anyspace,) * 19,
        scratch_shapes=[
            pltpu.VMEM((quarter, features), bf), pltpu.VMEM((tokens, features), bf), pltpu.VMEM((tokens, joined_width), bf),
            pltpu.VMEM((tokens, heads * HEAD_DIM), bf), pltpu.VMEM((heads, blocks, BLOCK), f32),
            pltpu.VMEM((features, joined_width), bf), pltpu.VMEM((8, features), f32), pltpu.VMEM((8, features), f32),
            pltpu.VMEM((2, 1, hidden), f32),
            pltpu.VMEM((2 * quarter, 2 * head_rows), bf), pltpu.VMEM((quarter, features), bf), pltpu.VMEM((quarter, 128), bf),
            pltpu.VMEM((2, features, hidden), bf), pltpu.VMEM((2, hidden + head_rows, features), bf),
            pltpu.VMEM((2, 8, hidden), f32), pltpu.VMEM((2 * quarter, features), bf), pltpu.VMEM((2 * quarter, features), bf),
            pltpu.VMEM((2 * quarter, features), bf), pltpu.VMEM((quarter, features), bf), pltpu.VMEM((quarter, features), bf),
            pltpu.VMEM((quarter, features), f32), pltpu.VMEM((quarter, features), f32), pltpu.VMEM((quarter, features), bf),
            pltpu.VMEM((2, 256, hidden), bf), pltpu.VMEM((tokens, width), bf), pltpu.VMEM((2 * quarter, head_rows), bf),
            pltpu.VMEM((tokens, head_rows), bf), pltpu.VMEM((2, 2, quarter, width), bf),
            pltpu.VMEM((tally_slots(bits, ("row", "col", "dp")), 16, features), f32),
            pltpu.VMEM((tally_slots(bits, ("row", "col", "dp")), 8, features), f32),
            pltpu.VMEM((tally_slots(bits, ("col", "dp")), 8, 128), f32),
            pltpu.VMEM((tokens, 128), bf), pltpu.VMEM((8, joined_width), f32),
            pltpu.SemaphoreType.REGULAR, pltpu.SemaphoreType.DMA((count,)), pltpu.SemaphoreType.DMA((count,)),
        ],
        compiler_params=pltpu.CompilerParams(vmem_limit_bytes=63 << 20, collective_id=1, has_side_effects=True),
        name="layer_stage",
    )(small, joined, layer_in, up, down, out, teacher, cot)
    return outs[:7]


def swap_with(value, axis, bit):
    size = lax.axis_size(axis)
    return lax.ppermute(value, axis, [(i, i ^ bit) for i in range(size)])


def low(value):
    return value.astype(jnp.bfloat16)


def sum_other_pairs(value):
    bit = 2
    while bit < lax.axis_size("dp"):
        value = value + swap_with(low(value), "dp", bit).astype(jnp.float32)
        bit *= 2
    return value


def on_device(
    layer_in,
    first_gain,
    first_shift,
    joined_weight,
    joined_bias,
    out_weight,
    out_bias,
    second_gain,
    second_shift,
    up_weight,
    up_bias,
    down_weight,
    down_bias,
    teacher,
    valid,
    cotangent,
):
    f32 = jnp.float32
    token_total = layer_in.shape[0] * lax.axis_size("dp") * lax.axis_size("col")
    arrays = (
        first_gain, first_shift, out_bias, second_gain, second_shift, down_bias, up_bias, joined_bias.reshape(-1), valid,
    )
    small = jnp.concatenate([a.astype(f32) for a in arrays]).reshape(-1, 128)
    layer_out, input_grad, up_grad, down_grad, out_grad, joined_grad, sums = layer_stage(
        small, joined_weight, layer_in, up_weight, down_weight, out_weight, teacher, cotangent, token_total
    )
    up_grad, down_grad, out_grad, joined_grad = (
        sum_other_pairs(g.astype(f32)) for g in (up_grad, down_grad, out_grad, joined_grad)
    )
    sums = sums.reshape(-1)
    pieces, at = [], 0
    for size in [layer_in.shape[1]] * 6 + [up_bias.shape[0], joined_bias.size, 1]:
        pieces.append(sums[at : at + size])
        at += size
    return (
        layer_out,
        pieces[8][0],
        input_grad.astype(f32),
        pieces[0],
        pieces[1],
        joined_grad,
        pieces[7].reshape(joined_bias.shape),
        out_grad.T,
        pieces[2],
        pieces[3],
        pieces[4],
        up_grad,
        pieces[6],
        down_grad.T,
        pieces[5],
    )


def solution(mesh):
    return jax.shard_map(
        on_device,
        mesh=mesh,
        in_specs=(
            P(("dp", "col"), "row"),
            P("row"),
            P("row"),
            P("row", "col"),
            P("col", None),
            P("col", "row"),
            P("row"),
            P("row"),
            P("row"),
            P("row", "col"),
            P("col"),
            P("col", "row"),
            P("row"),
            P(("dp", "col"), "row"),
            P(("dp", "col")),
            P(("dp", "col"), "row"),
        ),
        out_specs=(
            P(("dp", "col"), "row"),
            P(),
            P(("dp", "col"), "row"),
            P("row"),
            P("row"),
            P("row", "col"),
            P("col", None),
            P("col", "row"),
            P("row"),
            P("row"),
            P("row"),
            P("row", "col"),
            P("col"),
            P("col", "row"),
            P("row"),
        ),
        check_vma=False,
    )
```

```python
import functools
import math

import jax
import jax.numpy as jnp
from jax import lax
from jax.experimental import pallas as pl
from jax.experimental.pallas import tpu as pltpu
from jax.sharding import PartitionSpec as P

D = 1024
HEADS = 16
SEQ = 2048
EPSILON = 1e-05
LOG2E = 1.4426950408889634
HEAD_DIM=64
BLOCK=256
HALF=64
PAIR=128
SCALE2 = LOG2E/8.0

def nt(a,b):
    return lax.dot_general(a,b,(((1,),(1,)),((),())),preferred_element_type=jnp.float32)
def nn(a,b):
    return jnp.dot(a,b,preferred_element_type=jnp.float32)
def tn(a,b):
    return lax.dot_general(a,b,(((0,),(0,)),((),())),preferred_element_type=jnp.float32)

def low_lanes(rows):
    return lax.broadcasted_iota(jnp.int32,(rows,PAIR),1) < HALF

def swap(a):
    return jnp.concatenate([a[:,HALF:],a[:,:HALF]],axis=1)

def attention_rows(heads, order, after, slopes, mixed_ref, out_ref, lse_ref, qs, ks, vs, bias, sc, mx, ls, acc):
    pairs=heads//2
    blocks=mixed_ref.shape[0]//BLOCK
    lo=low_lanes(BLOCK)
    @pl.loop(0,blocks)
    def _(b):
        rows=pl.ds(pl.multiple_of(b*BLOCK,BLOCK),BLOCK)
        for p in range(pairs):
            t0,t1,t2=(mixed_ref[rows,(3*p+n)*PAIR:(3*p+n+1)*PAIR] for n in range(3))
            zero=jnp.zeros_like(t0)
            qs[2*p,b]=jnp.where(lo,t0,zero)
            qs[2*p+1,b]=jnp.where(lo,zero,t1)
            ks[p,b]=jnp.where(lo,swap(t0),swap(t2))
            vs[p,b,:BLOCK]=jnp.where(lo,t1,zero)
            vs[p,b,BLOCK:]=jnp.where(lo,zero,t2)
    il=lax.broadcasted_iota(jnp.int32,(BLOCK,BLOCK),0)
    jl=lax.broadcasted_iota(jnp.int32,(BLOCK,BLOCK),1)
    tent=jnp.minimum(jl,2*il-jl).astype(jnp.float32)
    for h in range(heads):
        bias[h]=tent*slopes[h]
    jrow=lax.broadcasted_iota(jnp.int32,(1,BLOCK),1)
    @pl.loop(0,blocks)
    def _(it):
        i=order(it)
        for h in range(heads):
            t=nt(qs[h,i],ks[h//2,i])*SCALE2+bias[h]
            sc[h,i]=t
            mx[h]=jnp.maximum(t[:,:PAIR],t[:,PAIR:])
        @pl.loop(0,i)
        def _(j):
            place=(jrow+(j-i)*BLOCK).astype(jnp.float32)
            for h in range(heads):
                t=nt(qs[h,i],ks[h//2,j])*SCALE2+place*slopes[h]
                sc[h,j]=t
                mx[h]=jnp.maximum(mx[h],jnp.maximum(t[:,:PAIR],t[:,PAIR:]))
        for h in range(heads):
            mx[h]=jnp.broadcast_to(jnp.max(mx[h],1,keepdims=True),(BLOCK,PAIR))
            ls[h]=jnp.zeros((BLOCK,PAIR),jnp.float32)
        for p in range(pairs):
            acc[p]=jnp.zeros((BLOCK,PAIR),jnp.float32)
        @pl.loop(0,i+1)
        def _(j):
            for p in range(pairs):
                both=[]
                for h in (2*p,2*p+1):
                    m=mx[h]
                    ea=jnp.exp2(sc[h,j,:,:PAIR]-m)
                    eb=jnp.exp2(sc[h,j,:,PAIR:]-m)
                    ls[h]+=ea+eb
                    both+=[ea.astype(jnp.bfloat16),eb.astype(jnp.bfloat16)]
                acc[p]+=nn(jnp.concatenate(both,1),vs[p,j])
        rows=pl.ds(pl.multiple_of(i*BLOCK,BLOCK),BLOCK)
        for p in range(pairs):
            tot=[jnp.broadcast_to(jnp.sum(ls[h],1,keepdims=True),(BLOCK,PAIR)) for h in (2*p,2*p+1)]
            out_ref[rows,p*PAIR:(p+1)*PAIR]=(acc[p]/jnp.where(lo,tot[0],tot[1])).astype(out_ref.dtype)
            for n,h in enumerate((2*p,2*p+1)):
                lse=mx[h]+jnp.log2(tot[n])
                lse_ref[h,pl.ds(i,1),:]=lse.T[:1]
        after(it,i)

def attention_rows_backward(heads, after, slopes, mixed_ref, dout_ref, out_ref, lse_ref, grad_ref, qs, ks, km, vp, ds_, delta, bias, steep, dq, dk, dv):
    pairs=heads//2
    blocks=mixed_ref.shape[0]//BLOCK
    lo=low_lanes(BLOCK)
    @pl.loop(0,blocks)
    def _(b):
        rows=pl.ds(pl.multiple_of(b*BLOCK,BLOCK),BLOCK)
        for p in range(pairs):
            t0,t1,t2=(mixed_ref[rows,(3*p+n)*PAIR:(3*p+n+1)*PAIR] for n in range(3))
            zero=jnp.zeros_like(t0)
            qs[p,b,:BLOCK]=jnp.where(lo,t0,zero)
            qs[p,b,BLOCK:]=jnp.where(lo,zero,t1)
            k=jnp.where(lo,swap(t0),swap(t2))
            ks[p,b]=k
            km[p,b,:BLOCK]=jnp.where(lo,k,zero)
            km[p,b,BLOCK:]=jnp.where(lo,zero,k)
            vp[p,b]=jnp.where(lo,t1,t2)
            d=dout_ref[rows,p*PAIR:(p+1)*PAIR]
            ds_[p,b,:BLOCK]=jnp.where(lo,d,zero)
            ds_[p,b,BLOCK:]=jnp.where(lo,zero,d)
            prod=(d.astype(jnp.float32)*out_ref[rows,p*PAIR:(p+1)*PAIR].astype(jnp.float32)).T
            delta[2*p,pl.ds(b,1),:]=jnp.sum(prod[:HALF],0,keepdims=True)
            delta[2*p+1,pl.ds(b,1),:]=jnp.sum(prod[HALF:],0,keepdims=True)
    kl=lax.broadcasted_iota(jnp.int32,(BLOCK,BLOCK),0)
    ql=lax.broadcasted_iota(jnp.int32,(BLOCK,BLOCK),1)
    tent=jnp.minimum(kl,2*ql-kl).astype(jnp.float32)
    ramp=kl.astype(jnp.float32)
    for h in range(heads):
        bias[h]=tent*slopes[h]
        steep[h]=ramp[:,:PAIR]*slopes[h]
    def block(i,j,first):
        for p in range(pairs):
            ps=[];gs=[]
            for n,h in enumerate((2*p,2*p+1)):
                q=qs[p,i,n*BLOCK:(n+1)*BLOCK]
                d=ds_[p,i,n*BLOCK:(n+1)*BLOCK]
                row=slopes[h]*((j-i)*BLOCK).astype(jnp.float32)-lse_ref[h,pl.ds(i,1),:]
                t=nt(ks[p,j],q)*SCALE2+row+(bias[h] if first else jnp.concatenate([steep[h],steep[h]],1))
                e=jnp.exp2(t)
                g=e*(nt(vp[p,j],d)-delta[h,pl.ds(i,1),:])
                ps.append(e.astype(jnp.bfloat16)); gs.append(g.astype(jnp.bfloat16))
            gv=nn(jnp.concatenate(ps,1),ds_[p,i])
            gk=nn(jnp.concatenate(gs,1),qs[p,i])
            gq=tn(jnp.concatenate(gs,0),km[p,j])
            if first:
                dv[p,j]=gv; dk[p,j]=gk; dq[p,i]=gq
            else:
                dv[p,j]+=gv; dk[p,j]+=gk; dq[p,i]+=gq
    @pl.loop(0,blocks)
    def _(i):
        block(i,i,True)
        @pl.loop(0,i)
        def _(j):
            block(i,j,False)
        after(i)
    @pl.loop(0,blocks)
    def _(b):
        rows=pl.ds(pl.multiple_of(b*BLOCK,BLOCK),BLOCK)
        for p in range(pairs):
            a=dq[p,b]*0.125; k=swap(dk[p,b]*0.125); v=dv[p,b]
            for n,t in enumerate((jnp.where(lo,a,k),jnp.where(lo,v,a),jnp.where(lo,k,v))):
                grad_ref[rows,(3*p+n)*PAIR:(3*p+n+1)*PAIR]=t.astype(grad_ref.dtype)


MESH = pl.DeviceIdType.MESH


def hint(index, size):
    return pl.ds(pl.multiple_of(index * size, size), size)


def remote(src, dst, sems, number, target):
    send, recv = sems
    return pltpu.make_async_remote_copy(
        src_ref=src, dst_ref=dst, send_sem=send.at[number], recv_sem=recv.at[number],
        device_id=target, device_id_type=MESH,
    )


def partner(index, bit):
    return index + bit - 2 * bit * ((index // bit) % 2)


class Place:
    def __init__(self):
        self.dp, self.row, self.col = (lax.axis_index(a) for a in ("dp", "row", "col"))
        self.dps = lax.axis_size("dp")
        self.core, self.chip = self.col % 2, self.col // 2
        self.near, self.far = partner(self.col, 1), partner(self.col, 2)
        self.twin = partner(self.dp, 1)
        self.half = self.dp % 2
        self.plane = 3 * self.core + self.chip - 2 * self.core * self.chip
        self.source = 2 * (((self.row + 1) // 2) % 2) + self.row // 2
        self.corner = partner(self.far, 1)
        self.stays = self.plane == self.row
        self.far_plane = 3 * self.core + (1 - self.chip) - 2 * self.core * (1 - self.chip)
        self.sender = 2 * self.chip + self.source % 2
        self.home = jnp.logical_or(self.stays, self.far_plane == self.row)


def greet(place):
    barrier = pltpu.get_barrier_semaphore()

    def signal(target):
        pl.semaphore_signal(barrier, inc=1, device_id=target, device_id_type=MESH)

    for step in (1, 2, 3):
        signal({"row": (place.row + step) % 4})
    for col in (place.near, place.far, place.corner):
        signal({"col": col})
    amount = 6
    bit = 1
    while bit < place.dps:
        signal({"dp": partner(place.dp, bit)})
        amount += 1
        bit *= 2

    for plane, stays in ((place.plane, place.stays), (place.far_plane, place.far_plane == place.row)):
        signal({"row": plane, "col": place.near})

        @pl.when(jnp.logical_not(stays))
        def _():
            signal({"row": plane, "col": place.col})

    for other in range(4):
        @pl.when(jnp.logical_not(jnp.logical_and(place.home, place.row == other)))
        def _():
            signal({"row": other, "col": place.sender})

        @pl.when(jnp.logical_not(jnp.logical_and(place.stays, place.col == other)))
        def _():
            signal({"row": place.plane, "col": other})

        @pl.when(jnp.logical_not(jnp.logical_and(place.stays, place.row == other)))
        def _():
            signal({"row": other, "col": place.source})

    amount = amount + 16 - 2 * place.home.astype(jnp.int32) - 2 * place.stays.astype(jnp.int32)
    pl.semaphore_wait(barrier, amount)


class Transpose:
    def __init__(self, place, src, dst, relay, sems, first, part=0, parts=1):
        self.p, self.src, self.dst, self.relay, self.sems, self.first = place, src, dst, relay, sems, first
        self.quarter, self.width = src.shape[0] // 4, src.shape[1]
        self.rows = self.quarter // parts
        self.offset = part * self.rows

    def tokens(self, quarter):
        return self.src.at[pl.ds(pl.multiple_of(quarter * self.quarter + self.offset, self.rows), self.rows)]

    def part(self):
        return self.dst.at[pl.ds(self.offset, self.rows), hint(self.p.row, self.width)]

    def cross(self, n):
        src = self.tokens(2 * (1 - self.p.chip) + n)
        return remote(src, self.relay.at[n], self.sems, self.first + 4 + n, {"col": self.p.far})

    def out(self, relayed, n):
        p = self.p
        col = p.col if n == 0 else p.near
        src = self.relay.at[col % 2] if relayed else self.tokens(col)
        return pltpu.make_async_remote_copy(
            src_ref=src, dst_ref=self.part(),
            send_sem=self.sems[0].at[self.first + 2 * relayed + n], recv_sem=self.sems[1].at[self.first + p.row],
            device_id={"row": p.far_plane if relayed else p.plane, "col": col}, device_id_type=MESH,
        )

    def kept(self, relayed):
        p = self.p
        src = self.relay.at[p.core] if relayed else self.tokens(p.col)
        return pltpu.make_async_copy(src, self.part(), self.sems[1].at[self.first + p.row])

    def leaves(self, relayed):
        return (self.p.far_plane if relayed else self.p.plane) != self.p.row

    def send(self, relayed):
        self.out(relayed, 1).start()

        @pl.when(self.leaves(relayed))
        def _():
            self.out(relayed, 0).start()

        @pl.when(jnp.logical_not(self.leaves(relayed)))
        def _():
            self.kept(relayed).start()

    def start_cross(self):
        for n in (0, 1):
            self.cross(n).start()

    def forward(self):
        for n in (0, 1):
            self.cross(n).wait_recv()
        self.send(1)

    def wait_recv(self):
        p = self.p
        for other in range(4):
            mine = jnp.logical_and(p.home, p.row == other)
            part = self.dst.at[pl.ds(self.offset, self.rows), pl.ds(other * self.width, self.width)]

            @pl.when(jnp.logical_not(mine))
            def _():
                pltpu.make_async_remote_copy(
                    src_ref=part, dst_ref=part, send_sem=self.sems[0].at[self.first + other],
                    recv_sem=self.sems[1].at[self.first + other],
                    device_id={"row": other, "col": p.sender}, device_id_type=MESH,
                ).wait_recv()

            @pl.when(mine)
            def _():
                self.kept(0).wait()

    def wait_send(self):
        for n in (0, 1):
            self.cross(n).wait_send()
        for relayed in (0, 1):
            self.out(relayed, 1).wait_send()

            @pl.when(self.leaves(relayed))
            def _():
                self.out(relayed, 0).wait_send()


TRANSPOSE_SEMS = 6


class Slopes:
    def __init__(self, heads):
        self.heads = heads
        col = lax.axis_index("col")
        self.column = jnp.float32(1.0)
        for c in range(1, lax.axis_size("col")):
            self.column = jnp.where(col == c, jnp.float32(2.0 ** (-8.0 * heads * c / HEADS)), self.column)

    def __getitem__(self, head):
        return self.column * (2.0 ** (-8.0 * (head + 1) / HEADS) * LOG2E)


class Weight:
    def __init__(self, place, src, dst, offset, by_rows, last, sems, first):
        self.p, self.src, self.dst, self.offset, self.by_rows, self.last = place, src, dst, offset, by_rows, last
        self.sems, self.first = sems, first
        self.rows, self.width = src.shape
        self.part = self.rows // 2

    def whole(self, side, row):
        if self.by_rows:
            return self.dst.at[side, hint(row, self.rows)]
        return self.dst.at[side, pl.ds(self.offset, self.rows), hint(row, self.width)]

    def piece(self, side, row, half):
        if self.by_rows:
            return self.dst.at[side, hint(row * 2 + half, self.part)]
        start = pl.multiple_of(self.offset + half * self.part, self.part)
        return self.dst.at[side, pl.ds(start, self.part), hint(row, self.width)]

    def other(self, step):
        return (self.p.row + 4 - step) % 4

    def move(self, src, dst, number, target):
        return remote(src, dst, self.sems, self.first + number, target)

    def pass_on(self, side, step, half, number, target):
        src = self.piece(side, self.other(step), half)
        dst = self.piece(1 if "col" in target else side, self.other(step), half)
        return self.move(src, dst, number + step - 1, target)

    def own(self):
        return pltpu.make_async_copy(self.src, self.whole(0, self.p.row), self.sems[1].at[self.first])

    def across(self):
        return self.move(self.src, self.whole(1, self.p.row), 1, {"col": self.p.far})

    def along(self, step):
        p = self.p
        return self.move(
            self.src.at[hint(p.half, self.part)], self.piece(0, p.row, p.half), 1 + step, {"row": (p.row + step) % 4}
        )

    def to_twin(self, step):
        return self.pass_on(0, step, self.p.half, 5, {"dp": self.p.twin})

    def to_far(self, step):
        return self.pass_on(0, step, self.p.half, 8, {"col": self.p.far})

    def onward(self, step):
        if self.last == "y":
            return self.pass_on(0, step, 1 - self.p.half, 11, {"col": self.p.far})
        return self.pass_on(1, step, self.p.half, 11, {"dp": self.p.twin})

    def arrival(self, side, step, half, number):
        part = self.piece(side, self.other(step), half)
        return self.move(part, part, number + step - 1, {"dp": self.p.twin})

    def start_along(self):
        for step in (1, 2, 3):
            self.along(step).start()

    def spread(self, steps=(1, 2, 3)):
        for step in steps:
            self.arrival(0, step, self.p.half, 2).wait_recv()
            self.to_twin(step).start()
            self.to_far(step).start()

    def spread_last(self, steps=(1, 2, 3)):
        p = self.p
        for step in steps:
            if self.last == "y":
                self.arrival(0, step, 1 - p.half, 5).wait_recv()
            else:
                self.arrival(1, step, p.half, 8).wait_recv()
            self.onward(step).start()

    def ready(self, side):
        p = self.p
        if side == 0:
            self.own().wait()
        else:
            self.across().wait_recv()
        for step in (1, 2, 3):
            if side == 0 and self.last == "x":
                self.arrival(0, step, 1 - p.half, 5).wait_recv()
            if side == 1 and self.last == "y":
                self.arrival(1, step, p.half, 8).wait_recv()
            if side == 1:
                self.arrival(1, step, 1 - p.half, 11).wait_recv()

    def sent(self):
        self.across().wait_send()
        for step in (1, 2, 3):
            for copy in (self.along(step), self.to_twin(step), self.to_far(step), self.onward(step)):
                copy.wait_send()


WEIGHT_SEMS = 14


class Halves:
    def __init__(self, place, src, dst, sems, first):
        self.p, self.src, self.dst, self.sems, self.first = place, src, dst, sems, first
        self.rows = src.shape[0]
        self.part = self.rows // 2

    def own(self):
        return pltpu.make_async_copy(self.src, self.dst.at[hint(self.p.row, self.rows)], self.sems[1].at[self.first])

    def along(self, step):
        p = self.p
        return remote(
            self.src.at[hint(p.half, self.part)], self.dst.at[hint(2 * p.row + p.half, self.part)], self.sems,
            self.first + step, {"row": (p.row + step) % 4},
        )

    def part_of(self, step, half):
        return self.dst.at[hint(2 * ((self.p.row + 4 - step) % 4) + half, self.part)]

    def to_twin(self, step, half):
        part = self.part_of(step, half)
        return remote(part, part, self.sems, self.first + 3 + step, {"dp": self.p.twin})

    def start(self):
        self.own().start()
        for step in (1, 2, 3):
            self.along(step).start()

    def spread(self):
        p = self.p
        for step in (1, 2, 3):
            part = self.part_of(step, p.half)
            remote(part, part, self.sems, self.first + step, {"dp": p.twin}).wait_recv()
            self.to_twin(step, p.half).start()

    def ready(self):
        p = self.p
        for step in (1, 2, 3):
            self.to_twin(step, 1 - p.half).wait_recv()
        self.own().wait()

    def sent(self):
        for step in (1, 2, 3):
            self.along(step).wait_send()
            self.to_twin(step, self.p.half).wait_send()


HALVES_SEMS = 7


GELU_ROOT = math.sqrt(2.0 / math.pi)
GELU_CUBE = 0.044715


def gelu_pair(x):
    square = x * x
    t = jnp.tanh(GELU_ROOT * x * (1.0 + GELU_CUBE * square))
    half = 0.5 * (1.0 + t)
    slope = half + 0.5 * x * (1.0 - t * t) * (GELU_ROOT * (1.0 + 3.0 * GELU_CUBE * square))
    return x * half, slope


def moments(x):
    center = jnp.mean(x, 1, keepdims=True)
    spread = jnp.mean(x * x, 1, keepdims=True) - center * center
    inverse = lax.rsqrt(spread + EPSILON)
    return (x - center) * inverse, inverse


class Chip:
    def __init__(self, place, sems, first):
        self.p, self.sems, self.first = place, sems, first

    def copy(self, number, src, dst):
        return remote(src, dst, self.sems, self.first + number, {"col": self.p.near})


class Untranspose:
    def __init__(self, place, src, dst, sems, first):
        self.place, self.src, self.dst, self.sems, self.first = place, src, dst, sems, first
        self.rows, self.width = src.shape[0], src.shape[1] // 4

    def out(self, other):
        p = self.place
        return pltpu.make_async_remote_copy(
            src_ref=self.src.at[:, pl.ds(other * self.width, self.width)],
            dst_ref=self.dst.at[hint(p.col, self.rows)],
            send_sem=self.sems[0].at[self.first + other], recv_sem=self.sems[1].at[self.first + p.col],
            device_id={"row": other, "col": p.source}, device_id_type=MESH,
        )

    def kept(self):
        p = self.place
        return pltpu.make_async_copy(
            self.src.at[:, hint(p.row, self.width)],
            self.dst.at[hint(p.col, self.rows)],
            self.sems[1].at[self.first + p.col],
        )

    def start(self):
        p = self.place
        for other in range(4):
            @pl.when(jnp.logical_not(jnp.logical_and(p.stays, p.row == other)))
            def _():
                self.out(other).start()

        @pl.when(p.stays)
        def _():
            self.kept().start()

    def wait_recv(self):
        p = self.place
        for other in range(4):
            mine = jnp.logical_and(p.stays, p.col == other)
            part = self.dst.at[pl.ds(other * self.rows, self.rows)]

            @pl.when(jnp.logical_not(mine))
            def _():
                pltpu.make_async_remote_copy(
                    src_ref=part, dst_ref=part, send_sem=self.sems[0].at[self.first + other],
                    recv_sem=self.sems[1].at[self.first + other],
                    device_id={"row": p.plane, "col": other}, device_id_type=MESH,
                ).wait_recv()

            @pl.when(mine)
            def _():
                self.kept().wait()

    def wait_send(self):
        p = self.place
        for other in range(4):
            @pl.when(jnp.logical_not(jnp.logical_and(p.stays, p.row == other)))
            def _():
                self.out(other).wait_send()


def add_rows(total, pieces, rows=64):
    @pl.loop(0, total.shape[0] // rows)
    def _(n):
        part = hint(n, rows)
        value = pieces[0][part, :].astype(jnp.float32)
        for piece in pieces[1:]:
            value = value + piece[part, :].astype(jnp.float32)
        total[part, :] = value.astype(total.dtype)


class Share:
    def __init__(self, place, kind, own, far, result, came, other, rows, totals, slots, sems, first):
        self.p, self.kind, self.own, self.far, self.result = place, kind, own, far, result
        self.came, self.other_ref, self.rows, self.totals, self.slots = came, other, rows, totals, slots
        self.sems, self.first = sems, first
        self.width = own.shape[1]
        self.part = self.width // 2
        self.block = own.shape[0] // 4
        self.mine, self.theirs = hint(place.half, self.part), hint(1 - place.half, self.part)

    def first_copies(self):
        p = self.p
        if self.kind == "xy":
            return [
                remote(src.at[:, self.theirs], self.came[n], self.sems, self.first + n, {"dp": p.twin})
                for n, src in enumerate((self.own, self.far))
            ]
        if self.kind == "yx":
            return [remote(self.far, self.came, self.sems, self.first, {"col": p.far})]
        return [remote(self.own.at[:, self.theirs], self.came, self.sems, self.first, {"dp": p.twin})]

    def start(self):
        for copy in self.first_copies():
            copy.start()

    def gather_sum(self, jobs):
        blocks = []
        for total, sources in jobs:
            for n in range(4):
                part = pl.ds(n * self.block, self.block)
                blocks.append((total.at[part], [src.at[part] for src in sources]))
        self.block_sums(blocks)

    def block_sums(self, blocks):
        copies = []
        for n, (_, sources) in enumerate(blocks):
            copies.append([
                pltpu.make_async_copy(
                    src, self.slots[2 * (n % 2) + m].at[:, : src.shape[1]],
                    self.sems[1].at[self.first + 8 + 2 * (n % 2) + m],
                )
                for m, src in enumerate(sources)
            ])
        for copy in copies[0]:
            copy.start()
        for n, (total, sources) in enumerate(blocks):
            if n + 1 < len(blocks):
                for copy in copies[n + 1]:
                    copy.start()
            for copy in copies[n]:
                copy.wait()
            add_rows(total, [self.slots[2 * (n % 2) + m].at[:, : total.shape[1]] for m in range(len(sources))])

    def second_copy(self):
        p = self.p
        if self.kind == "xy":
            return remote(self.totals[1], self.other_ref, self.sems, self.first + 2, {"col": p.far})
        return remote(self.totals[0].at[:, self.theirs], self.other_ref, self.sems, self.first + 2, {"dp": p.twin})

    def first_sum(self):
        for copy in self.first_copies():
            copy.wait()
        if self.kind == "xy":
            self.gather_sum([
                (self.totals[1], [self.came[1], self.far.at[:, self.mine]]),
                (self.totals[0], [self.came[0], self.own.at[:, self.mine]]),
            ])
        elif self.kind == "yx":
            self.gather_sum([(self.totals[0], [self.came, self.own])])
        else:
            self.gather_sum([(self.totals[0], [self.came, self.own.at[:, self.mine]])])

    def total(self):
        return self.totals[1] if self.kind == "yx" else self.totals[0]

    def second_sum(self):
        self.second_copy().wait()
        if self.kind == "xy":
            self.gather_sum([(self.totals[0], [self.other_ref, self.totals[0]])])
        else:
            self.gather_sum([(self.totals[1], [self.other_ref, self.totals[0].at[:, self.mine]])])

    def row_copy(self, step):
        row = self.p.row
        target = partner(row, 1) if step < 2 else partner(row, 2)
        block = partner(target, 2) if step == 1 else target
        return remote(
            self.total().at[hint(block, self.block)], self.rows.at[step], self.sems, self.first + 3 + step, {"row": target}
        )

    def start_rows(self):
        for step in (1, 0):
            self.row_copy(step).start()

    def row_add(self, block, step, target):
        load = pltpu.make_async_copy(
            self.rows.at[step], self.slots[step].at[:, : self.part], self.sems[1].at[self.first + 8 + step]
        )
        load.start()
        load.wait()
        add_rows(target, [self.total().at[hint(block, self.block)], self.slots[step].at[:, : self.part]])

    def row_half(self):
        other = partner(self.p.row, 2)
        self.row_copy(1).wait()
        self.row_add(other, 1, self.total().at[hint(other, self.block)])
        self.row_copy(2).start()
        self.row_copy(0).wait()
        self.row_add(self.p.row, 0, self.total().at[hint(self.p.row, self.block)])

    def last_copy(self, half):
        part = self.result.at[:, hint(half, self.part)]
        return remote(part, part, self.sems, self.first + 6, {"dp": self.p.twin})

    def row_sum(self):
        self.row_copy(2).wait()
        self.row_add(self.p.row, 2, self.result.at[:, self.mine])
        self.last_copy(self.p.half).start()

    def finish(self):
        self.last_copy(self.p.half).wait_send()
        self.last_copy(1 - self.p.half).wait_recv()


SHARE_SEMS = 12


class RowsFirst(Share):
    def __init__(self, place, own, far, result, from_next, from_other, from_far, from_twin, total, slots, sems, first):
        super().__init__(place, "zyx", own, far, result, None, None, None, None, slots, sems, first)
        self.from_next, self.from_other, self.from_far, self.from_twin = from_next, from_other, from_far, from_twin
        self.parts = [[total.at[pl.ds((2 * side + n) * self.block, self.block)] for n in (0, 1)] for side in (0, 1)]

    def next_copies(self):
        target = partner(self.p.row, 1)
        rows = (target, partner(target, 2))
        return [
            remote(
                source.at[hint(rows[n], self.block)], self.from_next.at[2 * side + n], self.sems,
                self.first + 2 * side + n, {"row": target},
            )
            for side, source in enumerate((self.own, self.far))
            for n in (0, 1)
        ]

    def start(self):
        for copy in self.next_copies():
            copy.start()

    def other_copies(self):
        return [
            remote(
                self.parts[side][1], self.from_other.at[side], self.sems, self.first + 4 + side,
                {"row": partner(self.p.row, 2)},
            )
            for side in (0, 1)
        ]

    def row_half(self):
        for copy in self.next_copies():
            copy.wait()
        rows = (self.p.row, partner(self.p.row, 2))
        for n in (1, 0):
            self.block_sums([
                (self.parts[side][n], [source.at[hint(rows[n], self.block)], self.from_next.at[2 * side + n]])
                for side, source in enumerate((self.own, self.far))
            ])
            if n == 1:
                for copy in self.other_copies():
                    copy.start()

    def far_copy(self):
        return remote(self.parts[1][0], self.from_far, self.sems, self.first + 6, {"col": self.p.far})

    def row_sum(self):
        for copy in self.other_copies():
            copy.wait()
        self.block_sums([(self.parts[side][0], [self.parts[side][0], self.from_other.at[side]]) for side in (1, 0)])
        self.far_copy().start()

    def twin_copy(self):
        return remote(self.parts[0][0].at[:, self.theirs], self.from_twin, self.sems, self.first + 7, {"dp": self.p.twin})

    def far_sum(self):
        self.far_copy().wait()
        self.block_sums([(self.parts[0][0], [self.parts[0][0], self.from_far])])
        self.twin_copy().start()

    def last_copy(self, half):
        part = self.result.at[:, hint(half, self.part)]
        return remote(part, part, self.sems, self.first + 12, {"dp": self.p.twin})

    def twin_sum(self):
        self.twin_copy().wait()
        self.block_sums([(self.result.at[:, self.mine], [self.parts[0][0].at[:, self.mine], self.from_twin])])
        self.last_copy(self.p.half).start()


ROWS_FIRST_SEMS = 13


class Tally:
    def __init__(self, place, slots, axes, sems, first):
        self.slots = slots
        p = place
        peers = dict(
            row=[{"row": (p.row + step) % 4} for step in (1, 2, 3)],
            col=[{"col": p.near}, {"col": p.far}, {"col": p.corner}],
        )
        bit = 1
        while bit < p.dps:
            peers["dp%d" % bit] = [{"dp": partner(p.dp, bit)}]
            bit *= 2
        names = []
        for axis in axes:
            names += [name for name in peers if name.startswith(axis)]
        self.stages, at = [], 0
        for name in names:
            copies = [
                remote(slots.at[at], slots.at[at + 1 + n], sems, first + n, target)
                for n, target in enumerate(peers[name])
            ]
            self.stages.append((at, copies))
            at += len(copies) + 1
            first += len(copies)
        self.names, self.last, self.next_sem = names, at, first

    def send(self, n):
        for copy in self.stages[n][1]:
            copy.start()

    def add(self, n):
        at, copies = self.stages[n]
        value = self.slots[at]
        for m, copy in enumerate(copies):
            copy.wait()
            value = value + self.slots[at + 1 + m]
        self.slots[at + len(copies) + 1] = value

    def after(self, n):
        at, copies = self.stages[n]
        return at + len(copies) + 1


def tally_slots(bits, axes):
    return sum({"row": 4, "col": 4, "dp": 2 * bits}[axis] for axis in axes) + 1


def layer_kernel(
    heads, token_total,
    small_ref, joined_ref, layer_ref, up_ref, down_ref, out_ref, teacher_ref, cot_ref,
    layer_out_ref, input_grad_ref, upg_ref, dng_ref, outg_ref, joinedg_ref, vector_sum_ref,
    upg_own, upg_far, dng_own, dng_far, came_up, came_down, came_out, came_joined, other_up, other_down, other_out,
    rows_up, rows_down, rows_out, rows_joined, from_next, from_other, from_far, from_twin,
    xt_ref, nall_ref, mixed_ref, att_ref, lse_ref, jall_ref, vall_ref, early_ref, up_sums_ref,
    chip_ref, gt_ref, vt_ref, up2_ref, dn2_ref, ub2_ref, normed, gchip, bchip, give, take, middle, gres, low_ref, stage,
    grad, gfar, dout, relay, vectors, late, count, valid_ref, bias_ref, sync, sends, recvs,
):
    sems = (sends, recvs)
    f32, bf = jnp.float32, jnp.bfloat16
    p = Place()
    quarter, features = xt_ref.shape
    hidden = down_ref.shape[0]
    moved = [
        Transpose(p, layer_ref, xt_ref, relay.at[0, :, pl.ds(256 * n, 256)], sems, n * TRANSPOSE_SEMS, n, 2) for n in (0, 1)
    ]
    target = Transpose(p, grad, gt_ref, relay.at[1], sems, 2 * TRANSPOSE_SEMS)
    base = 3 * TRANSPOSE_SEMS
    back = Untranspose(p, low_ref, layer_out_ref, sems, base)
    base += 4
    w_out = Weight(p, out_ref, dn2_ref, hidden, False, "y", sems, base)
    w_up = Weight(p, up_ref, up2_ref, 0, True, "x", sems, base + WEIGHT_SEMS)
    w_downs = [
        Weight(
            p, down_ref.at[pl.ds(n * (hidden // 2), hidden // 2)], dn2_ref, n * (hidden // 2), False, "xy"[n], sems,
            base + (2 + n) * WEIGHT_SEMS,
        )
        for n in (0, 1)
    ]
    weights = [w_out, w_up] + w_downs
    base += 4 * WEIGHT_SEMS
    w_joined = Halves(p, joined_ref, jall_ref, sems, base)
    base += HALVES_SEMS
    small_base, bias_base = base, base + 4
    base += 6

    def small(step):
        part = vall_ref.at[:, hint(p.row, 256)]
        return remote(part, part, sems, small_base + step, {"row": (p.row + step) % 4})

    def small_came(step):
        part = vall_ref.at[:, hint((p.row + 4 - step) % 4, 256)]
        return remote(part, part, sems, small_base + step, {"row": (p.row + step) % 4})

    bias_far = remote(ub2_ref.at[0], ub2_ref.at[1], sems, bias_base + 1, {"col": p.far})
    counted = Tally(p, count, ("col", "dp"), sems, base)
    base = counted.next_sem
    tokens = nall_ref.shape[0]
    greet(p)
    for half in moved:
        half.start_cross()
    moved[0].send(0)
    width = layer_ref.shape[1]
    lanes = width // 128
    for n in range(6):
        for m in range(lanes):
            place = pl.ds(pl.multiple_of(p.row * width + m * 128, 128), 128)
            vall_ref[n : n + 1, place] = small_ref[lanes * n + m : lanes * n + m + 1, :]
    vall_ref[6:8, hint(p.row, width)] = jnp.zeros((2, width), f32)
    at = 6 * lanes
    for n in range(hidden // 128):
        ub2_ref[0, :, n * 128 : (n + 1) * 128] = jnp.broadcast_to(small_ref[at + n : at + n + 1, :], (8, 128))
    at += hidden // 128
    lo = low_lanes(1)
    for n in range(heads // 2):
        even, odd = (small_ref[at + 2 * n + m : at + 2 * n + m + 1, :] for m in (0, 1))
        for m, part in enumerate(
            (jnp.where(lo, even, 0.0), jnp.where(lo, swap(even), swap(odd)), jnp.where(lo, 0.0, odd))
        ):
            bias_ref[0:1, (3 * n + m) * 128 : (3 * n + m + 1) * 128] = part
    at += heads
    number = jnp.zeros((1, 128), f32)
    for n in range(tokens // 128):
        row = small_ref[at + n : at + n + 1, :]
        number = number + row
        valid_ref[n * 128 : (n + 1) * 128, :] = jnp.broadcast_to(row, (128, 128)).T.astype(bf)
    count[0] = jnp.broadcast_to(jnp.sum(number, axis=1, keepdims=True), (8, 128))
    counted.send(0)
    for step in (1, 2, 3):
        small(step).start()
    bias_far.start()
    w_out.across().start()
    w_up.across().start()
    for w in weights:
        w.own().start()
    moved[0].forward()
    moved[1].send(0)
    moved[1].forward()
    for n in range(len(counted.stages)):
        counted.add(n)
        if n + 1 < len(counted.stages):
            counted.send(n + 1)

    scale = token_total / count[counted.last, :1, :1]

    @pl.loop(0, 32)
    def _(n):
        rows = hint(n, grad.shape[0] // 32)
        factor = valid_ref[rows, :].astype(f32) * scale
        for f in range(grad.shape[1] // 128):
            cols = slice(f * 128, (f + 1) * 128)
            grad[rows, cols] = (
                cot_ref[rows, cols].astype(f32) - factor * teacher_ref[rows, cols].astype(f32)
            ).astype(bf)

    valid_base = base
    base += 1

    def valid_out():
        return pltpu.make_async_remote_copy(
            src_ref=valid_ref.at[hint(p.row, quarter)], dst_ref=vt_ref,
            send_sem=sends.at[valid_base], recv_sem=recvs.at[valid_base],
            device_id={"row": p.plane, "col": p.row}, device_id_type=MESH,
        )

    same = jnp.logical_and(p.stays, p.col == p.row)
    valid_kept = pltpu.make_async_copy(valid_ref.at[hint(p.row, quarter)], vt_ref, recvs.at[valid_base])

    for step in (1, 2, 3):
        small_came(step).wait_recv()
        small(step).wait_send()
    first = p.col * quarter

    def norm_one(n):
        rows = hint(n, 128)
        standard, _ = moments(xt_ref[rows, :].astype(f32))
        place = pl.ds(pl.multiple_of(first + n * 128, 128), 128)
        nall_ref[place, :] = (standard * vall_ref[0:1, :] + vall_ref[1:2, :]).astype(bf)

    def half_of(col, n):
        return nall_ref.at[pl.ds(pl.multiple_of(col * quarter + n * 256, 256), 256)]

    def spread_copy(col, n, number, to):
        return remote(half_of(col, n), half_of(col, n), sems, gather_base + 2 * number + n, {"col": to})

    gather_base = base
    base += 6
    to_far = [spread_copy(p.col, n, 0, p.far) for n in (0, 1)]
    to_near = [spread_copy(p.col, n, 1, p.near) for n in (0, 1)]
    far_came = [spread_copy(p.far, n, 0, p.far) for n in (0, 1)]
    near_came = [spread_copy(p.near, n, 1, p.near) for n in (0, 1)]
    pass_on = [spread_copy(p.far, n, 2, p.near) for n in (0, 1)]
    corner_came = [spread_copy(p.corner, n, 2, p.near) for n in (0, 1)]
    for n in (0, 1):
        moved[n].wait_recv()
        pl.loop(2 * n, 2 * n + 2)(norm_one)
        to_far[n].start()
        to_near[n].start()
    for step in (1, 2, 3):
        pl.semaphore_signal(sync, inc=1, device_id={"row": (p.row + step) % 4}, device_id_type=MESH)
    pl.semaphore_wait(sync, 3)
    w_joined.start()
    target.start_cross()
    for w in w_downs:
        w.across().start()

    @pl.when(jnp.logical_not(same))
    def _():
        valid_out().start()

    @pl.when(same)
    def _():
        valid_kept.start()

    def project(index, n):
        rows = pl.ds(pl.multiple_of(index * quarter + n * 256, 256), 256)
        mixed_ref[rows, :] = (nn(nall_ref[rows, :], jall_ref[...]) + bias_ref[0:1, :]).astype(bf)

    far_came[0].wait_recv()
    pass_on[0].start()
    w_joined.spread()
    for w in weights:
        w.start_along()
    far_came[1].wait_recv()
    pass_on[1].start()
    w_joined.ready()
    for came in near_came + corner_came:
        came.wait_recv()

    @pl.loop(0, tokens // 256)
    def _(n):
        project(n // 2, n % 2)

    w_out.spread()

    own_heads = att_ref.shape[1]
    blocks = tokens // BLOCK
    per_chip = blocks // 2
    share_base = base
    base += per_chip

    def chip_place(n):
        half = per_chip // 2
        return ((n // half + p.core) % 2) * half + n % half

    def share(n, i):
        return pltpu.make_async_remote_copy(
            src_ref=att_ref.at[hint(i, BLOCK)], dst_ref=chip_ref.at[hint(chip_place(n), BLOCK), pl.ds(own_heads, own_heads)],
            send_sem=sends.at[share_base + n], recv_sem=recvs.at[share_base + n],
            device_id={"col": p.far}, device_id_type=MESH,
        )

    def after(it, i):
        @pl.when(it < per_chip)
        def _():
            share(it, i).start()

        @pl.when(it >= per_chip)
        def _():
            chip_ref[hint(chip_place(it - per_chip), BLOCK), :own_heads] = att_ref[hint(i, BLOCK), :]

        for units, action in plan:
            @pl.when(it == at_units(units))
            def _():
                action()

    order = (
        [per_chip + n + 1 for n in range(per_chip)] + [n + 1 for n in range(per_chip)],
        [n + 1 for n in range(blocks)],
    )

    def at_units(units):
        found = []
        for counts in order:
            total, it = 0, 0
            for it, n in enumerate(counts):
                total += n
                if total >= units:
                    break
            found.append(it)
        return found[0] * (1 - p.chip) + found[1] * p.chip

    plan = [
        (3, lambda: w_out.spread_last()),
        (6, lambda: w_up.spread((1,))),
        (11, lambda: w_up.spread((2,))),
        (18, lambda: w_up.spread((3,))),
        (27, lambda: w_up.spread_last((1, 2))),
        (29, lambda: (target.send(0), target.forward())),
        (32, lambda: w_downs[0].spread((1, 2))),
    ]

    def attend(*scratch):
        attention_rows(
            heads, lambda it: (it + per_chip * (1 - p.chip)) % blocks, after,
            Slopes(heads), mixed_ref, att_ref, lse_ref, *scratch,
        )

    pairs = heads // 2
    pl.run_scoped(
        attend,
        pltpu.VMEM((heads, blocks, BLOCK, PAIR), bf), pltpu.VMEM((pairs, blocks, BLOCK, PAIR), bf),
        pltpu.VMEM((pairs, blocks, 2 * BLOCK, PAIR), bf), pltpu.VMEM((heads, BLOCK, BLOCK), f32),
        pltpu.VMEM((heads, blocks, BLOCK, BLOCK), f32), pltpu.VMEM((heads, BLOCK, PAIR), f32),
        pltpu.VMEM((heads, BLOCK, PAIR), f32), pltpu.VMEM((pairs, BLOCK, PAIR), f32),
    )

    @pl.loop(0, per_chip)
    def _(n):
        share(n, n + per_chip * (1 - p.chip)).wait_recv()

    w_up.spread_last((3,))
    w_downs[0].spread((3,))
    w_out.ready(0)
    w_out.ready(1)
    core = Chip(p, sems, base)
    base += 12
    ROWS = 256
    halves = quarter // ROWS

    def swap_rows(number, buffer, n):
        return core.copy(
            number + n, buffer.at[pl.ds(n * ROWS, ROWS)], buffer.at[pl.ds(quarter + n * ROWS, ROWS)]
        )

    def swap_came(number, buffer, n):
        part = buffer.at[pl.ds(quarter + n * ROWS, ROWS)]
        return core.copy(number + n, part, part)

    def give_rows(number, n):
        return core.copy(number + n, give.at[pl.ds(n * ROWS, ROWS)], take.at[pl.ds(n * ROWS, ROWS)])

    def take_rows(number, n):
        part = take.at[pl.ds(n * ROWS, ROWS)]
        return core.copy(number + n, part, part)

    def partial(number, keep, product, again):
        if again:
            for n in range(halves):
                give_rows(number - 4, n).wait_send()
        for n in range(halves):
            give[n * ROWS : (n + 1) * ROWS, :] = product(pl.ds(quarter + n * ROWS, ROWS)).astype(bf)
            give_rows(number, n).start()
        for n in range(halves):
            keep[n * ROWS : (n + 1) * ROWS, :] = product(pl.ds(n * ROWS, ROWS))

    partial(
        0, middle,
        lambda rows: nn(chip_ref[rows, :own_heads], dn2_ref[0, hidden:, :])
        + nn(chip_ref[rows, own_heads:], dn2_ref[1, hidden:, :]),
        False,
    )
    w_downs[1].spread()
    for n in range(halves):
        take_rows(0, n).wait_recv()

        @pl.loop(0, ROWS // 64)
        def _(m):
            rows = pl.ds(pl.multiple_of(n * ROWS + m * 64, 64), 64)
            value = xt_ref[rows, :].astype(f32) + (
                middle[rows, :] + take[rows, :].astype(f32) + vall_ref[2:3, :]
            )
            middle[rows, :] = value
            standard, _ = moments(value)
            normed[rows, :] = (standard * vall_ref[3:4, :] + vall_ref[4:5, :]).astype(bf)

        swap_rows(2, normed, n).start()
    w_up.ready(0)
    bias_far.wait()

    slots = [give.at[pl.ds(256 * (n // 2), 256), pl.ds(hidden // 2 * (n % 2), hidden // 2)] for n in range(4)]
    outg_own, outg_far = (dn2_ref.at[0, :features, pl.ds(own_heads * n, own_heads)] for n in (0, 1))
    jgrad = dn2_ref.at[1, :features, : mixed_ref.shape[1]]
    low_part, high_part = pl.ds(0, hidden // 2), pl.ds(hidden // 2, hidden // 2)

    def both(ref, n):
        return [ref.at[n, :, pl.ds(hidden // 4 * m, hidden // 4)] for m in (0, 1)]

    s_down = Share(
        p, "xy", dng_own.at[:, low_part], dng_far.at[:, low_part], dng_ref.at[:, low_part], both(came_down, 0), other_down,
        rows_down, both(up2_ref, 1), slots, sems, base,
    )
    s_up = Share(
        p, "xy", upg_own.at[:, low_part], upg_far.at[:, low_part], upg_ref.at[:, low_part], both(came_up, 0), other_up,
        rows_up, both(up2_ref, 0), slots, sems, base + SHARE_SEMS,
    )
    z_down = RowsFirst(
        p, dng_own.at[:, high_part], dng_far.at[:, high_part], dng_ref.at[:, high_part], from_next.at[0], from_other.at[0],
        from_far.at[0], from_twin.at[0], up2_ref.at[1, :, high_part], slots, sems, base + 4 * SHARE_SEMS,
    )
    z_up = RowsFirst(
        p, upg_own.at[:, high_part], upg_far.at[:, high_part], upg_ref.at[:, high_part], from_next.at[1], from_other.at[1],
        from_far.at[1], from_twin.at[1], chip_ref, slots, sems, base + 4 * SHARE_SEMS + ROWS_FIRST_SEMS,
    )
    s_out = Share(
        p, "yx", outg_own, outg_far, outg_ref, came_out, other_out, rows_out,
        [dn2_ref.at[1, :features, pl.ds(768, 256)], dn2_ref.at[0, :features, pl.ds(896, 128)]], slots, sems,
        base + 2 * SHARE_SEMS,
    )
    s_joined = Share(
        p, "x", jgrad, None, joinedg_ref, came_joined, None, rows_joined,
        [dn2_ref.at[0, :features, pl.ds(512, 384)]], slots, sems, base + 3 * SHARE_SEMS,
    )
    base += 4 * SHARE_SEMS + 2 * ROWS_FIRST_SEMS

    def natural(chip, n):
        return hint(2 * chip + (p.core + n) % 2, quarter)

    att_base = base
    base += 2

    def share_grad(n):
        return remote(
            gfar.at[pl.ds(n * quarter, quarter)], dout.at[natural(p.chip, n)], sems, att_base + n, {"col": p.far}
        )

    def share_grad_came(n):
        part = dout.at[natural(1 - p.chip, n)]
        return remote(part, part, sems, att_base + n, {"col": p.far})

    stage_base = base
    base += 2

    def middle_part(act, der, keep):
        wide = 256

        def up_rows(side):
            def body(n):
                rows = hint(n, quarter)

                @pl.loop(0, hidden // wide, unroll=2)
                def _(m):
                    cols = hint(m, wide)
                    before = nn(normed[rows, :], up2_ref[side, :, cols]) + ub2_ref[side, 0:1, cols]
                    value, slope = gelu_pair(before)
                    act[side, rows, cols] = value.astype(bf)
                    der[side, rows, cols] = slope.astype(bf)

            return body

        up_rows(0)(0)
        for n in range(halves):
            swap_came(2, normed, n).wait_recv()
        up_rows(0)(1)
        w_up.ready(1)
        up_rows(1)(0)
        w_downs[0].spread_last()
        up_rows(1)(1)
        w_downs[1].spread_last()
        for w in w_downs:
            w.ready(0)
            w.ready(1)
        partial(
            4, gres,
            lambda rows: nn(act[0, rows, :], dn2_ref[0, :hidden, :]) + nn(act[1, rows, :], dn2_ref[1, :hidden, :]),
            True,
        )
        target.wait_recv()

        @pl.when(jnp.logical_not(same))
        def _():
            valid_out().wait_send()
            valid_out().wait_recv()

        @pl.when(same)
        def _():
            valid_kept.wait()

        early_ref[...] = jnp.zeros_like(early_ref)
        for n in range(halves):
            take_rows(4, n).wait_recv()

            @pl.loop(0, ROWS // 64)
            def _(m):
                rows = pl.ds(pl.multiple_of(n * ROWS + m * 64, 64), 64)
                result = middle[rows, :] + (gres[rows, :] + take[rows, :].astype(f32) + vall_ref[5:6, :])
                low_ref[rows, :] = result.astype(bf)
                factor = vt_ref[rows, :].astype(f32)[:, :1] * scale
                value = gt_ref[rows, :].astype(f32) + factor * result
                gres[rows, :] = value
                rounded = value.astype(bf)
                gchip[rows, :] = rounded
                early_ref[5:6, :] += jnp.sum(rounded.astype(f32), axis=0, keepdims=True)

            swap_rows(6, gchip, n).start()
        back.start()
        up_sums_ref[...] = jnp.zeros_like(up_sums_ref)

        def before_rows(n):
            rows = hint(n, quarter)

            @pl.loop(0, 2 * hidden // wide, unroll=2)
            def _(m):
                side, cols = m // (hidden // wide), hint(m % (hidden // wide), wide)
                value = nt(gchip[rows, :], dn2_ref[side, cols, :]) * der[side, rows, cols].astype(f32)
                rounded = value.astype(bf)
                der[side, rows, cols] = rounded
                up_sums_ref[side, 0:1, cols] += jnp.sum(rounded.astype(f32), axis=0, keepdims=True)

        def weight_grad(slot, source, values, sinks):
            @pl.loop(0, features // 512)
            def _(f):
                cols = hint(f, 512)
                turned = source[:, cols].T
                for side, sink in enumerate(sinks):
                    copy = pltpu.make_async_copy(stage.at[side], sink.at[cols], recvs.at[slot + side])

                    @pl.when(f > 0)
                    def _():
                        copy.wait()

                    stage[side] = nn(turned, values[side]).astype(bf)
                    copy.start()

            for side, sink in enumerate(sinks):
                pltpu.make_async_copy(stage.at[side], sink.at[pl.ds(0, 512)], recvs.at[slot + side]).wait()

        before_rows(0)
        for n in range(halves):
            swap_came(6, gchip, n).wait_recv()
        weight_grad(stage_base, gchip, act, (dng_own, dng_far))
        s_down.start()
        z_down.start()
        before_rows(1)
        partial(
            8, keep, lambda rows: nt(der[0, rows, :], up2_ref[0]) + nt(der[1, rows, :], up2_ref[1]), True
        )

        for n in range(halves):
            for number, buffer in ((2, normed), (6, gchip)):
                swap_rows(number, buffer, n).wait_send()
        for n in range(halves):
            take_rows(8, n).wait_recv()

            @pl.loop(0, ROWS // 64)
            def _(m):
                rows = pl.ds(pl.multiple_of(n * ROWS + m * 64, 64), 64)
                value = keep[rows, :] + take[rows, :].astype(f32)
                standard, inverse = moments(middle[rows, :])
                early_ref[3:4, :] += jnp.sum(value * standard, axis=0, keepdims=True)
                early_ref[4:5, :] += jnp.sum(value, axis=0, keepdims=True)
                scaled = value * vall_ref[3:4, :]
                one = jnp.mean(scaled, 1, keepdims=True)
                two = jnp.mean(scaled * standard, 1, keepdims=True)
                value = gres[rows, :] + inverse * (scaled - one - standard * two)
                gres[rows, :] = value
                rounded = value.astype(bf)
                bchip[rows, :] = rounded
                early_ref[2:3, :] += jnp.sum(rounded.astype(f32), axis=0, keepdims=True)

            swap_rows(10, bchip, n).start()
        for n in range(2 * halves):
            if n >= halves:
                swap_came(10, bchip, n - halves).wait_recv()
            rows = pl.ds(n * ROWS, ROWS)
            place = pl.ds(
                pl.multiple_of((2 * p.chip + (p.core + n // halves) % 2) * quarter + n % halves * ROWS, ROWS), ROWS
            )
            dout[place, :] = nt(bchip[rows, :], dn2_ref[0, hidden:, :]).astype(bf)
            gfar[rows, :] = nt(bchip[rows, :], dn2_ref[1, hidden:, :]).astype(bf)
            if n % halves == halves - 1:
                share_grad(n // halves).start()
        weight_grad(stage_base, normed, der, (upg_own, upg_far))
        s_up.start()
        z_up.start()

    pl.run_scoped(
        middle_part,
        pltpu.VMEM((2, 2 * quarter, hidden), bf), pltpu.VMEM((2, 2 * quarter, hidden), bf), pltpu.VMEM((quarter, features), f32),
    )

    for w in weights:
        w.sent()

    @pl.loop(0, features // 256)
    def _(f):
        cols = hint(f, 256)
        turned = bchip[:, cols].T
        outg_own[cols, :] = nn(turned, chip_ref[:, :own_heads]).astype(bf)
        outg_far[cols, :] = nn(turned, chip_ref[:, own_heads:]).astype(bf)

    for n in range(halves):
        give_rows(8, n).wait_send()
        swap_rows(10, bchip, n).wait_send()
    back.wait_recv()
    target.wait_send()
    fetch = pltpu.make_async_copy(layer_out_ref, grad, recvs.at[stage_base])
    fetch.start()
    fetch.wait()
    error = jnp.zeros((1, 128), f32)
    for n in range(tokens // 128):
        rows = slice(n * 128, (n + 1) * 128)
        for f in range(grad.shape[1] // 128):
            cols = slice(f * 128, (f + 1) * 128)
            off = grad[rows, cols].astype(f32) - teacher_ref[rows, cols].astype(f32)
            error = error + jnp.sum(off * off * valid_ref[rows, :].astype(f32), axis=0, keepdims=True)
    early_ref[6:7, 0:128] = error
    vectors[0, 0:8, :] = early_ref[...]
    vectors[0, 8:16, :] = jnp.zeros((8, features), f32)
    vectors[0, pl.ds(8 + p.col, 1), :] = up_sums_ref[0]
    vectors[0, pl.ds(8 + p.far, 1), :] = up_sums_ref[1]
    summed = Tally(p, vectors, ("row", "col", "dp"), sems, base)
    base = summed.next_sem
    lately = Tally(p, late, ("row", "dp", "col"), sems, base)
    base = lately.next_sem
    summed.send(0)
    for n in (0, 1):
        share_grad_came(n).wait_recv()
        share_grad(n).wait_send()
    s_out.start()


    def turn(i):
        for at, action in back_plan:
            @pl.when(i == at)
            def _():
                action()

    back_plan = [
        (2, lambda: (s_down.first_sum(), s_down.second_copy().start())),
        (3, lambda: (s_out.first_sum(), s_out.second_copy().start())),
        (4, lambda: z_down.row_half()),
        (5, lambda: (s_down.second_sum(), s_down.start_rows(), s_out.second_sum(), s_out.start_rows())),
        (6, lambda: (s_up.first_sum(), s_up.second_copy().start())),
        (7, lambda: (z_up.row_half(), z_down.row_sum(), summed.add(0), summed.send(1))),
    ]

    def attend_back(*scratch):
        attention_rows_backward(heads, turn, Slopes(heads), mixed_ref, dout, att_ref, lse_ref, mixed_ref, *scratch)

    pl.run_scoped(
        attend_back,
        pltpu.VMEM((pairs, blocks, 2 * BLOCK, PAIR), bf), pltpu.VMEM((pairs, blocks, BLOCK, PAIR), bf),
        pltpu.VMEM((pairs, blocks, 2 * BLOCK, PAIR), bf), pltpu.VMEM((pairs, blocks, BLOCK, PAIR), bf),
        pltpu.VMEM((pairs, blocks, 2 * BLOCK, PAIR), bf), pltpu.VMEM((heads, blocks, BLOCK), f32),
        pltpu.VMEM((heads, BLOCK, BLOCK), f32), pltpu.VMEM((heads, BLOCK, PAIR), f32),
        pltpu.VMEM((pairs, blocks, BLOCK, PAIR), f32), pltpu.VMEM((pairs, blocks, BLOCK, PAIR), f32),
        pltpu.VMEM((pairs, blocks, BLOCK, PAIR), f32),
    )

    @pl.loop(0, features // 128)
    def _(f):
        cols = hint(f, 128)
        jgrad[cols, :] = tn(nall_ref[:, cols], mixed_ref[...]).astype(bf)

    s_joined.start()

    sums_at = [bchip.at[pl.ds(0, quarter)], bchip.at[pl.ds(quarter, quarter)],
               normed.at[pl.ds(0, quarter)], normed.at[pl.ds(quarter, quarter)]]
    near_in = [gchip.at[pl.ds(0, quarter)], gchip.at[pl.ds(quarter, quarter)]]

    def product(index, slot):
        @pl.loop(0, quarter // 256)
        def _(n):
            rows = pl.ds(pl.multiple_of(index * quarter + n * 256, 256), 256)
            sums_at[slot][hint(n, 256), :] = nt(mixed_ref[rows, :], jall_ref[...]).astype(bf)

    grad_near = [remote(sums_at[n], near_in[n], sems, base + n, {"col": p.near}) for n in (0, 1)]
    grad_far = remote(sums_at[2], take, sems, base + 2, {"col": p.far})
    base += 3
    product(p.corner, 0)
    grad_near[0].start()
    product(p.near, 1)
    grad_near[1].start()
    product(p.far, 2)
    grad_near[0].wait()
    add_rows(sums_at[2], [sums_at[2], near_in[0]])
    grad_far.start()
    product(p.col, 3)
    s_up.second_sum()
    s_up.start_rows()
    z_down.far_sum()
    s_down.row_half()
    s_out.row_half()
    z_up.row_sum()
    sums = jnp.zeros((1, mixed_ref.shape[1]), f32)
    for n in range(tokens // 256):
        sums = sums + jnp.sum(mixed_ref[n * 256 : (n + 1) * 256, :].astype(f32), axis=0, keepdims=True)
    late[0] = jnp.zeros((8, features), f32)
    late[0, 2:3, 0 : sums.shape[1]] = sums
    s_joined.first_sum()
    s_joined.start_rows()
    s_up.row_half()
    z_down.twin_sum()
    grad_near[1].wait()
    grad_far.wait()
    gin = bchip.at[pl.ds(0, quarter)]
    grad_back = Untranspose(p, gin, input_grad_ref, sems, base)
    base += 4

    @pl.loop(0, quarter // 64)
    def _(n):
        rows = hint(n, 64)
        value = sums_at[3][rows, :].astype(f32) + near_in[1][rows, :].astype(f32) + take[rows, :].astype(f32)
        standard, inverse = moments(xt_ref[rows, :].astype(f32))
        late[0, 0:1, :] += jnp.sum(value * standard, axis=0, keepdims=True)
        late[0, 1:2, :] += jnp.sum(value, axis=0, keepdims=True)
        scaled = value * vall_ref[0:1, :]
        one = jnp.mean(scaled, 1, keepdims=True)
        two = jnp.mean(scaled * standard, 1, keepdims=True)
        gin[rows, :] = (gres[rows, :] + inverse * (scaled - one - standard * two)).astype(bf)

    lately.send(0)
    s_joined.row_half()
    grad_back.start()
    z_up.far_sum()
    s_down.row_sum()
    z_up.twin_sum()
    s_up.row_sum()
    s_out.row_sum()
    for n in range(1, len(summed.stages)):
        summed.add(n)
        if n + 1 < len(summed.stages):
            summed.send(n + 1)
    lately.add(0)
    lately.send(1)
    s_joined.row_sum()
    for n in range(1, len(lately.stages)):
        lately.add(n)
        if n + 1 < len(lately.stages):
            lately.send(n + 1)
    joined_at = lately.after(len(lately.stages) - 2)
    at = 0
    for n in range(6):
        place = hint(p.row, width)
        value = late[lately.last, n : n + 1, place] if n < 2 else vectors[summed.last, n : n + 1, place]
        for m in range(lanes):
            vector_sum_ref[at : at + 1, :] = value[:, m * 128 : (m + 1) * 128]
            at += 1
    value = vectors[summed.last, pl.ds(8 + p.col, 1), :]
    for m in range(hidden // 128):
        vector_sum_ref[at : at + 1, :] = value[:, m * 128 : (m + 1) * 128]
        at += 1
    for n in range(heads // 2):
        first, second, third = (
            late[joined_at, 2:3, (3 * n + m) * 128 : (3 * n + m + 1) * 128] for m in range(3)
        )
        vector_sum_ref[at : at + 1, :] = jnp.where(lo, first, swap(second))
        vector_sum_ref[at + 1 : at + 2, :] = jnp.where(lo, swap(second), third)
        at += 2
    value = jnp.sum(vectors[summed.last, 6:7, 0:128], axis=1, keepdims=True) * (scale * (1.0 / (features * token_total)))
    vector_sum_ref[at:, :] = jnp.broadcast_to(value, (vector_sum_ref.shape[0] - at, 128))
    for part in (s_down, s_up, z_down, z_up, s_joined, s_out):
        part.finish()
    grad_back.wait_recv()
    grad_back.wait_send()
    for n in (0, 1):
        moved[n].wait_send()
        for copies in (to_far, to_near, pass_on):
            copies[n].wait_send()
    w_joined.sent()
    back.wait_send()

    @pl.loop(0, per_chip)
    def _(n):
        share(n, n + per_chip * (1 - p.chip)).wait_send()


def layer_stage(small, joined, layer_in, up, down, out, teacher, cot, token_total):
    tokens, width = layer_in.shape
    quarter = tokens // 4
    features = width * lax.axis_size("row")
    joined_width = joined.shape[1]
    heads = joined_width // (3 * HEAD_DIM)
    blocks = tokens // BLOCK
    f32, bf = jnp.float32, jnp.bfloat16
    hidden, head_rows = down.shape[0], out.shape[0]
    vmem, anyspace = pl.BlockSpec(memory_space=pltpu.VMEM), pl.BlockSpec(memory_space=pl.ANY)
    shape = jax.ShapeDtypeStruct
    bits = 0
    while (1 << bits) < lax.axis_size("dp"):
        bits += 1
    count = (
        3 * TRANSPOSE_SEMS + 4 + 4 * WEIGHT_SEMS + HALVES_SEMS + 6 + (3 + bits) + 1 + 6 + blocks // 2 + 12
        + 4 * SHARE_SEMS + 2 * ROWS_FIRST_SEMS + 2 + 2 + 2 * (6 + bits) + 3 + 4
    )
    small_rows = 8 * ((6 * width // 128 + hidden // 128 + heads) // 8 + 1)
    outs = pl.pallas_call(
        functools.partial(layer_kernel, heads, token_total),
        out_shape=(
            shape((tokens, width), bf), shape((tokens, width), bf), shape((width, hidden), bf), shape((width, hidden), bf),
            shape((width, head_rows), bf), shape((width, joined_width), bf), shape((small_rows, 128), f32),
        ) + (shape((features, hidden), bf),) * 4 + (
            shape((1, features, hidden // 2), bf), shape((1, features, hidden // 2), bf), shape((features, head_rows), bf),
            shape((features, joined_width // 2), bf), shape((features, hidden // 4), bf), shape((features, hidden // 4), bf),
            shape((features, head_rows // 2), bf), shape((3, width, hidden // 4), bf), shape((3, width, hidden // 4), bf),
            shape((3, width, head_rows // 2), bf), shape((3, width, joined_width // 2), bf),
            shape((2, 4, width, hidden // 2), bf), shape((2, 2, width, hidden // 2), bf), shape((2, width, hidden // 2), bf),
            shape((2, width, hidden // 4), bf),
        ),
        in_specs=[vmem] + [anyspace] * 5 + [vmem] * 2,
        out_specs=(anyspace,) * 2 + (vmem,) * 5 + (anyspace,) * 19,
        scratch_shapes=[
            pltpu.VMEM((quarter, features), bf), pltpu.VMEM((tokens, features), bf), pltpu.VMEM((tokens, joined_width), bf),
            pltpu.VMEM((tokens, heads * HEAD_DIM), bf), pltpu.VMEM((heads, blocks, BLOCK), f32),
            pltpu.VMEM((features, joined_width), bf), pltpu.VMEM((8, features), f32), pltpu.VMEM((8, features), f32),
            pltpu.VMEM((2, 1, hidden), f32),
            pltpu.VMEM((2 * quarter, 2 * head_rows), bf), pltpu.VMEM((quarter, features), bf), pltpu.VMEM((quarter, 128), bf),
            pltpu.VMEM((2, features, hidden), bf), pltpu.VMEM((2, hidden + head_rows, features), bf),
            pltpu.VMEM((2, 8, hidden), f32), pltpu.VMEM((2 * quarter, features), bf), pltpu.VMEM((2 * quarter, features), bf),
            pltpu.VMEM((2 * quarter, features), bf), pltpu.VMEM((quarter, features), bf), pltpu.VMEM((quarter, features), bf),
            pltpu.VMEM((quarter, features), f32), pltpu.VMEM((quarter, features), f32), pltpu.VMEM((quarter, features), bf),
            pltpu.VMEM((2, 512, hidden), bf), pltpu.VMEM((tokens, width), bf), pltpu.VMEM((2 * quarter, head_rows), bf),
            pltpu.VMEM((tokens, head_rows), bf), pltpu.VMEM((2, 2, quarter, width), bf),
            pltpu.VMEM((tally_slots(bits, ("row", "col", "dp")), 16, features), f32),
            pltpu.VMEM((tally_slots(bits, ("row", "col", "dp")), 8, features), f32),
            pltpu.VMEM((tally_slots(bits, ("col", "dp")), 8, 128), f32),
            pltpu.VMEM((tokens, 128), bf), pltpu.VMEM((8, joined_width), f32),
            pltpu.SemaphoreType.REGULAR, pltpu.SemaphoreType.DMA((count,)), pltpu.SemaphoreType.DMA((count,)),
        ],
        compiler_params=pltpu.CompilerParams(vmem_limit_bytes=63 << 20, collective_id=1, has_side_effects=True),
        name="layer_stage",
    )(small, joined, layer_in, up, down, out, teacher, cot)
    return outs[:7]


def swap_with(value, axis, bit):
    size = lax.axis_size(axis)
    return lax.ppermute(value, axis, [(i, i ^ bit) for i in range(size)])


def low(value):
    return value.astype(jnp.bfloat16)


def sum_other_pairs(value):
    bit = 2
    while bit < lax.axis_size("dp"):
        value = value + swap_with(low(value), "dp", bit).astype(jnp.float32)
        bit *= 2
    return value


def on_device(
    layer_in,
    first_gain,
    first_shift,
    joined_weight,
    joined_bias,
    out_weight,
    out_bias,
    second_gain,
    second_shift,
    up_weight,
    up_bias,
    down_weight,
    down_bias,
    teacher,
    valid,
    cotangent,
):
    f32 = jnp.float32
    token_total = layer_in.shape[0] * lax.axis_size("dp") * lax.axis_size("col")
    arrays = (
        first_gain, first_shift, out_bias, second_gain, second_shift, down_bias, up_bias, joined_bias.reshape(-1), valid,
    )
    rows, at = sum(a.size for a in arrays), 0
    small = jnp.zeros((rows,), f32)
    for a in arrays:
        small = small + jnp.pad(a.astype(f32), (at, rows - at - a.size))
        at += a.size
    small = small.reshape(-1, 128)
    layer_out, input_grad, up_grad, down_grad, out_grad, joined_grad, sums = layer_stage(
        small, joined_weight, layer_in, up_weight, down_weight, out_weight, teacher, cotangent, token_total
    )
    up_grad, down_grad, out_grad, joined_grad = (
        sum_other_pairs(g.astype(f32)) for g in (up_grad, down_grad, out_grad, joined_grad)
    )
    sums = sums.reshape(-1)
    pieces, at = [], 0
    for size in [layer_in.shape[1]] * 6 + [up_bias.shape[0], joined_bias.size, 1]:
        pieces.append(sums[at : at + size])
        at += size
    return (
        layer_out,
        pieces[8][0],
        input_grad.astype(f32),
        pieces[0],
        pieces[1],
        joined_grad,
        pieces[7].reshape(joined_bias.shape),
        out_grad.T,
        pieces[2],
        pieces[3],
        pieces[4],
        up_grad,
        pieces[6],
        down_grad.T,
        pieces[5],
    )


def solution(mesh):
    return jax.shard_map(
        on_device,
        mesh=mesh,
        in_specs=(
            P(("dp", "col"), "row"),
            P("row"),
            P("row"),
            P("row", "col"),
            P("col", None),
            P("col", "row"),
            P("row"),
            P("row"),
            P("row"),
            P("row", "col"),
            P("col"),
            P("col", "row"),
            P("row"),
            P(("dp", "col"), "row"),
            P(("dp", "col")),
            P(("dp", "col"), "row"),
        ),
        out_specs=(
            P(("dp", "col"), "row"),
            P(),
            P(("dp", "col"), "row"),
            P("row"),
            P("row"),
            P("row", "col"),
            P("col", None),
            P("col", "row"),
            P("row"),
            P("row"),
            P("row"),
            P("row", "col"),
            P("col"),
            P("col", "row"),
            P("row"),
        ),
        check_vma=False,
    )
```

```python
import functools
import math

import jax
import jax.numpy as jnp
from jax import lax
from jax.experimental import pallas as pl
from jax.experimental.pallas import tpu as pltpu
from jax.sharding import PartitionSpec as P

D = 1024
HEADS = 16
SEQ = 2048
EPSILON = 1e-05
LOG2E = 1.4426950408889634
HEAD_DIM=64
BLOCK=256
HALF=64
PAIR=128
SCALE2 = LOG2E/8.0

def nt(a,b):
    return lax.dot_general(a,b,(((1,),(1,)),((),())),preferred_element_type=jnp.float32)
def nn(a,b):
    return jnp.dot(a,b,preferred_element_type=jnp.float32)
def tn(a,b):
    return lax.dot_general(a,b,(((0,),(0,)),((),())),preferred_element_type=jnp.float32)

def low_lanes(rows):
    return lax.broadcasted_iota(jnp.int32,(rows,PAIR),1) < HALF

def swap(a):
    return jnp.concatenate([a[:,HALF:],a[:,:HALF]],axis=1)

def attention_rows(heads, order, after, slopes, mixed_ref, out_ref, lse_ref, qs, ks, vs, bias, sc, mx, ls, acc):
    pairs=heads//2
    blocks=mixed_ref.shape[0]//BLOCK
    lo=low_lanes(BLOCK)
    @pl.loop(0,blocks)
    def _(b):
        rows=pl.ds(pl.multiple_of(b*BLOCK,BLOCK),BLOCK)
        for p in range(pairs):
            t0,t1,t2=(mixed_ref[rows,(3*p+n)*PAIR:(3*p+n+1)*PAIR] for n in range(3))
            zero=jnp.zeros_like(t0)
            qs[2*p,b]=jnp.where(lo,t0,zero)
            qs[2*p+1,b]=jnp.where(lo,zero,t1)
            ks[p,b]=jnp.where(lo,swap(t0),swap(t2))
            vs[p,b,:BLOCK]=jnp.where(lo,t1,zero)
            vs[p,b,BLOCK:]=jnp.where(lo,zero,t2)
    il=lax.broadcasted_iota(jnp.int32,(BLOCK,BLOCK),0)
    jl=lax.broadcasted_iota(jnp.int32,(BLOCK,BLOCK),1)
    tent=jnp.minimum(jl,2*il-jl).astype(jnp.float32)
    for h in range(heads):
        bias[h]=tent*slopes[h]
    jrow=lax.broadcasted_iota(jnp.int32,(1,BLOCK),1)
    @pl.loop(0,blocks)
    def _(it):
        i=order(it)
        for h in range(heads):
            t=nt(qs[h,i],ks[h//2,i])*SCALE2+bias[h]
            sc[h,i]=t
            mx[h]=jnp.maximum(t[:,:PAIR],t[:,PAIR:])
        @pl.loop(0,i)
        def _(j):
            place=(jrow+(j-i)*BLOCK).astype(jnp.float32)
            for h in range(heads):
                t=nt(qs[h,i],ks[h//2,j])*SCALE2+place*slopes[h]
                sc[h,j]=t
                mx[h]=jnp.maximum(mx[h],jnp.maximum(t[:,:PAIR],t[:,PAIR:]))
        for h in range(heads):
            mx[h]=jnp.broadcast_to(jnp.max(mx[h],1,keepdims=True),(BLOCK,PAIR))
            ls[h]=jnp.zeros((BLOCK,PAIR),jnp.float32)
        for p in range(pairs):
            acc[p]=jnp.zeros((BLOCK,PAIR),jnp.float32)
        @pl.loop(0,i+1)
        def _(j):
            for p in range(pairs):
                both=[]
                for h in (2*p,2*p+1):
                    m=mx[h]
                    ea=jnp.exp2(sc[h,j,:,:PAIR]-m)
                    eb=jnp.exp2(sc[h,j,:,PAIR:]-m)
                    ls[h]+=ea+eb
                    both+=[ea.astype(jnp.bfloat16),eb.astype(jnp.bfloat16)]
                acc[p]+=nn(jnp.concatenate(both,1),vs[p,j])
        rows=pl.ds(pl.multiple_of(i*BLOCK,BLOCK),BLOCK)
        for p in range(pairs):
            tot=[jnp.broadcast_to(jnp.sum(ls[h],1,keepdims=True),(BLOCK,PAIR)) for h in (2*p,2*p+1)]
            out_ref[rows,p*PAIR:(p+1)*PAIR]=(acc[p]/jnp.where(lo,tot[0],tot[1])).astype(out_ref.dtype)
            for n,h in enumerate((2*p,2*p+1)):
                lse=mx[h]+jnp.log2(tot[n])
                lse_ref[h,pl.ds(i,1),:]=lse.T[:1]
        after(it,i)

def attention_rows_backward(heads, after, slopes, mixed_ref, dout_ref, out_ref, lse_ref, grad_ref, qs, ks, km, vp, ds_, delta, bias, steep, dq, dk, dv):
    pairs=heads//2
    blocks=mixed_ref.shape[0]//BLOCK
    lo=low_lanes(BLOCK)
    @pl.loop(0,blocks)
    def _(b):
        rows=pl.ds(pl.multiple_of(b*BLOCK,BLOCK),BLOCK)
        for p in range(pairs):
            t0,t1,t2=(mixed_ref[rows,(3*p+n)*PAIR:(3*p+n+1)*PAIR] for n in range(3))
            zero=jnp.zeros_like(t0)
            qs[p,b,:BLOCK]=jnp.where(lo,t0,zero)
            qs[p,b,BLOCK:]=jnp.where(lo,zero,t1)
            k=jnp.where(lo,swap(t0),swap(t2))
            ks[p,b]=k
            km[p,b,:BLOCK]=jnp.where(lo,k,zero)
            km[p,b,BLOCK:]=jnp.where(lo,zero,k)
            vp[p,b]=jnp.where(lo,t1,t2)
            d=dout_ref[rows,p*PAIR:(p+1)*PAIR]
            ds_[p,b,:BLOCK]=jnp.where(lo,d,zero)
            ds_[p,b,BLOCK:]=jnp.where(lo,zero,d)
            prod=(d.astype(jnp.float32)*out_ref[rows,p*PAIR:(p+1)*PAIR].astype(jnp.float32)).T
            delta[2*p,pl.ds(b,1),:]=jnp.sum(prod[:HALF],0,keepdims=True)
            delta[2*p+1,pl.ds(b,1),:]=jnp.sum(prod[HALF:],0,keepdims=True)
    kl=lax.broadcasted_iota(jnp.int32,(BLOCK,BLOCK),0)
    ql=lax.broadcasted_iota(jnp.int32,(BLOCK,BLOCK),1)
    tent=jnp.minimum(kl,2*ql-kl).astype(jnp.float32)
    ramp=kl.astype(jnp.float32)
    for h in range(heads):
        bias[h]=tent*slopes[h]
        steep[h]=ramp[:,:PAIR]*slopes[h]
    def block(i,j,first):
        for p in range(pairs):
            ps=[];gs=[]
            for n,h in enumerate((2*p,2*p+1)):
                q=qs[p,i,n*BLOCK:(n+1)*BLOCK]
                d=ds_[p,i,n*BLOCK:(n+1)*BLOCK]
                row=slopes[h]*((j-i)*BLOCK).astype(jnp.float32)-lse_ref[h,pl.ds(i,1),:]
                t=nt(ks[p,j],q)*SCALE2+row+(bias[h] if first else jnp.concatenate([steep[h],steep[h]],1))
                e=jnp.exp2(t)
                g=e*(nt(vp[p,j],d)-delta[h,pl.ds(i,1),:])
                ps.append(e.astype(jnp.bfloat16)); gs.append(g.astype(jnp.bfloat16))
            gv=nn(jnp.concatenate(ps,1),ds_[p,i])
            gk=nn(jnp.concatenate(gs,1),qs[p,i])
            gq=tn(jnp.concatenate(gs,0),km[p,j])
            if first:
                dv[p,j]=gv; dk[p,j]=gk; dq[p,i]=gq
            else:
                dv[p,j]+=gv; dk[p,j]+=gk; dq[p,i]+=gq
    @pl.loop(0,blocks)
    def _(i):
        block(i,i,True)
        @pl.loop(0,i)
        def _(j):
            block(i,j,False)
        after(i)
    @pl.loop(0,blocks)
    def _(b):
        rows=pl.ds(pl.multiple_of(b*BLOCK,BLOCK),BLOCK)
        for p in range(pairs):
            a=dq[p,b]*0.125; k=swap(dk[p,b]*0.125); v=dv[p,b]
            for n,t in enumerate((jnp.where(lo,a,k),jnp.where(lo,v,a),jnp.where(lo,k,v))):
                grad_ref[rows,(3*p+n)*PAIR:(3*p+n+1)*PAIR]=t.astype(grad_ref.dtype)


MESH = pl.DeviceIdType.MESH


def hint(index, size):
    return pl.ds(pl.multiple_of(index * size, size), size)


def remote(src, dst, sems, number, target):
    send, recv = sems
    return pltpu.make_async_remote_copy(
        src_ref=src, dst_ref=dst, send_sem=send.at[number], recv_sem=recv.at[number],
        device_id=target, device_id_type=MESH,
    )


def partner(index, bit):
    return index + bit - 2 * bit * ((index // bit) % 2)


class Place:
    def __init__(self):
        self.dp, self.row, self.col = (lax.axis_index(a) for a in ("dp", "row", "col"))
        self.dps = lax.axis_size("dp")
        self.core, self.chip = self.col % 2, self.col // 2
        self.near, self.far = partner(self.col, 1), partner(self.col, 2)
        self.twin = partner(self.dp, 1)
        self.half = self.dp % 2
        self.plane = 3 * self.core + self.chip - 2 * self.core * self.chip
        self.source = 2 * (((self.row + 1) // 2) % 2) + self.row // 2
        self.corner = partner(self.far, 1)
        self.stays = self.plane == self.row
        self.far_plane = 3 * self.core + (1 - self.chip) - 2 * self.core * (1 - self.chip)
        self.sender = 2 * self.chip + self.source % 2
        self.home = jnp.logical_or(self.stays, self.far_plane == self.row)


def greet(place):
    barrier = pltpu.get_barrier_semaphore()

    def signal(target):
        pl.semaphore_signal(barrier, inc=1, device_id=target, device_id_type=MESH)

    for step in (1, 2, 3):
        signal({"row": (place.row + step) % 4})
    for col in (place.near, place.far, place.corner):
        signal({"col": col})
    amount = 6
    bit = 1
    while bit < place.dps:
        signal({"dp": partner(place.dp, bit)})
        amount += 1
        bit *= 2

    for plane, stays in ((place.plane, place.stays), (place.far_plane, place.far_plane == place.row)):
        signal({"row": plane, "col": place.near})

        @pl.when(jnp.logical_not(stays))
        def _():
            signal({"row": plane, "col": place.col})

    for other in range(4):
        @pl.when(jnp.logical_not(jnp.logical_and(place.home, place.row == other)))
        def _():
            signal({"row": other, "col": place.sender})

        @pl.when(jnp.logical_not(jnp.logical_and(place.stays, place.col == other)))
        def _():
            signal({"row": place.plane, "col": other})

        @pl.when(jnp.logical_not(jnp.logical_and(place.stays, place.row == other)))
        def _():
            signal({"row": other, "col": place.source})

    amount = amount + 16 - 2 * place.home.astype(jnp.int32) - 2 * place.stays.astype(jnp.int32)
    pl.semaphore_wait(barrier, amount)


class Transpose:
    def __init__(self, place, src, dst, relay, sems, first, part=0, parts=1):
        self.p, self.src, self.dst, self.relay, self.sems, self.first = place, src, dst, relay, sems, first
        self.quarter, self.width = src.shape[0] // 4, src.shape[1]
        self.rows = self.quarter // parts
        self.offset = part * self.rows

    def tokens(self, quarter):
        return self.src.at[pl.ds(pl.multiple_of(quarter * self.quarter + self.offset, self.rows), self.rows)]

    def part(self):
        return self.dst.at[pl.ds(self.offset, self.rows), hint(self.p.row, self.width)]

    def cross(self, n):
        src = self.tokens(2 * (1 - self.p.chip) + n)
        return remote(src, self.relay.at[n], self.sems, self.first + 4 + n, {"col": self.p.far})

    def out(self, relayed, n):
        p = self.p
        col = p.col if n == 0 else p.near
        src = self.relay.at[col % 2] if relayed else self.tokens(col)
        return pltpu.make_async_remote_copy(
            src_ref=src, dst_ref=self.part(),
            send_sem=self.sems[0].at[self.first + 2 * relayed + n], recv_sem=self.sems[1].at[self.first + p.row],
            device_id={"row": p.far_plane if relayed else p.plane, "col": col}, device_id_type=MESH,
        )

    def kept(self, relayed):
        p = self.p
        src = self.relay.at[p.core] if relayed else self.tokens(p.col)
        return pltpu.make_async_copy(src, self.part(), self.sems[1].at[self.first + p.row])

    def leaves(self, relayed):
        return (self.p.far_plane if relayed else self.p.plane) != self.p.row

    def send(self, relayed):
        self.out(relayed, 1).start()

        @pl.when(self.leaves(relayed))
        def _():
            self.out(relayed, 0).start()

        @pl.when(jnp.logical_not(self.leaves(relayed)))
        def _():
            self.kept(relayed).start()

    def start_cross(self):
        for n in (0, 1):
            self.cross(n).start()

    def forward(self):
        for n in (0, 1):
            self.cross(n).wait_recv()
        self.send(1)

    def wait_recv(self):
        p = self.p
        for other in range(4):
            mine = jnp.logical_and(p.home, p.row == other)
            part = self.dst.at[pl.ds(self.offset, self.rows), pl.ds(other * self.width, self.width)]

            @pl.when(jnp.logical_not(mine))
            def _():
                pltpu.make_async_remote_copy(
                    src_ref=part, dst_ref=part, send_sem=self.sems[0].at[self.first + other],
                    recv_sem=self.sems[1].at[self.first + other],
                    device_id={"row": other, "col": p.sender}, device_id_type=MESH,
                ).wait_recv()

            @pl.when(mine)
            def _():
                self.kept(0).wait()

    def wait_send(self):
        for n in (0, 1):
            self.cross(n).wait_send()
        for relayed in (0, 1):
            self.out(relayed, 1).wait_send()

            @pl.when(self.leaves(relayed))
            def _():
                self.out(relayed, 0).wait_send()


TRANSPOSE_SEMS = 6


class Slopes:
    def __init__(self, heads):
        self.heads = heads
        col = lax.axis_index("col")
        self.column = jnp.float32(1.0)
        for c in range(1, lax.axis_size("col")):
            self.column = jnp.where(col == c, jnp.float32(2.0 ** (-8.0 * heads * c / HEADS)), self.column)

    def __getitem__(self, head):
        return self.column * (2.0 ** (-8.0 * (head + 1) / HEADS) * LOG2E)


class Weight:
    def __init__(self, place, src, dst, offset, by_rows, last, sems, first):
        self.p, self.src, self.dst, self.offset, self.by_rows, self.last = place, src, dst, offset, by_rows, last
        self.sems, self.first = sems, first
        self.rows, self.width = src.shape
        self.part = self.rows // 2

    def whole(self, side, row):
        if self.by_rows:
            return self.dst.at[side, hint(row, self.rows)]
        return self.dst.at[side, pl.ds(self.offset, self.rows), hint(row, self.width)]

    def piece(self, side, row, half):
        if self.by_rows:
            return self.dst.at[side, hint(row * 2 + half, self.part)]
        start = pl.multiple_of(self.offset + half * self.part, self.part)
        return self.dst.at[side, pl.ds(start, self.part), hint(row, self.width)]

    def other(self, step):
        return (self.p.row + 4 - step) % 4

    def move(self, src, dst, number, target):
        return remote(src, dst, self.sems, self.first + number, target)

    def pass_on(self, side, step, half, number, target):
        src = self.piece(side, self.other(step), half)
        dst = self.piece(1 if "col" in target else side, self.other(step), half)
        return self.move(src, dst, number + step - 1, target)

    def own(self):
        return pltpu.make_async_copy(self.src, self.whole(0, self.p.row), self.sems[1].at[self.first])

    def across(self):
        return self.move(self.src, self.whole(1, self.p.row), 1, {"col": self.p.far})

    def along(self, step):
        p = self.p
        return self.move(
            self.src.at[hint(p.half, self.part)], self.piece(0, p.row, p.half), 1 + step, {"row": (p.row + step) % 4}
        )

    def to_twin(self, step):
        return self.pass_on(0, step, self.p.half, 5, {"dp": self.p.twin})

    def to_far(self, step):
        return self.pass_on(0, step, self.p.half, 8, {"col": self.p.far})

    def onward(self, step):
        if self.last == "y":
            return self.pass_on(0, step, 1 - self.p.half, 11, {"col": self.p.far})
        return self.pass_on(1, step, self.p.half, 11, {"dp": self.p.twin})

    def arrival(self, side, step, half, number):
        part = self.piece(side, self.other(step), half)
        return self.move(part, part, number + step - 1, {"dp": self.p.twin})

    def start_along(self):
        for step in (1, 2, 3):
            self.along(step).start()

    def spread(self, steps=(1, 2, 3)):
        for step in steps:
            self.arrival(0, step, self.p.half, 2).wait_recv()
            self.to_twin(step).start()
            self.to_far(step).start()

    def spread_last(self, steps=(1, 2, 3)):
        p = self.p
        for step in steps:
            if self.last == "y":
                self.arrival(0, step, 1 - p.half, 5).wait_recv()
            else:
                self.arrival(1, step, p.half, 8).wait_recv()
            self.onward(step).start()

    def ready(self, side):
        p = self.p
        if side == 0:
            self.own().wait()
        else:
            self.across().wait_recv()
        for step in (1, 2, 3):
            if side == 0 and self.last == "x":
                self.arrival(0, step, 1 - p.half, 5).wait_recv()
            if side == 1 and self.last == "y":
                self.arrival(1, step, p.half, 8).wait_recv()
            if side == 1:
                self.arrival(1, step, 1 - p.half, 11).wait_recv()

    def sent(self):
        self.across().wait_send()
        for step in (1, 2, 3):
            for copy in (self.along(step), self.to_twin(step), self.to_far(step), self.onward(step)):
                copy.wait_send()


WEIGHT_SEMS = 14


class Halves:
    def __init__(self, place, src, dst, sems, first):
        self.p, self.src, self.dst, self.sems, self.first = place, src, dst, sems, first
        self.rows = src.shape[0]
        self.part = self.rows // 2

    def own(self):
        return pltpu.make_async_copy(self.src, self.dst.at[hint(self.p.row, self.rows)], self.sems[1].at[self.first])

    def along(self, step):
        p = self.p
        return remote(
            self.src.at[hint(p.half, self.part)], self.dst.at[hint(2 * p.row + p.half, self.part)], self.sems,
            self.first + step, {"row": (p.row + step) % 4},
        )

    def part_of(self, step, half):
        return self.dst.at[hint(2 * ((self.p.row + 4 - step) % 4) + half, self.part)]

    def to_twin(self, step, half):
        part = self.part_of(step, half)
        return remote(part, part, self.sems, self.first + 3 + step, {"dp": self.p.twin})

    def start(self):
        self.own().start()
        for step in (1, 2, 3):
            self.along(step).start()

    def spread(self):
        p = self.p
        for step in (1, 2, 3):
            part = self.part_of(step, p.half)
            remote(part, part, self.sems, self.first + step, {"dp": p.twin}).wait_recv()
            self.to_twin(step, p.half).start()

    def ready(self):
        p = self.p
        for step in (1, 2, 3):
            self.to_twin(step, 1 - p.half).wait_recv()
        self.own().wait()

    def sent(self):
        for step in (1, 2, 3):
            self.along(step).wait_send()
            self.to_twin(step, self.p.half).wait_send()


HALVES_SEMS = 7


GELU_ROOT = math.sqrt(2.0 / math.pi)
GELU_CUBE = 0.044715


def gelu_pair(x):
    square = x * x
    t = jnp.tanh(GELU_ROOT * x * (1.0 + GELU_CUBE * square))
    half = 0.5 * (1.0 + t)
    slope = half + 0.5 * x * (1.0 - t * t) * (GELU_ROOT * (1.0 + 3.0 * GELU_CUBE * square))
    return x * half, slope


def moments(x):
    center = jnp.mean(x, 1, keepdims=True)
    spread = jnp.mean(x * x, 1, keepdims=True) - center * center
    inverse = lax.rsqrt(spread + EPSILON)
    return (x - center) * inverse, inverse


class Chip:
    def __init__(self, place, sems, first):
        self.p, self.sems, self.first = place, sems, first

    def copy(self, number, src, dst):
        return remote(src, dst, self.sems, self.first + number, {"col": self.p.near})


class Untranspose:
    def __init__(self, place, src, dst, sems, first):
        self.place, self.src, self.dst, self.sems, self.first = place, src, dst, sems, first
        self.rows, self.width = src.shape[0], src.shape[1] // 4

    def out(self, other):
        p = self.place
        return pltpu.make_async_remote_copy(
            src_ref=self.src.at[:, pl.ds(other * self.width, self.width)],
            dst_ref=self.dst.at[hint(p.col, self.rows)],
            send_sem=self.sems[0].at[self.first + other], recv_sem=self.sems[1].at[self.first + p.col],
            device_id={"row": other, "col": p.source}, device_id_type=MESH,
        )

    def kept(self):
        p = self.place
        return pltpu.make_async_copy(
            self.src.at[:, hint(p.row, self.width)],
            self.dst.at[hint(p.col, self.rows)],
            self.sems[1].at[self.first + p.col],
        )

    def start(self):
        p = self.place
        for other in range(4):
            @pl.when(jnp.logical_not(jnp.logical_and(p.stays, p.row == other)))
            def _():
                self.out(other).start()

        @pl.when(p.stays)
        def _():
            self.kept().start()

    def wait_recv(self):
        p = self.place
        for other in range(4):
            mine = jnp.logical_and(p.stays, p.col == other)
            part = self.dst.at[pl.ds(other * self.rows, self.rows)]

            @pl.when(jnp.logical_not(mine))
            def _():
                pltpu.make_async_remote_copy(
                    src_ref=part, dst_ref=part, send_sem=self.sems[0].at[self.first + other],
                    recv_sem=self.sems[1].at[self.first + other],
                    device_id={"row": p.plane, "col": other}, device_id_type=MESH,
                ).wait_recv()

            @pl.when(mine)
            def _():
                self.kept().wait()

    def wait_send(self):
        p = self.place
        for other in range(4):
            @pl.when(jnp.logical_not(jnp.logical_and(p.stays, p.row == other)))
            def _():
                self.out(other).wait_send()


def add_rows(total, pieces, rows=64):
    @pl.loop(0, total.shape[0] // rows)
    def _(n):
        part = hint(n, rows)
        value = pieces[0][part, :].astype(jnp.float32)
        for piece in pieces[1:]:
            value = value + piece[part, :].astype(jnp.float32)
        total[part, :] = value.astype(total.dtype)


class Share:
    def __init__(self, place, kind, own, far, result, came, other, rows, totals, slots, sems, first):
        self.p, self.kind, self.own, self.far, self.result = place, kind, own, far, result
        self.came, self.other_ref, self.rows, self.totals, self.slots = came, other, rows, totals, slots
        self.sems, self.first = sems, first
        self.width = own.shape[1]
        self.part = self.width // 2
        self.block = own.shape[0] // 4
        self.mine, self.theirs = hint(place.half, self.part), hint(1 - place.half, self.part)

    def first_copies(self):
        p = self.p
        if self.kind == "xy":
            return [
                remote(src.at[:, self.theirs], self.came[n], self.sems, self.first + n, {"dp": p.twin})
                for n, src in enumerate((self.own, self.far))
            ]
        if self.kind == "yx":
            return [remote(self.far, self.came, self.sems, self.first, {"col": p.far})]
        return [remote(self.own.at[:, self.theirs], self.came, self.sems, self.first, {"dp": p.twin})]

    def start(self):
        for copy in self.first_copies():
            copy.start()

    def gather_sum(self, jobs):
        blocks = []
        for total, sources in jobs:
            for n in range(4):
                part = pl.ds(n * self.block, self.block)
                blocks.append((total.at[part], [src.at[part] for src in sources]))
        self.block_sums(blocks)

    def block_sums(self, blocks):
        copies = []
        for n, (_, sources) in enumerate(blocks):
            copies.append([
                pltpu.make_async_copy(
                    src, self.slots[2 * (n % 2) + m].at[:, : src.shape[1]],
                    self.sems[1].at[self.first + 8 + 2 * (n % 2) + m],
                )
                for m, src in enumerate(sources)
            ])
        for copy in copies[0]:
            copy.start()
        for n, (total, sources) in enumerate(blocks):
            if n + 1 < len(blocks):
                for copy in copies[n + 1]:
                    copy.start()
            for copy in copies[n]:
                copy.wait()
            add_rows(total, [self.slots[2 * (n % 2) + m].at[:, : total.shape[1]] for m in range(len(sources))])

    def second_copy(self):
        p = self.p
        if self.kind == "xy":
            return remote(self.totals[1], self.other_ref, self.sems, self.first + 2, {"col": p.far})
        return remote(self.totals[0].at[:, self.theirs], self.other_ref, self.sems, self.first + 2, {"dp": p.twin})

    def first_sum(self):
        for copy in self.first_copies():
            copy.wait()
        if self.kind == "xy":
            self.gather_sum([
                (self.totals[1], [self.came[1], self.far.at[:, self.mine]]),
                (self.totals[0], [self.came[0], self.own.at[:, self.mine]]),
            ])
        elif self.kind == "yx":
            self.gather_sum([(self.totals[0], [self.came, self.own])])
        else:
            self.gather_sum([(self.totals[0], [self.came, self.own.at[:, self.mine]])])

    def total(self):
        return self.totals[1] if self.kind == "yx" else self.totals[0]

    def second_sum(self):
        self.second_copy().wait()
        if self.kind == "xy":
            self.gather_sum([(self.totals[0], [self.other_ref, self.totals[0]])])
        else:
            self.gather_sum([(self.totals[1], [self.other_ref, self.totals[0].at[:, self.mine]])])

    def row_copy(self, step):
        row = self.p.row
        target = partner(row, 1) if step < 2 else partner(row, 2)
        block = partner(target, 2) if step == 1 else target
        return remote(
            self.total().at[hint(block, self.block)], self.rows.at[step], self.sems, self.first + 3 + step, {"row": target}
        )

    def start_rows(self):
        for step in (1, 0):
            self.row_copy(step).start()

    def row_add(self, block, step, target):
        load = pltpu.make_async_copy(
            self.rows.at[step], self.slots[step].at[:, : self.part], self.sems[1].at[self.first + 8 + step]
        )
        load.start()
        load.wait()
        add_rows(target, [self.total().at[hint(block, self.block)], self.slots[step].at[:, : self.part]])

    def row_half(self):
        other = partner(self.p.row, 2)
        self.row_copy(1).wait()
        self.row_add(other, 1, self.total().at[hint(other, self.block)])
        self.row_copy(2).start()
        self.row_copy(0).wait()
        self.row_add(self.p.row, 0, self.total().at[hint(self.p.row, self.block)])

    def last_copy(self, half):
        part = self.result.at[:, hint(half, self.part)]
        return remote(part, part, self.sems, self.first + 6, {"dp": self.p.twin})

    def row_sum(self):
        self.row_copy(2).wait()
        self.row_add(self.p.row, 2, self.result.at[:, self.mine])
        self.last_copy(self.p.half).start()

    def finish(self):
        self.last_copy(self.p.half).wait_send()
        self.last_copy(1 - self.p.half).wait_recv()


SHARE_SEMS = 12


class RowsFirst(Share):
    def __init__(self, place, own, far, result, from_next, from_other, from_far, from_twin, total, slots, sems, first):
        super().__init__(place, "zyx", own, far, result, None, None, None, None, slots, sems, first)
        self.from_next, self.from_other, self.from_far, self.from_twin = from_next, from_other, from_far, from_twin
        self.parts = [[total.at[pl.ds((2 * side + n) * self.block, self.block)] for n in (0, 1)] for side in (0, 1)]

    def next_copies(self):
        target = partner(self.p.row, 1)
        rows = (target, partner(target, 2))
        return [
            remote(
                source.at[hint(rows[n], self.block)], self.from_next.at[2 * side + n], self.sems,
                self.first + 2 * side + n, {"row": target},
            )
            for side, source in enumerate((self.own, self.far))
            for n in (0, 1)
        ]

    def start(self):
        for copy in self.next_copies():
            copy.start()

    def other_copies(self):
        return [
            remote(
                self.parts[side][1], self.from_other.at[side], self.sems, self.first + 4 + side,
                {"row": partner(self.p.row, 2)},
            )
            for side in (0, 1)
        ]

    def row_half(self):
        for copy in self.next_copies():
            copy.wait()
        rows = (self.p.row, partner(self.p.row, 2))
        for n in (1, 0):
            self.block_sums([
                (self.parts[side][n], [source.at[hint(rows[n], self.block)], self.from_next.at[2 * side + n]])
                for side, source in enumerate((self.own, self.far))
            ])
            if n == 1:
                for copy in self.other_copies():
                    copy.start()

    def far_copy(self):
        return remote(self.parts[1][0], self.from_far, self.sems, self.first + 6, {"col": self.p.far})

    def row_sum(self):
        for copy in self.other_copies():
            copy.wait()
        self.block_sums([(self.parts[side][0], [self.parts[side][0], self.from_other.at[side]]) for side in (1, 0)])
        self.far_copy().start()

    def twin_copy(self):
        return remote(self.parts[0][0].at[:, self.theirs], self.from_twin, self.sems, self.first + 7, {"dp": self.p.twin})

    def far_sum(self):
        self.far_copy().wait()
        self.block_sums([(self.parts[0][0], [self.parts[0][0], self.from_far])])
        self.twin_copy().start()

    def last_copy(self, half):
        part = self.result.at[:, hint(half, self.part)]
        return remote(part, part, self.sems, self.first + 12, {"dp": self.p.twin})

    def twin_sum(self):
        self.twin_copy().wait()
        self.block_sums([(self.result.at[:, self.mine], [self.parts[0][0].at[:, self.mine], self.from_twin])])
        self.last_copy(self.p.half).start()


ROWS_FIRST_SEMS = 13


class Tally:
    def __init__(self, place, slots, axes, sems, first):
        self.slots = slots
        p = place
        peers = dict(
            row=[{"row": (p.row + step) % 4} for step in (1, 2, 3)],
            col=[{"col": p.near}, {"col": p.far}, {"col": p.corner}],
        )
        bit = 1
        while bit < p.dps:
            peers["dp%d" % bit] = [{"dp": partner(p.dp, bit)}]
            bit *= 2
        names = []
        for axis in axes:
            names += [name for name in peers if name.startswith(axis)]
        self.stages, at = [], 0
        for name in names:
            copies = [
                remote(slots.at[at], slots.at[at + 1 + n], sems, first + n, target)
                for n, target in enumerate(peers[name])
            ]
            self.stages.append((at, copies))
            at += len(copies) + 1
            first += len(copies)
        self.names, self.last, self.next_sem = names, at, first

    def send(self, n):
        for copy in self.stages[n][1]:
            copy.start()

    def add(self, n):
        at, copies = self.stages[n]
        value = self.slots[at]
        for m, copy in enumerate(copies):
            copy.wait()
            value = value + self.slots[at + 1 + m]
        self.slots[at + len(copies) + 1] = value

    def after(self, n):
        at, copies = self.stages[n]
        return at + len(copies) + 1


def tally_slots(bits, axes):
    return sum({"row": 4, "col": 4, "dp": 2 * bits}[axis] for axis in axes) + 1


def layer_kernel(
    heads, token_total,
    small_ref, joined_ref, layer_ref, up_ref, down_ref, out_ref, teacher_ref, cot_ref,
    layer_out_ref, input_grad_ref, upg_ref, dng_ref, outg_ref, joinedg_ref, vector_sum_ref,
    upg_own, upg_far, dng_own, dng_far, came_up, came_down, came_out, came_joined, other_up, other_down, other_out,
    rows_up, rows_down, rows_out, rows_joined, from_next, from_other, from_far, from_twin,
    xt_ref, nall_ref, mixed_ref, att_ref, lse_ref, jall_ref, vall_ref, early_ref, up_sums_ref,
    chip_ref, gt_ref, vt_ref, up2_ref, dn2_ref, ub2_ref, normed, gchip, bchip, give, take, middle, gres, low_ref, stage,
    grad, gfar, dout, relay, vectors, late, count, valid_ref, bias_ref, sync, sends, recvs,
):
    sems = (sends, recvs)
    f32, bf = jnp.float32, jnp.bfloat16
    p = Place()
    quarter, features = xt_ref.shape
    hidden = down_ref.shape[0]
    moved = [
        Transpose(p, layer_ref, xt_ref, relay.at[0, :, pl.ds(256 * n, 256)], sems, n * TRANSPOSE_SEMS, n, 2) for n in (0, 1)
    ]
    target = Transpose(p, grad, gt_ref, relay.at[1], sems, 2 * TRANSPOSE_SEMS)
    base = 3 * TRANSPOSE_SEMS
    back = Untranspose(p, low_ref, layer_out_ref, sems, base)
    base += 4
    w_out = Weight(p, out_ref, dn2_ref, hidden, False, "y", sems, base)
    w_up = Weight(p, up_ref, up2_ref, 0, True, "x", sems, base + WEIGHT_SEMS)
    w_downs = [
        Weight(
            p, down_ref.at[pl.ds(n * (hidden // 2), hidden // 2)], dn2_ref, n * (hidden // 2), False, "xy"[n], sems,
            base + (2 + n) * WEIGHT_SEMS,
        )
        for n in (0, 1)
    ]
    weights = [w_out, w_up] + w_downs
    base += 4 * WEIGHT_SEMS
    w_joined = Halves(p, joined_ref, jall_ref, sems, base)
    base += HALVES_SEMS
    small_base, bias_base = base, base + 4
    base += 6

    def small(step):
        part = vall_ref.at[:, hint(p.row, 256)]
        return remote(part, part, sems, small_base + step, {"row": (p.row + step) % 4})

    def small_came(step):
        part = vall_ref.at[:, hint((p.row + 4 - step) % 4, 256)]
        return remote(part, part, sems, small_base + step, {"row": (p.row + step) % 4})

    bias_far = remote(ub2_ref.at[0], ub2_ref.at[1], sems, bias_base + 1, {"col": p.far})
    counted = Tally(p, count, ("col", "dp"), sems, base)
    base = counted.next_sem
    tokens = nall_ref.shape[0]
    greet(p)
    for half in moved:
        half.start_cross()
    moved[0].send(0)
    width = layer_ref.shape[1]
    lanes = width // 128
    for n in range(6):
        for m in range(lanes):
            place = pl.ds(pl.multiple_of(p.row * width + m * 128, 128), 128)
            vall_ref[n : n + 1, place] = small_ref[lanes * n + m : lanes * n + m + 1, :]
    vall_ref[6:8, hint(p.row, width)] = jnp.zeros((2, width), f32)
    at = 6 * lanes
    for n in range(hidden // 128):
        ub2_ref[0, :, n * 128 : (n + 1) * 128] = jnp.broadcast_to(small_ref[at + n : at + n + 1, :], (8, 128))
    at += hidden // 128
    lo = low_lanes(1)
    for n in range(heads // 2):
        even, odd = (small_ref[at + 2 * n + m : at + 2 * n + m + 1, :] for m in (0, 1))
        for m, part in enumerate(
            (jnp.where(lo, even, 0.0), jnp.where(lo, swap(even), swap(odd)), jnp.where(lo, 0.0, odd))
        ):
            bias_ref[0:1, (3 * n + m) * 128 : (3 * n + m + 1) * 128] = part
    at += heads
    number = jnp.zeros((1, 128), f32)
    for n in range(tokens // 128):
        row = small_ref[at + n : at + n + 1, :]
        number = number + row
        valid_ref[n * 128 : (n + 1) * 128, :] = jnp.broadcast_to(row, (128, 128)).T.astype(bf)
    count[0] = jnp.broadcast_to(jnp.sum(number, axis=1, keepdims=True), (8, 128))
    counted.send(0)
    for step in (1, 2, 3):
        small(step).start()
    bias_far.start()
    w_out.across().start()
    w_up.across().start()
    for w in weights:
        w.own().start()
    moved[0].forward()
    moved[1].send(0)
    moved[1].forward()
    for n in range(len(counted.stages)):
        counted.add(n)
        if n + 1 < len(counted.stages):
            counted.send(n + 1)

    scale = token_total / count[counted.last, :1, :1]

    @pl.loop(0, 32)
    def _(n):
        rows = hint(n, grad.shape[0] // 32)
        factor = valid_ref[rows, :].astype(f32) * scale
        for f in range(grad.shape[1] // 128):
            cols = slice(f * 128, (f + 1) * 128)
            grad[rows, cols] = (
                cot_ref[rows, cols].astype(f32) - factor * teacher_ref[rows, cols].astype(f32)
            ).astype(bf)

    valid_base = base
    base += 1

    def valid_out():
        return pltpu.make_async_remote_copy(
            src_ref=valid_ref.at[hint(p.row, quarter)], dst_ref=vt_ref,
            send_sem=sends.at[valid_base], recv_sem=recvs.at[valid_base],
            device_id={"row": p.plane, "col": p.row}, device_id_type=MESH,
        )

    same = jnp.logical_and(p.stays, p.col == p.row)
    valid_kept = pltpu.make_async_copy(valid_ref.at[hint(p.row, quarter)], vt_ref, recvs.at[valid_base])

    for step in (1, 2, 3):
        small_came(step).wait_recv()
        small(step).wait_send()
    first = p.col * quarter

    def norm_one(n):
        rows = hint(n, 128)
        standard, _ = moments(xt_ref[rows, :].astype(f32))
        place = pl.ds(pl.multiple_of(first + n * 128, 128), 128)
        nall_ref[place, :] = (standard * vall_ref[0:1, :] + vall_ref[1:2, :]).astype(bf)

    def half_of(col, n):
        return nall_ref.at[pl.ds(pl.multiple_of(col * quarter + n * 256, 256), 256)]

    def spread_copy(col, n, number, to):
        return remote(half_of(col, n), half_of(col, n), sems, gather_base + 2 * number + n, {"col": to})

    gather_base = base
    base += 6
    to_far = [spread_copy(p.col, n, 0, p.far) for n in (0, 1)]
    to_near = [spread_copy(p.col, n, 1, p.near) for n in (0, 1)]
    far_came = [spread_copy(p.far, n, 0, p.far) for n in (0, 1)]
    near_came = [spread_copy(p.near, n, 1, p.near) for n in (0, 1)]
    pass_on = [spread_copy(p.far, n, 2, p.near) for n in (0, 1)]
    corner_came = [spread_copy(p.corner, n, 2, p.near) for n in (0, 1)]
    for n in (0, 1):
        moved[n].wait_recv()
        pl.loop(2 * n, 2 * n + 2)(norm_one)
        to_far[n].start()
        to_near[n].start()
    for step in (1, 2, 3):
        pl.semaphore_signal(sync, inc=1, device_id={"row": (p.row + step) % 4}, device_id_type=MESH)
    pl.semaphore_wait(sync, 3)
    w_joined.start()
    target.start_cross()
    for w in w_downs:
        w.across().start()

    @pl.when(jnp.logical_not(same))
    def _():
        valid_out().start()

    @pl.when(same)
    def _():
        valid_kept.start()

    def project(index, n):
        rows = pl.ds(pl.multiple_of(index * quarter + n * 256, 256), 256)
        mixed_ref[rows, :] = (nn(nall_ref[rows, :], jall_ref[...]) + bias_ref[0:1, :]).astype(bf)

    far_came[0].wait_recv()
    pass_on[0].start()
    w_joined.spread()
    for w in weights:
        w.start_along()
    far_came[1].wait_recv()
    pass_on[1].start()
    w_joined.ready()
    for came in near_came + corner_came:
        came.wait_recv()

    @pl.loop(0, tokens // 256)
    def _(n):
        project(n // 2, n % 2)

    w_out.spread()

    own_heads = att_ref.shape[1]
    blocks = tokens // BLOCK
    per_chip = blocks // 2
    share_base = base
    base += per_chip

    def chip_place(n):
        half = per_chip // 2
        return ((n // half + p.core) % 2) * half + n % half

    def share(n, i):
        return pltpu.make_async_remote_copy(
            src_ref=att_ref.at[hint(i, BLOCK)], dst_ref=chip_ref.at[hint(chip_place(n), BLOCK), pl.ds(own_heads, own_heads)],
            send_sem=sends.at[share_base + n], recv_sem=recvs.at[share_base + n],
            device_id={"col": p.far}, device_id_type=MESH,
        )

    def after(it, i):
        @pl.when(it < per_chip)
        def _():
            share(it, i).start()

        @pl.when(it >= per_chip)
        def _():
            chip_ref[hint(chip_place(it - per_chip), BLOCK), :own_heads] = att_ref[hint(i, BLOCK), :]

        for units, action in plan:
            @pl.when(it == at_units(units))
            def _():
                action()

    order = (
        [per_chip + n + 1 for n in range(per_chip)] + [n + 1 for n in range(per_chip)],
        [n + 1 for n in range(blocks)],
    )

    def at_units(units):
        found = []
        for counts in order:
            total, it = 0, 0
            for it, n in enumerate(counts):
                total += n
                if total >= units:
                    break
            found.append(it)
        return found[0] * (1 - p.chip) + found[1] * p.chip

    plan = [
        (3, lambda: w_out.spread_last()),
        (6, lambda: w_up.spread((1,))),
        (11, lambda: w_up.spread((2,))),
        (18, lambda: w_up.spread((3,))),
        (27, lambda: w_up.spread_last((1, 2))),
        (32, lambda: w_downs[0].spread((1, 2))),
    ]

    def attend(*scratch):
        attention_rows(
            heads, lambda it: (it + per_chip * (1 - p.chip)) % blocks, after,
            Slopes(heads), mixed_ref, att_ref, lse_ref, *scratch,
        )

    pairs = heads // 2
    pl.run_scoped(
        attend,
        pltpu.VMEM((heads, blocks, BLOCK, PAIR), bf), pltpu.VMEM((pairs, blocks, BLOCK, PAIR), bf),
        pltpu.VMEM((pairs, blocks, 2 * BLOCK, PAIR), bf), pltpu.VMEM((heads, BLOCK, BLOCK), f32),
        pltpu.VMEM((heads, blocks, BLOCK, BLOCK), f32), pltpu.VMEM((heads, BLOCK, PAIR), f32),
        pltpu.VMEM((heads, BLOCK, PAIR), f32), pltpu.VMEM((pairs, BLOCK, PAIR), f32),
    )

    @pl.loop(0, per_chip)
    def _(n):
        share(n, n + per_chip * (1 - p.chip)).wait_recv()

    w_up.spread_last((3,))
    w_downs[0].spread((3,))
    w_out.ready(0)
    w_out.ready(1)
    core = Chip(p, sems, base)
    base += 12
    ROWS = 256
    halves = quarter // ROWS

    def swap_rows(number, buffer, n):
        return core.copy(
            number + n, buffer.at[pl.ds(n * ROWS, ROWS)], buffer.at[pl.ds(quarter + n * ROWS, ROWS)]
        )

    def swap_came(number, buffer, n):
        part = buffer.at[pl.ds(quarter + n * ROWS, ROWS)]
        return core.copy(number + n, part, part)

    def give_rows(number, n):
        return core.copy(number + n, give.at[pl.ds(n * ROWS, ROWS)], take.at[pl.ds(n * ROWS, ROWS)])

    def take_rows(number, n):
        part = take.at[pl.ds(n * ROWS, ROWS)]
        return core.copy(number + n, part, part)

    def partial(number, keep, product, again):
        if again:
            for n in range(halves):
                give_rows(number - 4, n).wait_send()
        for n in range(halves):
            give[n * ROWS : (n + 1) * ROWS, :] = product(pl.ds(quarter + n * ROWS, ROWS)).astype(bf)
            give_rows(number, n).start()
        for n in range(halves):
            keep[n * ROWS : (n + 1) * ROWS, :] = product(pl.ds(n * ROWS, ROWS))

    partial(
        0, middle,
        lambda rows: nn(chip_ref[rows, :own_heads], dn2_ref[0, hidden:, :])
        + nn(chip_ref[rows, own_heads:], dn2_ref[1, hidden:, :]),
        False,
    )
    w_downs[1].spread()
    target.send(0)
    target.forward()
    for n in range(halves):
        take_rows(0, n).wait_recv()

        @pl.loop(0, ROWS // 64)
        def _(m):
            rows = pl.ds(pl.multiple_of(n * ROWS + m * 64, 64), 64)
            value = xt_ref[rows, :].astype(f32) + (
                middle[rows, :] + take[rows, :].astype(f32) + vall_ref[2:3, :]
            )
            middle[rows, :] = value
            standard, _ = moments(value)
            normed[rows, :] = (standard * vall_ref[3:4, :] + vall_ref[4:5, :]).astype(bf)

        swap_rows(2, normed, n).start()
    w_up.ready(0)
    bias_far.wait()

    slots = [give.at[pl.ds(256 * (n // 2), 256), pl.ds(hidden // 2 * (n % 2), hidden // 2)] for n in range(4)]
    outg_own, outg_far = (dn2_ref.at[0, :features, pl.ds(own_heads * n, own_heads)] for n in (0, 1))
    jgrad = dn2_ref.at[1, :features, : mixed_ref.shape[1]]
    low_part, high_part = pl.ds(0, hidden // 2), pl.ds(hidden // 2, hidden // 2)

    def both(ref, n):
        return [ref.at[n, :, pl.ds(hidden // 4 * m, hidden // 4)] for m in (0, 1)]

    s_down = Share(
        p, "xy", dng_own.at[:, low_part], dng_far.at[:, low_part], dng_ref.at[:, low_part], both(came_down, 0), other_down,
        rows_down, both(up2_ref, 1), slots, sems, base,
    )
    s_up = Share(
        p, "xy", upg_own.at[:, low_part], upg_far.at[:, low_part], upg_ref.at[:, low_part], both(came_up, 0), other_up,
        rows_up, both(up2_ref, 0), slots, sems, base + SHARE_SEMS,
    )
    z_down = RowsFirst(
        p, dng_own.at[:, high_part], dng_far.at[:, high_part], dng_ref.at[:, high_part], from_next.at[0], from_other.at[0],
        from_far.at[0], from_twin.at[0], up2_ref.at[1, :, high_part], slots, sems, base + 4 * SHARE_SEMS,
    )
    z_up = RowsFirst(
        p, upg_own.at[:, high_part], upg_far.at[:, high_part], upg_ref.at[:, high_part], from_next.at[1], from_other.at[1],
        from_far.at[1], from_twin.at[1], chip_ref, slots, sems, base + 4 * SHARE_SEMS + ROWS_FIRST_SEMS,
    )
    s_out = Share(
        p, "yx", outg_own, outg_far, outg_ref, came_out, other_out, rows_out,
        [dn2_ref.at[1, :features, pl.ds(768, 256)], dn2_ref.at[0, :features, pl.ds(896, 128)]], slots, sems,
        base + 2 * SHARE_SEMS,
    )
    s_joined = Share(
        p, "x", jgrad, None, joinedg_ref, came_joined, None, rows_joined,
        [dn2_ref.at[0, :features, pl.ds(512, 384)]], slots, sems, base + 3 * SHARE_SEMS,
    )
    base += 4 * SHARE_SEMS + 2 * ROWS_FIRST_SEMS

    def natural(chip, n):
        return hint(2 * chip + (p.core + n) % 2, quarter)

    att_base = base
    base += 2

    def share_grad(n):
        return remote(
            gfar.at[pl.ds(n * quarter, quarter)], dout.at[natural(p.chip, n)], sems, att_base + n, {"col": p.far}
        )

    def share_grad_came(n):
        part = dout.at[natural(1 - p.chip, n)]
        return remote(part, part, sems, att_base + n, {"col": p.far})

    stage_base = base
    base += 2

    def middle_part(act, der, keep):
        wide = 256

        def up_rows(side):
            def body(n):
                rows = hint(n, quarter)

                @pl.loop(0, hidden // wide, unroll=2)
                def _(m):
                    cols = hint(m, wide)
                    before = nn(normed[rows, :], up2_ref[side, :, cols]) + ub2_ref[side, 0:1, cols]
                    value, slope = gelu_pair(before)
                    act[side, rows, cols] = value.astype(bf)
                    der[side, rows, cols] = slope.astype(bf)

            return body

        up_rows(0)(0)
        for n in range(halves):
            swap_came(2, normed, n).wait_recv()
        up_rows(0)(1)
        w_up.ready(1)
        up_rows(1)(0)
        w_downs[0].spread_last()
        up_rows(1)(1)
        w_downs[1].spread_last()
        for w in w_downs:
            w.ready(0)
            w.ready(1)
        partial(
            4, gres,
            lambda rows: nn(act[0, rows, :], dn2_ref[0, :hidden, :]) + nn(act[1, rows, :], dn2_ref[1, :hidden, :]),
            True,
        )
        target.wait_recv()

        @pl.when(jnp.logical_not(same))
        def _():
            valid_out().wait_send()
            valid_out().wait_recv()

        @pl.when(same)
        def _():
            valid_kept.wait()

        early_ref[...] = jnp.zeros_like(early_ref)
        for n in range(halves):
            take_rows(4, n).wait_recv()

            @pl.loop(0, ROWS // 64)
            def _(m):
                rows = pl.ds(pl.multiple_of(n * ROWS + m * 64, 64), 64)
                result = middle[rows, :] + (gres[rows, :] + take[rows, :].astype(f32) + vall_ref[5:6, :])
                low_ref[rows, :] = result.astype(bf)
                factor = vt_ref[rows, :].astype(f32)[:, :1] * scale
                value = gt_ref[rows, :].astype(f32) + factor * result
                gres[rows, :] = value
                rounded = value.astype(bf)
                gchip[rows, :] = rounded
                early_ref[5:6, :] += jnp.sum(rounded.astype(f32), axis=0, keepdims=True)

            swap_rows(6, gchip, n).start()
        back.start()
        up_sums_ref[...] = jnp.zeros_like(up_sums_ref)

        def before_rows(n):
            rows = hint(n, quarter)

            @pl.loop(0, 2 * hidden // wide, unroll=2)
            def _(m):
                side, cols = m // (hidden // wide), hint(m % (hidden // wide), wide)
                value = nt(gchip[rows, :], dn2_ref[side, cols, :]) * der[side, rows, cols].astype(f32)
                rounded = value.astype(bf)
                der[side, rows, cols] = rounded
                up_sums_ref[side, 0:1, cols] += jnp.sum(rounded.astype(f32), axis=0, keepdims=True)

        def weight_grad(slot, source, values, sinks):
            @pl.loop(0, features // 512)
            def _(f):
                cols = hint(f, 512)
                turned = source[:, cols].T
                for side, sink in enumerate(sinks):
                    copy = pltpu.make_async_copy(stage.at[side], sink.at[cols], recvs.at[slot + side])

                    @pl.when(f > 0)
                    def _():
                        copy.wait()

                    stage[side] = nn(turned, values[side]).astype(bf)
                    copy.start()

            for side, sink in enumerate(sinks):
                pltpu.make_async_copy(stage.at[side], sink.at[pl.ds(0, 512)], recvs.at[slot + side]).wait()

        before_rows(0)
        for n in range(halves):
            swap_came(6, gchip, n).wait_recv()
        weight_grad(stage_base, gchip, act, (dng_own, dng_far))
        s_down.start()
        z_down.start()
        before_rows(1)
        partial(
            8, keep, lambda rows: nt(der[0, rows, :], up2_ref[0]) + nt(der[1, rows, :], up2_ref[1]), True
        )

        for n in range(halves):
            for number, buffer in ((2, normed), (6, gchip)):
                swap_rows(number, buffer, n).wait_send()
        for n in range(halves):
            take_rows(8, n).wait_recv()

            @pl.loop(0, ROWS // 64)
            def _(m):
                rows = pl.ds(pl.multiple_of(n * ROWS + m * 64, 64), 64)
                value = keep[rows, :] + take[rows, :].astype(f32)
                standard, inverse = moments(middle[rows, :])
                early_ref[3:4, :] += jnp.sum(value * standard, axis=0, keepdims=True)
                early_ref[4:5, :] += jnp.sum(value, axis=0, keepdims=True)
                scaled = value * vall_ref[3:4, :]
                one = jnp.mean(scaled, 1, keepdims=True)
                two = jnp.mean(scaled * standard, 1, keepdims=True)
                value = gres[rows, :] + inverse * (scaled - one - standard * two)
                gres[rows, :] = value
                rounded = value.astype(bf)
                bchip[rows, :] = rounded
                early_ref[2:3, :] += jnp.sum(rounded.astype(f32), axis=0, keepdims=True)

            swap_rows(10, bchip, n).start()
        for n in range(2 * halves):
            if n >= halves:
                swap_came(10, bchip, n - halves).wait_recv()
            rows = pl.ds(n * ROWS, ROWS)
            place = pl.ds(
                pl.multiple_of((2 * p.chip + (p.core + n // halves) % 2) * quarter + n % halves * ROWS, ROWS), ROWS
            )
            dout[place, :] = nt(bchip[rows, :], dn2_ref[0, hidden:, :]).astype(bf)
            gfar[rows, :] = nt(bchip[rows, :], dn2_ref[1, hidden:, :]).astype(bf)
            if n % halves == halves - 1:
                share_grad(n // halves).start()
        weight_grad(stage_base, normed, der, (upg_own, upg_far))
        s_up.start()
        z_up.start()

    pl.run_scoped(
        middle_part,
        pltpu.VMEM((2, 2 * quarter, hidden), bf), pltpu.VMEM((2, 2 * quarter, hidden), bf), pltpu.VMEM((quarter, features), f32),
    )

    for w in weights:
        w.sent()

    @pl.loop(0, features // 256)
    def _(f):
        cols = hint(f, 256)
        turned = bchip[:, cols].T
        outg_own[cols, :] = nn(turned, chip_ref[:, :own_heads]).astype(bf)
        outg_far[cols, :] = nn(turned, chip_ref[:, own_heads:]).astype(bf)

    for n in range(halves):
        give_rows(8, n).wait_send()
        swap_rows(10, bchip, n).wait_send()
    back.wait_recv()
    target.wait_send()
    fetch = pltpu.make_async_copy(layer_out_ref, grad, recvs.at[stage_base])
    fetch.start()
    fetch.wait()
    error = jnp.zeros((1, 128), f32)
    for n in range(tokens // 128):
        rows = slice(n * 128, (n + 1) * 128)
        for f in range(grad.shape[1] // 128):
            cols = slice(f * 128, (f + 1) * 128)
            off = grad[rows, cols].astype(f32) - teacher_ref[rows, cols].astype(f32)
            error = error + jnp.sum(off * off * valid_ref[rows, :].astype(f32), axis=0, keepdims=True)
    early_ref[6:7, 0:128] = error
    vectors[0, 0:8, :] = early_ref[...]
    vectors[0, 8:16, :] = jnp.zeros((8, features), f32)
    vectors[0, pl.ds(8 + p.col, 1), :] = up_sums_ref[0]
    vectors[0, pl.ds(8 + p.far, 1), :] = up_sums_ref[1]
    summed = Tally(p, vectors, ("row", "col", "dp"), sems, base)
    base = summed.next_sem
    lately = Tally(p, late, ("row", "dp", "col"), sems, base)
    base = lately.next_sem
    summed.send(0)
    for n in (0, 1):
        share_grad_came(n).wait_recv()
        share_grad(n).wait_send()
    s_out.start()


    def turn(i):
        for at, action in back_plan:
            @pl.when(i == at)
            def _():
                action()

    back_plan = [
        (2, lambda: (s_down.first_sum(), s_down.second_copy().start())),
        (3, lambda: (s_out.first_sum(), s_out.second_copy().start())),
        (4, lambda: z_down.row_half()),
        (5, lambda: (s_down.second_sum(), s_down.start_rows(), s_out.second_sum(), s_out.start_rows())),
        (6, lambda: (s_up.first_sum(), s_up.second_copy().start())),
        (7, lambda: (z_up.row_half(), z_down.row_sum(), summed.add(0), summed.send(1))),
    ]

    def attend_back(*scratch):
        attention_rows_backward(heads, turn, Slopes(heads), mixed_ref, dout, att_ref, lse_ref, mixed_ref, *scratch)

    pl.run_scoped(
        attend_back,
        pltpu.VMEM((pairs, blocks, 2 * BLOCK, PAIR), bf), pltpu.VMEM((pairs, blocks, BLOCK, PAIR), bf),
        pltpu.VMEM((pairs, blocks, 2 * BLOCK, PAIR), bf), pltpu.VMEM((pairs, blocks, BLOCK, PAIR), bf),
        pltpu.VMEM((pairs, blocks, 2 * BLOCK, PAIR), bf), pltpu.VMEM((heads, blocks, BLOCK), f32),
        pltpu.VMEM((heads, BLOCK, BLOCK), f32), pltpu.VMEM((heads, BLOCK, PAIR), f32),
        pltpu.VMEM((pairs, blocks, BLOCK, PAIR), f32), pltpu.VMEM((pairs, blocks, BLOCK, PAIR), f32),
        pltpu.VMEM((pairs, blocks, BLOCK, PAIR), f32),
    )

    @pl.loop(0, features // 128)
    def _(f):
        cols = hint(f, 128)
        jgrad[cols, :] = tn(nall_ref[:, cols], mixed_ref[...]).astype(bf)

    s_joined.start()

    sums_at = [bchip.at[pl.ds(0, quarter)], bchip.at[pl.ds(quarter, quarter)],
               normed.at[pl.ds(0, quarter)], normed.at[pl.ds(quarter, quarter)]]
    near_in = [gchip.at[pl.ds(0, quarter)], gchip.at[pl.ds(quarter, quarter)]]

    def product(index, slot):
        @pl.loop(0, quarter // 256)
        def _(n):
            rows = pl.ds(pl.multiple_of(index * quarter + n * 256, 256), 256)
            sums_at[slot][hint(n, 256), :] = nt(mixed_ref[rows, :], jall_ref[...]).astype(bf)

    grad_near = [remote(sums_at[n], near_in[n], sems, base + n, {"col": p.near}) for n in (0, 1)]
    grad_far = remote(sums_at[2], take, sems, base + 2, {"col": p.far})
    base += 3
    product(p.corner, 0)
    grad_near[0].start()
    product(p.near, 1)
    grad_near[1].start()
    product(p.far, 2)
    grad_near[0].wait()
    add_rows(sums_at[2], [sums_at[2], near_in[0]])
    grad_far.start()
    product(p.col, 3)
    s_up.second_sum()
    s_up.start_rows()
    z_down.far_sum()
    s_down.row_half()
    s_out.row_half()
    z_up.row_sum()
    sums = jnp.zeros((1, mixed_ref.shape[1]), f32)
    for n in range(tokens // 256):
        sums = sums + jnp.sum(mixed_ref[n * 256 : (n + 1) * 256, :].astype(f32), axis=0, keepdims=True)
    late[0] = jnp.zeros((8, features), f32)
    late[0, 2:3, 0 : sums.shape[1]] = sums
    s_joined.first_sum()
    s_joined.start_rows()
    s_up.row_half()
    z_down.twin_sum()
    grad_near[1].wait()
    grad_far.wait()
    gin = bchip.at[pl.ds(0, quarter)]
    grad_back = Untranspose(p, gin, input_grad_ref, sems, base)
    base += 4

    @pl.loop(0, quarter // 64)
    def _(n):
        rows = hint(n, 64)
        value = sums_at[3][rows, :].astype(f32) + near_in[1][rows, :].astype(f32) + take[rows, :].astype(f32)
        standard, inverse = moments(xt_ref[rows, :].astype(f32))
        late[0, 0:1, :] += jnp.sum(value * standard, axis=0, keepdims=True)
        late[0, 1:2, :] += jnp.sum(value, axis=0, keepdims=True)
        scaled = value * vall_ref[0:1, :]
        one = jnp.mean(scaled, 1, keepdims=True)
        two = jnp.mean(scaled * standard, 1, keepdims=True)
        gin[rows, :] = (gres[rows, :] + inverse * (scaled - one - standard * two)).astype(bf)

    lately.send(0)
    s_joined.row_half()
    grad_back.start()
    z_up.far_sum()
    s_down.row_sum()
    z_up.twin_sum()
    s_up.row_sum()
    s_out.row_sum()
    for n in range(1, len(summed.stages)):
        summed.add(n)
        if n + 1 < len(summed.stages):
            summed.send(n + 1)
    lately.add(0)
    lately.send(1)
    s_joined.row_sum()
    for n in range(1, len(lately.stages)):
        lately.add(n)
        if n + 1 < len(lately.stages):
            lately.send(n + 1)
    joined_at = lately.after(len(lately.stages) - 2)
    at = 0
    for n in range(6):
        place = hint(p.row, width)
        value = late[lately.last, n : n + 1, place] if n < 2 else vectors[summed.last, n : n + 1, place]
        for m in range(lanes):
            vector_sum_ref[at : at + 1, :] = value[:, m * 128 : (m + 1) * 128]
            at += 1
    value = vectors[summed.last, pl.ds(8 + p.col, 1), :]
    for m in range(hidden // 128):
        vector_sum_ref[at : at + 1, :] = value[:, m * 128 : (m + 1) * 128]
        at += 1
    for n in range(heads // 2):
        first, second, third = (
            late[joined_at, 2:3, (3 * n + m) * 128 : (3 * n + m + 1) * 128] for m in range(3)
        )
        vector_sum_ref[at : at + 1, :] = jnp.where(lo, first, swap(second))
        vector_sum_ref[at + 1 : at + 2, :] = jnp.where(lo, swap(second), third)
        at += 2
    value = jnp.sum(vectors[summed.last, 6:7, 0:128], axis=1, keepdims=True) * (scale * (1.0 / (features * token_total)))
    vector_sum_ref[at:, :] = jnp.broadcast_to(value, (vector_sum_ref.shape[0] - at, 128))
    for part in (s_down, s_up, z_down, z_up, s_joined, s_out):
        part.finish()
    grad_back.wait_recv()
    grad_back.wait_send()
    for n in (0, 1):
        moved[n].wait_send()
        for copies in (to_far, to_near, pass_on):
            copies[n].wait_send()
    w_joined.sent()
    back.wait_send()

    @pl.loop(0, per_chip)
    def _(n):
        share(n, n + per_chip * (1 - p.chip)).wait_send()


def layer_stage(small, joined, layer_in, up, down, out, teacher, cot, token_total):
    tokens, width = layer_in.shape
    quarter = tokens // 4
    features = width * lax.axis_size("row")
    joined_width = joined.shape[1]
    heads = joined_width // (3 * HEAD_DIM)
    blocks = tokens // BLOCK
    f32, bf = jnp.float32, jnp.bfloat16
    hidden, head_rows = down.shape[0], out.shape[0]
    vmem, anyspace = pl.BlockSpec(memory_space=pltpu.VMEM), pl.BlockSpec(memory_space=pl.ANY)
    shape = jax.ShapeDtypeStruct
    bits = 0
    while (1 << bits) < lax.axis_size("dp"):
        bits += 1
    count = (
        3 * TRANSPOSE_SEMS + 4 + 4 * WEIGHT_SEMS + HALVES_SEMS + 6 + (3 + bits) + 1 + 6 + blocks // 2 + 12
        + 4 * SHARE_SEMS + 2 * ROWS_FIRST_SEMS + 2 + 2 + 2 * (6 + bits) + 3 + 4
    )
    small_rows = 8 * ((6 * width // 128 + hidden // 128 + heads) // 8 + 1)
    outs = pl.pallas_call(
        functools.partial(layer_kernel, heads, token_total),
        out_shape=(
            shape((tokens, width), bf), shape((tokens, width), bf), shape((width, hidden), bf), shape((width, hidden), bf),
            shape((width, head_rows), bf), shape((width, joined_width), bf), shape((small_rows, 128), f32),
        ) + (shape((features, hidden), bf),) * 4 + (
            shape((1, features, hidden // 2), bf), shape((1, features, hidden // 2), bf), shape((features, head_rows), bf),
            shape((features, joined_width // 2), bf), shape((features, hidden // 4), bf), shape((features, hidden // 4), bf),
            shape((features, head_rows // 2), bf), shape((3, width, hidden // 4), bf), shape((3, width, hidden // 4), bf),
            shape((3, width, head_rows // 2), bf), shape((3, width, joined_width // 2), bf),
            shape((2, 4, width, hidden // 2), bf), shape((2, 2, width, hidden // 2), bf), shape((2, width, hidden // 2), bf),
            shape((2, width, hidden // 4), bf),
        ),
        in_specs=[vmem] + [anyspace] * 5 + [vmem] * 2,
        out_specs=(anyspace,) * 2 + (vmem,) * 5 + (anyspace,) * 19,
        scratch_shapes=[
            pltpu.VMEM((quarter, features), bf), pltpu.VMEM((tokens, features), bf), pltpu.VMEM((tokens, joined_width), bf),
            pltpu.VMEM((tokens, heads * HEAD_DIM), bf), pltpu.VMEM((heads, blocks, BLOCK), f32),
            pltpu.VMEM((features, joined_width), bf), pltpu.VMEM((8, features), f32), pltpu.VMEM((8, features), f32),
            pltpu.VMEM((2, 1, hidden), f32),
            pltpu.VMEM((2 * quarter, 2 * head_rows), bf), pltpu.VMEM((quarter, features), bf), pltpu.VMEM((quarter, 128), bf),
            pltpu.VMEM((2, features, hidden), bf), pltpu.VMEM((2, hidden + head_rows, features), bf),
            pltpu.VMEM((2, 8, hidden), f32), pltpu.VMEM((2 * quarter, features), bf), pltpu.VMEM((2 * quarter, features), bf),
            pltpu.VMEM((2 * quarter, features), bf), pltpu.VMEM((quarter, features), bf), pltpu.VMEM((quarter, features), bf),
            pltpu.VMEM((quarter, features), f32), pltpu.VMEM((quarter, features), f32), pltpu.VMEM((quarter, features), bf),
            pltpu.VMEM((2, 512, hidden), bf), pltpu.VMEM((tokens, width), bf), pltpu.VMEM((2 * quarter, head_rows), bf),
            pltpu.VMEM((tokens, head_rows), bf), pltpu.VMEM((2, 2, quarter, width), bf),
            pltpu.VMEM((tally_slots(bits, ("row", "col", "dp")), 16, features), f32),
            pltpu.VMEM((tally_slots(bits, ("row", "col", "dp")), 8, features), f32),
            pltpu.VMEM((tally_slots(bits, ("col", "dp")), 8, 128), f32),
            pltpu.VMEM((tokens, 128), bf), pltpu.VMEM((8, joined_width), f32),
            pltpu.SemaphoreType.REGULAR, pltpu.SemaphoreType.DMA((count,)), pltpu.SemaphoreType.DMA((count,)),
        ],
        compiler_params=pltpu.CompilerParams(vmem_limit_bytes=63 << 20, collective_id=1, has_side_effects=True),
        name="layer_stage",
    )(small, joined, layer_in, up, down, out, teacher, cot)
    return outs[:7]


def swap_with(value, axis, bit):
    size = lax.axis_size(axis)
    return lax.ppermute(value, axis, [(i, i ^ bit) for i in range(size)])


def low(value):
    return value.astype(jnp.bfloat16)


def sum_other_pairs(value):
    bit = 2
    while bit < lax.axis_size("dp"):
        value = value + swap_with(low(value), "dp", bit).astype(jnp.float32)
        bit *= 2
    return value


def on_device(
    layer_in,
    first_gain,
    first_shift,
    joined_weight,
    joined_bias,
    out_weight,
    out_bias,
    second_gain,
    second_shift,
    up_weight,
    up_bias,
    down_weight,
    down_bias,
    teacher,
    valid,
    cotangent,
):
    f32 = jnp.float32
    token_total = layer_in.shape[0] * lax.axis_size("dp") * lax.axis_size("col")
    arrays = (
        first_gain, first_shift, out_bias, second_gain, second_shift, down_bias, up_bias, joined_bias.reshape(-1), valid,
    )
    rows, at = sum(a.size for a in arrays), 0
    small = jnp.zeros((rows,), f32)
    for a in arrays:
        small = small + jnp.pad(a.astype(f32), (at, rows - at - a.size))
        at += a.size
    small = small.reshape(-1, 128)
    layer_out, input_grad, up_grad, down_grad, out_grad, joined_grad, sums = layer_stage(
        small, joined_weight, layer_in, up_weight, down_weight, out_weight, teacher, cotangent, token_total
    )
    up_grad, down_grad, out_grad, joined_grad = (
        sum_other_pairs(g.astype(f32)) for g in (up_grad, down_grad, out_grad, joined_grad)
    )
    sums = sums.reshape(-1)
    pieces, at = [], 0
    for size in [layer_in.shape[1]] * 6 + [up_bias.shape[0], joined_bias.size, 1]:
        pieces.append(sums[at : at + size])
        at += size
    return (
        layer_out,
        pieces[8][0],
        input_grad.astype(f32),
        pieces[0],
        pieces[1],
        joined_grad,
        pieces[7].reshape(joined_bias.shape),
        out_grad.T,
        pieces[2],
        pieces[3],
        pieces[4],
        up_grad,
        pieces[6],
        down_grad.T,
        pieces[5],
    )


def solution(mesh):
    return jax.shard_map(
        on_device,
        mesh=mesh,
        in_specs=(
            P(("dp", "col"), "row"),
            P("row"),
            P("row"),
            P("row", "col"),
            P("col", None),
            P("col", "row"),
            P("row"),
            P("row"),
            P("row"),
            P("row", "col"),
            P("col"),
            P("col", "row"),
            P("row"),
            P(("dp", "col"), "row"),
            P(("dp", "col")),
            P(("dp", "col"), "row"),
        ),
        out_specs=(
            P(("dp", "col"), "row"),
            P(),
            P(("dp", "col"), "row"),
            P("row"),
            P("row"),
            P("row", "col"),
            P("col", None),
            P("col", "row"),
            P("row"),
            P("row"),
            P("row"),
            P("row", "col"),
            P("col"),
            P("col", "row"),
            P("row"),
        ),
        check_vma=False,
    )
```
